256 devices in a mesh: depth: 32 (over y, z), lat: 8 (over x, core).
Axes of the slice: x: 4, y: 4, z: 8, core: 2. Of those that a mesh axis runs over, the one named last changes fastest.
Arguments:
- densities: float32 [8, 1024, 64], P('lat', 'depth'), may hold values from -6 to 6
- source: float32 [8, 1024, 64], P('lat', 'depth'), may hold values from -6 to 6
- jacobian: float32 [8, 1024, 4096], P('lat', 'depth'), may hold values from -0.75 to 0.75
- pattern: int32 [8, 8], replicated, may hold values 0 or 1
- transport: float32 [8, 1024, 64], P('lat', 'depth'), may hold values from 0.2 to 1
- lateral: float32 [8, 1024, 64], P('lat', 'depth'), may hold values from 0.1 to 1
- neighbours: int32 [8, 4], P('lat'), may hold values from 0 to 7, as said below
- factor: float32 [8, 1024, 4096], P('lat', 'depth'), may hold values from -6.1035156e-05 to 0.00012207031
- coupling: float32 [8, 1024, 64], P('lat', 'depth'), may hold values from 8192 to 32768
Outputs:
- correction: float32 [8, 1024, 64], P('lat', 'depth')
The draws below stay inside these ranges and needn't reach their ends.
Inputs may be any that keep to these rules, and one draw needn't show every extreme that they name: Each line's four neighbours (previous row, next row, previous place, next place) in a periodic arrangement of the lines in rows of 8, under a relabelling of the lines drawn from the seed.
All inputs are finite; a program needn't handle non-finite values.
Results may differ from the reference program's by a relative error of at most 0.0003.
Values sent between devices are 32-bit elements; how exact they have to be, the bound alone decides.
No kernel may reach another device: no remote copies, remote signals or barrier semaphores. Data moves between devices by JAX's collectives and lax.ppermute only.
A program may use at most 128 MiB of HBM per device.

```python
import math
import jax
import jax.numpy as jnp
from jax import lax

SPECIES = 64
TILE = 8
NTILE = 8
LATERAL_LINES = 8
DEPTH_CELLS = 1024
LINES_PER_ROW = 8


def factor_parts(key):
    base = jax.random.fold_in(key, 4101)
    random_keys = jax.random.split(base, 7)
    share = 0.5
    slow = jax.random.bernoulli(random_keys[0], share, (LATERAL_LINES, 1, SPECIES))
    fast_rate = jnp.exp(-1.0 / jax.random.uniform(random_keys[1], (LATERAL_LINES, 1, SPECIES), jnp.float32, 30.0, 50.0))
    slow_rate = jnp.exp(jnp.log(jax.random.uniform(random_keys[2], (LATERAL_LINES, 1, SPECIES), jnp.float32, 0.3, 0.6)) / DEPTH_CELLS)
    rate = jnp.where(slow, slow_rate, fast_rate)
    damaged_cells = jax.random.randint(random_keys[3], (3,), 0, DEPTH_CELLS)
    impacted_lines = jnp.zeros((DEPTH_CELLS,), jnp.float32).at[damaged_cells].set(1.0)
    losses = jax.random.uniform(random_keys[4], (LATERAL_LINES, 1, SPECIES), jnp.float32, 0.5, 0.8)
    hitting = jnp.logical_and(slow, impacted_lines[None, :, None] > 0.5)
    rate = rate * jnp.where(hitting, losses, 1.0)
    spread = 1.4 / math.sqrt(SPECIES * DEPTH_CELLS)
    mixing = jnp.clip(jax.random.normal(random_keys[5], (LATERAL_LINES, DEPTH_CELLS, SPECIES, SPECIES), jnp.float32), -6.0, 6.0) * spread
    identity = jnp.eye(SPECIES, dtype=jnp.float32)
    matrix = mixing * (1.0 - identity) + identity * rate[..., None]
    lowest = float(DEPTH_CELLS * DEPTH_CELLS // 128)
    highest = float(DEPTH_CELLS * DEPTH_CELLS // 32)
    coupling = jnp.exp(jax.random.uniform(random_keys[6], (LATERAL_LINES, DEPTH_CELLS, SPECIES), jnp.float32, math.log(lowest), math.log(highest)))
    inverse = matrix / coupling[:, :, None, :]
    return (inverse.reshape(LATERAL_LINES, DEPTH_CELLS, SPECIES * SPECIES), coupling)


def draw_factor(key, part):
    inverse, coupling = factor_parts(key)
    return inverse


def draw_coupling(key, part):
    inverse, coupling = factor_parts(key)
    return coupling


def draw_neighbours(key, part):
    line_labels = jax.random.permutation(jax.random.fold_in(key, 77), LATERAL_LINES).astype(jnp.int32)
    line_position = jnp.arange(LATERAL_LINES, dtype=jnp.int32)
    lateral_row_count = LATERAL_LINES // LINES_PER_ROW
    lateral_row_index = line_position // LINES_PER_ROW
    slot_index = line_position % LINES_PER_ROW

    def label_at(lateral_row_value, slot_value):
        return line_labels[lateral_row_value % lateral_row_count * LINES_PER_ROW + slot_value % LINES_PER_ROW]
    by_position = jnp.stack([label_at(lateral_row_index - 1, slot_index), label_at(lateral_row_index + 1, slot_index), label_at(lateral_row_index, slot_index - 1), label_at(lateral_row_index, slot_index + 1)], axis=1)
    table = jnp.zeros((LATERAL_LINES, 4), jnp.int32).at[line_labels].set(by_position)
    return table.astype(jnp.int32)


def plant(values, stream_key, least, largest):
    extent = values.shape
    index_at = [jax.random.randint(jax.random.fold_in(stream_key, axis), (), 0, extent[axis]) for axis in range(len(extent))]
    values = values.at[tuple(index_at)].set(least)
    longest = extent.index(max(extent))
    index_at[longest] = (index_at[longest] + 1) % extent[longest]
    return values.at[tuple(index_at)].set(largest)


def shard_levels(own_key, dims, cuts, low, top_value):
    gain = 1.0
    for dim, blocks in cuts:
        draws = jax.random.uniform(jax.random.fold_in(jax.random.fold_in(own_key, 6), dim), (blocks,), jnp.float32, low / len(cuts), top_value / len(cuts))
        gain = gain * jnp.repeat(jnp.exp(draws), dims[dim] // blocks).reshape((-1,) + (1,) * (len(dims) - 1 - dim))
    return gain


def normal_values(key, extent, scale, limit, shards=(), kind=jnp.bfloat16):
    level = shard_levels(key, extent, shards, -0.22, 0.18) if shards else 1.0
    drawn = jax.random.normal(key, extent, jnp.float32) * scale * level
    return jnp.minimum(jnp.maximum(drawn, -limit), limit).astype(kind)


def setup_inputs(seed: int = 0) -> dict:
    splits = jax.random.split(jax.random.key(seed), 10)
    densities = normal_values(splits[0], (LATERAL_LINES, DEPTH_CELLS, SPECIES), 1.0, 6.0, ((0, 8), (1, 32)), jnp.float32)
    source = normal_values(splits[1], (LATERAL_LINES, DEPTH_CELLS, SPECIES), 1.0, 6.0, ((0, 8), (1, 32)), jnp.float32)
    jacobian = normal_values(splits[2], (LATERAL_LINES, DEPTH_CELLS, SPECIES * SPECIES), SPECIES ** -0.5, 0.75, ((0, 8), (1, 32)), jnp.float32)
    pattern = plant((jax.random.randint(splits[3], (NTILE, NTILE), 0, 2) < 1).astype(jnp.int32), jax.random.fold_in(splits[3], 1), 0, 1)
    transport = jnp.clip(jnp.exp(math.log(1.0) - 1.609438 * jax.random.uniform(splits[4], (LATERAL_LINES, DEPTH_CELLS, SPECIES), jnp.float32) ** shard_levels(splits[4], (LATERAL_LINES, DEPTH_CELLS, SPECIES), ((0, 8), (1, 32)), -0.2, 0.2)), 0.2, 1.0)
    lateral = jnp.clip(jnp.exp(math.log(1.0) - 2.3025851 * jax.random.uniform(splits[5], (LATERAL_LINES, DEPTH_CELLS, SPECIES), jnp.float32) ** shard_levels(splits[5], (LATERAL_LINES, DEPTH_CELLS, SPECIES), ((0, 8), (1, 32)), -0.2, 0.2)), 0.1, 1.0)
    neighbours = draw_neighbours(jax.random.fold_in(splits[9], 71), 0)
    factor = draw_factor(jax.random.fold_in(splits[9], 71), 0)
    coupling = draw_coupling(jax.random.fold_in(splits[9], 71), 0)
    return {"densities": densities, "source": source, "jacobian": jacobian, "pattern": pattern, "transport": transport, "lateral": lateral, "neighbours": neighbours, "factor": factor, "coupling": coupling}


def reference(densities, source, jacobian, pattern, transport, lateral, neighbours, factor, coupling):
    highest = lax.Precision.HIGHEST
    mask = jnp.repeat(jnp.repeat(pattern, TILE, axis=0), TILE, axis=1).astype(jnp.float32)
    neighbour_sum = jnp.sum(densities[neighbours], axis=1)

    def one_line(line_items):
        line_dens, line_source, line_jac, line_trans, line_lat, line_nsum, line_factor, line_coup = line_items
        blocks = line_jac.reshape(DEPTH_CELLS, SPECIES, SPECIES) * mask
        reaction = jnp.einsum("kij,kj->ki", blocks, line_dens, precision=highest)
        flux = line_trans * line_dens
        zero_row = jnp.zeros((1, SPECIES), jnp.float32)
        lower_flux = jnp.concatenate([zero_row, flux[:-1]], axis=0)
        upper_cells = jnp.concatenate([line_dens[1:], zero_row], axis=0)
        operator = reaction - lower_flux - line_trans * upper_cells + line_lat * (4.0 * line_dens - line_nsum)
        residual = line_source - operator
        inverse = line_factor.reshape(DEPTH_CELLS, SPECIES, SPECIES)

        def forward(passed, inputs):
            matrix, rhs_vals, coup_vals = inputs
            value = jnp.dot(matrix, rhs_vals + passed, precision=highest)
            return coup_vals * value, value

        start = jnp.zeros((SPECIES,), jnp.float32)
        unused, forward_vals = lax.scan(forward, start, (inverse, residual, line_coup))

        def backward(after, inputs):
            matrix, fwd_vals, coup_vals = inputs
            value = fwd_vals + jnp.dot(matrix, coup_vals * after, precision=highest)
            return value, value

        unused_two, correction = lax.scan(backward, start, (inverse, forward_vals, line_coup), reverse=True)
        return correction

    return lax.map(one_line, (densities, source, jacobian, transport, lateral, neighbour_sum, factor, coupling))
```

```python
import jax
import jax.numpy as jnp
from jax import lax
from jax.experimental import pallas as pl
from jax.experimental.pallas import tpu as pltpu
from jax.sharding import PartitionSpec as P

f32 = jnp.float32
bf16 = jnp.bfloat16

CELLS = 32
N = 64
ZS = 8
VLIM = 16 << 20


def lanes(shape):
    return lax.broadcasted_iota(jnp.int32, shape, len(shape) - 1)


def roll(x, shift):
    shift = shift % x.shape[-1]
    return x if shift == 0 else pltpu.roll(x, shift, x.ndim - 1)


def pack(dup):
    hi = dup.astype(bf16).astype(f32)
    return jnp.where(lanes(dup.shape) < N, hi, dup - hi).astype(bf16)


def mm(a, b):
    r = jnp.dot(a, jnp.concatenate([b, b], axis=0), preferred_element_type=f32)
    return r + roll(r, N)


def rhs(x):
    hi = x.astype(bf16).astype(f32)
    y = jnp.where((lanes(x.shape) // CELLS) % 2 == 0, hi, x - hi).astype(bf16)
    return jnp.concatenate([y, y], axis=0)


def fold(r):
    return r + roll(r, CELLS)


def mv(a, x):
    return fold(jnp.dot(a, rhs(x), preferred_element_type=f32))


def stage(mats, x):
    y = rhs(x)
    lane = lanes((N, 128)) % CELLS
    acc = jnp.zeros((N, 128), f32)
    for at, load in mats:
        acc = jnp.where(lane == at, jnp.dot(load(), y, preferred_element_type=f32), acc)
    return fold(acc)


def dup4(x):
    return jnp.concatenate([x, x, x, x], axis=0).T


def eye2():
    return jnp.where(lanes((N, 128)) % N == lax.broadcasted_iota(jnp.int32, (N, 128), 0), 1.0, 0.0)


def put(node, full, j, p, q, w):
    node[j, 0], node[j, 1], node[j, 2] = pack(p), pack(q), pack(w)
    full[j, 0], full[j, 1], full[j, 2] = p, q, w


def tree_leaves(fac_ref, coup_ref, leaf_ref, n1_ref, full_ref, rows):
    c = coup_ref[...]
    c2 = jnp.concatenate([c, c], axis=1)
    low = lanes((CELLS, 128)) < N
    eye = eye2()

    def leaf(k):
        g, s = divmod(k, 8)
        x = fac_ref[pl.ds(g * 256 + s, 32, stride=8), :]
        y = roll(x, N)
        rows[k % 2, pl.ds(0, 32, stride=2), :] = jnp.where(low, x, y)
        rows[k % 2, pl.ds(1, 32, stride=2), :] = jnp.where(low, y, x)
        a = rows[k % 2]
        leaf_ref[k] = pack(a)
        before = max(k - 1, 0)
        return a * c2[before : before + 1] - eye, a * c2[k : k + 1] - eye

    for j in range(CELLS // 2):
        p1, q1 = leaf(2 * j)
        p2, q2 = leaf(2 * j + 1)
        kq1 = pack(q1)
        p = p1 + p2 + mm(pack(p2), pack(p1))
        q = q1 + q2 + mm(kq1, pack(q2))
        w = (eye + eye) + p1 + q1 + p + mm(kq1, pack(p))
        put(n1_ref, full_ref, j, p, q, w)


def tree_upper(n1_ref, full_ref, n2_ref, n3_ref, n4_ref, root_ref, fa, fb):
    node, full = n1_ref, full_ref
    for count, node_to, full_to in ((8, n2_ref, fa), (4, n3_ref, fb), (2, n4_ref, fa), (1, None, None)):
        for j in range(count):
            one, two = 2 * j, 2 * j + 1
            kp1, kq1 = node[one, 0], node[one, 1]
            p = full[one, 0] + full[two, 0] + mm(node[two, 0], kp1)
            t = full[two, 2] + mm(node[two, 2], kp1)
            q = full[one, 1] + full[two, 1] + mm(kq1, node[two, 1])
            w = full[one, 2] + t + mm(kq1, pack(t))
            if node_to is None:
                eye = eye2()
                root_ref[:N] = jnp.where(lanes((N, 128)) < N, p, q) + eye
                root_ref[N:] = w
            else:
                put(node_to, full_to, j, p, q, w)
        node, full = node_to, full_to


def react(jac_ref, dens_ref, src_ref, tran_ref, pat_ref, top_ref, out_ref):
    u = dens_ref[...]
    u2 = jnp.concatenate([u, u], axis=1)
    lane8 = lanes((8, 128))
    pat = pat_ref[...].astype(f32)
    mask_rows = jnp.zeros((8, 128), f32)
    for t in range(8):
        mask_rows = jnp.where((lane8 % N) // 8 == t, pat[:, t : t + 1], mask_rows)
    half = lanes((128, N)) % 2 == lax.broadcasted_iota(jnp.int32, (128, N), 0) // N
    half = jnp.where(half, 1.0, 0.0).astype(bf16)
    lane = lanes((CELLS, N))
    acc = jnp.zeros((CELLS, N), f32)
    for m in range(32):
        y = jac_ref[:, m * 128 : (m + 1) * 128] * (u2 * mask_rows[m // 4 : m // 4 + 1])
        hi = y.astype(bf16)
        lo = (y - hi.astype(f32)).astype(bf16)
        z = jnp.dot(hi, half, preferred_element_type=f32) + jnp.dot(lo, half, preferred_element_type=f32)
        acc = jnp.where(lane // 2 == m, z, acc)
    tran = tran_ref[...]
    flux = tran * u
    row = lax.broadcasted_iota(jnp.int32, (CELLS, N), 0)
    lower = jnp.where(row == 0, 0.0, pltpu.roll(flux, 1, 0))
    upper = jnp.where(row == CELLS - 1, top_ref[0:1], pltpu.roll(u, CELLS - 1, 0))
    out_ref[...] = src_ref[...] - acc + lower + tran * upper


def upsweep(neigh_ref, part_ref, lines_ref, dens_ref, tran_ref, lat_ref, coup_ref, leaf_ref, n1_ref, n2_ref,
            n3_ref, n4_ref, root_ref, pay_ref, vec_ref):
    me = lax.axis_index("lat")
    u = dens_ref[...]
    total = jnp.zeros((CELLS, N), f32)
    for slot, offset in enumerate((0, 1, 2, 3, 6, 7, 4, 5)):
        line = me ^ offset
        count = jnp.int32(0)
        for j in range(4):
            count = count + (neigh_ref[0, j] == line).astype(jnp.int32)
        total = total + count.astype(f32) * lines_ref[slot]
    r_rows = part_ref[...] - lat_ref[...] * (4.0 * u - total)
    r = dup4(r_rows)
    coup = dup4(coup_ref[...])
    lane = lanes((N, 128)) % CELLS
    prev = jnp.where(lane == 0, coup, roll(coup, 1))
    even = [(2 * j, lambda j=j: leaf_ref[2 * j]) for j in range(16)]
    odd = [(2 * j + 1, lambda j=j: leaf_ref[2 * j + 1]) for j in range(16)]
    first = stage(even, r)
    v = stage(odd, r + prev * roll(first, 1))
    w = stage(even, r + coup * roll(v, -1))
    vec_ref[0] = r
    vec_ref[1] = coup
    vec_ref[2] = v
    vec_ref[3] = w
    at = 4
    for h, ref in ((2, n1_ref), (4, n2_ref), (8, n3_ref), (16, n4_ref)):
        count = CELLS // (2 * h)
        v1 = roll(v, 1)
        vs = roll(v, h)
        new_v = v + vs + stage([(2 * h * (j + 1) - 1, lambda j=j, ref=ref: ref[2 * j + 1, 0]) for j in range(count)], vs)
        t = w + stage([(2 * h * j + h, lambda j=j, ref=ref: ref[2 * j + 1, 2]) for j in range(count)], v1)
        ts = roll(t, -h)
        w = w + ts + stage([(2 * h * j, lambda j=j, ref=ref: ref[2 * j, 1]) for j in range(count)], ts)
        v = new_v
        if h < 16:
            vec_ref[at] = v
            vec_ref[at + 1] = w
            at += 2
    last = coup[:, CELLS - 1 : CELLS]
    flux = dup4(tran_ref[...] * u)[:, CELLS - 1 : CELLS]
    low = lanes((N, 128)) < N
    top = root_ref[:N]
    first_c = coup_ref[0:1]
    scale = 1.0 / jnp.concatenate([first_c, first_c], axis=1)
    pay_ref[:N] = jnp.where(low, top * last * scale, top)
    out_v = v[:, CELLS - 1 : CELLS] * last + flux
    tail = jnp.where(lanes((N, 128)) == N, out_v, w[:, 0:1])
    pay_ref[N:] = jnp.where(low, root_ref[N:] * scale, tail)


def unpack(b):
    low = lanes((N, 128)) < N
    b1, b2 = b[:N], b[N:]
    r1, r2 = roll(b1, N), roll(b2, N)
    x = jnp.where(low, b1, r1)
    y = jnp.where(low, r1, b1)
    z = jnp.where(low, b2, r2)
    g = jnp.broadcast_to(b2[:, N : N + 1], (N, 128))
    h = jnp.broadcast_to(b2[:, N + 1 : N + 2], (N, 128))
    return x, y, z, g, h


def repack(ref, x, y, z, g, h):
    lane = lanes((N, 128))
    low = lane < N
    ref[:N] = jnp.where(low, x, y)
    ref[N:] = jnp.where(low, z, jnp.where(lane == N, g, h))


def combine(level, *refs):
    if level == 0:
        own_ref, other_ref, out_ref, fun_out = refs
    else:
        own_ref, other_ref, fun_ref, out_ref, fun_out = refs
    z = lax.axis_index("depth") % ZS
    is_low = ((z // (1, 2, 4)[level]) % 2) == 0
    own, other = own_ref[...], other_ref[...]
    p1, q1, w1, v1, h1 = unpack(jnp.where(is_low, own, other))
    p2, q2, w2, v2, h2 = unpack(jnp.where(is_low, other, own))
    kp1, kq1, kp2, kq2, kw2 = pack(p1), pack(q1), pack(p2), pack(q2), pack(w2)
    t = mm(kw2, kp1)
    th = h2 + mv(kw2, v1)
    p = mm(kp2, kp1)
    v = v2 + mv(kp2, v1)
    q = mm(kq1, kq2)
    kt = pack(t)
    w = w1 + mm(kq1, kt)
    h = h1 + mv(kq1, th)
    repack(out_ref, p, q, w, v, h)
    if level == 0:
        lane = lanes((N, 128))
        eye = jnp.where(lane % N == lax.broadcasted_iota(jnp.int32, (N, 128), 0), 1.0, 0.0)
        repack(
            fun_out,
            jnp.where(is_low, eye, p1),
            jnp.where(is_low, q2, eye),
            jnp.where(is_low, t, 0.0),
            jnp.where(is_low, 0.0, v1),
            jnp.where(is_low, th, 0.0),
        )
    else:
        f, hh, k, g, e = unpack(fun_ref[...])
        kf, kh, kk = pack(f), pack(hh), pack(k)
        x1 = jnp.where(is_low, hh, f)
        kx1 = pack(x1)
        y1 = pack(jnp.where(is_low, q2, p1))
        x2 = pack(jnp.where(is_low, hh, k))
        y2 = pack(jnp.where(is_low, t, p1))
        prod1 = mm(kx1, y1)
        prod2 = mm(x2, y2)
        vec2 = mv(x2, jnp.where(is_low, th, v1))
        vec1 = mv(kf, v1)
        repack(
            fun_out,
            jnp.where(is_low, f, prod1),
            jnp.where(is_low, prod1, hh),
            jnp.where(is_low, k + prod2, prod2),
            jnp.where(is_low, g, g + vec1),
            e + vec2,
        )


def downsweep(own_ref, y1_ref, y3_ref, y2_ref, fun_ref, vec_ref, leaf_ref, n1_ref, n2_ref, n3_ref, n4_ref,
              out_ref, slots):
    yi = lax.axis_index("depth") // ZS
    slots[yi] = own_ref[...]
    slots[yi ^ 1] = y1_ref[...]
    slots[yi ^ 3] = y3_ref[...]
    slots[yi ^ 2] = y2_ref[...]
    f, hh, k, g, e = unpack(fun_ref[...])
    maps = [unpack(slots[i]) for i in range(4)]
    s1 = maps[0][3]
    s2 = mv(pack(maps[1][0]), s1) + maps[1][3]
    s3 = mv(pack(maps[2][0]), s2) + maps[2][3]
    a2 = mv(pack(maps[3][2]), s3) + maps[3][4]
    a1 = mv(pack(maps[2][1]), a2) + mv(pack(maps[2][2]), s2) + maps[2][4]
    a0 = mv(pack(maps[1][1]), a1) + mv(pack(maps[1][2]), s1) + maps[1][4]
    s = jnp.where(yi == 0, 0.0, jnp.where(yi == 1, s1, jnp.where(yi == 2, s2, s3)))
    a = jnp.where(yi == 3, 0.0, jnp.where(yi == 2, a2, jnp.where(yi == 1, a1, a0)))
    s_in = mv(pack(f), s) + g
    a_in = mv(pack(hh), a) + mv(pack(k), s) + e
    lane = lanes((N, 128)) % CELLS
    r, coup = vec_ref[0], vec_ref[1]
    prev = jnp.where(lane == 0, coup, roll(coup, 1))
    ss, aa = s_in / coup[:, 0:1], a_in
    at = 8
    for h, ref in ((16, n4_ref), (8, n3_ref), (4, n2_ref), (2, n1_ref)):
        count = CELLS // (2 * h)
        v, w = vec_ref[at], vec_ref[at + 1]
        at -= 2
        x1 = stage([(2 * h * j, lambda j=j, ref=ref: ref[2 * j, 0]) for j in range(count)], ss)
        x2 = stage([(2 * h * (j + 1) - 1, lambda j=j, ref=ref: ref[2 * j + 1, 1]) for j in range(count)], aa)
        mid = lane % (2 * h) == h
        ss = jnp.where(mid, roll(ss + x1, h) + roll(v, 1), ss)
        x3 = stage([(2 * h * j + h, lambda j=j, ref=ref: ref[2 * j + 1, 2]) for j in range(count)], ss)
        z = roll(aa + x2, -(h - 1)) + x3 + w
        aa = jnp.where(lane % (2 * h) == h - 1, roll(z, -1), aa)
    even = [(2 * j, lambda j=j: leaf_ref[2 * j]) for j in range(16)]
    odd = [(2 * j + 1, lambda j=j: leaf_ref[2 * j + 1]) for j in range(16)]
    base = r + prev * ss
    f1 = stage(even, base)
    x2 = stage(odd, r + prev * roll(f1, 1) + coup * aa)
    x1 = stage(even, base + coup * roll(x2, -1))
    x = jnp.where(lane % 2 == 0, x1, x2)
    out_ref[...] = x.T[:CELLS]


def sds(*shape, dtype=f32):
    return jax.ShapeDtypeStruct(shape, dtype)


def vmem():
    return pl.BlockSpec(memory_space=pltpu.VMEM)


def call(body, outs, n_in, *args, scratch=(), smem=0, flops=0, moved=0, name=None):
    return pl.pallas_call(
        body,
        out_shape=outs,
        in_specs=[pl.BlockSpec(memory_space=pltpu.SMEM)] * smem + [vmem()] * (n_in - smem),
        out_specs=jax.tree.map(lambda _: vmem(), outs),
        scratch_shapes=scratch,
        cost_estimate=pl.CostEstimate(flops=flops, bytes_accessed=moved, transcendentals=0),
        name=name,
        compiler_params=pltpu.CompilerParams(vmem_limit_bytes=VLIM),
    )(*args)


def on_device(densities, source, jacobian, pattern, transport, lateral, neighbours, factor, coupling):
    line_count, cell_count, species = densities.shape
    u = densities.reshape(CELLS, N)
    src = source.reshape(CELLS, N)
    tran = transport.reshape(CELLS, N)
    lat = lateral.reshape(CELLS, N)
    coup = coupling.reshape(CELLS, N)
    jac = jacobian.reshape(CELLS, N * N)
    fac = factor.reshape(4, 8, 32, 128).transpose(0, 2, 1, 3).reshape(1024, 128)

    def xor_lat(value, bits):
        return lax.ppermute(value, "lat", [(i, i ^ bits) for i in range(8)])

    def xor_depth(value, bits):
        return lax.ppermute(value, "depth", [(i, i ^ bits) for i in range(32)])

    top = lax.ppermute(u[0:8], "depth", [(i + 1, i) for i in range(31)])
    lines = u[None]
    lines = jnp.concatenate([lines, xor_lat(lines, 1)], axis=0)
    lines = jnp.concatenate([lines, xor_lat(lines, 2)], axis=0)
    lines = jnp.concatenate([lines, xor_lat(lines, 6)], axis=0)

    leaf, n1, full = call(
        tree_leaves,
        (sds(CELLS, N, 128, dtype=bf16), sds(16, 3, N, 128, dtype=bf16), sds(16, 3, N, 128)),
        2, fac, coup,
        scratch=[pltpu.VMEM((2, N, 128), f32)], flops=2 << 30, moved=1 << 21, name="tree_leaves",
    )
    n2, n3, n4, root = call(
        tree_upper,
        (sds(8, 3, N, 128, dtype=bf16), sds(4, 3, N, 128, dtype=bf16), sds(2, 3, N, 128, dtype=bf16), sds(128, 128)),
        2, n1, full,
        scratch=[pltpu.VMEM((8, 3, N, 128), f32), pltpu.VMEM((4, 3, N, 128), f32)],
        flops=2 << 30, moved=1 << 21, name="tree_upper",
    )
    part = call(react, sds(CELLS, N), 6, jac, u, src, tran, pattern, top, flops=1 << 30, moved=1 << 19, name="react")
    pay, vec = call(
        upsweep, (sds(128, 128), sds(10, N, 128)), 13,
        neighbours, part, lines, u, tran, lat, coup, leaf, n1, n2, n3, n4, root,
        smem=1, flops=1 << 25, moved=1 << 20, name="upsweep",
    )
    fun = None
    for level, bits in enumerate((1, 2, 7)):
        other = xor_depth(pay, bits)
        args = (pay, other) if level == 0 else (pay, other, fun)
        pay, fun = call(
            lambda *refs, level=level: combine(level, *refs), (sds(128, 128), sds(128, 128)), len(args), *args,
            flops=1 << 24, moved=1 << 18, name=f"combine{level}",
        )
    y1, y3, y2 = xor_depth(pay, 8), xor_depth(pay, 24), xor_depth(pay, 16)
    out = call(
        downsweep, sds(CELLS, N), 11, pay, y1, y3, y2, fun, vec, leaf, n1, n2, n3, n4,
        scratch=[pltpu.VMEM((4, 128, 128), f32)], flops=1 << 25, moved=1 << 20, name="downsweep",
    )
    return out.reshape(line_count, cell_count, species)


def solution(mesh):
    return jax.shard_map(
        on_device,
        mesh=mesh,
        in_specs=(
            P("lat", "depth", None),
            P("lat", "depth", None),
            P("lat", "depth", None),
            P(),
            P("lat", "depth", None),
            P("lat", "depth", None),
            P("lat", None),
            P("lat", "depth", None),
            P("lat", "depth", None),
        ),
        out_specs=P("lat", "depth", None),
        check_vma=False,
    )
```

```python
import jax
import jax.numpy as jnp
from jax import lax
from jax.experimental import pallas as pl
from jax.experimental.pallas import tpu as pltpu
from jax.sharding import PartitionSpec as P

f32 = jnp.float32
bf16 = jnp.bfloat16

CELLS = 32
N = 64
ZS = 8
VLIM = 16 << 20


def lanes(shape):
    return lax.broadcasted_iota(jnp.int32, shape, len(shape) - 1)


def roll(x, shift):
    shift = shift % x.shape[-1]
    return x if shift == 0 else pltpu.roll(x, shift, x.ndim - 1)


def pack(dup):
    hi = dup.astype(bf16).astype(f32)
    return jnp.where(lanes(dup.shape) < N, hi, dup - hi).astype(bf16)


def mm(a, b):
    r = jnp.dot(a, jnp.concatenate([b, b], axis=0), preferred_element_type=f32)
    return r + roll(r, N)


def rhs(x):
    hi = x.astype(bf16).astype(f32)
    y = jnp.where((lanes(x.shape) // CELLS) % 2 == 0, hi, x - hi).astype(bf16)
    return jnp.concatenate([y, y], axis=0)


def fold(r):
    return r + roll(r, CELLS)


def mv(a, x):
    return fold(jnp.dot(a, rhs(x), preferred_element_type=f32))


def stage(mats, x):
    y = rhs(x)
    lane = lanes((N, 128)) % CELLS
    acc = jnp.zeros((N, 128), f32)
    for at, load in mats:
        acc = jnp.where(lane == at, jnp.dot(load(), y, preferred_element_type=f32), acc)
    return fold(acc)


def dup4(x):
    return jnp.concatenate([x, x, x, x], axis=0).T


def eye2():
    return jnp.where(lanes((N, 128)) % N == lax.broadcasted_iota(jnp.int32, (N, 128), 0), 1.0, 0.0)


def put(node, full, j, p, q, w, u):
    node[j, 0], node[j, 1], node[j, 2], node[j, 3] = pack(p), pack(q), pack(w), pack(u)
    full[j, 0], full[j, 1], full[j, 2] = p, q, w


def tree_leaves(fac_ref, coup_ref, after_ref, leaf_ref, n1_ref, full_ref, rows):
    del after_ref
    c = coup_ref[...]
    c2 = jnp.concatenate([c, c], axis=1)
    low = lanes((CELLS, 128)) < N
    eye = eye2()

    def leaf(k):
        g, s = divmod(k, 8)
        x = fac_ref[pl.ds(g * 256 + s, 32, stride=8), :]
        y = roll(x, N)
        rows[k % 2, pl.ds(0, 32, stride=2), :] = jnp.where(low, x, y)
        rows[k % 2, pl.ds(1, 32, stride=2), :] = jnp.where(low, y, x)
        a = rows[k % 2]
        before = max(k - 1, 0)
        return a * c2[before : before + 1] - eye, a * c2[k : k + 1] - eye

    for j in range(CELLS // 2):
        p1, q1 = leaf(2 * j)
        p2, q2 = leaf(2 * j + 1)
        kp1, kq1, kp2, kq2 = pack(p1), pack(q1), pack(p2), pack(q2)
        leaf_ref[j, 0], leaf_ref[j, 1] = kp2, kq2
        p = p1 + p2 + mm(kp2, kp1)
        q = q1 + q2 + mm(kq1, kq2)
        u = eye + q1 + p2 + mm(kq1, kp2)
        w = (eye + eye) + p1 + q1 + p + mm(kq1, pack(p))
        put(n1_ref, full_ref, j, p, q, w, u)


def tree_upper(n1_ref, full_ref, n2_ref, n3_ref, n4_ref, n5_ref, root_ref, fa, fb):
    node, full = n1_ref, full_ref
    for count, node_to, full_to in ((8, n2_ref, fa), (4, n3_ref, fb), (2, n4_ref, fa), (1, None, None)):
        for j in range(count):
            one, two = 2 * j, 2 * j + 1
            kp1, kq1 = node[one, 0], node[one, 1]
            u = full[two, 2] + mm(kq1, node[two, 2])
            p = full[one, 0] + full[two, 0] + mm(node[two, 0], kp1)
            q = full[one, 1] + full[two, 1] + mm(kq1, node[two, 1])
            ku = pack(u)
            w = full[one, 2] + u + mm(ku, kp1)
            if node_to is None:
                eye = eye2()
                n5_ref[0] = ku
                root_ref[:N] = jnp.where(lanes((N, 128)) < N, p, q) + eye
                root_ref[N:] = w
            else:
                put(node_to, full_to, j, p, q, w, u)
        node, full = node_to, full_to


def react(jac_hbm, dens_hbm, src_hbm, tran_hbm, pat_hbm, out_ref, jac_ref, dens_ref, src_ref, tran_ref, pat_ref,
          sems):
    pairs = ((dens_hbm, dens_ref), (pat_hbm, pat_ref), (jac_hbm, jac_ref), (src_hbm, src_ref), (tran_hbm, tran_ref))
    copies = [pltpu.make_async_copy(a, b, sems.at[i]) for i, (a, b) in enumerate(pairs)]
    for copy in copies:
        copy.start()
    half = lanes((128, N)) % 2 == lax.broadcasted_iota(jnp.int32, (128, N), 0) // N
    half = jnp.where(half, 1.0, 0.0).astype(bf16)
    for copy in copies:
        copy.wait()
    u = dens_ref[...]
    u2 = jnp.concatenate([u, u], axis=1)
    lane8 = lanes((8, 128))
    pat = pat_ref[...].astype(f32)
    mask_rows = jnp.zeros((8, 128), f32)
    for t in range(8):
        mask_rows = jnp.where((lane8 % N) // 8 == t, pat[:, t : t + 1], mask_rows)
    lane = lanes((CELLS, N))
    acc = jnp.zeros((CELLS, N), f32)
    for m in range(32):
        y = jac_ref[:, m * 128 : (m + 1) * 128] * (u2 * mask_rows[m // 4 : m // 4 + 1])
        hi = y.astype(bf16)
        lo = (y - hi.astype(f32)).astype(bf16)
        z = jnp.dot(hi, half, preferred_element_type=f32) + jnp.dot(lo, half, preferred_element_type=f32)
        acc = jnp.where(lane // 2 == m, z, acc)
    tran = tran_ref[...]
    flux = tran * u
    row = lax.broadcasted_iota(jnp.int32, (CELLS, N), 0)
    lower = jnp.where(row == 0, 0.0, pltpu.roll(flux, 1, 0))
    upper = jnp.where(row == CELLS - 1, 0.0, pltpu.roll(u, CELLS - 1, 0))
    out_ref[...] = src_ref[...] - acc + lower + tran * upper


LEVELS = (2, 4, 8, 16)


def upsweep(neigh_ref, part_ref, a_ref, b_ref, c_ref, top_ref, dens_ref, tran_ref, lat_ref, coup_ref, leaf_ref,
            n1_ref, n2_ref, n3_ref, n4_ref, n5_ref, root_ref, pay_ref, vec_ref):
    me = lax.axis_index("lat")
    u = dens_ref[...]
    total = jnp.zeros((CELLS, N), f32)
    lines = [(0, u), (1, a_ref[0])] + [(2 + i, b_ref[i]) for i in range(2)]
    lines += [((6, 7, 4, 5)[i], c_ref[i]) for i in range(4)]
    for offset, value in lines:
        line = me ^ offset
        count = jnp.int32(0)
        for j in range(4):
            count = count + (neigh_ref[0, j] == line).astype(jnp.int32)
        total = total + count.astype(f32) * value
    tran = tran_ref[...]
    row = lax.broadcasted_iota(jnp.int32, (CELLS, N), 0)
    r = part_ref[...] - lat_ref[...] * (4.0 * u - total) + jnp.where(row == CELLS - 1, tran * top_ref[0, 0:1], 0.0)
    c = coup_ref[...]
    g = dup4(r / jnp.where(row == 0, c, pltpu.roll(c, 1, 0)))
    lane = lanes((N, 128)) % CELLS
    x = g + stage([(k, (lambda k=k: leaf_ref[k // 2, 0]) if k % 2 else (lambda k=k: n1_ref[k // 2, 0]))
                   for k in range(CELLS)], g)
    v = x + roll(x, 1)
    y = stage([(k, lambda k=k: n1_ref[k // 2, 3 if k % 2 else 2]) for k in range(CELLS)], g)
    w = y + roll(y, -1)
    vec_ref[0], vec_ref[1] = v, w
    refs = (n1_ref, n2_ref, n3_ref, n4_ref, n5_ref)
    for i, h in enumerate(LEVELS):
        count = CELLS // (2 * h)
        ref, above = refs[i], refs[i + 1]
        start = lane % (2 * h) == 0
        x = jnp.where(start, roll(w, -h), roll(v, h))
        x = x + stage([(2 * h * (j + 1) - 1, lambda j=j, ref=ref: ref[2 * j + 1, 0]) for j in range(count)]
                      + [(2 * h * j, lambda j=j, ref=ref: ref[2 * j, 1]) for j in range(count)], x)
        if h < 16:
            y = stage([(2 * h * j, lambda j=j, above=above: above[j, 3]) for j in range(count)], roll(v, -(h - 1)))
        else:
            y = stage([(0, lambda above=above: above[0])], roll(v, -(h - 1)))
        v, w = v + x, w + x + y
        if h < 16:
            vec_ref[2 * i + 2], vec_ref[2 * i + 3] = v, w
    last = dup4(c)[:, CELLS - 1 : CELLS]
    flux = dup4(tran * u)[:, CELLS - 1 : CELLS]
    low = lanes((N, 128)) < N
    first_c = c[0:1]
    scale = 1.0 / jnp.concatenate([first_c, first_c], axis=1)
    pay_ref[:N] = jnp.where(low, root_ref[:N] * last * scale, root_ref[:N])
    out_v = v[:, CELLS - 1 : CELLS] * last + flux
    tail = jnp.where(lanes((N, 128)) == N, out_v, w[:, 0:1])
    pay_ref[N:] = jnp.where(low, root_ref[N:] * scale, tail)


def prepare(vec_ref, n1_ref, n2_ref, n3_ref, n4_ref, t_ref, t0_ref):
    refs = (n1_ref, n2_ref, n3_ref, n4_ref)
    at = 0
    for i, h in enumerate(LEVELS):
        ref = refs[i]
        for j in range(CELLS // (2 * h)):
            kw = ref[2 * j + 1, 2]
            wide = kw.astype(f32)
            t_ref[at] = pack(wide + roll(wide, N) + mm(kw, ref[2 * j, 0]))
            at += 1
        v, w = vec_ref[2 * i], vec_ref[2 * i + 1]
        t0_ref[i] = w + stage([(2 * h * j + h, lambda j=j, ref=ref: ref[2 * j + 1, 2])
                               for j in range(CELLS // (2 * h))], roll(v, 1))


def unpack(b):
    low = lanes((N, 128)) < N
    b1, b2 = b[:N], b[N:]
    r1, r2 = roll(b1, N), roll(b2, N)
    x = jnp.where(low, b1, r1)
    y = jnp.where(low, r1, b1)
    z = jnp.where(low, b2, r2)
    g = jnp.broadcast_to(b2[:, N : N + 1], (N, 128))
    h = jnp.broadcast_to(b2[:, N + 1 : N + 2], (N, 128))
    return x, y, z, g, h


def repack(ref, x, y, z, g, h):
    lane = lanes((N, 128))
    low = lane < N
    ref[:N] = jnp.where(low, x, y)
    ref[N:] = jnp.where(low, z, jnp.where(lane == N, g, h))


def combine(level, *refs):
    if level == 0:
        own_ref, other_ref, out_ref, fun_out = refs
    else:
        own_ref, other_ref, fun_ref, out_ref, fun_out = refs
    at = lax.axis_index("depth")
    is_low = ((at // (1, 2, 4, 8)[level]) % 2) == 0
    own, other = own_ref[...], other_ref[...]
    p1, q1, w1, v1, h1 = unpack(jnp.where(is_low, own, other))
    p2, q2, w2, v2, h2 = unpack(jnp.where(is_low, other, own))
    kp1, kq1, kp2, kw2 = pack(p1), pack(q1), pack(p2), pack(w2)
    t = mm(kw2, kp1)
    th = h2 + mv(kw2, v1)
    v = v2 + mv(kp2, v1)
    w = w1 + mm(kq1, pack(t))
    h = h1 + mv(kq1, th)
    lane = lanes((N, 128))
    low = lane < N
    tail = jnp.where(low, w, jnp.where(lane == N, v, h))
    if level == 3:
        out_ref[...] = tail
    else:
        out_ref[:N] = jnp.where(low, mm(kp2, kp1), mm(kq1, pack(q2)))
        out_ref[N:] = tail
    if level == 0:
        eye = eye2()
        repack(
            fun_out,
            jnp.where(is_low, eye, p1),
            jnp.where(is_low, q2, eye),
            jnp.where(is_low, t, 0.0),
            jnp.where(is_low, 0.0, v1),
            jnp.where(is_low, th, 0.0),
        )
    else:
        f, hh, k, g, e = unpack(fun_ref[...])
        x1 = pack(jnp.where(is_low, hh, f))
        y1 = pack(jnp.where(is_low, q2, p1))
        x2 = pack(jnp.where(is_low, hh, k))
        y2 = pack(jnp.where(is_low, t, p1))
        prod1 = mm(x1, y1)
        prod2 = mm(x2, y2)
        vec1 = mv(x1, v1)
        vec2 = mv(x2, jnp.where(is_low, th, v1))
        repack(
            fun_out,
            jnp.where(is_low, f, prod1),
            jnp.where(is_low, prod1, hh),
            jnp.where(is_low, k + prod2, prod2),
            jnp.where(is_low, g, g + vec1),
            e + vec2,
        )


def downsweep(own_ref, other_ref, fun_ref, vec_ref, t0_ref, coup_ref, leaf_ref, n1_ref, n2_ref, n3_ref, n4_ref, t_ref,
              out_ref):
    is_low = lax.axis_index("depth") < 2 * ZS
    f, hh, k, g, e = unpack(fun_ref[...])
    own, other = own_ref[...], other_ref[...]
    other_w = jnp.where(lanes((N, 128)) < N, other, roll(other, N))
    v_own = jnp.broadcast_to(own[:, N : N + 1], (N, 128))
    v_other = jnp.broadcast_to(other[:, N : N + 1], (N, 128))
    w_other = jnp.broadcast_to(other[:, N + 1 : N + 2], (N, 128))
    up = g + mv(pack(f), v_other)
    t = w_other + mv(pack(other_w), v_own)
    a_in = e + mv(pack(jnp.where(is_low, hh, k)), jnp.where(is_low, t, v_other))
    s_in = jnp.where(is_low, g, up)
    lane = lanes((N, 128)) % CELLS
    ss, aa = s_in / dup4(coup_ref[...])[:, 0:1], a_in
    first = (14, 12, 8, 0)
    for i, h, ref in ((3, 16, n4_ref), (2, 8, n3_ref), (1, 4, n2_ref), (0, 2, n1_ref)):
        count = CELLS // (2 * h)
        base = first[3 - i]
        v = vec_ref[2 * i]
        x = jnp.where(lane % (2 * h) == 0, ss, aa)
        y = x + stage([(2 * h * j, lambda j=j, ref=ref: ref[2 * j, 0]) for j in range(count)]
                      + [(2 * h * (j + 1) - 1, lambda j=j, ref=ref: ref[2 * j + 1, 1]) for j in range(count)], x)
        z = stage([(2 * h * j, lambda j=j, base=base: t_ref[base + j]) for j in range(count)], ss)
        ss = jnp.where(lane % (2 * h) == h, roll(y, h) + roll(v, 1), ss)
        aa = jnp.where(lane % (2 * h) == h - 1, roll(y, -h) + roll(z, h - 1) + roll(t0_ref[i], -1), aa)
    even = lane % 2 == 0
    x = jnp.where(even, ss, aa)
    y = stage([(k, lambda k=k: n1_ref[k // 2, 1 if k % 2 else 2]) for k in range(CELLS)], x)
    z = x + stage([(k, (lambda k=k: leaf_ref[k // 2, 1]) if k % 2 else (lambda k=k: n1_ref[k // 2, 0]))
                   for k in range(CELLS)], x)
    x1 = y + roll(aa + y, -1) + vec_ref[1]
    x2 = z + roll(z, 1) + vec_ref[0]
    out_ref[...] = jnp.where(even, x1, x2).T[:CELLS]


def sds(*shape, dtype=f32):
    return jax.ShapeDtypeStruct(shape, dtype)


def call(body, outs, *args, scratch=(), smem=0, hbm=0, flops=0, name=None):
    args = [pltpu.with_memory_space_constraint(x, pltpu.HBM) if smem <= i < smem + hbm else x for i, x in enumerate(args)]
    spaces = [pltpu.SMEM] * smem + [pltpu.HBM] * hbm + [pltpu.VMEM] * (len(args) - smem - hbm)
    return pl.pallas_call(
        body,
        out_shape=outs,
        in_specs=[pl.BlockSpec(memory_space=space) for space in spaces],
        out_specs=jax.tree.map(lambda _: pl.BlockSpec(memory_space=pltpu.VMEM), outs),
        scratch_shapes=scratch,
        cost_estimate=pl.CostEstimate(flops=flops, bytes_accessed=1 << 16, transcendentals=0),
        name=name,
        compiler_params=pltpu.CompilerParams(vmem_limit_bytes=VLIM),
    )(*args)


def node(count):
    return sds(count, 4, N, 128, dtype=bf16)


def on_device(densities, source, jacobian, pattern, transport, lateral, neighbours, factor, coupling):
    line_count, cell_count, species = densities.shape
    u = densities.reshape(CELLS, N)
    src = source.reshape(CELLS, N)
    tran = transport.reshape(CELLS, N)
    lat = lateral.reshape(CELLS, N)
    coup = coupling.reshape(CELLS, N)
    jac = jacobian.reshape(CELLS, N * N)
    fac = factor.reshape(4, 8, 32, 128).transpose(0, 2, 1, 3).reshape(1024, 128)

    def xor_lat(value, bits):
        return lax.ppermute(value, "lat", [(i, i ^ bits) for i in range(8)])

    def xor_depth(value, bits):
        return lax.ppermute(value, "depth", [(i, i ^ bits) for i in range(32)])

    line_a = xor_lat(densities, 1)
    part = call(
        react, sds(CELLS, N), jac, u, src, tran, pattern, hbm=5, flops=1 << 30, name="react",
        scratch=[pltpu.VMEM((CELLS, N * N), f32)] + [pltpu.VMEM((CELLS, N), f32)] * 3
        + [pltpu.VMEM((8, 8), jnp.int32), pltpu.SemaphoreType.DMA((5,))],
    )
    line_b = xor_lat(jnp.concatenate([densities, line_a], axis=0), 2)
    leaf, n1, full = call(
        tree_leaves,
        (sds(16, 2, N, 128, dtype=bf16), node(16), sds(16, 3, N, 128)),
        fac, coup, part, scratch=[pltpu.VMEM((2, N, 128), f32)], flops=2 << 30, name="tree_leaves",
    )
    top = lax.ppermute(densities, "depth", [(i + 1, i) for i in range(31)])
    line_c = xor_lat(jnp.concatenate([densities, line_a, line_b], axis=0), 6)
    n2, n3, n4, n5, root = call(
        tree_upper,
        (node(8), node(4), node(2), sds(1, N, 128, dtype=bf16), sds(128, 128)),
        n1, full, scratch=[pltpu.VMEM((8, 3, N, 128), f32), pltpu.VMEM((4, 3, N, 128), f32)],
        flops=2 << 30, name="tree_upper",
    )
    pay, vec = call(
        upsweep, (sds(128, 128), sds(8, N, 128)),
        neighbours, part, line_a, line_b, line_c, top, u, tran, lat, coup, leaf, n1, n2, n3, n4, n5, root,
        smem=1, flops=1 << 25, name="upsweep",
    )
    fun = None
    for level, bits in enumerate((1, 2, 7, 8)):
        other = xor_depth(pay, bits)
        if level == 0:
            tees, t0 = call(
                prepare, (sds(15, N, 128, dtype=bf16), sds(4, N, 128)), vec, n1, n2, n3, n4,
                flops=1 << 30, name="prepare",
            )
        args = (pay, other) if level == 0 else (pay, other, fun)
        pay, fun = call(
            lambda *refs, level=level: combine(level, *refs),
            (sds(N if level == 3 else 128, 128), sds(128, 128)), *args, flops=1 << 24, name=f"combine{level}",
        )
    other = xor_depth(pay, 24)
    out = call(
        downsweep, sds(CELLS, N), pay, other, fun, vec, t0, coup, leaf, n1, n2, n3, n4, tees, flops=1 << 25,
        name="downsweep",
    )
    return out.reshape(line_count, cell_count, species)


def solution(mesh):
    return jax.shard_map(
        on_device,
        mesh=mesh,
        in_specs=(
            P("lat", "depth", None),
            P("lat", "depth", None),
            P("lat", "depth", None),
            P(),
            P("lat", "depth", None),
            P("lat", "depth", None),
            P("lat", None),
            P("lat", "depth", None),
            P("lat", "depth", None),
        ),
        out_specs=P("lat", "depth", None),
        check_vma=False,
    )
```

```python
import jax
import jax.numpy as jnp
from jax import lax
from jax.experimental import pallas as pl
from jax.experimental.pallas import tpu as pltpu
from jax.sharding import PartitionSpec as P

f32 = jnp.float32
bf16 = jnp.bfloat16

CELLS = 32
N = 64
ZS = 8
VLIM = 16 << 20


def lanes(shape):
    return lax.broadcasted_iota(jnp.int32, shape, len(shape) - 1)


def roll(x, shift):
    shift = shift % x.shape[-1]
    return x if shift == 0 else pltpu.roll(x, shift, x.ndim - 1)


def pack(dup):
    hi = dup.astype(bf16).astype(f32)
    return jnp.where(lanes(dup.shape) < N, hi, dup - hi).astype(bf16)


def mm(a, b):
    r = jnp.dot(a, jnp.concatenate([b, b], axis=0), preferred_element_type=f32)
    return r + roll(r, N)


def rhs(x):
    hi = x.astype(bf16)
    lo = (x - hi.astype(f32)).astype(bf16)
    return jnp.concatenate([hi, hi, lo, lo], axis=0)


def dot(a, y):
    return jnp.dot(jnp.concatenate([a, a], axis=1), y, preferred_element_type=f32)


def column(row):
    return jnp.broadcast_to(row, (128, N)).T


def eye2():
    return jnp.where(lanes((N, 128)) % N == lax.broadcasted_iota(jnp.int32, (N, 128), 0), 1.0, 0.0)


def put(node, full, j, p, q, w, u):
    node[j, 0], node[j, 1], node[j, 2], node[j, 3] = pack(p), pack(q), pack(w), pack(u)
    full[j, 0], full[j, 1], full[j, 2] = p, q, w


def tree_leaves(fac_ref, coup_ref, after_ref, leaf_ref, n1_ref, full_ref, cols_ref, rows):
    del after_ref
    c = coup_ref[...]
    cols_ref[0] = column(c[CELLS - 1 : CELLS])
    cols_ref[1] = column(1.0 / c[0:1])
    c2 = jnp.concatenate([c, c], axis=1)
    low = lanes((CELLS, 128)) < N
    eye = eye2()

    def leaf(k):
        g, s = divmod(k, 8)
        x = fac_ref[pl.ds(g * 256 + s, 32, stride=8), :]
        y = roll(x, N)
        rows[k % 2, pl.ds(0, 32, stride=2), :] = jnp.where(low, x, y)
        rows[k % 2, pl.ds(1, 32, stride=2), :] = jnp.where(low, y, x)
        a = rows[k % 2]
        before = max(k - 1, 0)
        return a * c2[before : before + 1] - eye, a * c2[k : k + 1] - eye

    for j in range(CELLS // 2):
        p1, q1 = leaf(2 * j)
        p2, q2 = leaf(2 * j + 1)
        kp1, kq1, kp2, kq2 = pack(p1), pack(q1), pack(p2), pack(q2)
        leaf_ref[j, 0], leaf_ref[j, 1] = kp2, kq2
        p = p1 + p2 + mm(kp2, kp1)
        q = q1 + q2 + mm(kq1, kq2)
        u = eye + q1 + p2 + mm(kq1, kp2)
        w = (eye + eye) + p1 + q1 + p + mm(kq1, pack(p))
        put(n1_ref, full_ref, j, p, q, w, u)


def tree_upper(n1_ref, full_ref, coup_ref, cols_ref, n2_ref, n3_ref, n4_ref, n5_ref, root_ref, fa, fb):
    node, full = n1_ref, full_ref
    for count, node_to, full_to in ((8, n2_ref, fa), (4, n3_ref, fb), (2, n4_ref, fa), (1, None, None)):
        for j in range(count):
            one, two = 2 * j, 2 * j + 1
            kp1, kq1 = node[one, 0], node[one, 1]
            u = full[two, 2] + mm(kq1, node[two, 2])
            p = full[one, 0] + full[two, 0] + mm(node[two, 0], kp1)
            q = full[one, 1] + full[two, 1] + mm(kq1, node[two, 1])
            ku = pack(u)
            w = full[one, 2] + u + mm(ku, kp1)
            if node_to is None:
                eye = eye2()
                n5_ref[0] = ku
                first = coup_ref[0:1]
                scale = 1.0 / jnp.concatenate([first, first], axis=1)
                root_ref[:N] = jnp.where(lanes((N, 128)) < N, (p + eye) * cols_ref[0] * scale, q + eye)
                root_ref[N:] = w * scale
            else:
                put(node_to, full_to, j, p, q, w, u)
        node, full = node_to, full_to


def react(jac_hbm, dens_hbm, src_hbm, tran_hbm, pat_hbm, out_ref, flux_ref, jac_ref, dens_ref, src_ref, tran_ref,
          pat_ref, sems):
    pairs = ((dens_hbm, dens_ref), (pat_hbm, pat_ref), (jac_hbm, jac_ref), (src_hbm, src_ref), (tran_hbm, tran_ref))
    copies = [pltpu.make_async_copy(a, b, sems.at[i]) for i, (a, b) in enumerate(pairs)]
    for copy in copies:
        copy.start()
    half = lanes((128, N)) % 2 == lax.broadcasted_iota(jnp.int32, (128, N), 0) // N
    half = jnp.where(half, 1.0, 0.0).astype(bf16)
    for copy in copies:
        copy.wait()
    u = dens_ref[...]
    u2 = jnp.concatenate([u, u], axis=1)
    lane8 = lanes((8, 128))
    pat = pat_ref[...].astype(f32)
    mask_rows = jnp.zeros((8, 128), f32)
    for t in range(8):
        mask_rows = jnp.where((lane8 % N) // 8 == t, pat[:, t : t + 1], mask_rows)
    lane = lanes((CELLS, N))
    acc = jnp.zeros((CELLS, N), f32)
    for m in range(32):
        y = jac_ref[:, m * 128 : (m + 1) * 128] * (u2 * mask_rows[m // 4 : m // 4 + 1])
        hi = y.astype(bf16)
        lo = (y - hi.astype(f32)).astype(bf16)
        z = jnp.dot(hi, half, preferred_element_type=f32) + jnp.dot(lo, half, preferred_element_type=f32)
        acc = jnp.where(lane // 2 == m, z, acc)
    tran = tran_ref[...]
    flux = tran * u
    flux_ref[...] = column(flux[CELLS - 1 : CELLS])
    row = lax.broadcasted_iota(jnp.int32, (CELLS, N), 0)
    lower = jnp.where(row == 0, 0.0, pltpu.roll(flux, 1, 0))
    upper = jnp.where(row == CELLS - 1, 0.0, pltpu.roll(u, CELLS - 1, 0))
    out_ref[...] = src_ref[...] - acc + lower + tran * upper


def upsweep(neigh_ref, part_ref, a_ref, b_ref, c_ref, top_ref, flux_ref, dens_ref, tran_ref, lat_ref, coup_ref, cols_ref,
            leaf_ref, n1_ref, n2_ref, n3_ref, n4_ref, n5_ref, root_ref, pay_ref, pair_ref, v_ref, w_ref):
    me = lax.axis_index("lat")
    u = dens_ref[...]
    total = jnp.zeros((CELLS, N), f32)
    lines = [(0, u), (1, a_ref[0])] + [(2 + i, b_ref[i]) for i in range(2)]
    lines += [((6, 7, 4, 5)[i], c_ref[i]) for i in range(4)]
    for offset, value in lines:
        line = me ^ offset
        count = jnp.int32(0)
        for j in range(4):
            count = count + (neigh_ref[0, j] == line).astype(jnp.int32)
        total = total + count.astype(f32) * value
    row = lax.broadcasted_iota(jnp.int32, (CELLS, N), 0)
    r = part_ref[...] - lat_ref[...] * (4.0 * u - total)
    r = r + jnp.where(row == CELLS - 1, tran_ref[...] * top_ref[0, 0:1], 0.0)
    c = coup_ref[...]
    g = r / jnp.where(row == 0, c, pltpu.roll(c, 1, 0))
    x = [(g if i == 0 else pltpu.roll(g, CELLS - i, 0)).T for i in range(4)]
    y = [rhs(t) for t in x]
    lane = lanes((N, CELLS))
    pair_v, pair_w = [], []
    for half in range(2):
        y0, y1 = y[2 * half], y[2 * half + 1]
        v = jnp.zeros((N, CELLS), f32)
        w = jnp.zeros((N, CELLS), f32)
        for j in range(8):
            at = 2 * j + half
            here = lane == 4 * j
            v = jnp.where(here, dot(n1_ref[at, 0], y0) + dot(leaf_ref[at, 0], y1), v)
            w = jnp.where(here, dot(n1_ref[at, 2], y0) + dot(n1_ref[at, 3], y1), w)
        pair_v.append(v + x[2 * half] + x[2 * half + 1])
        pair_w.append(w)
        pair_ref[half, :, 0:CELLS] = pair_v[half]
        pair_ref[2 + half, :, 0:CELLS] = w
    yv, yw = rhs(pair_v[0]), rhs(pair_w[1])
    v, w = pair_v[0] + pair_v[1], pair_w[0] + pair_w[1]
    dv = jnp.zeros((N, CELLS), f32)
    dw = jnp.zeros((N, CELLS), f32)
    for j in range(8):
        here = lane == 4 * j
        dv = jnp.where(here, dot(n1_ref[2 * j + 1, 0], yv), dv)
        dw = jnp.where(here, dot(n1_ref[2 * j, 1], yw) + dot(n2_ref[j, 3], yv), dw)
    v, w = v + dv, w + dw
    vs = [jnp.broadcast_to(v[:, 4 * j : 4 * j + 1], (N, 128)) for j in range(8)]
    ws = [jnp.broadcast_to(w[:, 4 * j : 4 * j + 1], (N, 128)) for j in range(8)]
    at = 0
    for count, ref, above in ((4, n2_ref, n3_ref), (2, n3_ref, n4_ref), (1, n4_ref, n5_ref)):
        next_v, next_w = [], []
        for j in range(count):
            v1, v2, w1, w2 = vs[2 * j], vs[2 * j + 1], ws[2 * j], ws[2 * j + 1]
            v_ref[at], w_ref[at] = v1, w2
            at += 1
            yv, yw = rhs(v1), rhs(w2)
            u_map = above[j, 3] if count > 1 else above[0]
            next_v.append(v1 + v2 + dot(ref[2 * j + 1, 0], yv))
            next_w.append(w1 + w2 + dot(ref[2 * j, 1], yw) + dot(u_map, yv))
        vs, ws = next_v, next_w
    lane = lanes((N, 128))
    pay_ref[:N] = root_ref[:N]
    tail = jnp.where(lane == N, vs[0] * cols_ref[0] + flux_ref[...], ws[0])
    pay_ref[N:] = jnp.where(lane < N, root_ref[N:], tail)


def prepare(pair_ref, v_ref, w_ref, n1_ref, n2_ref, n3_ref, n4_ref, t_ref, add_v, add_a, add_x):
    lane = lanes((N, 128))
    at, vec = 0, 0
    for level, size, ref in ((1, 8, n2_ref), (2, 16, n3_ref), (3, 32, n4_ref)):
        acc_v = jnp.zeros((N, 128), f32)
        acc_a = jnp.zeros((N, 128), f32)
        for j in range(CELLS // size):
            kw = ref[2 * j + 1, 2]
            wide = kw.astype(f32)
            t_ref[at] = pack(wide + roll(wide, N) + mm(kw, ref[2 * j, 0]))
            at += 1
            here = lane // size == j
            acc_v = jnp.where(here, v_ref[vec], acc_v)
            acc_a = jnp.where(here, w_ref[vec] + dot(kw, rhs(v_ref[vec])), acc_a)
            vec += 1
        add_v[level], add_a[level] = acc_v, acc_a
    first = lane % 4 == 0
    v0, v1, w0, w1 = [jnp.where(first, pair_ref[i], 0.0) for i in range(4)]
    y = rhs(v0)
    acc_a = jnp.zeros((N, 128), f32)
    for j in range(8):
        kw = n1_ref[2 * j + 1, 2]
        wide = kw.astype(f32)
        t_ref[at] = pack(wide + roll(wide, N) + mm(kw, n1_ref[2 * j, 0]))
        at += 1
        acc_a = jnp.where(lane == 4 * j, dot(kw, y), acc_a)
    acc_a = acc_a + w1
    spread_v = v0 + roll(v0, 1)
    spread_a = acc_a + roll(acc_a, 1)
    add_v[0] = spread_v + roll(spread_v, 2)
    add_a[0] = spread_a + roll(spread_a, 2)
    add_x[...] = w0 + roll(w1, 2) + roll(v0, 1) + roll(v1, 3)


def unpack(b):
    low = lanes((N, 128)) < N
    b1, b2 = b[:N], b[N:]
    r1, r2 = roll(b1, N), roll(b2, N)
    x = jnp.where(low, b1, r1)
    y = jnp.where(low, r1, b1)
    z = jnp.where(low, b2, r2)
    g = jnp.broadcast_to(b2[:, N : N + 1], (N, 128))
    h = jnp.broadcast_to(b2[:, N + 1 : N + 2], (N, 128))
    return x, y, z, g, h


def repack(ref, x, y, z, g, h):
    lane = lanes((N, 128))
    low = lane < N
    ref[:N] = jnp.where(low, x, y)
    ref[N:] = jnp.where(low, z, jnp.where(lane == N, g, h))


def combine(level, *refs):
    if level == 0:
        own_ref, other_ref, out_ref, fun_out = refs
    else:
        own_ref, other_ref, fun_ref, out_ref, fun_out = refs
    at = lax.axis_index("depth")
    is_low = ((at // (1, 2, 4, 8)[level]) % 2) == 0
    own, other = own_ref[...], other_ref[...]
    p1, q1, w1, v1, h1 = unpack(jnp.where(is_low, own, other))
    p2, q2, w2, v2, h2 = unpack(jnp.where(is_low, other, own))
    kq1, kp2, kw2 = pack(q1), pack(p2), pack(w2)
    yp1, yv1 = rhs(p1), rhs(v1)
    t = dot(kw2, yp1)
    th = h2 + dot(kw2, yv1)
    v = v2 + dot(kp2, yv1)
    yt, yth = rhs(t), rhs(th)
    w = w1 + dot(kq1, yt)
    h = h1 + dot(kq1, yth)
    lane = lanes((N, 128))
    low = lane < N
    tail = jnp.where(low, w, jnp.where(lane == N, v, h))
    if level == 3:
        out_ref[...] = tail
    else:
        out_ref[:N] = jnp.where(low, dot(kp2, yp1), dot(kq1, rhs(q2)))
        out_ref[N:] = tail
    if level == 0:
        eye = eye2()
        repack(
            fun_out,
            jnp.where(is_low, eye, p1),
            jnp.where(is_low, q2, eye),
            jnp.where(is_low, t, 0.0),
            jnp.where(is_low, 0.0, v1),
            jnp.where(is_low, th, 0.0),
        )
    else:
        f, hh, k, g, e = unpack(fun_ref[...])
        x1 = pack(jnp.where(is_low, hh, f))
        x2 = pack(jnp.where(is_low, hh, k))
        prod1 = dot(x1, rhs(jnp.where(is_low, q2, p1)))
        prod2 = dot(x2, jnp.where(is_low, yt, yp1))
        vec1 = dot(x1, yv1)
        vec2 = dot(x2, jnp.where(is_low, yth, yv1))
        repack(
            fun_out,
            jnp.where(is_low, f, prod1),
            jnp.where(is_low, prod1, hh),
            jnp.where(is_low, k + prod2, prod2),
            jnp.where(is_low, g, g + vec1),
            e + vec2,
        )


def downsweep(own_ref, other_ref, fun_ref, cols_ref, add_v, add_a, add_x, leaf_ref, n1_ref, n2_ref, n3_ref, n4_ref, t_ref,
              out_ref):
    is_low = lax.axis_index("depth") < 2 * ZS
    f, hh, k, g, e = unpack(fun_ref[...])
    own, other = own_ref[...], other_ref[...]
    other_w = jnp.where(lanes((N, 128)) < N, other, roll(other, N))
    v_own = jnp.broadcast_to(own[:, N : N + 1], (N, 128))
    v_other = jnp.broadcast_to(other[:, N : N + 1], (N, 128))
    w_other = jnp.broadcast_to(other[:, N + 1 : N + 2], (N, 128))
    y_other = rhs(v_other)
    t = w_other + dot(pack(other_w), rhs(v_own))
    up = g + dot(pack(f), y_other)
    aa = e + dot(pack(jnp.where(is_low, hh, k)), rhs(jnp.where(is_low, t, v_other)))
    ss = jnp.where(is_low, g, up) * cols_ref[1]
    lane = lanes((N, 128))
    for level, size, ref, base in ((3, 32, n4_ref, 6), (2, 16, n3_ref, 4), (1, 8, n2_ref, 0), (0, 4, n1_ref, 7)):
        ys, ya = rhs(ss), rhs(aa)
        ds = jnp.zeros((N, 128), f32)
        da = jnp.zeros((N, 128), f32)
        for j in range(CELLS // size):
            here = lane // size == j
            ds = jnp.where(here, dot(ref[2 * j, 0], ys), ds)
            da = jnp.where(here, dot(ref[2 * j + 1, 1], ya) + dot(t_ref[base + j], ys), da)
        upper = lane % size >= size // 2
        new_s = ss + add_v[level] + ds
        new_a = aa + add_a[level] + da
        ss = jnp.where(upper, new_s, ss)
        aa = jnp.where(upper, aa, new_a)
    ys, ya = rhs(ss), rhs(aa)
    x = jnp.zeros((N, 128), f32)
    for j in range(CELLS // 2):
        x = jnp.where(lane == 2 * j, dot(n1_ref[j, 2], ys) + dot(n1_ref[j, 1], ya), x)
        x = jnp.where(lane == 2 * j + 1, dot(n1_ref[j, 0], ys) + dot(leaf_ref[j, 1], ya), x)
    x = x + aa + add_x[...] + jnp.where(lane % 2 == 1, ss, 0.0)
    out_ref[...] = x.T[:CELLS]


def sds(*shape, dtype=f32):
    return jax.ShapeDtypeStruct(shape, dtype)


def call(body, outs, *args, scratch=(), smem=0, hbm=0, flops=0, name=None):
    args = [pltpu.with_memory_space_constraint(x, pltpu.HBM) if smem <= i < smem + hbm else x for i, x in enumerate(args)]
    spaces = [pltpu.SMEM] * smem + [pltpu.HBM] * hbm + [pltpu.VMEM] * (len(args) - smem - hbm)
    return pl.pallas_call(
        body,
        out_shape=outs,
        in_specs=[pl.BlockSpec(memory_space=space) for space in spaces],
        out_specs=jax.tree.map(lambda _: pl.BlockSpec(memory_space=pltpu.VMEM), outs),
        scratch_shapes=scratch,
        cost_estimate=pl.CostEstimate(flops=flops, bytes_accessed=1 << 16, transcendentals=0),
        name=name,
        compiler_params=pltpu.CompilerParams(vmem_limit_bytes=VLIM),
    )(*args)


def node(count):
    return sds(count, 4, N, 128, dtype=bf16)


def on_device(densities, source, jacobian, pattern, transport, lateral, neighbours, factor, coupling):
    line_count, cell_count, species = densities.shape
    u = densities.reshape(CELLS, N)
    src = source.reshape(CELLS, N)
    tran = transport.reshape(CELLS, N)
    lat = lateral.reshape(CELLS, N)
    coup = coupling.reshape(CELLS, N)
    jac = jacobian.reshape(CELLS, N * N)
    fac = factor.reshape(4, 8, 32, 128).transpose(0, 2, 1, 3).reshape(1024, 128)

    def xor_lat(value, bits):
        return lax.ppermute(value, "lat", [(i, i ^ bits) for i in range(8)])

    def xor_depth(value, bits):
        return lax.ppermute(value, "depth", [(i, i ^ bits) for i in range(32)])

    line_a = xor_lat(densities, 1)
    part, flux = call(
        react, (sds(CELLS, N), sds(N, 128)), jac, u, src, tran, pattern, hbm=5, flops=1 << 30, name="react",
        scratch=[pltpu.VMEM((CELLS, N * N), f32)] + [pltpu.VMEM((CELLS, N), f32)] * 3
        + [pltpu.VMEM((8, 8), jnp.int32), pltpu.SemaphoreType.DMA((5,))],
    )
    line_b = xor_lat(jnp.concatenate([densities, line_a], axis=0), 2)
    leaf, n1, full, cols = call(
        tree_leaves,
        (sds(16, 2, N, 128, dtype=bf16), node(16), sds(16, 3, N, 128), sds(2, N, 128)),
        fac, coup, part, scratch=[pltpu.VMEM((2, N, 128), f32)], flops=2 << 30, name="tree_leaves",
    )
    top = lax.ppermute(lax.optimization_barrier((densities, part))[0], "depth", [(i + 1, i) for i in range(31)])
    line_c = xor_lat(jnp.concatenate([densities, line_a, line_b], axis=0), 6)
    n2, n3, n4, n5, root = call(
        tree_upper,
        (node(8), node(4), node(2), sds(1, N, 128, dtype=bf16), sds(128, 128)),
        n1, full, coup, cols, scratch=[pltpu.VMEM((8, 3, N, 128), f32), pltpu.VMEM((4, 3, N, 128), f32)],
        flops=2 << 30, name="tree_upper",
    )
    pay, pair, vs, ws = call(
        upsweep, (sds(128, 128), sds(4, N, 128), sds(7, N, 128), sds(7, N, 128)),
        neighbours, part, line_a, line_b, line_c, top, flux, u, tran, lat, coup, cols, leaf, n1, n2, n3, n4, n5, root,
        smem=1, flops=1 << 25, name="upsweep",
    )
    fun = None
    for level, bits in enumerate((1, 2, 7, 8)):
        other = xor_depth(pay, bits)
        if level == 0:
            tees, add_v, add_a, add_x = call(
                prepare, (sds(15, N, 128, dtype=bf16), sds(4, N, 128), sds(4, N, 128), sds(N, 128)),
                pair, vs, ws, n1, n2, n3, n4, flops=1 << 30, name="prepare",
            )
        args = (pay, other) if level == 0 else (pay, other, fun)
        pay, fun = call(
            lambda *refs, level=level: combine(level, *refs),
            (sds(N if level == 3 else 128, 128), sds(128, 128)), *args, flops=1 << 24, name=f"combine{level}",
        )
    other = xor_depth(pay, 24)
    out = call(
        downsweep, sds(CELLS, N), pay, other, fun, cols, add_v, add_a, add_x, leaf, n1, n2, n3, n4, tees,
        flops=1 << 25, name="downsweep",
    )
    return out.reshape(line_count, cell_count, species)


def solution(mesh):
    return jax.shard_map(
        on_device,
        mesh=mesh,
        in_specs=(
            P("lat", "depth", None),
            P("lat", "depth", None),
            P("lat", "depth", None),
            P(),
            P("lat", "depth", None),
            P("lat", "depth", None),
            P("lat", None),
            P("lat", "depth", None),
            P("lat", "depth", None),
        ),
        out_specs=P("lat", "depth", None),
        check_vma=False,
    )
```

```python
import jax
import jax.numpy as jnp
from jax import lax
from jax.experimental import pallas as pl
from jax.experimental.pallas import tpu as pltpu
from jax.sharding import PartitionSpec as P

f32 = jnp.float32
bf16 = jnp.bfloat16

CELLS = 32
N = 64
ZS = 8
VLIM = 16 << 20


def lanes(shape):
    return lax.broadcasted_iota(jnp.int32, shape, len(shape) - 1)


def roll(x, shift):
    shift = shift % x.shape[-1]
    return x if shift == 0 else pltpu.roll(x, shift, x.ndim - 1)


def pack(dup):
    hi = dup.astype(bf16).astype(f32)
    return jnp.where(lanes(dup.shape) < N, hi, dup - hi).astype(bf16)


def mm(a, b):
    r = jnp.dot(a, jnp.concatenate([b, b], axis=0), preferred_element_type=f32)
    return r + roll(r, N)


def rhs(x):
    hi = x.astype(bf16)
    lo = (x - hi.astype(f32)).astype(bf16)
    return jnp.concatenate([hi, hi, lo, lo], axis=0)


def dot(a, y):
    return jnp.dot(jnp.concatenate([a, a], axis=1), y, preferred_element_type=f32)


def column(row):
    return jnp.broadcast_to(row, (128, N)).T


def eye2():
    return jnp.where(lanes((N, 128)) % N == lax.broadcasted_iota(jnp.int32, (N, 128), 0), 1.0, 0.0)


def put(node, full, j, p, q, w, u):
    node[j, 0], node[j, 1], node[j, 2], node[j, 3] = pack(p), pack(q), pack(w), pack(u)
    full[j, 0], full[j, 1], full[j, 2] = p, q, w


def tree_leaves(fac_ref, coup_ref, after_ref, leaf_ref, n1_ref, full_ref, cols_ref, rows):
    del after_ref
    c = coup_ref[...]
    cols_ref[0] = column(c[CELLS - 1 : CELLS])
    cols_ref[1] = column(1.0 / c[0:1])
    c2 = jnp.concatenate([c, c], axis=1)
    low = lanes((CELLS, 128)) < N
    eye = eye2()

    def leaf(k):
        g, s = divmod(k, 8)
        x = fac_ref[pl.ds(g * 256 + s, 32, stride=8), :]
        y = roll(x, N)
        rows[k % 2, pl.ds(0, 32, stride=2), :] = jnp.where(low, x, y)
        rows[k % 2, pl.ds(1, 32, stride=2), :] = jnp.where(low, y, x)
        a = rows[k % 2]
        before = max(k - 1, 0)
        return a * c2[before : before + 1] - eye, a * c2[k : k + 1] - eye

    for j in range(CELLS // 2):
        p1, q1 = leaf(2 * j)
        p2, q2 = leaf(2 * j + 1)
        kp1, kq1, kp2, kq2 = pack(p1), pack(q1), pack(p2), pack(q2)
        leaf_ref[j, 0], leaf_ref[j, 1] = kp2, kq2
        p = p1 + p2 + mm(kp2, kp1)
        q = q1 + q2 + mm(kq1, kq2)
        u = eye + q1 + p2 + mm(kq1, kp2)
        w = (eye + eye) + p1 + q1 + p + mm(kq1, pack(p))
        put(n1_ref, full_ref, j, p, q, w, u)


def tree_upper(n1_ref, full_ref, coup_ref, cols_ref, after_ref, n2_ref, n3_ref, n4_ref, n5_ref, root_ref, fa, fb):
    del after_ref
    node, full = n1_ref, full_ref
    for count, node_to, full_to in ((8, n2_ref, fa), (4, n3_ref, fb), (2, n4_ref, fa), (1, None, None)):
        for j in range(count):
            one, two = 2 * j, 2 * j + 1
            kp1, kq1 = node[one, 0], node[one, 1]
            u = full[two, 2] + mm(kq1, node[two, 2])
            p = full[one, 0] + full[two, 0] + mm(node[two, 0], kp1)
            q = full[one, 1] + full[two, 1] + mm(kq1, node[two, 1])
            ku = pack(u)
            w = full[one, 2] + u + mm(ku, kp1)
            if node_to is None:
                eye = eye2()
                n5_ref[0] = ku
                first = coup_ref[0:1]
                scale = 1.0 / jnp.concatenate([first, first], axis=1)
                root_ref[:N] = jnp.where(lanes((N, 128)) < N, (p + eye) * cols_ref[0] * scale, q + eye)
                root_ref[N:] = w * scale
            else:
                put(node_to, full_to, j, p, q, w, u)
        node, full = node_to, full_to


def react(jac_hbm, dens_hbm, src_hbm, tran_hbm, pat_hbm, out_ref, flux_ref, jac_ref, dens_ref, src_ref, tran_ref,
          pat_ref, sems):
    parts = [(slice(None), pl.ds(i * 1024, 1024)) for i in range(4)]
    pairs = [(dens_hbm, dens_ref), (pat_hbm, pat_ref)] + [(jac_hbm.at[part], jac_ref.at[part]) for part in parts]
    pairs += [(src_hbm, src_ref), (tran_hbm, tran_ref)]
    copies = [pltpu.make_async_copy(a, b, sems.at[i]) for i, (a, b) in enumerate(pairs)]
    for copy in copies:
        copy.start()
    half = lanes((128, N)) % 2 == lax.broadcasted_iota(jnp.int32, (128, N), 0) // N
    half = jnp.where(half, 1.0, 0.0).astype(bf16)
    copies[0].wait()
    copies[1].wait()
    u = dens_ref[...]
    u2 = jnp.concatenate([u, u], axis=1)
    lane8 = lanes((8, 128))
    pat = pat_ref[...].astype(f32)
    mask_rows = jnp.zeros((8, 128), f32)
    for t in range(8):
        mask_rows = jnp.where((lane8 % N) // 8 == t, pat[:, t : t + 1], mask_rows)
    lane = lanes((CELLS, N))
    acc = jnp.zeros((CELLS, N), f32)
    for m in range(32):
        if m % 8 == 0:
            copies[2 + m // 8].wait()
        y = jac_ref[:, m * 128 : (m + 1) * 128] * (u2 * mask_rows[m // 4 : m // 4 + 1])
        hi = y.astype(bf16)
        lo = (y - hi.astype(f32)).astype(bf16)
        z = jnp.dot(hi, half, preferred_element_type=f32) + jnp.dot(lo, half, preferred_element_type=f32)
        acc = jnp.where(lane // 2 == m, z, acc)
    copies[6].wait()
    copies[7].wait()
    tran = tran_ref[...]
    flux = tran * u
    flux_ref[...] = column(flux[CELLS - 1 : CELLS])
    row = lax.broadcasted_iota(jnp.int32, (CELLS, N), 0)
    lower = jnp.where(row == 0, 0.0, pltpu.roll(flux, 1, 0))
    upper = jnp.where(row == CELLS - 1, 0.0, pltpu.roll(u, CELLS - 1, 0))
    out_ref[...] = src_ref[...] - acc + lower + tran * upper


def upsweep(neigh_ref, part_ref, a_ref, b_ref, c_ref, top_ref, flux_ref, dens_ref, tran_ref, lat_ref, coup_ref, cols_ref,
            leaf_ref, n1_ref, n2_ref, n3_ref, n4_ref, n5_ref, root_ref, pay_ref, pair_ref, v_ref, w_ref):
    me = lax.axis_index("lat")
    u = dens_ref[...]
    total = jnp.zeros((CELLS, N), f32)
    lines = [(0, u), (1, a_ref[0])] + [(2 + i, b_ref[i]) for i in range(2)]
    lines += [((6, 7, 4, 5)[i], c_ref[i]) for i in range(4)]
    for offset, value in lines:
        line = me ^ offset
        count = jnp.int32(0)
        for j in range(4):
            count = count + (neigh_ref[0, j] == line).astype(jnp.int32)
        total = total + count.astype(f32) * value
    row = lax.broadcasted_iota(jnp.int32, (CELLS, N), 0)
    r = part_ref[...] - lat_ref[...] * (4.0 * u - total)
    r = r + jnp.where(row == CELLS - 1, tran_ref[...] * top_ref[0, 0:1], 0.0)
    c = coup_ref[...]
    g = r / jnp.where(row == 0, c, pltpu.roll(c, 1, 0))
    x = [(g if i == 0 else pltpu.roll(g, CELLS - i, 0)).T for i in range(4)]
    y = [rhs(t) for t in x]
    lane = lanes((N, CELLS))
    pair_v, pair_w = [], []
    for half in range(2):
        y0, y1 = y[2 * half], y[2 * half + 1]
        v = jnp.zeros((N, CELLS), f32)
        w = jnp.zeros((N, CELLS), f32)
        for j in range(8):
            at = 2 * j + half
            here = lane == 4 * j
            v = jnp.where(here, dot(n1_ref[at, 0], y0) + dot(leaf_ref[at, 0], y1), v)
            w = jnp.where(here, dot(n1_ref[at, 2], y0) + dot(n1_ref[at, 3], y1), w)
        pair_v.append(v + x[2 * half] + x[2 * half + 1])
        pair_w.append(w)
        pair_ref[half, :, 0:CELLS] = pair_v[half]
        pair_ref[2 + half, :, 0:CELLS] = w
    yv, yw = rhs(pair_v[0]), rhs(pair_w[1])
    v, w = pair_v[0] + pair_v[1], pair_w[0] + pair_w[1]
    dv = jnp.zeros((N, CELLS), f32)
    dw = jnp.zeros((N, CELLS), f32)
    for j in range(8):
        here = lane == 4 * j
        dv = jnp.where(here, dot(n1_ref[2 * j + 1, 0], yv), dv)
        dw = jnp.where(here, dot(n1_ref[2 * j, 1], yw) + dot(n2_ref[j, 3], yv), dw)
    v, w = v + dv, w + dw
    vs = [jnp.broadcast_to(v[:, 4 * j : 4 * j + 1], (N, 128)) for j in range(8)]
    ws = [jnp.broadcast_to(w[:, 4 * j : 4 * j + 1], (N, 128)) for j in range(8)]
    at = 0
    for count, ref, above in ((4, n2_ref, n3_ref), (2, n3_ref, n4_ref), (1, n4_ref, n5_ref)):
        next_v, next_w = [], []
        for j in range(count):
            v1, v2, w1, w2 = vs[2 * j], vs[2 * j + 1], ws[2 * j], ws[2 * j + 1]
            v_ref[at], w_ref[at] = v1, w2
            at += 1
            yv, yw = rhs(v1), rhs(w2)
            u_map = above[j, 3] if count > 1 else above[0]
            next_v.append(v1 + v2 + dot(ref[2 * j + 1, 0], yv))
            next_w.append(w1 + w2 + dot(ref[2 * j, 1], yw) + dot(u_map, yv))
        vs, ws = next_v, next_w
    lane = lanes((N, 128))
    pay_ref[:N] = root_ref[:N]
    tail = jnp.where(lane == N, vs[0] * cols_ref[0] + flux_ref[...], ws[0])
    pay_ref[N:] = jnp.where(lane < N, root_ref[N:], tail)


def prepare(pair_ref, v_ref, w_ref, n1_ref, n2_ref, n3_ref, n4_ref, t_ref, add_v, add_a, add_x):
    lane = lanes((N, 128))
    at, vec = 0, 0
    for level, size, ref in ((1, 8, n2_ref), (2, 16, n3_ref), (3, 32, n4_ref)):
        acc_v = jnp.zeros((N, 128), f32)
        acc_a = jnp.zeros((N, 128), f32)
        for j in range(CELLS // size):
            kw = ref[2 * j + 1, 2]
            wide = kw.astype(f32)
            t_ref[at] = pack(wide + roll(wide, N) + mm(kw, ref[2 * j, 0]))
            at += 1
            here = lane // size == j
            acc_v = jnp.where(here, v_ref[vec], acc_v)
            acc_a = jnp.where(here, w_ref[vec] + dot(kw, rhs(v_ref[vec])), acc_a)
            vec += 1
        add_v[level], add_a[level] = acc_v, acc_a
    first = lane % 4 == 0
    v0, v1, w0, w1 = [jnp.where(first, pair_ref[i], 0.0) for i in range(4)]
    y = rhs(v0)
    acc_a = jnp.zeros((N, 128), f32)
    for j in range(8):
        kw = n1_ref[2 * j + 1, 2]
        wide = kw.astype(f32)
        t_ref[at] = pack(wide + roll(wide, N) + mm(kw, n1_ref[2 * j, 0]))
        at += 1
        acc_a = jnp.where(lane == 4 * j, dot(kw, y), acc_a)
    acc_a = acc_a + w1
    spread_v = v0 + roll(v0, 1)
    spread_a = acc_a + roll(acc_a, 1)
    add_v[0] = spread_v + roll(spread_v, 2)
    add_a[0] = spread_a + roll(spread_a, 2)
    add_x[...] = w0 + roll(w1, 2) + roll(v0, 1) + roll(v1, 3)


def unpack(b):
    low = lanes((N, 128)) < N
    b1, b2 = b[:N], b[N:]
    r1, r2 = roll(b1, N), roll(b2, N)
    x = jnp.where(low, b1, r1)
    y = jnp.where(low, r1, b1)
    z = jnp.where(low, b2, r2)
    g = jnp.broadcast_to(b2[:, N : N + 1], (N, 128))
    h = jnp.broadcast_to(b2[:, N + 1 : N + 2], (N, 128))
    return x, y, z, g, h


def join(one, two, last=False):
    p1, q1, w1, v1, h1 = one
    p2, q2, w2, v2, h2 = two
    kq1, kp2, kw2 = pack(q1), pack(p2), pack(w2)
    yp1, yv1 = rhs(p1), rhs(v1)
    t = dot(kw2, yp1)
    th = h2 + dot(kw2, yv1)
    v = v2 + dot(kp2, yv1)
    yt, yth = rhs(t), rhs(th)
    w = w1 + dot(kq1, yt)
    h = h1 + dot(kq1, yth)
    yq2 = rhs(q2)
    p, q = (None, None) if last else (dot(kp2, yp1), dot(kq1, yq2))
    return (p, q, w, v, h), (t, th, yp1, yv1, yq2, yt, yth)


def track_first(is_low, one, two, extra):
    eye = eye2()
    t, th = extra[:2]
    return (
        jnp.where(is_low, eye, one[0]),
        jnp.where(is_low, two[1], eye),
        jnp.where(is_low, t, 0.0),
        jnp.where(is_low, 0.0, one[3]),
        jnp.where(is_low, th, 0.0),
    )


def track(is_low, fun, extra):
    f, hh, k, g, e = fun
    t, th, yp1, yv1, yq2, yt, yth = extra
    x1 = pack(jnp.where(is_low, hh, f))
    x2 = pack(jnp.where(is_low, hh, k))
    prod1 = dot(x1, jnp.where(is_low, yq2, yp1))
    prod2 = dot(x2, jnp.where(is_low, yt, yp1))
    vec1 = dot(x1, yv1)
    vec2 = dot(x2, jnp.where(is_low, yth, yv1))
    return (
        jnp.where(is_low, f, prod1),
        jnp.where(is_low, prod1, hh),
        jnp.where(is_low, k + prod2, prod2),
        jnp.where(is_low, g, g + vec1),
        e + vec2,
    )


def put_map(ref, p, q, w, v, h, last=False):
    lane = lanes((N, 128))
    low = lane < N
    tail = jnp.where(low, w, jnp.where(lane == N, v, h))
    if last:
        ref[...] = tail
    else:
        ref[:N] = jnp.where(low, p, q)
        ref[N:] = tail


def combine_two(level, own_ref, other_ref, fun_ref, out_ref, fun_out):
    is_low = ((lax.axis_index("depth") // (1, 2, 4, 8)[level]) % 2) == 0
    own, other = own_ref[...], other_ref[...]
    one = unpack(jnp.where(is_low, own, other))
    two = unpack(jnp.where(is_low, other, own))
    total, extra = join(one, two, last=level == 3)
    put_map(out_ref, *total, last=level == 3)
    put_map(fun_out, *track(is_low, unpack(fun_ref[...]), extra))


def combine_four(own_ref, x1_ref, x2_ref, x3_ref, out_ref, fun_out, slots):
    at = lax.axis_index("depth") % 4
    slots[at] = own_ref[...]
    slots[at ^ 1] = x1_ref[...]
    slots[at ^ 2] = x2_ref[...]
    slots[at ^ 3] = x3_ref[...]
    maps = [unpack(slots[i]) for i in range(4)]
    lower, extra_lower = join(maps[0], maps[1])
    upper, extra_upper = join(maps[2], maps[3])
    in_lower = at < 2
    mine = lambda a, b: jnp.where(in_lower, a, b)
    fun = track_first(
        at % 2 == 0,
        [mine(a, b) for a, b in zip(maps[0], maps[2])],
        [mine(a, b) for a, b in zip(maps[1], maps[3])],
        [mine(a, b) for a, b in zip(extra_lower[:2], extra_upper[:2])],
    )
    total, extra = join(lower, upper)
    put_map(out_ref, *total)
    put_map(fun_out, *track(in_lower, fun, extra))


def downsweep(own_ref, other_ref, fun_ref, cols_ref, add_v, add_a, add_x, leaf_ref, n1_ref, n2_ref, n3_ref, n4_ref, t_ref,
              out_ref):
    is_low = lax.axis_index("depth") < 2 * ZS
    f, hh, k, g, e = unpack(fun_ref[...])
    own, other = own_ref[...], other_ref[...]
    other_w = jnp.where(lanes((N, 128)) < N, other, roll(other, N))
    v_own = jnp.broadcast_to(own[:, N : N + 1], (N, 128))
    v_other = jnp.broadcast_to(other[:, N : N + 1], (N, 128))
    w_other = jnp.broadcast_to(other[:, N + 1 : N + 2], (N, 128))
    y_other = rhs(v_other)
    t = w_other + dot(pack(other_w), rhs(v_own))
    up = g + dot(pack(f), y_other)
    aa = e + dot(pack(jnp.where(is_low, hh, k)), rhs(jnp.where(is_low, t, v_other)))
    ss = jnp.where(is_low, g, up) * cols_ref[1]
    lane = lanes((N, 128))
    for level, size, ref, base in ((3, 32, n4_ref, 6), (2, 16, n3_ref, 4), (1, 8, n2_ref, 0), (0, 4, n1_ref, 7)):
        ys, ya = rhs(ss), rhs(aa)
        ds = jnp.zeros((N, 128), f32)
        da = jnp.zeros((N, 128), f32)
        for j in range(CELLS // size):
            here = lane // size == j
            ds = jnp.where(here, dot(ref[2 * j, 0], ys), ds)
            da = jnp.where(here, dot(ref[2 * j + 1, 1], ya) + dot(t_ref[base + j], ys), da)
        upper = lane % size >= size // 2
        new_s = ss + add_v[level] + ds
        new_a = aa + add_a[level] + da
        ss = jnp.where(upper, new_s, ss)
        aa = jnp.where(upper, aa, new_a)
    ys, ya = rhs(ss), rhs(aa)
    x = jnp.zeros((N, 128), f32)
    for j in range(CELLS // 2):
        x = jnp.where(lane == 2 * j, dot(n1_ref[j, 2], ys) + dot(n1_ref[j, 1], ya), x)
        x = jnp.where(lane == 2 * j + 1, dot(n1_ref[j, 0], ys) + dot(leaf_ref[j, 1], ya), x)
    x = x + aa + add_x[...] + jnp.where(lane % 2 == 1, ss, 0.0)
    out_ref[...] = x.T[:CELLS]


def sds(*shape, dtype=f32):
    return jax.ShapeDtypeStruct(shape, dtype)


def call(body, outs, *args, scratch=(), smem=0, hbm=0, flops=0, name=None):
    args = [pltpu.with_memory_space_constraint(x, pltpu.HBM) if smem <= i < smem + hbm else x for i, x in enumerate(args)]
    spaces = [pltpu.SMEM] * smem + [pltpu.HBM] * hbm + [pltpu.VMEM] * (len(args) - smem - hbm)
    return pl.pallas_call(
        body,
        out_shape=outs,
        in_specs=[pl.BlockSpec(memory_space=space) for space in spaces],
        out_specs=jax.tree.map(lambda _: pl.BlockSpec(memory_space=pltpu.VMEM), outs),
        scratch_shapes=scratch,
        cost_estimate=pl.CostEstimate(flops=flops, bytes_accessed=1 << 16, transcendentals=0),
        name=name,
        compiler_params=pltpu.CompilerParams(vmem_limit_bytes=VLIM),
    )(*args)


def node(count):
    return sds(count, 4, N, 128, dtype=bf16)


def on_device(densities, source, jacobian, pattern, transport, lateral, neighbours, factor, coupling):
    line_count, cell_count, species = densities.shape
    u = densities.reshape(CELLS, N)
    src = source.reshape(CELLS, N)
    tran = transport.reshape(CELLS, N)
    lat = lateral.reshape(CELLS, N)
    coup = coupling.reshape(CELLS, N)
    jac = jacobian.reshape(CELLS, N * N)
    fac = factor.reshape(4, 8, 32, 128).transpose(0, 2, 1, 3).reshape(1024, 128)

    def xor_lat(value, bits):
        return lax.ppermute(value, "lat", [(i, i ^ bits) for i in range(8)])

    def xor_depth(value, bits):
        return lax.ppermute(value, "depth", [(i, i ^ bits) for i in range(32)])

    line_a = xor_lat(densities, 1)
    part, flux = call(
        react, (sds(CELLS, N), sds(N, 128)), jac, u, src, tran, pattern, hbm=5, flops=1 << 30, name="react",
        scratch=[pltpu.VMEM((CELLS, N * N), f32)] + [pltpu.VMEM((CELLS, N), f32)] * 3
        + [pltpu.VMEM((8, 8), jnp.int32), pltpu.SemaphoreType.DMA((8,))],
    )
    line_b = xor_lat(jnp.concatenate([densities, line_a], axis=0), 2)
    leaf, n1, full, cols = call(
        tree_leaves,
        (sds(16, 2, N, 128, dtype=bf16), node(16), sds(16, 3, N, 128), sds(2, N, 128)),
        fac, coup, part, scratch=[pltpu.VMEM((2, N, 128), f32)], flops=2 << 30, name="tree_leaves",
    )
    top = lax.ppermute(lax.optimization_barrier((densities, cols))[0], "depth", [(i + 1, i) for i in range(31)])
    line_c = xor_lat(jnp.concatenate([densities, line_a, line_b], axis=0), 6)
    n2, n3, n4, n5, root = call(
        tree_upper,
        (node(8), node(4), node(2), sds(1, N, 128, dtype=bf16), sds(128, 128)),
        n1, full, coup, cols, part, scratch=[pltpu.VMEM((8, 3, N, 128), f32), pltpu.VMEM((4, 3, N, 128), f32)],
        flops=2 << 30, name="tree_upper",
    )
    pay, pair, vs, ws = call(
        upsweep, (sds(128, 128), sds(4, N, 128), sds(7, N, 128), sds(7, N, 128)),
        neighbours, part, line_a, line_b, line_c, top, flux, u, tran, lat, coup, cols, leaf, n1, n2, n3, n4, n5, root,
        smem=1, flops=1 << 25, name="upsweep",
    )
    others = [xor_depth(pay, bits) for bits in (1, 2, 3)]
    tees, add_v, add_a, add_x = call(
        prepare, (sds(15, N, 128, dtype=bf16), sds(4, N, 128), sds(4, N, 128), sds(N, 128)),
        pair, vs, ws, n1, n2, n3, n4, flops=1 << 30, name="prepare",
    )
    pay, fun = call(
        combine_four, (sds(128, 128), sds(128, 128)), pay, *others, scratch=[pltpu.VMEM((4, 128, 128), f32)],
        flops=1 << 24, name="combine_four",
    )
    for level, bits in ((2, 7), (3, 8)):
        other = xor_depth(pay, bits)
        pay, fun = call(
            lambda *refs, level=level: combine_two(level, *refs),
            (sds(N if level == 3 else 128, 128), sds(128, 128)), pay, other, fun, flops=1 << 24,
            name=f"combine{level}",
        )
    other = xor_depth(pay, 24)
    out = call(
        downsweep, sds(CELLS, N), pay, other, fun, cols, add_v, add_a, add_x, leaf, n1, n2, n3, n4, tees,
        flops=1 << 25, name="downsweep",
    )
    return out.reshape(line_count, cell_count, species)


def solution(mesh):
    return jax.shard_map(
        on_device,
        mesh=mesh,
        in_specs=(
            P("lat", "depth", None),
            P("lat", "depth", None),
            P("lat", "depth", None),
            P(),
            P("lat", "depth", None),
            P("lat", "depth", None),
            P("lat", None),
            P("lat", "depth", None),
            P("lat", "depth", None),
        ),
        out_specs=P("lat", "depth", None),
        check_vma=False,
    )
```

```python
import jax
import jax.numpy as jnp
from jax import lax
from jax.experimental import pallas as pl
from jax.experimental.pallas import tpu as pltpu
from jax.sharding import PartitionSpec as P


f32 = jnp.float32
bf16 = jnp.bfloat16

CELLS = 32
N = 64
ZS = 8
VLIM = 16 << 20


def lanes(shape):
    return lax.broadcasted_iota(jnp.int32, shape, len(shape) - 1)


def roll(x, shift):
    shift = shift % x.shape[-1]
    return x if shift == 0 else pltpu.roll(x, shift, x.ndim - 1)


def pack(dup):
    hi = dup.astype(bf16).astype(f32)
    return jnp.where(lanes(dup.shape) < N, hi, dup - hi).astype(bf16)


def mm(a, b):
    r = jnp.dot(a, jnp.concatenate([b, b], axis=0), preferred_element_type=f32)
    return r + roll(r, N)


def rhs(x):
    hi = x.astype(bf16)
    lo = (x - hi.astype(f32)).astype(bf16)
    return jnp.concatenate([hi, hi, lo, lo], axis=0)


def dot(a, y):
    return jnp.dot(jnp.concatenate([a, a], axis=1), y, preferred_element_type=f32)


def column(row):
    return jnp.broadcast_to(row, (128, N)).T


def pair(a, b):
    low = lanes(a.shape) < N
    a_hi, b_hi = a.astype(bf16).astype(f32), b.astype(bf16).astype(f32)
    hi = jnp.where(low, a_hi, b_hi).astype(bf16)
    lo = jnp.where(low, a - a_hi, b - b_hi).astype(bf16)
    return jnp.concatenate([hi, lo], axis=1)


def pair_rhs(x, y):
    def split(z):
        hi = z.astype(bf16).astype(f32)
        return jnp.where(lanes(z.shape) % 64 < CELLS, hi, z - hi).astype(bf16)

    a, b = split(x), split(y)
    return jnp.concatenate([a, b, a, b], axis=0)


def eye2():
    return jnp.where(lanes((N, 128)) % N == lax.broadcasted_iota(jnp.int32, (N, 128), 0), 1.0, 0.0)


def put(node, full, j, p, q, w, u=None):
    node[j, 0], node[j, 1], node[j, 2] = pack(p), pack(q), pack(w)
    full[j, 0], full[j, 1], full[j, 2] = p, q, w
    if u is not None:
        node[j, 3] = pack(u)


def tree_leaves(fac_ref, coup_ref, after_ref, quad_ref, n1_ref, full_ref, cols_ref, rows):
    del after_ref
    c = coup_ref[...]
    cols_ref[0] = column(c[CELLS - 1 : CELLS])
    cols_ref[1] = column(1.0 / c[0:1])
    c2 = jnp.concatenate([c, c], axis=1)
    low = lanes((CELLS, 128)) < N
    eye = eye2()

    def leaf(k):
        g, s = divmod(k, 8)
        x = fac_ref[pl.ds(g * 256 + s, 32, stride=8), :]
        y = roll(x, N)
        rows[k % 2, pl.ds(0, 32, stride=2), :] = jnp.where(low, x, y)
        rows[k % 2, pl.ds(1, 32, stride=2), :] = jnp.where(low, y, x)
        a = rows[k % 2]
        before = max(k - 1, 0)
        return a * c2[before : before + 1] - eye, a * c2[k : k + 1] - eye

    for j in range(CELLS // 2):
        p1, q1 = leaf(2 * j)
        p2, q2 = leaf(2 * j + 1)
        kq1 = pack(q1)
        p = p1 + p2 + dot(pack(p2), rhs(p1))
        q = q1 + q2 + dot(kq1, rhs(q2))
        u = eye + q1 + p2 + dot(kq1, rhs(p2))
        w = (eye + eye) + p1 + q1 + p + dot(kq1, rhs(p))
        put(n1_ref, full_ref, j, p, q, w)
        quad_ref[j, 0] = pair(p, p2)
        quad_ref[j, 1] = pair(w, u)
        quad_ref[j, 2] = pair(w, q)
        quad_ref[j, 3] = pair(p, q2)


def tree_upper(n1_ref, full_ref, coup_ref, cols_ref, after_ref, n2_ref, n3_ref, n4_ref, n5_ref, root_ref, fa, fb):
    del after_ref
    node, full = n1_ref, full_ref
    for count, node_to, full_to in ((8, n2_ref, fa), (4, n3_ref, fb), (2, n4_ref, fa), (1, None, None)):
        for j in range(count):
            one, two = 2 * j, 2 * j + 1
            kq1, yp1 = node[one, 1], rhs(full[one, 0])
            u = full[two, 2] + dot(kq1, rhs(full[two, 2]))
            p = full[one, 0] + full[two, 0] + dot(node[two, 0], yp1)
            q = full[one, 1] + full[two, 1] + dot(kq1, rhs(full[two, 1]))
            ku = pack(u)
            w = full[one, 2] + u + dot(ku, yp1)
            if node_to is None:
                eye = eye2()
                n5_ref[0] = ku
                first = coup_ref[0:1]
                scale = 1.0 / jnp.concatenate([first, first], axis=1)
                root_ref[:N] = jnp.where(lanes((N, 128)) < N, (p + eye) * cols_ref[0] * scale, q + eye)
                root_ref[N:] = w * scale
            else:
                put(node_to, full_to, j, p, q, w, u)
        node, full = node_to, full_to


def react(jac_hbm, dens_hbm, src_hbm, tran_hbm, pat_hbm, out_ref, flux_ref, jac_ref, dens_ref, src_ref, tran_ref,
          pat_ref, sems):
    parts = [(slice(None), pl.ds(i * 1024, 1024)) for i in range(4)]
    pairs = [(dens_hbm, dens_ref), (pat_hbm, pat_ref)] + [(jac_hbm.at[part], jac_ref.at[part]) for part in parts]
    pairs += [(src_hbm, src_ref), (tran_hbm, tran_ref)]
    copies = [pltpu.make_async_copy(a, b, sems.at[i]) for i, (a, b) in enumerate(pairs)]
    for copy in copies:
        copy.start()
    half = lanes((128, N)) % 2 == lax.broadcasted_iota(jnp.int32, (128, N), 0) // N
    half = jnp.where(half, 1.0, 0.0).astype(bf16)
    copies[0].wait()
    copies[1].wait()
    u = dens_ref[...]
    u2 = jnp.concatenate([u, u], axis=1)
    lane8 = lanes((8, 128))
    pat = pat_ref[...].astype(f32)
    mask_rows = jnp.zeros((8, 128), f32)
    for t in range(8):
        mask_rows = jnp.where((lane8 % N) // 8 == t, pat[:, t : t + 1], mask_rows)
    lane = lanes((CELLS, N))
    acc = jnp.zeros((CELLS, N), f32)
    for m in range(32):
        if m % 8 == 0:
            copies[2 + m // 8].wait()
        y = jac_ref[:, m * 128 : (m + 1) * 128] * (u2 * mask_rows[m // 4 : m // 4 + 1])
        hi = y.astype(bf16)
        lo = (y - hi.astype(f32)).astype(bf16)
        z = jnp.dot(hi, half, preferred_element_type=f32) + jnp.dot(lo, half, preferred_element_type=f32)
        acc = jnp.where(lane // 2 == m, z, acc)
    copies[6].wait()
    copies[7].wait()
    tran = tran_ref[...]
    flux = tran * u
    flux_ref[...] = column(flux[CELLS - 1 : CELLS])
    row = lax.broadcasted_iota(jnp.int32, (CELLS, N), 0)
    lower = jnp.where(row == 0, 0.0, pltpu.roll(flux, 1, 0))
    upper = jnp.where(row == CELLS - 1, 0.0, pltpu.roll(u, CELLS - 1, 0))
    out_ref[...] = src_ref[...] - acc + lower + tran * upper


def upsweep(neigh_ref, part_ref, a_ref, b_ref, c_ref, top_ref, flux_ref, dens_ref, tran_ref, lat_ref, coup_ref, cols_ref,
            quad_ref, n1_ref, n2_ref, n3_ref, n4_ref, n5_ref, root_ref, pay_ref, pair_ref, v_ref, w_ref):
    me = lax.axis_index("lat")
    u = dens_ref[...]
    total = jnp.zeros((CELLS, N), f32)
    lines = [(0, u), (1, a_ref[0])] + [(2 + i, b_ref[i]) for i in range(2)]
    lines += [((6, 7, 4, 5)[i], c_ref[i]) for i in range(4)]
    for offset, value in lines:
        line = me ^ offset
        count = jnp.int32(0)
        for j in range(4):
            count = count + (neigh_ref[0, j] == line).astype(jnp.int32)
        total = total + count.astype(f32) * value
    row = lax.broadcasted_iota(jnp.int32, (CELLS, N), 0)
    r = part_ref[...] - lat_ref[...] * (4.0 * u - total)
    r = r + jnp.where(row == CELLS - 1, tran_ref[...] * top_ref[0, 0:1], 0.0)
    c = coup_ref[...]
    g = r / jnp.where(row == 0, c, pltpu.roll(c, 1, 0))
    x = []
    for i in range(4):
        rolled = g if i == 0 else pltpu.roll(g, CELLS - i, 0)
        x.append(jnp.concatenate([rolled, rolled], axis=0).T)
    lane2 = lanes((N, N)) % CELLS
    lane = lanes((N, CELLS))
    pair_v, pair_w = [], []
    for half in range(2):
        x0, x1 = x[2 * half], x[2 * half + 1]
        y = pair_rhs(x0, x1)
        v = jnp.zeros((N, N), f32)
        w = jnp.zeros((N, N), f32)
        for j in range(8):
            at = 2 * j + half
            here = lane2 == 4 * j
            v = jnp.where(here, jnp.dot(quad_ref[at, 0], y, preferred_element_type=f32), v)
            w = jnp.where(here, jnp.dot(quad_ref[at, 1], y, preferred_element_type=f32), w)
        v = v[:, :CELLS] + v[:, CELLS:] + x0[:, :CELLS] + x1[:, :CELLS]
        w = w[:, :CELLS] + w[:, CELLS:]
        pair_v.append(v)
        pair_w.append(w)
        pair_ref[half, :, 0:CELLS] = pair_v[half]
        pair_ref[2 + half, :, 0:CELLS] = w
    yv, yw = rhs(pair_v[0]), rhs(pair_w[1])
    v, w = pair_v[0] + pair_v[1], pair_w[0] + pair_w[1]
    dv = jnp.zeros((N, CELLS), f32)
    dw = jnp.zeros((N, CELLS), f32)
    for j in range(8):
        here = lane == 4 * j
        dv = jnp.where(here, dot(n1_ref[2 * j + 1, 0], yv), dv)
        dw = jnp.where(here, dot(n1_ref[2 * j, 1], yw) + dot(n2_ref[j, 3], yv), dw)
    v, w = v + dv, w + dw
    vs = [jnp.broadcast_to(v[:, 4 * j : 4 * j + 1], (N, 128)) for j in range(8)]
    ws = [jnp.broadcast_to(w[:, 4 * j : 4 * j + 1], (N, 128)) for j in range(8)]
    at = 0
    for count, ref, above in ((4, n2_ref, n3_ref), (2, n3_ref, n4_ref), (1, n4_ref, n5_ref)):
        next_v, next_w = [], []
        for j in range(count):
            v1, v2, w1, w2 = vs[2 * j], vs[2 * j + 1], ws[2 * j], ws[2 * j + 1]
            v_ref[at], w_ref[at] = v1, w2
            at += 1
            yv, yw = rhs(v1), rhs(w2)
            u_map = above[j, 3] if count > 1 else above[0]
            next_v.append(v1 + v2 + dot(ref[2 * j + 1, 0], yv))
            next_w.append(w1 + w2 + dot(ref[2 * j, 1], yw) + dot(u_map, yv))
        vs, ws = next_v, next_w
    lane = lanes((N, 128))
    pay_ref[:N] = root_ref[:N]
    tail = jnp.where(lane == N, vs[0] * cols_ref[0] + flux_ref[...], ws[0])
    pay_ref[N:] = jnp.where(lane < N, root_ref[N:], tail)


def prepare(pair_ref, v_ref, w_ref, n1_ref, n2_ref, n3_ref, n4_ref, t_ref, add_v, add_a, add_x):
    lane = lanes((N, 128))
    part = lane % CELLS
    at, vec = 0, 0
    for level, size, ref in ((1, 8, n2_ref), (2, 16, n3_ref), (3, 32, n4_ref)):
        acc_v = jnp.zeros((N, 128), f32)
        acc_a = jnp.zeros((N, 128), f32)
        for j in range(CELLS // size):
            kw = ref[2 * j + 1, 2]
            wide = kw.astype(f32)
            t_ref[at] = pack(wide + roll(wide, N) + mm(kw, ref[2 * j, 0]))
            at += 1
            here = part // size == j
            acc_v = jnp.where(here, v_ref[vec], acc_v)
            acc_a = jnp.where(here, w_ref[vec] + dot(kw, rhs(v_ref[vec])), acc_a)
            vec += 1
        add_v[level], add_a[level] = acc_v, acc_a

    def repeat(x):
        x = x + roll(x, CELLS)
        return x + roll(x, 2 * CELLS)

    first = jnp.logical_and(lane % 4 == 0, lane < CELLS)
    v0, v1, w0, w1 = [jnp.where(first, pair_ref[i], 0.0) for i in range(4)]
    y = rhs(v0)
    acc_a = jnp.zeros((N, 128), f32)
    for j in range(8):
        kw = n1_ref[2 * j + 1, 2]
        wide = kw.astype(f32)
        t_ref[at] = pack(wide + roll(wide, N) + mm(kw, n1_ref[2 * j, 0]))
        at += 1
        acc_a = jnp.where(lane == 4 * j, dot(kw, y), acc_a)
    acc_a = acc_a + w1
    spread_v = v0 + roll(v0, 1)
    spread_a = acc_a + roll(acc_a, 1)
    add_v[0] = repeat(spread_v + roll(spread_v, 2))
    add_a[0] = repeat(spread_a + roll(spread_a, 2))
    add_x[...] = repeat(w0 + roll(w1, 2) + roll(v0, 1) + roll(v1, 3))


def prepare_last(own_ref, fun_ref, maps_ref, vecs_ref, own_rhs):
    is_low = lax.axis_index("depth") < 2 * ZS
    f, hh, k, g, e = unpack(fun_ref[...])
    maps_ref[0], maps_ref[1] = pack(f), pack(jnp.where(is_low, hh, k))
    vecs_ref[0], vecs_ref[1] = g, e
    v = jnp.broadcast_to(own_ref[:, N : N + 1], (N, 128))
    hi = v.astype(bf16)
    lo = (v - hi.astype(f32)).astype(bf16)
    zero = jnp.zeros((N, 128), bf16)
    own_rhs[0] = jnp.concatenate([hi, zero, hi, zero], axis=0)
    own_rhs[1] = jnp.concatenate([lo, zero, lo, zero], axis=0)


def unpack(b):
    low = lanes((N, 128)) < N
    b1, b2 = b[:N], b[N:]
    r1, r2 = roll(b1, N), roll(b2, N)
    x = jnp.where(low, b1, r1)
    y = jnp.where(low, r1, b1)
    z = jnp.where(low, b2, r2)
    g = jnp.broadcast_to(b2[:, N : N + 1], (N, 128))
    h = jnp.broadcast_to(b2[:, N + 1 : N + 2], (N, 128))
    return x, y, z, g, h


def join(one, two, last=False):
    p1, q1, w1, v1, h1 = one
    p2, q2, w2, v2, h2 = two
    kq1, kp2, kw2 = pack(q1), pack(p2), pack(w2)
    yp1, yv1 = rhs(p1), rhs(v1)
    t = dot(kw2, yp1)
    th = h2 + dot(kw2, yv1)
    v = v2 + dot(kp2, yv1)
    yt, yth = rhs(t), rhs(th)
    w = w1 + dot(kq1, yt)
    h = h1 + dot(kq1, yth)
    yq2 = rhs(q2)
    p, q = (None, None) if last else (dot(kp2, yp1), dot(kq1, yq2))
    return (p, q, w, v, h), (t, th, yp1, yv1, yq2, yt, yth)


def track_first(is_low, one, two, extra):
    eye = eye2()
    t, th = extra[:2]
    return (
        jnp.where(is_low, eye, one[0]),
        jnp.where(is_low, two[1], eye),
        jnp.where(is_low, t, 0.0),
        jnp.where(is_low, 0.0, one[3]),
        jnp.where(is_low, th, 0.0),
    )


def track(is_low, fun, extra):
    f, hh, k, g, e = fun
    _, _, yp1, yv1, yq2, yt, yth = extra
    x1 = pack(jnp.where(is_low, hh, f))
    x2 = pack(jnp.where(is_low, hh, k))
    prod1 = dot(x1, jnp.where(is_low, yq2, yp1))
    prod2 = dot(x2, jnp.where(is_low, yt, yp1))
    vec1 = dot(x1, yv1)
    vec2 = dot(x2, jnp.where(is_low, yth, yv1))
    return (
        jnp.where(is_low, f, prod1),
        jnp.where(is_low, prod1, hh),
        jnp.where(is_low, k + prod2, prod2),
        jnp.where(is_low, g, g + vec1),
        e + vec2,
    )


def put_map(ref, p, q, w, v, h, last=False):
    lane = lanes((N, 128))
    low = lane < N
    tail = jnp.where(low, w, jnp.where(lane == N, v, h))
    if last:
        ref[...] = tail
    else:
        ref[:N] = jnp.where(low, p, q)
        ref[N:] = tail


def combine_two(level, own_ref, other_ref, fun_ref, out_ref, fun_out):
    is_low = ((lax.axis_index("depth") // (1, 2, 4, 8)[level]) % 2) == 0
    own, other = own_ref[...], other_ref[...]
    one = unpack(jnp.where(is_low, own, other))
    two = unpack(jnp.where(is_low, other, own))
    total, extra = join(one, two, last=level == 3)
    put_map(out_ref, *total, last=level == 3)
    put_map(fun_out, *track(is_low, unpack(fun_ref[...]), extra))


def combine_four(own_ref, x1_ref, x2_ref, x3_ref, out_ref, fun_out, slots):
    at = lax.axis_index("depth") % 4
    slots[at] = own_ref[...]
    slots[at ^ 1] = x1_ref[...]
    slots[at ^ 2] = x2_ref[...]
    slots[at ^ 3] = x3_ref[...]
    maps = [unpack(slots[i]) for i in range(4)]
    lower, extra_lower = join(maps[0], maps[1])
    upper, extra_upper = join(maps[2], maps[3])
    in_lower = at < 2
    mine = lambda a, b: jnp.where(in_lower, a, b)
    fun = track_first(
        at % 2 == 0,
        [mine(a, b) for a, b in zip(maps[0], maps[2])],
        [mine(a, b) for a, b in zip(maps[1], maps[3])],
        [mine(a, b) for a, b in zip(extra_lower[:2], extra_upper[:2])],
    )
    total, extra = join(lower, upper)
    put_map(out_ref, *total)
    put_map(fun_out, *track(in_lower, fun, extra))


def downsweep(other_ref, maps_ref, vecs_ref, own_rhs, cols_ref, add_v, add_a, add_x, quad_ref, n1_ref, n2_ref, n3_ref,
              n4_ref, t_ref, out_ref):
    is_low = lax.axis_index("depth") < 2 * ZS
    g, e = vecs_ref[0], vecs_ref[1]
    other = other_ref[...]
    hi = other.astype(bf16)
    wide = jnp.concatenate([hi, (other - hi.astype(f32)).astype(bf16)], axis=1)
    v_other = jnp.broadcast_to(other[:, N : N + 1], (N, 128))
    w_other = jnp.broadcast_to(other[:, N + 1 : N + 2], (N, 128))
    t = w_other + jnp.dot(wide, own_rhs[0], preferred_element_type=f32)
    t = t + jnp.dot(wide, own_rhs[1], preferred_element_type=f32)
    up = g + dot(maps_ref[0], rhs(v_other))
    aa = e + dot(maps_ref[1], rhs(jnp.where(is_low, t, v_other)))
    ss = jnp.where(is_low, g, up) * cols_ref[1]
    lane = lanes((N, 128)) % CELLS
    for level, size, ref, base in ((3, 32, n4_ref, 6), (2, 16, n3_ref, 4), (1, 8, n2_ref, 0), (0, 4, n1_ref, 7)):
        ys, ya = rhs(ss), rhs(aa)
        ds = jnp.zeros((N, 128), f32)
        da = jnp.zeros((N, 128), f32)
        for j in range(CELLS // size):
            here = lane // size == j
            ds = jnp.where(here, dot(ref[2 * j, 0], ys), ds)
            da = jnp.where(here, dot(ref[2 * j + 1, 1], ya) + dot(t_ref[base + j], ys), da)
        upper = lane % size >= size // 2
        new_s = ss + add_v[level] + ds
        new_a = aa + add_a[level] + da
        ss = jnp.where(upper, new_s, ss)
        aa = jnp.where(upper, aa, new_a)
    y = pair_rhs(ss, aa)
    x = jnp.zeros((N, 128), f32)
    for j in range(CELLS // 2):
        x = jnp.where(lane == 2 * j, jnp.dot(quad_ref[j, 2], y, preferred_element_type=f32), x)
        x = jnp.where(lane == 2 * j + 1, jnp.dot(quad_ref[j, 3], y, preferred_element_type=f32), x)
    x = x + roll(x, CELLS) + (aa + add_x[...] + jnp.where(lane % 2 == 1, ss, 0.0))
    out_ref[...] = x.T[:CELLS]


def sds(*shape, dtype=f32):
    return jax.ShapeDtypeStruct(shape, dtype)


def call(body, outs, *args, scratch=(), smem=0, hbm=0, flops=0):
    args = [pltpu.with_memory_space_constraint(x, pltpu.HBM) if smem <= i < smem + hbm else x for i, x in enumerate(args)]
    spaces = [pltpu.SMEM] * smem + [pltpu.HBM] * hbm + [pltpu.VMEM] * (len(args) - smem - hbm)
    return pl.pallas_call(
        body,
        out_shape=outs,
        in_specs=[pl.BlockSpec(memory_space=space) for space in spaces],
        out_specs=jax.tree.map(lambda _: pl.BlockSpec(memory_space=pltpu.VMEM), outs),
        scratch_shapes=scratch,
        cost_estimate=pl.CostEstimate(flops=flops, bytes_accessed=1 << 16, transcendentals=0),
        compiler_params=pltpu.CompilerParams(vmem_limit_bytes=VLIM),
    )(*args)


def node(count):
    return sds(count, 4, N, 128, dtype=bf16)


def on_device(densities, source, jacobian, pattern, transport, lateral, neighbours, factor, coupling):
    line_count, cell_count, species = densities.shape
    u = densities.reshape(CELLS, N)
    src = source.reshape(CELLS, N)
    tran = transport.reshape(CELLS, N)
    lat = lateral.reshape(CELLS, N)
    coup = coupling.reshape(CELLS, N)
    jac = jacobian.reshape(CELLS, N * N)
    fac = factor.reshape(4, 8, 32, 128).transpose(0, 2, 1, 3).reshape(1024, 128)

    def xor_lat(value, bits):
        return lax.ppermute(value, "lat", [(i, i ^ bits) for i in range(8)])

    def xor_depth(value, bits):
        return lax.ppermute(value, "depth", [(i, i ^ bits) for i in range(32)])

    top = lax.ppermute(densities, "depth", [(i + 1, i) for i in range(31)])
    line_a = xor_lat(densities, 1)
    part, flux = call(
        react, (sds(CELLS, N), sds(N, 128)), jac, u, src, tran, pattern, hbm=5, flops=1 << 30,
        scratch=[pltpu.VMEM((CELLS, N * N), f32)] + [pltpu.VMEM((CELLS, N), f32)] * 3
        + [pltpu.VMEM((8, 8), jnp.int32), pltpu.SemaphoreType.DMA((8,))],
    )
    line_b = xor_lat(jnp.concatenate([densities, line_a], axis=0), 2)
    quad, n1, full, cols = call(
        tree_leaves,
        (sds(16, 4, N, 256, dtype=bf16), sds(16, 3, N, 128, dtype=bf16), sds(16, 3, N, 128), sds(2, N, 128)),
        fac, coup, part, scratch=[pltpu.VMEM((2, N, 128), f32)], flops=2 << 30,
    )
    line_c = xor_lat(jnp.concatenate([densities, line_a, line_b], axis=0), 6)
    n2, n3, n4, n5, root = call(
        tree_upper,
        (node(8), node(4), node(2), sds(1, N, 128, dtype=bf16), sds(128, 128)),
        n1, full, coup, cols, part, scratch=[pltpu.VMEM((8, 3, N, 128), f32), pltpu.VMEM((4, 3, N, 128), f32)],
        flops=2 << 30,
    )
    pay, pair, vs, ws = call(
        upsweep, (sds(128, 128), sds(4, N, 128), sds(7, N, 128), sds(7, N, 128)),
        neighbours, part, line_a, line_b, line_c, top, flux, u, tran, lat, coup, cols, quad, n1, n2, n3, n4, n5, root,
        smem=1, flops=1 << 25,
    )
    others = [xor_depth(pay, bits) for bits in (1, 2, 3)]
    tees, add_v, add_a, add_x = call(
        prepare, (sds(15, N, 128, dtype=bf16), sds(4, N, 128), sds(4, N, 128), sds(N, 128)),
        pair, vs, ws, n1, n2, n3, n4, flops=1 << 30,
    )
    pay, fun = call(
        combine_four, (sds(128, 128), sds(128, 128)), pay, *others, scratch=[pltpu.VMEM((4, 128, 128), f32)],
        flops=1 << 24,
    )
    for level, bits in ((2, 7), (3, 8)):
        other = xor_depth(pay, bits)
        pay, fun = call(
            lambda *refs, level=level: combine_two(level, *refs),
            (sds(N if level == 3 else 128, 128), sds(128, 128)), pay, other, fun, flops=1 << 24,
        )
    other = xor_depth(pay, 24)
    maps, vecs, own_rhs = call(
        prepare_last,
        (sds(2, N, 128, dtype=bf16), sds(2, N, 128), sds(2, 256, 128, dtype=bf16)),
        pay, fun, flops=1 << 30,
    )
    out = call(
        downsweep, sds(CELLS, N), other, maps, vecs, own_rhs, cols, add_v, add_a, add_x, quad, n1, n2, n3, n4, tees,
        flops=1 << 25,
    )
    return out.reshape(line_count, cell_count, species)


def solution(mesh):
    return jax.shard_map(
        on_device,
        mesh=mesh,
        in_specs=(
            P("lat", "depth", None),
            P("lat", "depth", None),
            P("lat", "depth", None),
            P(),
            P("lat", "depth", None),
            P("lat", "depth", None),
            P("lat", None),
            P("lat", "depth", None),
            P("lat", "depth", None),
        ),
        out_specs=P("lat", "depth", None),
        check_vma=False,
    )
```

```python
import jax
import jax.numpy as jnp
from jax import lax
from jax.experimental import pallas as pl
from jax.experimental.pallas import tpu as pltpu
from jax.sharding import PartitionSpec as P

f32 = jnp.float32
bf16 = jnp.bfloat16

CELLS = 32
N = 64
ZS = 8
VLIM = 16 << 20


def lanes(shape):
    return lax.broadcasted_iota(jnp.int32, shape, len(shape) - 1)


def roll(x, shift):
    shift = shift % x.shape[-1]
    return x if shift == 0 else pltpu.roll(x, shift, x.ndim - 1)


def pack(dup):
    hi = dup.astype(bf16).astype(f32)
    return jnp.where(lanes(dup.shape) < N, hi, dup - hi).astype(bf16)


def mm(a, b):
    r = jnp.dot(a, jnp.concatenate([b, b], axis=0), preferred_element_type=f32)
    return r + roll(r, N)


def rhs(x):
    hi = x.astype(bf16)
    lo = (x - hi.astype(f32)).astype(bf16)
    return jnp.concatenate([hi, hi, lo, lo], axis=0)


def dot(a, y):
    return jnp.dot(jnp.concatenate([a, a], axis=1), y, preferred_element_type=f32)


def column(row):
    return jnp.broadcast_to(row, (128, N)).T


def pair(a, b):
    low = lanes(a.shape) < N
    a_hi, b_hi = a.astype(bf16).astype(f32), b.astype(bf16).astype(f32)
    hi = jnp.where(low, a_hi, b_hi).astype(bf16)
    lo = jnp.where(low, a - a_hi, b - b_hi).astype(bf16)
    return jnp.concatenate([hi, lo], axis=1)


def pair_rhs(x, y):
    def split(z):
        hi = z.astype(bf16).astype(f32)
        return jnp.where(lanes(z.shape) % 64 < CELLS, hi, z - hi).astype(bf16)

    a, b = split(x), split(y)
    return jnp.concatenate([a, b, a, b], axis=0)


def eye2():
    return jnp.where(lanes((N, 128)) % N == lax.broadcasted_iota(jnp.int32, (N, 128), 0), 1.0, 0.0)


def put(node, full, j, p, q, w, u=None):
    node[j, 0], node[j, 1], node[j, 2] = pack(p), pack(q), pack(w)
    full[j, 0], full[j, 1], full[j, 2] = p, q, w
    if u is not None:
        node[j, 3] = pack(u)


def tree_leaves(fac_ref, coup_ref, after_ref, quad_ref, n1_ref, full_ref, cols_ref, rows):
    del after_ref
    c = coup_ref[...]
    cols_ref[0] = column(c[CELLS - 1 : CELLS])
    cols_ref[1] = column(1.0 / c[0:1])
    c2 = jnp.concatenate([c, c], axis=1)
    low = lanes((CELLS, 128)) < N
    eye = eye2()

    def leaf(k):
        g, s = divmod(k, 8)
        x = fac_ref[pl.ds(g * 256 + s, 32, stride=8), :]
        y = roll(x, N)
        rows[k % 2, pl.ds(0, 32, stride=2), :] = jnp.where(low, x, y)
        rows[k % 2, pl.ds(1, 32, stride=2), :] = jnp.where(low, y, x)
        a = rows[k % 2]
        before = max(k - 1, 0)
        return a * c2[before : before + 1] - eye, a * c2[k : k + 1] - eye

    for j in range(CELLS // 2):
        p1, q1 = leaf(2 * j)
        p2, q2 = leaf(2 * j + 1)
        kq1 = pack(q1)
        p = p1 + p2 + dot(pack(p2), rhs(p1))
        q = q1 + q2 + dot(kq1, rhs(q2))
        u = eye + q1 + p2 + dot(kq1, rhs(p2))
        w = (eye + eye) + p1 + q1 + p + dot(kq1, rhs(p))
        put(n1_ref, full_ref, j, p, q, w)
        quad_ref[j, 0] = pair(p, p2)
        quad_ref[j, 1] = pair(w, u)
        quad_ref[j, 2] = pair(w, q)
        quad_ref[j, 3] = pair(p, q2)


def tree_upper(n1_ref, full_ref, coup_ref, cols_ref, after_ref, n2_ref, n3_ref, n4_ref, n5_ref, root_ref, fa, fb):
    del after_ref
    node, full = n1_ref, full_ref
    for count, node_to, full_to in ((8, n2_ref, fa), (4, n3_ref, fb), (2, n4_ref, fa), (1, None, None)):
        for j in range(count):
            one, two = 2 * j, 2 * j + 1
            kq1, yp1 = node[one, 1], rhs(full[one, 0])
            u = full[two, 2] + dot(kq1, rhs(full[two, 2]))
            p = full[one, 0] + full[two, 0] + dot(node[two, 0], yp1)
            q = full[one, 1] + full[two, 1] + dot(kq1, rhs(full[two, 1]))
            ku = pack(u)
            w = full[one, 2] + u + dot(ku, yp1)
            if node_to is None:
                eye = eye2()
                n5_ref[0] = ku
                first = coup_ref[0:1]
                scale = 1.0 / jnp.concatenate([first, first], axis=1)
                root_ref[:N] = jnp.where(lanes((N, 128)) < N, (p + eye) * cols_ref[0] * scale, q + eye)
                root_ref[N:] = w * scale
            else:
                put(node_to, full_to, j, p, q, w, u)
        node, full = node_to, full_to


def react(jac_hbm, dens_hbm, src_hbm, tran_hbm, pat_hbm, out_ref, flux_ref, jac_ref, dens_ref, src_ref, tran_ref,
          pat_ref, sems):
    parts = [(slice(None), pl.ds(i * 1024, 1024)) for i in range(4)]
    pairs = [(dens_hbm, dens_ref), (pat_hbm, pat_ref)] + [(jac_hbm.at[part], jac_ref.at[part]) for part in parts]
    pairs += [(src_hbm, src_ref), (tran_hbm, tran_ref)]
    copies = [pltpu.make_async_copy(a, b, sems.at[i]) for i, (a, b) in enumerate(pairs)]
    for copy in copies:
        copy.start()
    half = lanes((128, N)) % 2 == lax.broadcasted_iota(jnp.int32, (128, N), 0) // N
    half = jnp.where(half, 1.0, 0.0).astype(bf16)
    copies[0].wait()
    copies[1].wait()
    u = dens_ref[...]
    u2 = jnp.concatenate([u, u], axis=1)
    lane8 = lanes((8, 128))
    pat = pat_ref[...].astype(f32)
    mask_rows = jnp.zeros((8, 128), f32)
    for t in range(8):
        mask_rows = jnp.where((lane8 % N) // 8 == t, pat[:, t : t + 1], mask_rows)
    lane = lanes((CELLS, N))
    acc = jnp.zeros((CELLS, N), f32)
    for m in range(32):
        if m % 8 == 0:
            copies[2 + m // 8].wait()
        y = jac_ref[:, m * 128 : (m + 1) * 128] * (u2 * mask_rows[m // 4 : m // 4 + 1])
        hi = y.astype(bf16)
        lo = (y - hi.astype(f32)).astype(bf16)
        z = jnp.dot(hi, half, preferred_element_type=f32) + jnp.dot(lo, half, preferred_element_type=f32)
        acc = jnp.where(lane // 2 == m, z, acc)
    copies[6].wait()
    copies[7].wait()
    tran = tran_ref[...]
    flux = tran * u
    flux_ref[...] = column(flux[CELLS - 1 : CELLS])
    row = lax.broadcasted_iota(jnp.int32, (CELLS, N), 0)
    lower = jnp.where(row == 0, 0.0, pltpu.roll(flux, 1, 0))
    upper = jnp.where(row == CELLS - 1, 0.0, pltpu.roll(u, CELLS - 1, 0))
    out_ref[...] = src_ref[...] - acc + lower + tran * upper


def upsweep(neigh_ref, part_ref, a_ref, b_ref, c_ref, even_ref, odd_ref, flux_ref, dens_ref, tran_ref, lat_ref, coup_ref, cols_ref,
            quad_ref, n1_ref, n2_ref, n3_ref, n4_ref, n5_ref, root_ref, pay_ref, pair_ref, v_ref, w_ref):
    me = lax.axis_index("lat")
    u = dens_ref[...]
    total = jnp.zeros((CELLS, N), f32)
    lines = [(0, u), (1, a_ref[0])] + [(2 + i, b_ref[i]) for i in range(2)]
    lines += [((6, 7, 4, 5)[i], c_ref[i]) for i in range(4)]
    for offset, value in lines:
        line = me ^ offset
        count = jnp.int32(0)
        for j in range(4):
            count = count + (neigh_ref[0, j] == line).astype(jnp.int32)
        total = total + count.astype(f32) * value
    row = lax.broadcasted_iota(jnp.int32, (CELLS, N), 0)
    r = part_ref[...] - lat_ref[...] * (4.0 * u - total)
    depth = lax.axis_index("depth")
    above = jnp.where(depth % 2 == 0, even_ref[0, 0:1], odd_ref[0, 0:1])
    above = jnp.where(depth == lax.axis_size("depth") - 1, 0.0, above)
    r = r + jnp.where(row == CELLS - 1, tran_ref[...] * above, 0.0)
    c = coup_ref[...]
    g = r / jnp.where(row == 0, c, pltpu.roll(c, 1, 0))
    x = []
    for i in range(4):
        rolled = g if i == 0 else pltpu.roll(g, CELLS - i, 0)
        x.append(jnp.concatenate([rolled, rolled], axis=0).T)
    lane2 = lanes((N, N)) % CELLS
    lane = lanes((N, CELLS))
    pair_v, pair_w = [], []
    for half in range(2):
        x0, x1 = x[2 * half], x[2 * half + 1]
        y = pair_rhs(x0, x1)
        v = jnp.zeros((N, N), f32)
        w = jnp.zeros((N, N), f32)
        for j in range(8):
            at = 2 * j + half
            here = lane2 == 4 * j
            v = jnp.where(here, jnp.dot(quad_ref[at, 0], y, preferred_element_type=f32), v)
            w = jnp.where(here, jnp.dot(quad_ref[at, 1], y, preferred_element_type=f32), w)
        v = v[:, :CELLS] + v[:, CELLS:] + x0[:, :CELLS] + x1[:, :CELLS]
        w = w[:, :CELLS] + w[:, CELLS:]
        pair_v.append(v)
        pair_w.append(w)
        pair_ref[half, :, 0:CELLS] = pair_v[half]
        pair_ref[2 + half, :, 0:CELLS] = w
    yv, yw = rhs(pair_v[0]), rhs(pair_w[1])
    v, w = pair_v[0] + pair_v[1], pair_w[0] + pair_w[1]
    dv = jnp.zeros((N, CELLS), f32)
    dw = jnp.zeros((N, CELLS), f32)
    for j in range(8):
        here = lane == 4 * j
        dv = jnp.where(here, dot(n1_ref[2 * j + 1, 0], yv), dv)
        dw = jnp.where(here, dot(n1_ref[2 * j, 1], yw) + dot(n2_ref[j, 3], yv), dw)
    v, w = v + dv, w + dw
    vs = [jnp.broadcast_to(v[:, 4 * j : 4 * j + 1], (N, 128)) for j in range(8)]
    ws = [jnp.broadcast_to(w[:, 4 * j : 4 * j + 1], (N, 128)) for j in range(8)]
    at = 0
    for count, ref, above in ((4, n2_ref, n3_ref), (2, n3_ref, n4_ref), (1, n4_ref, n5_ref)):
        next_v, next_w = [], []
        for j in range(count):
            v1, v2, w1, w2 = vs[2 * j], vs[2 * j + 1], ws[2 * j], ws[2 * j + 1]
            v_ref[at], w_ref[at] = v1, w2
            at += 1
            yv, yw = rhs(v1), rhs(w2)
            u_map = above[j, 3] if count > 1 else above[0]
            next_v.append(v1 + v2 + dot(ref[2 * j + 1, 0], yv))
            next_w.append(w1 + w2 + dot(ref[2 * j, 1], yw) + dot(u_map, yv))
        vs, ws = next_v, next_w
    lane = lanes((N, 128))
    pay_ref[:N] = root_ref[:N]
    tail = jnp.where(lane == N, vs[0] * cols_ref[0] + flux_ref[...], ws[0])
    pay_ref[N:] = jnp.where(lane < N, root_ref[N:], tail)


def prepare(pair_ref, v_ref, w_ref, n1_ref, n2_ref, n3_ref, n4_ref, t_ref, add_v, add_a, add_x):
    lane = lanes((N, 128))
    part = lane % CELLS
    at, vec = 0, 0
    for level, size, ref in ((1, 8, n2_ref), (2, 16, n3_ref), (3, 32, n4_ref)):
        acc_v = jnp.zeros((N, 128), f32)
        acc_a = jnp.zeros((N, 128), f32)
        for j in range(CELLS // size):
            kw = ref[2 * j + 1, 2]
            wide = kw.astype(f32)
            t_ref[at] = pack(wide + roll(wide, N) + mm(kw, ref[2 * j, 0]))
            at += 1
            here = part // size == j
            acc_v = jnp.where(here, v_ref[vec], acc_v)
            acc_a = jnp.where(here, w_ref[vec] + dot(kw, rhs(v_ref[vec])), acc_a)
            vec += 1
        add_v[level], add_a[level] = acc_v, acc_a

    def repeat(x):
        x = x + roll(x, CELLS)
        return x + roll(x, 2 * CELLS)

    first = jnp.logical_and(lane % 4 == 0, lane < CELLS)
    v0, v1, w0, w1 = [jnp.where(first, pair_ref[i], 0.0) for i in range(4)]
    y = rhs(v0)
    acc_a = jnp.zeros((N, 128), f32)
    for j in range(8):
        kw = n1_ref[2 * j + 1, 2]
        wide = kw.astype(f32)
        t_ref[at] = pack(wide + roll(wide, N) + mm(kw, n1_ref[2 * j, 0]))
        at += 1
        acc_a = jnp.where(lane == 4 * j, dot(kw, y), acc_a)
    acc_a = acc_a + w1
    spread_v = v0 + roll(v0, 1)
    spread_a = acc_a + roll(acc_a, 1)
    add_v[0] = repeat(spread_v + roll(spread_v, 2))
    add_a[0] = repeat(spread_a + roll(spread_a, 2))
    add_x[...] = repeat(w0 + roll(w1, 2) + roll(v0, 1) + roll(v1, 3))


def prepare_last(own_ref, fun_ref, maps_ref, vecs_ref, own_rhs):
    is_low = lax.axis_index("depth") < 2 * ZS
    f, hh, k, g, e = unpack(fun_ref[...])
    maps_ref[0], maps_ref[1] = pack(f), pack(jnp.where(is_low, hh, k))
    vecs_ref[0], vecs_ref[1] = g, e
    v = jnp.broadcast_to(own_ref[:, N : N + 1], (N, 128))
    hi = v.astype(bf16)
    lo = (v - hi.astype(f32)).astype(bf16)
    zero = jnp.zeros((N, 128), bf16)
    own_rhs[0] = jnp.concatenate([hi, zero, hi, zero], axis=0)
    own_rhs[1] = jnp.concatenate([lo, zero, lo, zero], axis=0)


def unpack(b):
    low = lanes((N, 128)) < N
    b1, b2 = b[:N], b[N:]
    r1, r2 = roll(b1, N), roll(b2, N)
    x = jnp.where(low, b1, r1)
    y = jnp.where(low, r1, b1)
    z = jnp.where(low, b2, r2)
    g = jnp.broadcast_to(b2[:, N : N + 1], (N, 128))
    h = jnp.broadcast_to(b2[:, N + 1 : N + 2], (N, 128))
    return x, y, z, g, h


def join(one, two, last=False):
    p1, q1, w1, v1, h1 = one
    p2, q2, w2, v2, h2 = two
    kq1, kp2, kw2 = pack(q1), pack(p2), pack(w2)
    yp1, yv1 = rhs(p1), rhs(v1)
    t = dot(kw2, yp1)
    th = h2 + dot(kw2, yv1)
    v = v2 + dot(kp2, yv1)
    yt, yth = rhs(t), rhs(th)
    w = w1 + dot(kq1, yt)
    h = h1 + dot(kq1, yth)
    yq2 = rhs(q2)
    p, q = (None, None) if last else (dot(kp2, yp1), dot(kq1, yq2))
    return (p, q, w, v, h), (t, th, yp1, yv1, yq2, yt, yth)


def track_first(is_low, one, two, extra):
    eye = eye2()
    t, th = extra[:2]
    return (
        jnp.where(is_low, eye, one[0]),
        jnp.where(is_low, two[1], eye),
        jnp.where(is_low, t, 0.0),
        jnp.where(is_low, 0.0, one[3]),
        jnp.where(is_low, th, 0.0),
    )


def track(is_low, fun, extra):
    f, hh, k, g, e = fun
    t, th, yp1, yv1, yq2, yt, yth = extra
    x1 = pack(jnp.where(is_low, hh, f))
    x2 = pack(jnp.where(is_low, hh, k))
    prod1 = dot(x1, jnp.where(is_low, yq2, yp1))
    prod2 = dot(x2, jnp.where(is_low, yt, yp1))
    vec1 = dot(x1, yv1)
    vec2 = dot(x2, jnp.where(is_low, yth, yv1))
    return (
        jnp.where(is_low, f, prod1),
        jnp.where(is_low, prod1, hh),
        jnp.where(is_low, k + prod2, prod2),
        jnp.where(is_low, g, g + vec1),
        e + vec2,
    )


def put_map(ref, p, q, w, v, h, last=False):
    lane = lanes((N, 128))
    low = lane < N
    tail = jnp.where(low, w, jnp.where(lane == N, v, h))
    if last:
        ref[...] = tail
    else:
        ref[:N] = jnp.where(low, p, q)
        ref[N:] = tail


def combine_four(last, *refs):
    if last:
        own_ref, x1_ref, x2_ref, x3_ref, fun_ref, out_ref, fun_out, slots = refs
    else:
        own_ref, x1_ref, x2_ref, x3_ref, out_ref, fun_out, slots = refs
    depth = lax.axis_index("depth")
    at = ((depth // ZS) % 2) * 2 + (depth % ZS) // 4 if last else depth % 4
    slots[at] = own_ref[...]
    slots[at ^ 1] = x1_ref[...]
    slots[at ^ 2] = x2_ref[...]
    slots[at ^ 3] = x3_ref[...]
    maps = [unpack(slots[i]) for i in range(4)]
    lower, extra_lower = join(maps[0], maps[1])
    upper, extra_upper = join(maps[2], maps[3])
    in_lower = at < 2
    mine = lambda x, y: [jnp.where(in_lower, a, b) for a, b in zip(x, y)]
    if last:
        fun = track(at % 2 == 0, unpack(fun_ref[...]), mine(extra_lower, extra_upper))
    else:
        fun = track_first(
            at % 2 == 0, mine(maps[0], maps[2]), mine(maps[1], maps[3]), mine(extra_lower[:2], extra_upper[:2])
        )
    total, extra = join(lower, upper, last)
    put_map(out_ref, *total, last=last)
    put_map(fun_out, *track(in_lower, fun, extra))


def downsweep(other_ref, maps_ref, vecs_ref, own_rhs, cols_ref, add_v, add_a, add_x, quad_ref, n1_ref, n2_ref, n3_ref,
              n4_ref, t_ref, out_ref):
    is_low = lax.axis_index("depth") < 2 * ZS
    g, e = vecs_ref[0], vecs_ref[1]
    other = other_ref[...]
    hi = other.astype(bf16)
    wide = jnp.concatenate([hi, (other - hi.astype(f32)).astype(bf16)], axis=1)
    v_other = jnp.broadcast_to(other[:, N : N + 1], (N, 128))
    w_other = jnp.broadcast_to(other[:, N + 1 : N + 2], (N, 128))
    t = w_other + jnp.dot(wide, own_rhs[0], preferred_element_type=f32)
    t = t + jnp.dot(wide, own_rhs[1], preferred_element_type=f32)
    up = g + dot(maps_ref[0], rhs(v_other))
    aa = e + dot(maps_ref[1], rhs(jnp.where(is_low, t, v_other)))
    ss = jnp.where(is_low, g, up) * cols_ref[1]
    lane = lanes((N, 128)) % CELLS
    for level, size, ref, base in ((3, 32, n4_ref, 6), (2, 16, n3_ref, 4), (1, 8, n2_ref, 0), (0, 4, n1_ref, 7)):
        ys, ya = rhs(ss), rhs(aa)
        ds = jnp.zeros((N, 128), f32)
        da = jnp.zeros((N, 128), f32)
        for j in range(CELLS // size):
            here = lane // size == j
            ds = jnp.where(here, dot(ref[2 * j, 0], ys), ds)
            da = jnp.where(here, dot(ref[2 * j + 1, 1], ya) + dot(t_ref[base + j], ys), da)
        upper = lane % size >= size // 2
        new_s = ss + add_v[level] + ds
        new_a = aa + add_a[level] + da
        ss = jnp.where(upper, new_s, ss)
        aa = jnp.where(upper, aa, new_a)
    y = pair_rhs(ss, aa)
    x = jnp.zeros((N, 128), f32)
    for j in range(CELLS // 2):
        x = jnp.where(lane == 2 * j, jnp.dot(quad_ref[j, 2], y, preferred_element_type=f32), x)
        x = jnp.where(lane == 2 * j + 1, jnp.dot(quad_ref[j, 3], y, preferred_element_type=f32), x)
    x = x + roll(x, CELLS) + (aa + add_x[...] + jnp.where(lane % 2 == 1, ss, 0.0))
    out_ref[...] = x.T[:CELLS]


def sds(*shape, dtype=f32):
    return jax.ShapeDtypeStruct(shape, dtype)


def call(body, outs, *args, scratch=(), smem=0, hbm=0, flops=0, name=None):
    args = [pltpu.with_memory_space_constraint(x, pltpu.HBM) if smem <= i < smem + hbm else x for i, x in enumerate(args)]
    spaces = [pltpu.SMEM] * smem + [pltpu.HBM] * hbm + [pltpu.VMEM] * (len(args) - smem - hbm)
    return pl.pallas_call(
        body,
        out_shape=outs,
        in_specs=[pl.BlockSpec(memory_space=space) for space in spaces],
        out_specs=jax.tree.map(lambda _: pl.BlockSpec(memory_space=pltpu.VMEM), outs),
        scratch_shapes=scratch,
        cost_estimate=pl.CostEstimate(flops=flops, bytes_accessed=1 << 16, transcendentals=0),
        name=name,
        compiler_params=pltpu.CompilerParams(vmem_limit_bytes=VLIM),
    )(*args)


def node(count):
    return sds(count, 4, N, 128, dtype=bf16)


def on_device(densities, source, jacobian, pattern, transport, lateral, neighbours, factor, coupling):
    line_count, cell_count, species = densities.shape
    u = densities.reshape(CELLS, N)
    src = source.reshape(CELLS, N)
    tran = transport.reshape(CELLS, N)
    lat = lateral.reshape(CELLS, N)
    coup = coupling.reshape(CELLS, N)
    jac = jacobian.reshape(CELLS, N * N)
    fac = factor.reshape(4, 8, 32, 128).transpose(0, 2, 1, 3).reshape(1024, 128)

    def xor_lat(value, bits):
        return lax.ppermute(value, "lat", [(i, i ^ bits) for i in range(8)])

    def xor_depth(value, bits):
        return lax.ppermute(value, "depth", [(i, i ^ bits) for i in range(32)])

    line_a = xor_lat(densities, 1)
    part, flux = call(
        react, (sds(CELLS, N), sds(N, 128)), jac, u, src, tran, pattern, hbm=5, flops=1 << 30, name="react",
        scratch=[pltpu.VMEM((CELLS, N * N), f32)] + [pltpu.VMEM((CELLS, N), f32)] * 3
        + [pltpu.VMEM((8, 8), jnp.int32), pltpu.SemaphoreType.DMA((8,))],
    )
    line_b = xor_lat(jnp.concatenate([densities, line_a], axis=0), 2)
    quad, n1, full, cols = call(
        tree_leaves,
        (sds(16, 4, N, 256, dtype=bf16), sds(16, 3, N, 128, dtype=bf16), sds(16, 3, N, 128), sds(2, N, 128)),
        fac, coup, part, scratch=[pltpu.VMEM((2, N, 128), f32)], flops=2 << 30, name="tree_leaves",
    )
    top_even = xor_depth(lax.optimization_barrier((densities, cols))[0], 1)
    top_odd = lax.ppermute(
        lax.optimization_barrier((densities, line_b))[0], "depth",
        [(i, (i + 1) % 32 if i % 2 else (i - 1) % 32) for i in range(32)],
    )
    line_c = xor_lat(jnp.concatenate([densities, line_a, line_b], axis=0), 6)
    n2, n3, n4, n5, root = call(
        tree_upper,
        (node(8), node(4), node(2), sds(1, N, 128, dtype=bf16), sds(128, 128)),
        n1, full, coup, cols, part, scratch=[pltpu.VMEM((8, 3, N, 128), f32), pltpu.VMEM((4, 3, N, 128), f32)],
        flops=2 << 30, name="tree_upper",
    )
    pay, pair, vs, ws = call(
        upsweep, (sds(128, 128), sds(4, N, 128), sds(7, N, 128), sds(7, N, 128)),
        neighbours, part, line_a, line_b, line_c, top_even, top_odd, flux, u, tran, lat, coup, cols, quad, n1, n2, n3, n4, n5, root,
        smem=1, flops=1 << 25, name="upsweep",
    )
    others = [xor_depth(pay, bits) for bits in (1, 2, 3)]
    tees, add_v, add_a, add_x = call(
        prepare, (sds(15, N, 128, dtype=bf16), sds(4, N, 128), sds(4, N, 128), sds(N, 128)),
        pair, vs, ws, n1, n2, n3, n4, flops=1 << 30, name="prepare",
    )
    slots = [pltpu.VMEM((4, 128, 128), f32)]
    pay, fun = call(
        lambda *refs: combine_four(False, *refs), (sds(128, 128), sds(128, 128)), pay, *others, scratch=slots,
        flops=1 << 24, name="combine_low",
    )
    others = [xor_depth(pay, bits) for bits in (7, 8, 15)]
    pay, fun = call(
        lambda *refs: combine_four(True, *refs), (sds(N, 128), sds(128, 128)), pay, *others, fun, scratch=slots,
        flops=1 << 24, name="combine_high",
    )
    other = xor_depth(pay, 24)
    maps, vecs, own_rhs = call(
        prepare_last,
        (sds(2, N, 128, dtype=bf16), sds(2, N, 128), sds(2, 256, 128, dtype=bf16)),
        pay, fun, flops=1 << 30, name="prepare_last",
    )
    out = call(
        downsweep, sds(CELLS, N), other, maps, vecs, own_rhs, cols, add_v, add_a, add_x, quad, n1, n2, n3, n4, tees,
        flops=1 << 25, name="downsweep",
    )
    return out.reshape(line_count, cell_count, species)


def solution(mesh):
    return jax.shard_map(
        on_device,
        mesh=mesh,
        in_specs=(
            P("lat", "depth", None),
            P("lat", "depth", None),
            P("lat", "depth", None),
            P(),
            P("lat", "depth", None),
            P("lat", "depth", None),
            P("lat", None),
            P("lat", "depth", None),
            P("lat", "depth", None),
        ),
        out_specs=P("lat", "depth", None),
        check_vma=False,
    )
```

```python
import jax
import jax.numpy as jnp
from jax import lax
from jax.experimental import pallas as pl
from jax.experimental.pallas import tpu as pltpu
from jax.sharding import PartitionSpec as P

f32 = jnp.float32
bf16 = jnp.bfloat16

CELLS = 32
N = 64
ZS = 8
VLIM = 16 << 20


def lanes(shape):
    return lax.broadcasted_iota(jnp.int32, shape, len(shape) - 1)


def roll(x, shift):
    shift = shift % x.shape[-1]
    return x if shift == 0 else pltpu.roll(x, shift, x.ndim - 1)


def pack(dup):
    hi = dup.astype(bf16).astype(f32)
    return jnp.where(lanes(dup.shape) < N, hi, dup - hi).astype(bf16)


def mm(a, b):
    r = jnp.dot(a, jnp.concatenate([b, b], axis=0), preferred_element_type=f32)
    return r + roll(r, N)


def rhs(x):
    hi = x.astype(bf16)
    lo = (x - hi.astype(f32)).astype(bf16)
    return jnp.concatenate([hi, hi, lo, lo], axis=0)


def dot(a, y):
    return jnp.dot(jnp.concatenate([a, a], axis=1), y, preferred_element_type=f32)


def column(row):
    return jnp.broadcast_to(row, (128, N)).T


def pair(a, b):
    low = lanes(a.shape) < N
    a_hi, b_hi = a.astype(bf16).astype(f32), b.astype(bf16).astype(f32)
    hi = jnp.where(low, a_hi, b_hi).astype(bf16)
    lo = jnp.where(low, a - a_hi, b - b_hi).astype(bf16)
    return jnp.concatenate([hi, lo], axis=1)


def pair_rhs(x, y):
    def split(z):
        hi = z.astype(bf16).astype(f32)
        return jnp.where(lanes(z.shape) % 64 < CELLS, hi, z - hi).astype(bf16)

    a, b = split(x), split(y)
    return jnp.concatenate([a, b, a, b], axis=0)


def eye2():
    return jnp.where(lanes((N, 128)) % N == lax.broadcasted_iota(jnp.int32, (N, 128), 0), 1.0, 0.0)


def put(node, full, j, p, q, w, u=None):
    node[j, 0], node[j, 1], node[j, 2] = pack(p), pack(q), pack(w)
    full[j, 0], full[j, 1], full[j, 2] = p, q, w
    if u is not None:
        node[j, 3] = pack(u)


def tree_leaves(fac_ref, coup_ref, after_ref, quad_ref, n1_ref, full_ref, cols_ref, rows):
    del after_ref
    c = coup_ref[...]
    cols_ref[0] = column(c[CELLS - 1 : CELLS])
    cols_ref[1] = column(1.0 / c[0:1])
    c2 = jnp.concatenate([c, c], axis=1)
    low = lanes((CELLS, 128)) < N
    eye = eye2()

    def leaf(k):
        g, s = divmod(k, 8)
        x = fac_ref[pl.ds(g * 256 + s, 32, stride=8), :]
        y = roll(x, N)
        rows[k % 2, pl.ds(0, 32, stride=2), :] = jnp.where(low, x, y)
        rows[k % 2, pl.ds(1, 32, stride=2), :] = jnp.where(low, y, x)
        a = rows[k % 2]
        before = max(k - 1, 0)
        return a * c2[before : before + 1] - eye, a * c2[k : k + 1] - eye

    for j in range(CELLS // 2):
        p1, q1 = leaf(2 * j)
        p2, q2 = leaf(2 * j + 1)
        kq1 = pack(q1)
        p = p1 + p2 + dot(pack(p2), rhs(p1))
        q = q1 + q2 + dot(kq1, rhs(q2))
        u = eye + q1 + p2 + dot(kq1, rhs(p2))
        w = (eye + eye) + p1 + q1 + p + dot(kq1, rhs(p))
        put(n1_ref, full_ref, j, p, q, w)
        quad_ref[j, 0] = pair(p, p2)
        quad_ref[j, 1] = pair(w, u)
        quad_ref[j, 2] = pair(w, q)
        quad_ref[j, 3] = pair(p, q2)


def tree_upper(n1_ref, full_ref, coup_ref, cols_ref, after_ref, n2_ref, n3_ref, n4_ref, n5_ref, root_ref, fa, fb):
    del after_ref
    node, full = n1_ref, full_ref
    for count, node_to, full_to in ((8, n2_ref, fa), (4, n3_ref, fb), (2, n4_ref, fa), (1, None, None)):
        for j in range(count):
            one, two = 2 * j, 2 * j + 1
            kq1, yp1 = node[one, 1], rhs(full[one, 0])
            u = full[two, 2] + dot(kq1, rhs(full[two, 2]))
            p = full[one, 0] + full[two, 0] + dot(node[two, 0], yp1)
            q = full[one, 1] + full[two, 1] + dot(kq1, rhs(full[two, 1]))
            ku = pack(u)
            w = full[one, 2] + u + dot(ku, yp1)
            if node_to is None:
                eye = eye2()
                n5_ref[0] = ku
                first = coup_ref[0:1]
                scale = 1.0 / jnp.concatenate([first, first], axis=1)
                root_ref[:N] = jnp.where(lanes((N, 128)) < N, (p + eye) * cols_ref[0] * scale, q + eye)
                root_ref[N:] = w * scale
            else:
                put(node_to, full_to, j, p, q, w, u)
        node, full = node_to, full_to


def react(jac_hbm, dens_hbm, src_hbm, tran_hbm, pat_hbm, out_ref, flux_ref, jac_ref, dens_ref, src_ref, tran_ref,
          pat_ref, sems):
    parts = [(slice(None), pl.ds(i * 1024, 1024)) for i in range(4)]
    pairs = [(dens_hbm, dens_ref), (pat_hbm, pat_ref)] + [(jac_hbm.at[part], jac_ref.at[part]) for part in parts]
    pairs += [(src_hbm, src_ref), (tran_hbm, tran_ref)]
    copies = [pltpu.make_async_copy(a, b, sems.at[i]) for i, (a, b) in enumerate(pairs)]
    for copy in copies:
        copy.start()
    half = lanes((128, N)) % 2 == lax.broadcasted_iota(jnp.int32, (128, N), 0) // N
    half = jnp.where(half, 1.0, 0.0).astype(bf16)
    copies[0].wait()
    copies[1].wait()
    u = dens_ref[...]
    u2 = jnp.concatenate([u, u], axis=1)
    lane8 = lanes((8, 128))
    pat = pat_ref[...].astype(f32)
    mask_rows = jnp.zeros((8, 128), f32)
    for t in range(8):
        mask_rows = jnp.where((lane8 % N) // 8 == t, pat[:, t : t + 1], mask_rows)
    lane = lanes((CELLS, N))
    acc = jnp.zeros((CELLS, N), f32)
    for m in range(32):
        if m % 8 == 0:
            copies[2 + m // 8].wait()
        y = jac_ref[:, m * 128 : (m + 1) * 128] * (u2 * mask_rows[m // 4 : m // 4 + 1])
        hi = y.astype(bf16)
        lo = (y - hi.astype(f32)).astype(bf16)
        z = jnp.dot(hi, half, preferred_element_type=f32) + jnp.dot(lo, half, preferred_element_type=f32)
        acc = jnp.where(lane // 2 == m, z, acc)
    copies[6].wait()
    copies[7].wait()
    tran = tran_ref[...]
    flux = tran * u
    flux_ref[...] = column(flux[CELLS - 1 : CELLS])
    row = lax.broadcasted_iota(jnp.int32, (CELLS, N), 0)
    lower = jnp.where(row == 0, 0.0, pltpu.roll(flux, 1, 0))
    upper = jnp.where(row == CELLS - 1, 0.0, pltpu.roll(u, CELLS - 1, 0))
    out_ref[...] = src_ref[...] - acc + lower + tran * upper


def upsweep(neigh_ref, part_ref, a_ref, b_ref, c_ref, even_ref, odd_ref, flux_ref, dens_ref, tran_ref, lat_ref, coup_ref, cols_ref,
            quad_ref, n1_ref, n2_ref, n3_ref, n4_ref, n5_ref, root_ref, pay_ref, pair_ref, v_ref, w_ref):
    me = lax.axis_index("lat")
    u = dens_ref[...]
    total = jnp.zeros((CELLS, N), f32)
    lines = [(0, u), (1, a_ref[0])] + [(2 + i, b_ref[i]) for i in range(2)]
    lines += [((6, 7, 4, 5)[i], c_ref[i]) for i in range(4)]
    for offset, value in lines:
        line = me ^ offset
        count = jnp.int32(0)
        for j in range(4):
            count = count + (neigh_ref[0, j] == line).astype(jnp.int32)
        total = total + count.astype(f32) * value
    row = lax.broadcasted_iota(jnp.int32, (CELLS, N), 0)
    r = part_ref[...] - lat_ref[...] * (4.0 * u - total)
    depth = lax.axis_index("depth")
    above = jnp.where(depth % 2 == 0, even_ref[0, 0:1], odd_ref[0, 0:1])
    above = jnp.where(depth == lax.axis_size("depth") - 1, 0.0, above)
    r = r + jnp.where(row == CELLS - 1, tran_ref[...] * above, 0.0)
    c = coup_ref[...]
    g = r / jnp.where(row == 0, c, pltpu.roll(c, 1, 0))
    x = []
    for i in range(4):
        rolled = g if i == 0 else pltpu.roll(g, CELLS - i, 0)
        x.append(jnp.concatenate([rolled, rolled], axis=0).T)
    lane2 = lanes((N, N)) % CELLS
    lane = lanes((N, CELLS))
    pair_v, pair_w = [], []
    for half in range(2):
        x0, x1 = x[2 * half], x[2 * half + 1]
        y = pair_rhs(x0, x1)
        v = jnp.zeros((N, N), f32)
        w = jnp.zeros((N, N), f32)
        for j in range(8):
            at = 2 * j + half
            here = lane2 == 4 * j
            v = jnp.where(here, jnp.dot(quad_ref[at, 0], y, preferred_element_type=f32), v)
            w = jnp.where(here, jnp.dot(quad_ref[at, 1], y, preferred_element_type=f32), w)
        v = v[:, :CELLS] + v[:, CELLS:] + x0[:, :CELLS] + x1[:, :CELLS]
        w = w[:, :CELLS] + w[:, CELLS:]
        pair_v.append(v)
        pair_w.append(w)
        pair_ref[half, :, 0:CELLS] = pair_v[half]
        pair_ref[2 + half, :, 0:CELLS] = w
    yv, yw = rhs(pair_v[0]), rhs(pair_w[1])
    v, w = pair_v[0] + pair_v[1], pair_w[0] + pair_w[1]
    dv = jnp.zeros((N, CELLS), f32)
    dw = jnp.zeros((N, CELLS), f32)
    for j in range(8):
        here = lane == 4 * j
        dv = jnp.where(here, dot(n1_ref[2 * j + 1, 0], yv), dv)
        dw = jnp.where(here, dot(n1_ref[2 * j, 1], yw) + dot(n2_ref[j, 3], yv), dw)
    v, w = v + dv, w + dw
    vs = [jnp.broadcast_to(v[:, 4 * j : 4 * j + 1], (N, 128)) for j in range(8)]
    ws = [jnp.broadcast_to(w[:, 4 * j : 4 * j + 1], (N, 128)) for j in range(8)]
    at = 0
    for count, ref, above in ((4, n2_ref, n3_ref), (2, n3_ref, n4_ref), (1, n4_ref, n5_ref)):
        next_v, next_w = [], []
        for j in range(count):
            v1, v2, w1, w2 = vs[2 * j], vs[2 * j + 1], ws[2 * j], ws[2 * j + 1]
            v_ref[at], w_ref[at] = v1, w2
            at += 1
            yv, yw = rhs(v1), rhs(w2)
            u_map = above[j, 3] if count > 1 else above[0]
            next_v.append(v1 + v2 + dot(ref[2 * j + 1, 0], yv))
            next_w.append(w1 + w2 + dot(ref[2 * j, 1], yw) + dot(u_map, yv))
        vs, ws = next_v, next_w
    lane = lanes((N, 128))
    pay_ref[:N] = root_ref[:N]
    tail = jnp.where(lane == N, vs[0] * cols_ref[0] + flux_ref[...], ws[0])
    pay_ref[N:] = jnp.where(lane < N, root_ref[N:], tail)


def prepare(pair_ref, v_ref, w_ref, n1_ref, n2_ref, n3_ref, n4_ref, t_ref, add_v, add_a, add_x):
    lane = lanes((N, 128))
    part = lane % CELLS
    at, vec = 0, 0
    for level, size, ref in ((1, 8, n2_ref), (2, 16, n3_ref), (3, 32, n4_ref)):
        acc_v = jnp.zeros((N, 128), f32)
        acc_a = jnp.zeros((N, 128), f32)
        for j in range(CELLS // size):
            kw = ref[2 * j + 1, 2]
            wide = kw.astype(f32)
            t_ref[at] = pack(wide + roll(wide, N) + mm(kw, ref[2 * j, 0]))
            at += 1
            here = part // size == j
            acc_v = jnp.where(here, v_ref[vec], acc_v)
            acc_a = jnp.where(here, w_ref[vec] + dot(kw, rhs(v_ref[vec])), acc_a)
            vec += 1
        add_v[level], add_a[level] = acc_v, acc_a

    def repeat(x):
        x = x + roll(x, CELLS)
        return x + roll(x, 2 * CELLS)

    first = jnp.logical_and(lane % 4 == 0, lane < CELLS)
    v0, v1, w0, w1 = [jnp.where(first, pair_ref[i], 0.0) for i in range(4)]
    y = rhs(v0)
    acc_a = jnp.zeros((N, 128), f32)
    for j in range(8):
        kw = n1_ref[2 * j + 1, 2]
        wide = kw.astype(f32)
        t_ref[at] = pack(wide + roll(wide, N) + mm(kw, n1_ref[2 * j, 0]))
        at += 1
        acc_a = jnp.where(lane == 4 * j, dot(kw, y), acc_a)
    acc_a = acc_a + w1
    spread_v = v0 + roll(v0, 1)
    spread_a = acc_a + roll(acc_a, 1)
    add_v[0] = repeat(spread_v + roll(spread_v, 2))
    add_a[0] = repeat(spread_a + roll(spread_a, 2))
    add_x[...] = repeat(w0 + roll(w1, 2) + roll(v0, 1) + roll(v1, 3))


def prepare_last(own_ref, fun_ref, maps_ref, vecs_ref, own_rhs):
    is_low = lax.axis_index("depth") < 2 * ZS
    f, hh, k, g, e = unpack(fun_ref[...])
    maps_ref[0], maps_ref[1] = pack(f), pack(jnp.where(is_low, hh, k))
    vecs_ref[0], vecs_ref[1] = g, e
    v = jnp.broadcast_to(own_ref[:, N : N + 1], (N, 128))
    hi = v.astype(bf16)
    lo = (v - hi.astype(f32)).astype(bf16)
    zero = jnp.zeros((N, 128), bf16)
    own_rhs[0] = jnp.concatenate([hi, zero, hi, zero], axis=0)
    own_rhs[1] = jnp.concatenate([lo, zero, lo, zero], axis=0)


def unpack(b):
    low = lanes((N, 128)) < N
    b1, b2 = b[:N], b[N:]
    r1, r2 = roll(b1, N), roll(b2, N)
    x = jnp.where(low, b1, r1)
    y = jnp.where(low, r1, b1)
    z = jnp.where(low, b2, r2)
    g = jnp.broadcast_to(b2[:, N : N + 1], (N, 128))
    h = jnp.broadcast_to(b2[:, N + 1 : N + 2], (N, 128))
    return x, y, z, g, h


def join(one, two, last=False):
    p1, q1, w1, v1, h1 = one
    p2, q2, w2, v2, h2 = two
    kq1, kp2, kw2 = pack(q1), pack(p2), pack(w2)
    yp1, yv1 = rhs(p1), rhs(v1)
    t = dot(kw2, yp1)
    th = h2 + dot(kw2, yv1)
    v = v2 + dot(kp2, yv1)
    yt, yth = rhs(t), rhs(th)
    w = w1 + dot(kq1, yt)
    h = h1 + dot(kq1, yth)
    yq2 = rhs(q2)
    p, q = (None, None) if last else (dot(kp2, yp1), dot(kq1, yq2))
    return (p, q, w, v, h), (t, th, yp1, yv1, yq2, yt, yth)


def track_first(is_low, one, two, extra):
    eye = eye2()
    t, th = extra[:2]
    return (
        jnp.where(is_low, eye, one[0]),
        jnp.where(is_low, two[1], eye),
        jnp.where(is_low, t, 0.0),
        jnp.where(is_low, 0.0, one[3]),
        jnp.where(is_low, th, 0.0),
    )


def track(is_low, fun, extra):
    f, hh, k, g, e = fun
    t, th, yp1, yv1, yq2, yt, yth = extra
    x1 = pack(jnp.where(is_low, hh, f))
    x2 = pack(jnp.where(is_low, hh, k))
    prod1 = dot(x1, jnp.where(is_low, yq2, yp1))
    prod2 = dot(x2, jnp.where(is_low, yt, yp1))
    vec1 = dot(x1, yv1)
    vec2 = dot(x2, jnp.where(is_low, yth, yv1))
    return (
        jnp.where(is_low, f, prod1),
        jnp.where(is_low, prod1, hh),
        jnp.where(is_low, k + prod2, prod2),
        jnp.where(is_low, g, g + vec1),
        e + vec2,
    )


def put_map(ref, p, q, w, v, h, last=False):
    lane = lanes((N, 128))
    low = lane < N
    tail = jnp.where(low, w, jnp.where(lane == N, v, h))
    if last:
        ref[...] = tail
    else:
        ref[:N] = jnp.where(low, p, q)
        ref[N:] = tail


def combine_two(level, own_ref, other_ref, fun_ref, out_ref, fun_out):
    is_low = ((lax.axis_index("depth") // (1, 2, 4, 8)[level]) % 2) == 0
    own, other = own_ref[...], other_ref[...]
    one = unpack(jnp.where(is_low, own, other))
    two = unpack(jnp.where(is_low, other, own))
    total, extra = join(one, two, last=level == 3)
    put_map(out_ref, *total, last=level == 3)
    put_map(fun_out, *track(is_low, unpack(fun_ref[...]), extra))


def combine_four(own_ref, x1_ref, x2_ref, x3_ref, out_ref, fun_out, slots):
    at = lax.axis_index("depth") % 4
    slots[at] = own_ref[...]
    slots[at ^ 1] = x1_ref[...]
    slots[at ^ 2] = x2_ref[...]
    slots[at ^ 3] = x3_ref[...]
    maps = [unpack(slots[i]) for i in range(4)]
    lower, extra_lower = join(maps[0], maps[1])
    upper, extra_upper = join(maps[2], maps[3])
    in_lower = at < 2
    mine = lambda a, b: jnp.where(in_lower, a, b)
    fun = track_first(
        at % 2 == 0,
        [mine(a, b) for a, b in zip(maps[0], maps[2])],
        [mine(a, b) for a, b in zip(maps[1], maps[3])],
        [mine(a, b) for a, b in zip(extra_lower[:2], extra_upper[:2])],
    )
    total, extra = join(lower, upper)
    put_map(out_ref, *total)
    put_map(fun_out, *track(in_lower, fun, extra))


def downsweep(other_ref, maps_ref, vecs_ref, own_rhs, cols_ref, add_v, add_a, add_x, quad_ref, n1_ref, n2_ref, n3_ref,
              n4_ref, t_ref, out_ref):
    is_low = lax.axis_index("depth") < 2 * ZS
    g, e = vecs_ref[0], vecs_ref[1]
    other = other_ref[...]
    hi = other.astype(bf16)
    wide = jnp.concatenate([hi, (other - hi.astype(f32)).astype(bf16)], axis=1)
    v_other = jnp.broadcast_to(other[:, N : N + 1], (N, 128))
    w_other = jnp.broadcast_to(other[:, N + 1 : N + 2], (N, 128))
    t = w_other + jnp.dot(wide, own_rhs[0], preferred_element_type=f32)
    t = t + jnp.dot(wide, own_rhs[1], preferred_element_type=f32)
    up = g + dot(maps_ref[0], rhs(v_other))
    aa = e + dot(maps_ref[1], rhs(jnp.where(is_low, t, v_other)))
    ss = jnp.where(is_low, g, up) * cols_ref[1]
    lane = lanes((N, 128)) % CELLS
    for level, size, ref, base in ((3, 32, n4_ref, 6), (2, 16, n3_ref, 4), (1, 8, n2_ref, 0), (0, 4, n1_ref, 7)):
        ys, ya = rhs(ss), rhs(aa)
        ds = jnp.zeros((N, 128), f32)
        da = jnp.zeros((N, 128), f32)
        for j in range(CELLS // size):
            here = lane // size == j
            ds = jnp.where(here, dot(ref[2 * j, 0], ys), ds)
            da = jnp.where(here, dot(ref[2 * j + 1, 1], ya) + dot(t_ref[base + j], ys), da)
        upper = lane % size >= size // 2
        new_s = ss + add_v[level] + ds
        new_a = aa + add_a[level] + da
        ss = jnp.where(upper, new_s, ss)
        aa = jnp.where(upper, aa, new_a)
    y = pair_rhs(ss, aa)
    x = jnp.zeros((N, 128), f32)
    for j in range(CELLS // 2):
        x = jnp.where(lane == 2 * j, jnp.dot(quad_ref[j, 2], y, preferred_element_type=f32), x)
        x = jnp.where(lane == 2 * j + 1, jnp.dot(quad_ref[j, 3], y, preferred_element_type=f32), x)
    x = x + roll(x, CELLS) + (aa + add_x[...] + jnp.where(lane % 2 == 1, ss, 0.0))
    out_ref[...] = x.T[:CELLS]


def sds(*shape, dtype=f32):
    return jax.ShapeDtypeStruct(shape, dtype)


def call(body, outs, *args, scratch=(), smem=0, hbm=0, flops=0, name=None):
    args = [pltpu.with_memory_space_constraint(x, pltpu.HBM) if smem <= i < smem + hbm else x for i, x in enumerate(args)]
    spaces = [pltpu.SMEM] * smem + [pltpu.HBM] * hbm + [pltpu.VMEM] * (len(args) - smem - hbm)
    return pl.pallas_call(
        body,
        out_shape=outs,
        in_specs=[pl.BlockSpec(memory_space=space) for space in spaces],
        out_specs=jax.tree.map(lambda _: pl.BlockSpec(memory_space=pltpu.VMEM), outs),
        scratch_shapes=scratch,
        cost_estimate=pl.CostEstimate(flops=flops, bytes_accessed=1 << 16, transcendentals=0),
        name=name,
        compiler_params=pltpu.CompilerParams(vmem_limit_bytes=VLIM),
    )(*args)


def node(count):
    return sds(count, 4, N, 128, dtype=bf16)


def on_device(densities, source, jacobian, pattern, transport, lateral, neighbours, factor, coupling):
    line_count, cell_count, species = densities.shape
    u = densities.reshape(CELLS, N)
    src = source.reshape(CELLS, N)
    tran = transport.reshape(CELLS, N)
    lat = lateral.reshape(CELLS, N)
    coup = coupling.reshape(CELLS, N)
    jac = jacobian.reshape(CELLS, N * N)
    fac = factor.reshape(4, 8, 32, 128).transpose(0, 2, 1, 3).reshape(1024, 128)

    def xor_lat(value, bits):
        return lax.ppermute(value, "lat", [(i, i ^ bits) for i in range(8)])

    def xor_depth(value, bits):
        return lax.ppermute(value, "depth", [(i, i ^ bits) for i in range(32)])

    line_a = xor_lat(densities, 1)
    part, flux = call(
        react, (sds(CELLS, N), sds(N, 128)), jac, u, src, tran, pattern, hbm=5, flops=1 << 30, name="react",
        scratch=[pltpu.VMEM((CELLS, N * N), f32)] + [pltpu.VMEM((CELLS, N), f32)] * 3
        + [pltpu.VMEM((8, 8), jnp.int32), pltpu.SemaphoreType.DMA((8,))],
    )
    line_b = xor_lat(jnp.concatenate([densities, line_a], axis=0), 2)
    quad, n1, full, cols = call(
        tree_leaves,
        (sds(16, 4, N, 256, dtype=bf16), sds(16, 3, N, 128, dtype=bf16), sds(16, 3, N, 128), sds(2, N, 128)),
        fac, coup, part, scratch=[pltpu.VMEM((2, N, 128), f32)], flops=2 << 30, name="tree_leaves",
    )
    top_even = xor_depth(lax.optimization_barrier((densities, cols))[0], 1)
    top_odd = lax.ppermute(
        lax.optimization_barrier((densities, line_b))[0], "depth",
        [(i, (i + 1) % 32 if i % 2 else (i - 1) % 32) for i in range(32)],
    )
    line_c = xor_lat(jnp.concatenate([densities, line_a, line_b], axis=0), 6)
    n2, n3, n4, n5, root = call(
        tree_upper,
        (node(8), node(4), node(2), sds(1, N, 128, dtype=bf16), sds(128, 128)),
        n1, full, coup, cols, part, scratch=[pltpu.VMEM((8, 3, N, 128), f32), pltpu.VMEM((4, 3, N, 128), f32)],
        flops=2 << 30, name="tree_upper",
    )
    pay, pair, vs, ws = call(
        upsweep, (sds(128, 128), sds(4, N, 128), sds(7, N, 128), sds(7, N, 128)),
        neighbours, part, line_a, line_b, line_c, top_even, top_odd, flux, u, tran, lat, coup, cols, quad, n1, n2, n3, n4, n5, root,
        smem=1, flops=1 << 25, name="upsweep",
    )
    others = [xor_depth(pay, bits) for bits in (1, 2, 3)]
    tees, add_v, add_a, add_x = call(
        prepare, (sds(15, N, 128, dtype=bf16), sds(4, N, 128), sds(4, N, 128), sds(N, 128)),
        pair, vs, ws, n1, n2, n3, n4, flops=1 << 30, name="prepare",
    )
    pay, fun = call(
        combine_four, (sds(128, 128), sds(128, 128)), pay, *others, scratch=[pltpu.VMEM((4, 128, 128), f32)],
        flops=1 << 24, name="combine_four",
    )
    for level, bits in ((2, 7), (3, 8)):
        other = xor_depth(pay, bits)
        pay, fun = call(
            lambda *refs, level=level: combine_two(level, *refs),
            (sds(N if level == 3 else 128, 128), sds(128, 128)), pay, other, fun, flops=1 << 24,
            name=f"combine{level}",
        )
    other = xor_depth(pay, 24)
    maps, vecs, own_rhs = call(
        prepare_last,
        (sds(2, N, 128, dtype=bf16), sds(2, N, 128), sds(2, 256, 128, dtype=bf16)),
        pay, fun, flops=1 << 30, name="prepare_last",
    )
    out = call(
        downsweep, sds(CELLS, N), other, maps, vecs, own_rhs, cols, add_v, add_a, add_x, quad, n1, n2, n3, n4, tees,
        flops=1 << 25, name="downsweep",
    )
    return out.reshape(line_count, cell_count, species)


def solution(mesh):
    return jax.shard_map(
        on_device,
        mesh=mesh,
        in_specs=(
            P("lat", "depth", None),
            P("lat", "depth", None),
            P("lat", "depth", None),
            P(),
            P("lat", "depth", None),
            P("lat", "depth", None),
            P("lat", None),
            P("lat", "depth", None),
            P("lat", "depth", None),
        ),
        out_specs=P("lat", "depth", None),
        check_vma=False,
    )
```

```python
import jax
import jax.numpy as jnp
from jax import lax
from jax.experimental import pallas as pl
from jax.experimental.pallas import tpu as pltpu
from jax.sharding import PartitionSpec as P

f32 = jnp.float32
bf16 = jnp.bfloat16

CELLS = 32
N = 64
ZS = 8
VLIM = 16 << 20


def lanes(shape):
    return lax.broadcasted_iota(jnp.int32, shape, len(shape) - 1)


def roll(x, shift):
    shift = shift % x.shape[-1]
    return x if shift == 0 else pltpu.roll(x, shift, x.ndim - 1)


def pack(dup):
    hi = dup.astype(bf16).astype(f32)
    return jnp.where(lanes(dup.shape) < N, hi, dup - hi).astype(bf16)


def mm(a, b):
    r = jnp.dot(a, jnp.concatenate([b, b], axis=0), preferred_element_type=f32)
    return r + roll(r, N)


def rhs(x):
    hi = x.astype(bf16)
    lo = (x - hi.astype(f32)).astype(bf16)
    return jnp.concatenate([hi, hi, lo, lo], axis=0)


def dot(a, y):
    return jnp.dot(jnp.concatenate([a, a], axis=1), y, preferred_element_type=f32)


def column(row):
    return jnp.broadcast_to(row, (128, N)).T


def pair(a, b):
    low = lanes(a.shape) < N
    a_hi, b_hi = a.astype(bf16).astype(f32), b.astype(bf16).astype(f32)
    hi = jnp.where(low, a_hi, b_hi).astype(bf16)
    lo = jnp.where(low, a - a_hi, b - b_hi).astype(bf16)
    return jnp.concatenate([hi, lo], axis=1)


def pair_rhs(x, y):
    def split(z):
        hi = z.astype(bf16).astype(f32)
        return jnp.where(lanes(z.shape) % 64 < CELLS, hi, z - hi).astype(bf16)

    a, b = split(x), split(y)
    return jnp.concatenate([a, b, a, b], axis=0)


def eye2():
    return jnp.where(lanes((N, 128)) % N == lax.broadcasted_iota(jnp.int32, (N, 128), 0), 1.0, 0.0)


def put(node, full, j, p, q, w, u=None):
    node[j, 0], node[j, 1], node[j, 2] = pack(p), pack(q), pack(w)
    full[j, 0], full[j, 1], full[j, 2] = p, q, w
    if u is not None:
        node[j, 3] = pack(u)


def tree_leaves(fac_ref, coup_ref, after_ref, quad_ref, n1_ref, full_ref, cols_ref, rows):
    del after_ref
    c = coup_ref[...]
    cols_ref[0] = column(c[CELLS - 1 : CELLS])
    cols_ref[1] = column(1.0 / c[0:1])
    c2 = jnp.concatenate([c, c], axis=1)
    low = lanes((CELLS, 128)) < N
    eye = eye2()

    def leaf(k):
        g, s = divmod(k, 8)
        x = fac_ref[pl.ds(g * 256 + s, 32, stride=8), :]
        y = roll(x, N)
        rows[k % 2, pl.ds(0, 32, stride=2), :] = jnp.where(low, x, y)
        rows[k % 2, pl.ds(1, 32, stride=2), :] = jnp.where(low, y, x)
        a = rows[k % 2]
        before = max(k - 1, 0)
        return a * c2[before : before + 1] - eye, a * c2[k : k + 1] - eye

    for j in range(CELLS // 2):
        p1, q1 = leaf(2 * j)
        p2, q2 = leaf(2 * j + 1)
        kq1 = pack(q1)
        p = p1 + p2 + dot(pack(p2), rhs(p1))
        q = q1 + q2 + dot(kq1, rhs(q2))
        u = eye + q1 + p2 + dot(kq1, rhs(p2))
        w = (eye + eye) + p1 + q1 + p + dot(kq1, rhs(p))
        put(n1_ref, full_ref, j, p, q, w)
        quad_ref[j, 0] = pair(p, p2)
        quad_ref[j, 1] = pair(w, u)
        quad_ref[j, 2] = pair(w, q)
        quad_ref[j, 3] = pair(p, q2)


def tree_upper(n1_ref, full_ref, coup_ref, cols_ref, after_ref, n2_ref, n3_ref, n4_ref, n5_ref, root_ref, fa, fb):
    del after_ref
    node, full = n1_ref, full_ref
    for count, node_to, full_to in ((8, n2_ref, fa), (4, n3_ref, fb), (2, n4_ref, fa), (1, None, None)):
        for j in range(count):
            one, two = 2 * j, 2 * j + 1
            kq1, yp1 = node[one, 1], rhs(full[one, 0])
            u = full[two, 2] + dot(kq1, rhs(full[two, 2]))
            p = full[one, 0] + full[two, 0] + dot(node[two, 0], yp1)
            q = full[one, 1] + full[two, 1] + dot(kq1, rhs(full[two, 1]))
            ku = pack(u)
            w = full[one, 2] + u + dot(ku, yp1)
            if node_to is None:
                eye = eye2()
                n5_ref[0] = ku
                first = coup_ref[0:1]
                scale = 1.0 / jnp.concatenate([first, first], axis=1)
                root_ref[:N] = jnp.where(lanes((N, 128)) < N, (p + eye) * cols_ref[0] * scale, q + eye)
                root_ref[N:] = w * scale
            else:
                put(node_to, full_to, j, p, q, w, u)
        node, full = node_to, full_to


def react(jac_hbm, dens_hbm, src_hbm, tran_hbm, pat_hbm, out_ref, flux_ref, jac_ref, dens_ref, src_ref, tran_ref,
          pat_ref, sems):
    parts = [(slice(None), pl.ds(i * 1024, 1024)) for i in range(4)]
    pairs = [(dens_hbm, dens_ref), (pat_hbm, pat_ref)] + [(jac_hbm.at[part], jac_ref.at[part]) for part in parts]
    pairs += [(src_hbm, src_ref), (tran_hbm, tran_ref)]
    copies = [pltpu.make_async_copy(a, b, sems.at[i]) for i, (a, b) in enumerate(pairs)]
    for copy in copies:
        copy.start()
    half = lanes((128, N)) % 2 == lax.broadcasted_iota(jnp.int32, (128, N), 0) // N
    half = jnp.where(half, 1.0, 0.0).astype(bf16)
    copies[0].wait()
    copies[1].wait()
    u = dens_ref[...]
    u2 = jnp.concatenate([u, u], axis=1)
    lane8 = lanes((8, 128))
    pat = pat_ref[...].astype(f32)
    mask_rows = jnp.zeros((8, 128), f32)
    for t in range(8):
        mask_rows = jnp.where((lane8 % N) // 8 == t, pat[:, t : t + 1], mask_rows)
    lane = lanes((CELLS, N))
    acc = jnp.zeros((CELLS, N), f32)
    for m in range(32):
        if m % 8 == 0:
            copies[2 + m // 8].wait()
        y = jac_ref[:, m * 128 : (m + 1) * 128] * (u2 * mask_rows[m // 4 : m // 4 + 1])
        hi = y.astype(bf16)
        lo = (y - hi.astype(f32)).astype(bf16)
        z = jnp.dot(hi, half, preferred_element_type=f32) + jnp.dot(lo, half, preferred_element_type=f32)
        acc = jnp.where(lane // 2 == m, z, acc)
    copies[6].wait()
    copies[7].wait()
    tran = tran_ref[...]
    flux = tran * u
    flux_ref[...] = column(flux[CELLS - 1 : CELLS])
    row = lax.broadcasted_iota(jnp.int32, (CELLS, N), 0)
    lower = jnp.where(row == 0, 0.0, pltpu.roll(flux, 1, 0))
    upper = jnp.where(row == CELLS - 1, 0.0, pltpu.roll(u, CELLS - 1, 0))
    out_ref[...] = src_ref[...] - acc + lower + tran * upper


def upsweep(neigh_ref, part_ref, a_ref, b_ref, c_ref, even_ref, odd_ref, flux_ref, dens_ref, tran_ref, lat_ref, coup_ref, cols_ref,
            quad_ref, n1_ref, n2_ref, n3_ref, n4_ref, n5_ref, root_ref, pay_ref, pair_ref, v_ref, w_ref):
    me = lax.axis_index("lat")
    u = dens_ref[...]
    total = jnp.zeros((CELLS, N), f32)
    lines = [(0, u), (1, a_ref[0])] + [(2 + i, b_ref[i]) for i in range(2)]
    lines += [((6, 7, 4, 5)[i], c_ref[i]) for i in range(4)]
    for offset, value in lines:
        line = me ^ offset
        count = jnp.int32(0)
        for j in range(4):
            count = count + (neigh_ref[0, j] == line).astype(jnp.int32)
        total = total + count.astype(f32) * value
    row = lax.broadcasted_iota(jnp.int32, (CELLS, N), 0)
    r = part_ref[...] - lat_ref[...] * (4.0 * u - total)
    depth = lax.axis_index("depth")
    above = jnp.where(depth % 2 == 0, even_ref[0, 0:1], odd_ref[0, 0:1])
    above = jnp.where(depth == lax.axis_size("depth") - 1, 0.0, above)
    r = r + jnp.where(row == CELLS - 1, tran_ref[...] * above, 0.0)
    c = coup_ref[...]
    g = r / jnp.where(row == 0, c, pltpu.roll(c, 1, 0))
    x = []
    for i in range(4):
        rolled = g if i == 0 else pltpu.roll(g, CELLS - i, 0)
        x.append(jnp.concatenate([rolled, rolled], axis=0).T)
    lane2 = lanes((N, N)) % CELLS
    lane = lanes((N, CELLS))
    pair_v, pair_w = [], []
    for half in range(2):
        x0, x1 = x[2 * half], x[2 * half + 1]
        y = pair_rhs(x0, x1)
        v = jnp.zeros((N, N), f32)
        w = jnp.zeros((N, N), f32)
        for j in range(8):
            at = 2 * j + half
            here = lane2 == 4 * j
            v = jnp.where(here, jnp.dot(quad_ref[at, 0], y, preferred_element_type=f32), v)
            w = jnp.where(here, jnp.dot(quad_ref[at, 1], y, preferred_element_type=f32), w)
        v = v[:, :CELLS] + v[:, CELLS:] + x0[:, :CELLS] + x1[:, :CELLS]
        w = w[:, :CELLS] + w[:, CELLS:]
        pair_v.append(v)
        pair_w.append(w)
        pair_ref[half, :, 0:CELLS] = pair_v[half]
        pair_ref[2 + half, :, 0:CELLS] = w
    yv, yw = rhs(pair_v[0]), rhs(pair_w[1])
    v, w = pair_v[0] + pair_v[1], pair_w[0] + pair_w[1]
    dv = jnp.zeros((N, CELLS), f32)
    dw = jnp.zeros((N, CELLS), f32)
    for j in range(8):
        here = lane == 4 * j
        dv = jnp.where(here, dot(n1_ref[2 * j + 1, 0], yv), dv)
        dw = jnp.where(here, dot(n1_ref[2 * j, 1], yw) + dot(n2_ref[j, 3], yv), dw)
    v, w = v + dv, w + dw
    vs = [jnp.broadcast_to(v[:, 4 * j : 4 * j + 1], (N, 128)) for j in range(8)]
    ws = [jnp.broadcast_to(w[:, 4 * j : 4 * j + 1], (N, 128)) for j in range(8)]
    at = 0
    for count, ref, above in ((4, n2_ref, n3_ref), (2, n3_ref, n4_ref), (1, n4_ref, n5_ref)):
        next_v, next_w = [], []
        for j in range(count):
            v1, v2, w1, w2 = vs[2 * j], vs[2 * j + 1], ws[2 * j], ws[2 * j + 1]
            v_ref[at], w_ref[at] = v1, w2
            at += 1
            yv, yw = rhs(v1), rhs(w2)
            u_map = above[j, 3] if count > 1 else above[0]
            next_v.append(v1 + v2 + dot(ref[2 * j + 1, 0], yv))
            next_w.append(w1 + w2 + dot(ref[2 * j, 1], yw) + dot(u_map, yv))
        vs, ws = next_v, next_w
    lane = lanes((N, 128))
    pay_ref[:N] = root_ref[:N]
    tail = jnp.where(lane == N, vs[0] * cols_ref[0] + flux_ref[...], ws[0])
    pay_ref[N:] = jnp.where(lane < N, root_ref[N:], tail)


def prepare(pair_ref, v_ref, w_ref, n1_ref, n2_ref, n3_ref, n4_ref, t_ref, add_v, add_a, add_x):
    lane = lanes((N, 128))
    part = lane % CELLS
    at, vec = 0, 0
    for level, size, ref in ((1, 8, n2_ref), (2, 16, n3_ref), (3, 32, n4_ref)):
        acc_v = jnp.zeros((N, 128), f32)
        acc_a = jnp.zeros((N, 128), f32)
        for j in range(CELLS // size):
            kw = ref[2 * j + 1, 2]
            wide = kw.astype(f32)
            t_ref[at] = pack(wide + roll(wide, N) + mm(kw, ref[2 * j, 0]))
            at += 1
            here = part // size == j
            acc_v = jnp.where(here, v_ref[vec], acc_v)
            acc_a = jnp.where(here, w_ref[vec] + dot(kw, rhs(v_ref[vec])), acc_a)
            vec += 1
        add_v[level], add_a[level] = acc_v, acc_a

    def repeat(x):
        x = x + roll(x, CELLS)
        return x + roll(x, 2 * CELLS)

    first = jnp.logical_and(lane % 4 == 0, lane < CELLS)
    v0, v1, w0, w1 = [jnp.where(first, pair_ref[i], 0.0) for i in range(4)]
    y = rhs(v0)
    acc_a = jnp.zeros((N, 128), f32)
    for j in range(8):
        kw = n1_ref[2 * j + 1, 2]
        wide = kw.astype(f32)
        t_ref[at] = pack(wide + roll(wide, N) + mm(kw, n1_ref[2 * j, 0]))
        at += 1
        acc_a = jnp.where(lane == 4 * j, dot(kw, y), acc_a)
    acc_a = acc_a + w1
    spread_v = v0 + roll(v0, 1)
    spread_a = acc_a + roll(acc_a, 1)
    add_v[0] = repeat(spread_v + roll(spread_v, 2))
    add_a[0] = repeat(spread_a + roll(spread_a, 2))
    add_x[...] = repeat(w0 + roll(w1, 2) + roll(v0, 1) + roll(v1, 3))


def prepare_last(own_ref, fun_ref, maps_ref, vecs_ref, own_rhs):
    is_low = lax.axis_index("depth") < 2 * ZS
    f, hh, k, g, e = unpack(fun_ref[...])
    maps_ref[0], maps_ref[1] = pack(f), pack(jnp.where(is_low, hh, k))
    vecs_ref[0], vecs_ref[1] = g, e
    v = jnp.broadcast_to(own_ref[:, N : N + 1], (N, 128))
    hi = v.astype(bf16)
    lo = (v - hi.astype(f32)).astype(bf16)
    zero = jnp.zeros((N, 128), bf16)
    own_rhs[0] = jnp.concatenate([hi, zero, hi, zero], axis=0)
    own_rhs[1] = jnp.concatenate([lo, zero, lo, zero], axis=0)


def unpack(b):
    low = lanes((N, 128)) < N
    b1, b2 = b[:N], b[N:]
    r1, r2 = roll(b1, N), roll(b2, N)
    x = jnp.where(low, b1, r1)
    y = jnp.where(low, r1, b1)
    z = jnp.where(low, b2, r2)
    g = jnp.broadcast_to(b2[:, N : N + 1], (N, 128))
    h = jnp.broadcast_to(b2[:, N + 1 : N + 2], (N, 128))
    return x, y, z, g, h


def join(one, two, last=False):
    p1, q1, w1, v1, h1 = one
    p2, q2, w2, v2, h2 = two
    kq1, kp2, kw2 = pack(q1), pack(p2), pack(w2)
    yp1, yv1 = rhs(p1), rhs(v1)
    t = dot(kw2, yp1)
    th = h2 + dot(kw2, yv1)
    v = v2 + dot(kp2, yv1)
    yt, yth = rhs(t), rhs(th)
    w = w1 + dot(kq1, yt)
    h = h1 + dot(kq1, yth)
    yq2 = rhs(q2)
    p, q = (None, None) if last else (dot(kp2, yp1), dot(kq1, yq2))
    return (p, q, w, v, h), (t, th, yp1, yv1, yq2, yt, yth)


def track_first(is_low, one, two, extra):
    eye = eye2()
    t, th = extra[:2]
    return (
        jnp.where(is_low, eye, one[0]),
        jnp.where(is_low, two[1], eye),
        jnp.where(is_low, t, 0.0),
        jnp.where(is_low, 0.0, one[3]),
        jnp.where(is_low, th, 0.0),
    )


def track(is_low, fun, extra):
    f, hh, k, g, e = fun
    t, th, yp1, yv1, yq2, yt, yth = extra
    x1 = pack(jnp.where(is_low, hh, f))
    x2 = pack(jnp.where(is_low, hh, k))
    prod1 = dot(x1, jnp.where(is_low, yq2, yp1))
    prod2 = dot(x2, jnp.where(is_low, yt, yp1))
    vec1 = dot(x1, yv1)
    vec2 = dot(x2, jnp.where(is_low, yth, yv1))
    return (
        jnp.where(is_low, f, prod1),
        jnp.where(is_low, prod1, hh),
        jnp.where(is_low, k + prod2, prod2),
        jnp.where(is_low, g, g + vec1),
        e + vec2,
    )


def put_map(ref, p, q, w, v, h, last=False):
    lane = lanes((N, 128))
    low = lane < N
    tail = jnp.where(low, w, jnp.where(lane == N, v, h))
    if last:
        ref[...] = tail
    else:
        ref[:N] = jnp.where(low, p, q)
        ref[N:] = tail


def combine_four(last, *refs):
    if last:
        own_ref, x1_ref, x2_ref, x3_ref, fun_ref, out_ref, fun_out, slots = refs
    else:
        own_ref, x1_ref, x2_ref, x3_ref, out_ref, fun_out, slots = refs
    depth = lax.axis_index("depth")
    at = ((depth // ZS) % 2) * 2 + (depth % ZS) // 4 if last else depth % 4
    slots[at] = own_ref[...]
    slots[at ^ 1] = x1_ref[...]
    slots[at ^ 2] = x2_ref[...]
    slots[at ^ 3] = x3_ref[...]
    maps = [unpack(slots[i]) for i in range(4)]
    lower, extra_lower = join(maps[0], maps[1])
    upper, extra_upper = join(maps[2], maps[3])
    in_lower = at < 2
    mine = lambda x, y: [jnp.where(in_lower, a, b) for a, b in zip(x, y)]
    if last:
        fun = track(at % 2 == 0, unpack(fun_ref[...]), mine(extra_lower, extra_upper))
    else:
        fun = track_first(
            at % 2 == 0, mine(maps[0], maps[2]), mine(maps[1], maps[3]), mine(extra_lower[:2], extra_upper[:2])
        )
    total, extra = join(lower, upper, last)
    put_map(out_ref, *total, last=last)
    put_map(fun_out, *track(in_lower, fun, extra))


def downsweep(other_ref, maps_ref, vecs_ref, own_rhs, cols_ref, add_v, add_a, add_x, quad_ref, n1_ref, n2_ref, n3_ref,
              n4_ref, t_ref, out_ref):
    is_low = lax.axis_index("depth") < 2 * ZS
    g, e = vecs_ref[0], vecs_ref[1]
    other = other_ref[...]
    hi = other.astype(bf16)
    wide = jnp.concatenate([hi, (other - hi.astype(f32)).astype(bf16)], axis=1)
    v_other = jnp.broadcast_to(other[:, N : N + 1], (N, 128))
    w_other = jnp.broadcast_to(other[:, N + 1 : N + 2], (N, 128))
    t = w_other + jnp.dot(wide, own_rhs[0], preferred_element_type=f32)
    t = t + jnp.dot(wide, own_rhs[1], preferred_element_type=f32)
    up = g + dot(maps_ref[0], rhs(v_other))
    aa = e + dot(maps_ref[1], rhs(jnp.where(is_low, t, v_other)))
    ss = jnp.where(is_low, g, up) * cols_ref[1]
    lane = lanes((N, 128)) % CELLS
    for level, size, ref, base in ((3, 32, n4_ref, 6), (2, 16, n3_ref, 4), (1, 8, n2_ref, 0), (0, 4, n1_ref, 7)):
        ys, ya = rhs(ss), rhs(aa)
        ds = jnp.zeros((N, 128), f32)
        da = jnp.zeros((N, 128), f32)
        for j in range(CELLS // size):
            here = lane // size == j
            ds = jnp.where(here, dot(ref[2 * j, 0], ys), ds)
            da = jnp.where(here, dot(ref[2 * j + 1, 1], ya) + dot(t_ref[base + j], ys), da)
        upper = lane % size >= size // 2
        new_s = ss + add_v[level] + ds
        new_a = aa + add_a[level] + da
        ss = jnp.where(upper, new_s, ss)
        aa = jnp.where(upper, aa, new_a)
    y = pair_rhs(ss, aa)
    x = jnp.zeros((N, 128), f32)
    for j in range(CELLS // 2):
        x = jnp.where(lane == 2 * j, jnp.dot(quad_ref[j, 2], y, preferred_element_type=f32), x)
        x = jnp.where(lane == 2 * j + 1, jnp.dot(quad_ref[j, 3], y, preferred_element_type=f32), x)
    x = x + roll(x, CELLS) + (aa + add_x[...] + jnp.where(lane % 2 == 1, ss, 0.0))
    out_ref[...] = x.T[:CELLS]


def sds(*shape, dtype=f32):
    return jax.ShapeDtypeStruct(shape, dtype)


def call(body, outs, *args, scratch=(), smem=0, hbm=0, flops=0, name=None):
    args = [pltpu.with_memory_space_constraint(x, pltpu.HBM) if smem <= i < smem + hbm else x for i, x in enumerate(args)]
    spaces = [pltpu.SMEM] * smem + [pltpu.HBM] * hbm + [pltpu.VMEM] * (len(args) - smem - hbm)
    return pl.pallas_call(
        body,
        out_shape=outs,
        in_specs=[pl.BlockSpec(memory_space=space) for space in spaces],
        out_specs=jax.tree.map(lambda _: pl.BlockSpec(memory_space=pltpu.VMEM), outs),
        scratch_shapes=scratch,
        cost_estimate=pl.CostEstimate(flops=flops, bytes_accessed=1 << 16, transcendentals=0),
        name=name,
        compiler_params=pltpu.CompilerParams(vmem_limit_bytes=VLIM),
    )(*args)


def node(count):
    return sds(count, 4, N, 128, dtype=bf16)


def on_device(densities, source, jacobian, pattern, transport, lateral, neighbours, factor, coupling):
    line_count, cell_count, species = densities.shape
    u = densities.reshape(CELLS, N)
    src = source.reshape(CELLS, N)
    tran = transport.reshape(CELLS, N)
    lat = lateral.reshape(CELLS, N)
    coup = coupling.reshape(CELLS, N)
    jac = jacobian.reshape(CELLS, N * N)
    fac = factor.reshape(4, 8, 32, 128).transpose(0, 2, 1, 3).reshape(1024, 128)

    def xor_lat(value, bits):
        return lax.ppermute(value, "lat", [(i, i ^ bits) for i in range(8)])

    def xor_depth(value, bits):
        return lax.ppermute(value, "depth", [(i, i ^ bits) for i in range(32)])

    line_a = xor_lat(densities, 1)
    part, flux = call(
        react, (sds(CELLS, N), sds(N, 128)), jac, u, src, tran, pattern, hbm=5, flops=1 << 30, name="react",
        scratch=[pltpu.VMEM((CELLS, N * N), f32)] + [pltpu.VMEM((CELLS, N), f32)] * 3
        + [pltpu.VMEM((8, 8), jnp.int32), pltpu.SemaphoreType.DMA((8,))],
    )
    line_b = xor_lat(jnp.concatenate([densities, line_a], axis=0), 2)
    quad, n1, full, cols = call(
        tree_leaves,
        (sds(16, 4, N, 256, dtype=bf16), sds(16, 3, N, 128, dtype=bf16), sds(16, 3, N, 128), sds(2, N, 128)),
        fac, coup, part, scratch=[pltpu.VMEM((2, N, 128), f32)], flops=2 << 30, name="tree_leaves",
    )
    top_even = xor_depth(lax.optimization_barrier((densities, cols))[0], 1)
    top_odd = lax.ppermute(
        lax.optimization_barrier((densities, line_b))[0], "depth",
        [(i, i + 1 if i % 2 else i - 1) for i in range(1, 31)],
    )
    line_c = xor_lat(jnp.concatenate([densities, line_a, line_b], axis=0), 6)
    n2, n3, n4, n5, root = call(
        tree_upper,
        (node(8), node(4), node(2), sds(1, N, 128, dtype=bf16), sds(128, 128)),
        n1, full, coup, cols, part, scratch=[pltpu.VMEM((8, 3, N, 128), f32), pltpu.VMEM((4, 3, N, 128), f32)],
        flops=2 << 30, name="tree_upper",
    )
    pay, pair, vs, ws = call(
        upsweep, (sds(128, 128), sds(4, N, 128), sds(7, N, 128), sds(7, N, 128)),
        neighbours, part, line_a, line_b, line_c, top_even, top_odd, flux, u, tran, lat, coup, cols, quad, n1, n2, n3, n4, n5, root,
        smem=1, flops=1 << 25, name="upsweep",
    )
    others = [xor_depth(pay, bits) for bits in (1, 2, 3)]
    tees, add_v, add_a, add_x = call(
        prepare, (sds(15, N, 128, dtype=bf16), sds(4, N, 128), sds(4, N, 128), sds(N, 128)),
        pair, vs, ws, n1, n2, n3, n4, flops=1 << 30, name="prepare",
    )
    slots = [pltpu.VMEM((4, 128, 128), f32)]
    pay, fun = call(
        lambda *refs: combine_four(False, *refs), (sds(128, 128), sds(128, 128)), pay, *others, scratch=slots,
        flops=1 << 24, name="combine_low",
    )
    others = [xor_depth(pay, bits) for bits in (7, 8, 15)]
    pay, fun = call(
        lambda *refs: combine_four(True, *refs), (sds(N, 128), sds(128, 128)), pay, *others, fun, scratch=slots,
        flops=1 << 24, name="combine_high",
    )
    other = xor_depth(pay, 24)
    maps, vecs, own_rhs = call(
        prepare_last,
        (sds(2, N, 128, dtype=bf16), sds(2, N, 128), sds(2, 256, 128, dtype=bf16)),
        pay, fun, flops=1 << 30, name="prepare_last",
    )
    out = call(
        downsweep, sds(CELLS, N), other, maps, vecs, own_rhs, cols, add_v, add_a, add_x, quad, n1, n2, n3, n4, tees,
        flops=1 << 25, name="downsweep",
    )
    return out.reshape(line_count, cell_count, species)


def solution(mesh):
    return jax.shard_map(
        on_device,
        mesh=mesh,
        in_specs=(
            P("lat", "depth", None),
            P("lat", "depth", None),
            P("lat", "depth", None),
            P(),
            P("lat", "depth", None),
            P("lat", "depth", None),
            P("lat", None),
            P("lat", "depth", None),
            P("lat", "depth", None),
        ),
        out_specs=P("lat", "depth", None),
        check_vma=False,
    )
```

```python
import jax
import jax.numpy as jnp
from jax import lax
from jax.experimental import pallas as pl
from jax.experimental.pallas import tpu as pltpu
from jax.sharding import PartitionSpec as P

f32 = jnp.float32
bf16 = jnp.bfloat16

CELLS = 32
N = 64
ZS = 8
VLIM = 16 << 20


def lanes(shape):
    return lax.broadcasted_iota(jnp.int32, shape, len(shape) - 1)


def roll(x, shift):
    shift = shift % x.shape[-1]
    return x if shift == 0 else pltpu.roll(x, shift, x.ndim - 1)


def pack(dup):
    hi = dup.astype(bf16).astype(f32)
    return jnp.where(lanes(dup.shape) < N, hi, dup - hi).astype(bf16)


def mm(a, b):
    r = jnp.dot(a, jnp.concatenate([b, b], axis=0), preferred_element_type=f32)
    return r + roll(r, N)


def rhs(x):
    hi = x.astype(bf16)
    lo = (x - hi.astype(f32)).astype(bf16)
    return jnp.concatenate([hi, hi, lo, lo], axis=0)


def dot(a, y):
    return jnp.dot(jnp.concatenate([a, a], axis=1), y, preferred_element_type=f32)


def column(row):
    return jnp.broadcast_to(row, (128, N)).T


def pair(a, b):
    low = lanes(a.shape) < N
    a_hi, b_hi = a.astype(bf16).astype(f32), b.astype(bf16).astype(f32)
    hi = jnp.where(low, a_hi, b_hi).astype(bf16)
    lo = jnp.where(low, a - a_hi, b - b_hi).astype(bf16)
    return jnp.concatenate([hi, lo], axis=1)


def pair_rhs(x, y):
    def split(z):
        hi = z.astype(bf16).astype(f32)
        return jnp.where(lanes(z.shape) % 64 < CELLS, hi, z - hi).astype(bf16)

    a, b = split(x), split(y)
    return jnp.concatenate([a, b, a, b], axis=0)


def eye2():
    return jnp.where(lanes((N, 128)) % N == lax.broadcasted_iota(jnp.int32, (N, 128), 0), 1.0, 0.0)


def put(node, full, j, p, q, w, u=None):
    node[j, 0], node[j, 1], node[j, 2] = pack(p), pack(q), pack(w)
    full[j, 0], full[j, 1], full[j, 2] = p, q, w
    if u is not None:
        node[j, 3] = pack(u)


def tree_leaves(fac_ref, coup_ref, after_ref, quad_ref, n1_ref, full_ref, cols_ref, rows):
    del after_ref
    c = coup_ref[...]
    cols_ref[0] = column(c[CELLS - 1 : CELLS])
    cols_ref[1] = column(1.0 / c[0:1])
    c2 = jnp.concatenate([c, c], axis=1)
    low = lanes((CELLS, 128)) < N
    eye = eye2()

    def leaf(k):
        g, s = divmod(k, 8)
        x = fac_ref[pl.ds(g * 256 + s, 32, stride=8), :]
        y = roll(x, N)
        rows[k % 2, pl.ds(0, 32, stride=2), :] = jnp.where(low, x, y)
        rows[k % 2, pl.ds(1, 32, stride=2), :] = jnp.where(low, y, x)
        a = rows[k % 2]
        before = max(k - 1, 0)
        return a * c2[before : before + 1] - eye, a * c2[k : k + 1] - eye

    for j in range(CELLS // 2):
        p1, q1 = leaf(2 * j)
        p2, q2 = leaf(2 * j + 1)
        kq1 = pack(q1)
        p = p1 + p2 + dot(pack(p2), rhs(p1))
        q = q1 + q2 + dot(kq1, rhs(q2))
        u = eye + q1 + p2 + dot(kq1, rhs(p2))
        w = (eye + eye) + p1 + q1 + p + dot(kq1, rhs(p))
        put(n1_ref, full_ref, j, p, q, w)
        quad_ref[j, 0] = pair(p, p2)
        quad_ref[j, 1] = pair(w, u)
        quad_ref[j, 2] = pair(w, q)
        quad_ref[j, 3] = pair(p, q2)


def tree_upper(n1_ref, full_ref, coup_ref, cols_ref, after_ref, n2_ref, n3_ref, n4_ref, n5_ref, root_ref, fa, fb):
    del after_ref
    node, full = n1_ref, full_ref
    for count, node_to, full_to in ((8, n2_ref, fa), (4, n3_ref, fb), (2, n4_ref, fa), (1, None, None)):
        for j in range(count):
            one, two = 2 * j, 2 * j + 1
            kq1, yp1 = node[one, 1], rhs(full[one, 0])
            u = full[two, 2] + dot(kq1, rhs(full[two, 2]))
            p = full[one, 0] + full[two, 0] + dot(node[two, 0], yp1)
            q = full[one, 1] + full[two, 1] + dot(kq1, rhs(full[two, 1]))
            ku = pack(u)
            w = full[one, 2] + u + dot(ku, yp1)
            if node_to is None:
                eye = eye2()
                n5_ref[0] = ku
                first = coup_ref[0:1]
                scale = 1.0 / jnp.concatenate([first, first], axis=1)
                root_ref[:N] = jnp.where(lanes((N, 128)) < N, (p + eye) * cols_ref[0] * scale, q + eye)
                root_ref[N:] = w * scale
            else:
                put(node_to, full_to, j, p, q, w, u)
        node, full = node_to, full_to


def react(jac_hbm, dens_hbm, src_hbm, tran_hbm, pat_hbm, out_ref, flux_ref, jac_ref, dens_ref, src_ref, tran_ref,
          pat_ref, sems):
    parts = [(slice(None), pl.ds(i * 1024, 1024)) for i in range(4)]
    pairs = [(dens_hbm, dens_ref), (pat_hbm, pat_ref)] + [(jac_hbm.at[part], jac_ref.at[part]) for part in parts]
    pairs += [(src_hbm, src_ref), (tran_hbm, tran_ref)]
    copies = [pltpu.make_async_copy(a, b, sems.at[i]) for i, (a, b) in enumerate(pairs)]
    for copy in copies:
        copy.start()
    half = lanes((128, N)) % 2 == lax.broadcasted_iota(jnp.int32, (128, N), 0) // N
    half = jnp.where(half, 1.0, 0.0).astype(bf16)
    copies[0].wait()
    copies[1].wait()
    u = dens_ref[...]
    u2 = jnp.concatenate([u, u], axis=1)
    lane8 = lanes((8, 128))
    pat = pat_ref[...].astype(f32)
    mask_rows = jnp.zeros((8, 128), f32)
    for t in range(8):
        mask_rows = jnp.where((lane8 % N) // 8 == t, pat[:, t : t + 1], mask_rows)
    lane = lanes((CELLS, N))
    acc = jnp.zeros((CELLS, N), f32)
    for m in range(32):
        if m % 8 == 0:
            copies[2 + m // 8].wait()
        y = jac_ref[:, m * 128 : (m + 1) * 128] * (u2 * mask_rows[m // 4 : m // 4 + 1])
        hi = y.astype(bf16)
        lo = (y - hi.astype(f32)).astype(bf16)
        z = jnp.dot(hi, half, preferred_element_type=f32) + jnp.dot(lo, half, preferred_element_type=f32)
        acc = jnp.where(lane // 2 == m, z, acc)
    copies[6].wait()
    copies[7].wait()
    tran = tran_ref[...]
    flux = tran * u
    flux_ref[...] = column(flux[CELLS - 1 : CELLS])
    row = lax.broadcasted_iota(jnp.int32, (CELLS, N), 0)
    lower = jnp.where(row == 0, 0.0, pltpu.roll(flux, 1, 0))
    upper = jnp.where(row == CELLS - 1, 0.0, pltpu.roll(u, CELLS - 1, 0))
    out_ref[...] = src_ref[...] - acc + lower + tran * upper


def upsweep(neigh_ref, part_ref, a_ref, b_ref, c_ref, even_ref, odd_ref, flux_ref, dens_ref, tran_ref, lat_ref, coup_ref, cols_ref,
            quad_ref, n1_ref, n2_ref, n3_ref, n4_ref, n5_ref, root_ref, pay_ref, pair_ref, v_ref, w_ref):
    me = lax.axis_index("lat")
    u = dens_ref[...]
    total = jnp.zeros((CELLS, N), f32)
    lines = [(0, u), (1, a_ref[0])] + [(2 + i, b_ref[i]) for i in range(2)]
    lines += [((6, 7, 4, 5)[i], c_ref[i]) for i in range(4)]
    for offset, value in lines:
        line = me ^ offset
        count = jnp.int32(0)
        for j in range(4):
            count = count + (neigh_ref[0, j] == line).astype(jnp.int32)
        total = total + count.astype(f32) * value
    row = lax.broadcasted_iota(jnp.int32, (CELLS, N), 0)
    r = part_ref[...] - lat_ref[...] * (4.0 * u - total)
    depth = lax.axis_index("depth")
    above = jnp.where(depth % 2 == 0, even_ref[0, 0:1], odd_ref[0, 0:1])
    above = jnp.where(depth == lax.axis_size("depth") - 1, 0.0, above)
    r = r + jnp.where(row == CELLS - 1, tran_ref[...] * above, 0.0)
    c = coup_ref[...]
    g = r / jnp.where(row == 0, c, pltpu.roll(c, 1, 0))
    x = []
    for i in range(4):
        rolled = g if i == 0 else pltpu.roll(g, CELLS - i, 0)
        x.append(jnp.concatenate([rolled, rolled], axis=0).T)
    lane2 = lanes((N, N)) % CELLS
    lane = lanes((N, CELLS))
    pair_v, pair_w = [], []
    for half in range(2):
        x0, x1 = x[2 * half], x[2 * half + 1]
        y = pair_rhs(x0, x1)
        v = jnp.zeros((N, N), f32)
        w = jnp.zeros((N, N), f32)
        for j in range(8):
            at = 2 * j + half
            here = lane2 == 4 * j
            v = jnp.where(here, jnp.dot(quad_ref[at, 0], y, preferred_element_type=f32), v)
            w = jnp.where(here, jnp.dot(quad_ref[at, 1], y, preferred_element_type=f32), w)
        v = v[:, :CELLS] + v[:, CELLS:] + x0[:, :CELLS] + x1[:, :CELLS]
        w = w[:, :CELLS] + w[:, CELLS:]
        pair_v.append(v)
        pair_w.append(w)
        pair_ref[half, :, 0:CELLS] = pair_v[half]
        pair_ref[2 + half, :, 0:CELLS] = w
    yv, yw = rhs(pair_v[0]), rhs(pair_w[1])
    v, w = pair_v[0] + pair_v[1], pair_w[0] + pair_w[1]
    dv = jnp.zeros((N, CELLS), f32)
    dw = jnp.zeros((N, CELLS), f32)
    for j in range(8):
        here = lane == 4 * j
        dv = jnp.where(here, dot(n1_ref[2 * j + 1, 0], yv), dv)
        dw = jnp.where(here, dot(n1_ref[2 * j, 1], yw) + dot(n2_ref[j, 3], yv), dw)
    v, w = v + dv, w + dw
    vs = [jnp.broadcast_to(v[:, 4 * j : 4 * j + 1], (N, 128)) for j in range(8)]
    ws = [jnp.broadcast_to(w[:, 4 * j : 4 * j + 1], (N, 128)) for j in range(8)]
    at = 0
    for count, ref, above in ((4, n2_ref, n3_ref), (2, n3_ref, n4_ref), (1, n4_ref, n5_ref)):
        next_v, next_w = [], []
        for j in range(count):
            v1, v2, w1, w2 = vs[2 * j], vs[2 * j + 1], ws[2 * j], ws[2 * j + 1]
            v_ref[at], w_ref[at] = v1, w2
            at += 1
            yv, yw = rhs(v1), rhs(w2)
            u_map = above[j, 3] if count > 1 else above[0]
            next_v.append(v1 + v2 + dot(ref[2 * j + 1, 0], yv))
            next_w.append(w1 + w2 + dot(ref[2 * j, 1], yw) + dot(u_map, yv))
        vs, ws = next_v, next_w
    lane = lanes((N, 128))
    pay_ref[:N] = root_ref[:N]
    tail = jnp.where(lane == N, vs[0] * cols_ref[0] + flux_ref[...], ws[0])
    pay_ref[N:] = jnp.where(lane < N, root_ref[N:], tail)


def prepare(pair_ref, v_ref, w_ref, n1_ref, n2_ref, n3_ref, n4_ref, t_ref, add_v, add_a, add_x):
    lane = lanes((N, 128))
    part = lane % CELLS
    at, vec = 0, 0
    for level, size, ref in ((1, 8, n2_ref), (2, 16, n3_ref), (3, 32, n4_ref)):
        acc_v = jnp.zeros((N, 128), f32)
        acc_a = jnp.zeros((N, 128), f32)
        for j in range(CELLS // size):
            kw = ref[2 * j + 1, 2]
            wide = kw.astype(f32)
            t_ref[at] = pack(wide + roll(wide, N) + mm(kw, ref[2 * j, 0]))
            at += 1
            here = part // size == j
            acc_v = jnp.where(here, v_ref[vec], acc_v)
            acc_a = jnp.where(here, w_ref[vec] + dot(kw, rhs(v_ref[vec])), acc_a)
            vec += 1
        add_v[level], add_a[level] = acc_v, acc_a

    def repeat(x):
        x = x + roll(x, CELLS)
        return x + roll(x, 2 * CELLS)

    first = jnp.logical_and(lane % 4 == 0, lane < CELLS)
    v0, v1, w0, w1 = [jnp.where(first, pair_ref[i], 0.0) for i in range(4)]
    y = rhs(v0)
    acc_a = jnp.zeros((N, 128), f32)
    for j in range(8):
        kw = n1_ref[2 * j + 1, 2]
        wide = kw.astype(f32)
        t_ref[at] = pack(wide + roll(wide, N) + mm(kw, n1_ref[2 * j, 0]))
        at += 1
        acc_a = jnp.where(lane == 4 * j, dot(kw, y), acc_a)
    acc_a = acc_a + w1
    spread_v = v0 + roll(v0, 1)
    spread_a = acc_a + roll(acc_a, 1)
    add_v[0] = repeat(spread_v + roll(spread_v, 2))
    add_a[0] = repeat(spread_a + roll(spread_a, 2))
    add_x[...] = repeat(w0 + roll(w1, 2) + roll(v0, 1) + roll(v1, 3))


def prepare_last(own_ref, fun_ref, maps_ref, vecs_ref, own_rhs):
    is_low = lax.axis_index("depth") < 2 * ZS
    f, hh, k, g, e = unpack(fun_ref[...])
    maps_ref[0], maps_ref[1] = pack(f), pack(jnp.where(is_low, hh, k))
    vecs_ref[0], vecs_ref[1] = g, e
    v = jnp.broadcast_to(own_ref[:, N : N + 1], (N, 128))
    hi = v.astype(bf16)
    lo = (v - hi.astype(f32)).astype(bf16)
    zero = jnp.zeros((N, 128), bf16)
    own_rhs[0] = jnp.concatenate([hi, zero, hi, zero], axis=0)
    own_rhs[1] = jnp.concatenate([lo, zero, lo, zero], axis=0)


def unpack(b):
    low = lanes((N, 128)) < N
    b1, b2 = b[:N], b[N:]
    r1, r2 = roll(b1, N), roll(b2, N)
    x = jnp.where(low, b1, r1)
    y = jnp.where(low, r1, b1)
    z = jnp.where(low, b2, r2)
    g = jnp.broadcast_to(b2[:, N : N + 1], (N, 128))
    h = jnp.broadcast_to(b2[:, N + 1 : N + 2], (N, 128))
    return x, y, z, g, h


def join(one, two, last=False):
    p1, q1, w1, v1, h1 = one
    p2, q2, w2, v2, h2 = two
    kq1, kp2, kw2 = pack(q1), pack(p2), pack(w2)
    yp1, yv1 = rhs(p1), rhs(v1)
    t = dot(kw2, yp1)
    th = h2 + dot(kw2, yv1)
    v = v2 + dot(kp2, yv1)
    yt, yth = rhs(t), rhs(th)
    w = w1 + dot(kq1, yt)
    h = h1 + dot(kq1, yth)
    yq2 = rhs(q2)
    p, q = (None, None) if last else (dot(kp2, yp1), dot(kq1, yq2))
    return (p, q, w, v, h), (t, th, yp1, yv1, yq2, yt, yth)


def track_first(is_low, one, two, extra):
    eye = eye2()
    t, th = extra[:2]
    return (
        jnp.where(is_low, eye, one[0]),
        jnp.where(is_low, two[1], eye),
        jnp.where(is_low, t, 0.0),
        jnp.where(is_low, 0.0, one[3]),
        jnp.where(is_low, th, 0.0),
    )


def track(is_low, fun, extra):
    f, hh, k, g, e = fun
    t, th, yp1, yv1, yq2, yt, yth = extra
    x1 = pack(jnp.where(is_low, hh, f))
    x2 = pack(jnp.where(is_low, hh, k))
    prod1 = dot(x1, jnp.where(is_low, yq2, yp1))
    prod2 = dot(x2, jnp.where(is_low, yt, yp1))
    vec1 = dot(x1, yv1)
    vec2 = dot(x2, jnp.where(is_low, yth, yv1))
    return (
        jnp.where(is_low, f, prod1),
        jnp.where(is_low, prod1, hh),
        jnp.where(is_low, k + prod2, prod2),
        jnp.where(is_low, g, g + vec1),
        e + vec2,
    )


def put_map(ref, p, q, w, v, h, last=False):
    lane = lanes((N, 128))
    low = lane < N
    tail = jnp.where(low, w, jnp.where(lane == N, v, h))
    if last:
        ref[...] = tail
    else:
        ref[:N] = jnp.where(low, p, q)
        ref[N:] = tail


def combine_four(last, *refs):
    if last:
        own_ref, x1_ref, x2_ref, x3_ref, fun_ref, out_ref, fun_out, slots = refs
    else:
        own_ref, x1_ref, x2_ref, x3_ref, out_ref, fun_out, slots = refs
    depth = lax.axis_index("depth")
    at = ((depth // ZS) % 2) * 2 + (depth % ZS) // 4 if last else depth % 4
    slots[at] = own_ref[...]
    slots[at ^ 1] = x1_ref[...]
    slots[at ^ 2] = x2_ref[...]
    slots[at ^ 3] = x3_ref[...]
    maps = [unpack(slots[i]) for i in range(4)]
    lower, extra_lower = join(maps[0], maps[1])
    upper, extra_upper = join(maps[2], maps[3])
    in_lower = at < 2
    mine = lambda x, y: [jnp.where(in_lower, a, b) for a, b in zip(x, y)]
    if last:
        fun = track(at % 2 == 0, unpack(fun_ref[...]), mine(extra_lower, extra_upper))
    else:
        fun = track_first(
            at % 2 == 0, mine(maps[0], maps[2]), mine(maps[1], maps[3]), mine(extra_lower[:2], extra_upper[:2])
        )
    total, extra = join(lower, upper, last)
    put_map(out_ref, *total, last=last)
    put_map(fun_out, *track(in_lower, fun, extra))


def downsweep(other_ref, maps_ref, vecs_ref, own_rhs, cols_ref, add_v, add_a, add_x, quad_ref, n1_ref, n2_ref, n3_ref,
              n4_ref, t_ref, out_ref):
    is_low = lax.axis_index("depth") < 2 * ZS
    g, e = vecs_ref[0], vecs_ref[1]
    other = other_ref[...]
    hi = other.astype(bf16)
    wide = jnp.concatenate([hi, (other - hi.astype(f32)).astype(bf16)], axis=1)
    v_other = jnp.broadcast_to(other[:, N : N + 1], (N, 128))
    w_other = jnp.broadcast_to(other[:, N + 1 : N + 2], (N, 128))
    t = w_other + jnp.dot(wide, own_rhs[0], preferred_element_type=f32)
    t = t + jnp.dot(wide, own_rhs[1], preferred_element_type=f32)
    up = g + dot(maps_ref[0], rhs(v_other))
    aa = e + dot(maps_ref[1], rhs(jnp.where(is_low, t, v_other)))
    ss = jnp.where(is_low, g, up) * cols_ref[1]
    lane = lanes((N, 128)) % CELLS
    for level, size, ref, base in ((3, 32, n4_ref, 6), (2, 16, n3_ref, 4), (1, 8, n2_ref, 0), (0, 4, n1_ref, 7)):
        ys, ya = rhs(ss), rhs(aa)
        ds = jnp.zeros((N, 128), f32)
        da = jnp.zeros((N, 128), f32)
        for j in range(CELLS // size):
            here = lane // size == j
            ds = jnp.where(here, dot(ref[2 * j, 0], ys), ds)
            da = jnp.where(here, dot(ref[2 * j + 1, 1], ya) + dot(t_ref[base + j], ys), da)
        upper = lane % size >= size // 2
        new_s = ss + add_v[level] + ds
        new_a = aa + add_a[level] + da
        ss = jnp.where(upper, new_s, ss)
        aa = jnp.where(upper, aa, new_a)
    y = pair_rhs(ss, aa)
    x = jnp.zeros((N, 128), f32)
    for j in range(CELLS // 2):
        x = jnp.where(lane == 2 * j, jnp.dot(quad_ref[j, 2], y, preferred_element_type=f32), x)
        x = jnp.where(lane == 2 * j + 1, jnp.dot(quad_ref[j, 3], y, preferred_element_type=f32), x)
    x = x + roll(x, CELLS) + (aa + add_x[...] + jnp.where(lane % 2 == 1, ss, 0.0))
    out_ref[...] = x.T[:CELLS]


def sds(*shape, dtype=f32):
    return jax.ShapeDtypeStruct(shape, dtype)


def call(body, outs, *args, scratch=(), smem=0, hbm=0, flops=0, name=None):
    args = [pltpu.with_memory_space_constraint(x, pltpu.HBM) if smem <= i < smem + hbm else x for i, x in enumerate(args)]
    spaces = [pltpu.SMEM] * smem + [pltpu.HBM] * hbm + [pltpu.VMEM] * (len(args) - smem - hbm)
    return pl.pallas_call(
        body,
        out_shape=outs,
        in_specs=[pl.BlockSpec(memory_space=space) for space in spaces],
        out_specs=jax.tree.map(lambda _: pl.BlockSpec(memory_space=pltpu.VMEM), outs),
        scratch_shapes=scratch,
        cost_estimate=pl.CostEstimate(flops=flops, bytes_accessed=1 << 16, transcendentals=0),
        name=name,
        compiler_params=pltpu.CompilerParams(vmem_limit_bytes=VLIM),
    )(*args)


def node(count):
    return sds(count, 4, N, 128, dtype=bf16)


def on_device(densities, source, jacobian, pattern, transport, lateral, neighbours, factor, coupling):
    line_count, cell_count, species = densities.shape
    u = densities.reshape(CELLS, N)
    src = source.reshape(CELLS, N)
    tran = transport.reshape(CELLS, N)
    lat = lateral.reshape(CELLS, N)
    coup = coupling.reshape(CELLS, N)
    jac = jacobian.reshape(CELLS, N * N)
    fac = factor.reshape(4, 8, 32, 128).transpose(0, 2, 1, 3).reshape(1024, 128)

    def xor_lat(value, bits):
        return lax.ppermute(value, "lat", [(i, i ^ bits) for i in range(8)])

    def xor_depth(value, bits):
        return lax.ppermute(value, "depth", [(i, i ^ bits) for i in range(32)])

    line_a = xor_lat(densities, 1)
    part, flux = call(
        react, (sds(CELLS, N), sds(N, 128)), jac, u, src, tran, pattern, hbm=5, flops=1 << 30, name="react",
        scratch=[pltpu.VMEM((CELLS, N * N), f32)] + [pltpu.VMEM((CELLS, N), f32)] * 3
        + [pltpu.VMEM((8, 8), jnp.int32), pltpu.SemaphoreType.DMA((8,))],
    )
    line_b = xor_lat(jnp.concatenate([densities, line_a], axis=0), 2)
    quad, n1, full, cols = call(
        tree_leaves,
        (sds(16, 4, N, 256, dtype=bf16), sds(16, 3, N, 128, dtype=bf16), sds(16, 3, N, 128), sds(2, N, 128)),
        fac, coup, part, scratch=[pltpu.VMEM((2, N, 128), f32)], flops=2 << 30, name="tree_leaves",
    )
    top_even = xor_depth(lax.optimization_barrier((densities, cols))[0], 1)
    top_odd = lax.ppermute(
        lax.optimization_barrier((densities, line_b))[0], "depth",
        [(i, i if i in (0, 31) else i + 1 if i % 2 else i - 1) for i in range(32)],
    )
    line_c = xor_lat(jnp.concatenate([densities, line_a, line_b], axis=0), 6)
    n2, n3, n4, n5, root = call(
        tree_upper,
        (node(8), node(4), node(2), sds(1, N, 128, dtype=bf16), sds(128, 128)),
        n1, full, coup, cols, part, scratch=[pltpu.VMEM((8, 3, N, 128), f32), pltpu.VMEM((4, 3, N, 128), f32)],
        flops=2 << 30, name="tree_upper",
    )
    pay, pair, vs, ws = call(
        upsweep, (sds(128, 128), sds(4, N, 128), sds(7, N, 128), sds(7, N, 128)),
        neighbours, part, line_a, line_b, line_c, top_even, top_odd, flux, u, tran, lat, coup, cols, quad, n1, n2, n3, n4, n5, root,
        smem=1, flops=1 << 25, name="upsweep",
    )
    others = [xor_depth(pay, bits) for bits in (1, 2, 3)]
    tees, add_v, add_a, add_x = call(
        prepare, (sds(15, N, 128, dtype=bf16), sds(4, N, 128), sds(4, N, 128), sds(N, 128)),
        pair, vs, ws, n1, n2, n3, n4, flops=1 << 30, name="prepare",
    )
    slots = [pltpu.VMEM((4, 128, 128), f32)]
    pay, fun = call(
        lambda *refs: combine_four(False, *refs), (sds(128, 128), sds(128, 128)), pay, *others, scratch=slots,
        flops=1 << 24, name="combine_low",
    )
    others = [xor_depth(pay, bits) for bits in (7, 8, 15)]
    pay, fun = call(
        lambda *refs: combine_four(True, *refs), (sds(N, 128), sds(128, 128)), pay, *others, fun, scratch=slots,
        flops=1 << 24, name="combine_high",
    )
    other = xor_depth(pay, 24)
    maps, vecs, own_rhs = call(
        prepare_last,
        (sds(2, N, 128, dtype=bf16), sds(2, N, 128), sds(2, 256, 128, dtype=bf16)),
        pay, fun, flops=1 << 30, name="prepare_last",
    )
    out = call(
        downsweep, sds(CELLS, N), other, maps, vecs, own_rhs, cols, add_v, add_a, add_x, quad, n1, n2, n3, n4, tees,
        flops=1 << 25, name="downsweep",
    )
    return out.reshape(line_count, cell_count, species)


def solution(mesh):
    return jax.shard_map(
        on_device,
        mesh=mesh,
        in_specs=(
            P("lat", "depth", None),
            P("lat", "depth", None),
            P("lat", "depth", None),
            P(),
            P("lat", "depth", None),
            P("lat", "depth", None),
            P("lat", None),
            P("lat", "depth", None),
            P("lat", "depth", None),
        ),
        out_specs=P("lat", "depth", None),
        check_vma=False,
    )
```

```python
import jax
import jax.numpy as jnp
from jax import lax
from jax.experimental import pallas as pl
from jax.experimental.pallas import tpu as pltpu
from jax.sharding import PartitionSpec as P

f32 = jnp.float32
bf16 = jnp.bfloat16

CELLS = 32
N = 64
ZS = 8
VLIM = 16 << 20


def lanes(shape):
    return lax.broadcasted_iota(jnp.int32, shape, len(shape) - 1)


def roll(x, shift):
    shift = shift % x.shape[-1]
    return x if shift == 0 else pltpu.roll(x, shift, x.ndim - 1)


def pack(dup):
    hi = dup.astype(bf16).astype(f32)
    return jnp.where(lanes(dup.shape) < N, hi, dup - hi).astype(bf16)


def mm(a, b):
    r = jnp.dot(a, jnp.concatenate([b, b], axis=0), preferred_element_type=f32)
    return r + roll(r, N)


def rhs(x):
    hi = x.astype(bf16)
    lo = (x - hi.astype(f32)).astype(bf16)
    return jnp.concatenate([hi, hi, lo, lo], axis=0)


def dot(a, y):
    return jnp.dot(jnp.concatenate([a, a], axis=1), y, preferred_element_type=f32)


def column(row):
    return jnp.broadcast_to(row, (128, N)).T


def pair(a, b):
    low = lanes(a.shape) < N
    a_hi, b_hi = a.astype(bf16).astype(f32), b.astype(bf16).astype(f32)
    hi = jnp.where(low, a_hi, b_hi).astype(bf16)
    lo = jnp.where(low, a - a_hi, b - b_hi).astype(bf16)
    return jnp.concatenate([hi, lo], axis=1)


def pair_rhs(x, y):
    def split(z):
        hi = z.astype(bf16).astype(f32)
        return jnp.where(lanes(z.shape) % 64 < CELLS, hi, z - hi).astype(bf16)

    a, b = split(x), split(y)
    return jnp.concatenate([a, b, a, b], axis=0)


def eye2():
    return jnp.where(lanes((N, 128)) % N == lax.broadcasted_iota(jnp.int32, (N, 128), 0), 1.0, 0.0)


def put(node, full, j, p, q, w, u=None):
    node[j, 0], node[j, 1], node[j, 2] = pack(p), pack(q), pack(w)
    full[j, 0], full[j, 1], full[j, 2] = p, q, w
    if u is not None:
        node[j, 3] = pack(u)


def tree_leaves(fac_ref, coup_ref, after_ref, quad_ref, n1_ref, full_ref, cols_ref, rows):
    del after_ref
    c = coup_ref[...]
    cols_ref[0] = column(c[CELLS - 1 : CELLS])
    cols_ref[1] = column(1.0 / c[0:1])
    c2 = jnp.concatenate([c, c], axis=1)
    low = lanes((CELLS, 128)) < N
    eye = eye2()

    def leaf(k):
        g, s = divmod(k, 8)
        x = fac_ref[pl.ds(g * 256 + s, 32, stride=8), :]
        y = roll(x, N)
        rows[k % 2, pl.ds(0, 32, stride=2), :] = jnp.where(low, x, y)
        rows[k % 2, pl.ds(1, 32, stride=2), :] = jnp.where(low, y, x)
        a = rows[k % 2]
        before = max(k - 1, 0)
        return a * c2[before : before + 1] - eye, a * c2[k : k + 1] - eye

    for j in range(CELLS // 2):
        p1, q1 = leaf(2 * j)
        p2, q2 = leaf(2 * j + 1)
        kq1 = pack(q1)
        p = p1 + p2 + dot(pack(p2), rhs(p1))
        q = q1 + q2 + dot(kq1, rhs(q2))
        u = eye + q1 + p2 + dot(kq1, rhs(p2))
        w = (eye + eye) + p1 + q1 + p + dot(kq1, rhs(p))
        put(n1_ref, full_ref, j, p, q, w)
        quad_ref[j, 0] = pair(p, p2)
        quad_ref[j, 1] = pair(w, u)
        quad_ref[j, 2] = pair(w, q)
        quad_ref[j, 3] = pair(p, q2)


def tree_upper(n1_ref, full_ref, coup_ref, cols_ref, after_ref, n2_ref, n3_ref, n4_ref, n5_ref, root_ref, fa, fb):
    del after_ref
    node, full = n1_ref, full_ref
    for count, node_to, full_to in ((8, n2_ref, fa), (4, n3_ref, fb), (2, n4_ref, fa), (1, None, None)):
        for j in range(count):
            one, two = 2 * j, 2 * j + 1
            kq1, yp1 = node[one, 1], rhs(full[one, 0])
            u = full[two, 2] + dot(kq1, rhs(full[two, 2]))
            p = full[one, 0] + full[two, 0] + dot(node[two, 0], yp1)
            q = full[one, 1] + full[two, 1] + dot(kq1, rhs(full[two, 1]))
            ku = pack(u)
            w = full[one, 2] + u + dot(ku, yp1)
            if node_to is None:
                eye = eye2()
                n5_ref[0] = ku
                first = coup_ref[0:1]
                scale = 1.0 / jnp.concatenate([first, first], axis=1)
                root_ref[:N] = jnp.where(lanes((N, 128)) < N, (p + eye) * cols_ref[0] * scale, q + eye)
                root_ref[N:] = w * scale
            else:
                put(node_to, full_to, j, p, q, w, u)
        node, full = node_to, full_to


def react(jac_hbm, dens_hbm, src_hbm, tran_hbm, pat_hbm, out_ref, flux_ref, jac_ref, dens_ref, src_ref, tran_ref,
          pat_ref, sems):
    parts = [(slice(None), pl.ds(i * 1024, 1024)) for i in range(4)]
    pairs = [(dens_hbm, dens_ref), (pat_hbm, pat_ref)] + [(jac_hbm.at[part], jac_ref.at[part]) for part in parts]
    pairs += [(src_hbm, src_ref), (tran_hbm, tran_ref)]
    copies = [pltpu.make_async_copy(a, b, sems.at[i]) for i, (a, b) in enumerate(pairs)]
    for copy in copies:
        copy.start()
    half = lanes((128, N)) % 2 == lax.broadcasted_iota(jnp.int32, (128, N), 0) // N
    half = jnp.where(half, 1.0, 0.0).astype(bf16)
    copies[0].wait()
    copies[1].wait()
    u = dens_ref[...]
    u2 = jnp.concatenate([u, u], axis=1)
    lane8 = lanes((8, 128))
    pat = pat_ref[...].astype(f32)
    mask_rows = jnp.zeros((8, 128), f32)
    for t in range(8):
        mask_rows = jnp.where((lane8 % N) // 8 == t, pat[:, t : t + 1], mask_rows)
    lane = lanes((CELLS, N))
    acc = jnp.zeros((CELLS, N), f32)
    for m in range(32):
        if m % 8 == 0:
            copies[2 + m // 8].wait()
        y = jac_ref[:, m * 128 : (m + 1) * 128] * (u2 * mask_rows[m // 4 : m // 4 + 1])
        hi = y.astype(bf16)
        lo = (y - hi.astype(f32)).astype(bf16)
        z = jnp.dot(hi, half, preferred_element_type=f32) + jnp.dot(lo, half, preferred_element_type=f32)
        acc = jnp.where(lane // 2 == m, z, acc)
    copies[6].wait()
    copies[7].wait()
    tran = tran_ref[...]
    flux = tran * u
    flux_ref[...] = column(flux[CELLS - 1 : CELLS])
    row = lax.broadcasted_iota(jnp.int32, (CELLS, N), 0)
    lower = jnp.where(row == 0, 0.0, pltpu.roll(flux, 1, 0))
    upper = jnp.where(row == CELLS - 1, 0.0, pltpu.roll(u, CELLS - 1, 0))
    out_ref[...] = src_ref[...] - acc + lower + tran * upper


def upsweep(neigh_ref, part_ref, a_ref, b_ref, c_ref, even_ref, odd_ref, flux_ref, dens_ref, tran_ref, lat_ref, coup_ref, cols_ref,
            quad_ref, n1_ref, n2_ref, n3_ref, n4_ref, n5_ref, root_ref, pay_ref, pair_ref, v_ref, w_ref):
    me = lax.axis_index("lat")
    u = dens_ref[...]
    total = jnp.zeros((CELLS, N), f32)
    lines = [(0, u), (1, a_ref[0])] + [(2 + i, b_ref[i]) for i in range(2)]
    lines += [((6, 7, 4, 5)[i], c_ref[i]) for i in range(4)]
    for offset, value in lines:
        line = me ^ offset
        count = jnp.int32(0)
        for j in range(4):
            count = count + (neigh_ref[0, j] == line).astype(jnp.int32)
        total = total + count.astype(f32) * value
    row = lax.broadcasted_iota(jnp.int32, (CELLS, N), 0)
    r = part_ref[...] - lat_ref[...] * (4.0 * u - total)
    depth = lax.axis_index("depth")
    above = jnp.where(depth % 2 == 0, even_ref[0, 0:1], odd_ref[0, 0:1])
    above = jnp.where(depth == lax.axis_size("depth") - 1, 0.0, above)
    r = r + jnp.where(row == CELLS - 1, tran_ref[...] * above, 0.0)
    c = coup_ref[...]
    g = r / jnp.where(row == 0, c, pltpu.roll(c, 1, 0))
    x = []
    for i in range(4):
        rolled = g if i == 0 else pltpu.roll(g, CELLS - i, 0)
        x.append(jnp.concatenate([rolled, rolled], axis=0).T)
    lane2 = lanes((N, N)) % CELLS
    lane = lanes((N, CELLS))
    pair_v, pair_w = [], []
    for half in range(2):
        x0, x1 = x[2 * half], x[2 * half + 1]
        y = pair_rhs(x0, x1)
        v = jnp.zeros((N, N), f32)
        w = jnp.zeros((N, N), f32)
        for j in range(8):
            at = 2 * j + half
            here = lane2 == 4 * j
            v = jnp.where(here, jnp.dot(quad_ref[at, 0], y, preferred_element_type=f32), v)
            w = jnp.where(here, jnp.dot(quad_ref[at, 1], y, preferred_element_type=f32), w)
        v = v[:, :CELLS] + v[:, CELLS:] + x0[:, :CELLS] + x1[:, :CELLS]
        w = w[:, :CELLS] + w[:, CELLS:]
        pair_v.append(v)
        pair_w.append(w)
        pair_ref[half, :, 0:CELLS] = pair_v[half]
        pair_ref[2 + half, :, 0:CELLS] = w
    yv, yw = rhs(pair_v[0]), rhs(pair_w[1])
    v, w = pair_v[0] + pair_v[1], pair_w[0] + pair_w[1]
    dv = jnp.zeros((N, CELLS), f32)
    dw = jnp.zeros((N, CELLS), f32)
    for j in range(8):
        here = lane == 4 * j
        dv = jnp.where(here, dot(n1_ref[2 * j + 1, 0], yv), dv)
        dw = jnp.where(here, dot(n1_ref[2 * j, 1], yw) + dot(n2_ref[j, 3], yv), dw)
    v, w = v + dv, w + dw
    vs = [jnp.broadcast_to(v[:, 4 * j : 4 * j + 1], (N, 128)) for j in range(8)]
    ws = [jnp.broadcast_to(w[:, 4 * j : 4 * j + 1], (N, 128)) for j in range(8)]
    at = 0
    for count, ref, above in ((4, n2_ref, n3_ref), (2, n3_ref, n4_ref), (1, n4_ref, n5_ref)):
        next_v, next_w = [], []
        for j in range(count):
            v1, v2, w1, w2 = vs[2 * j], vs[2 * j + 1], ws[2 * j], ws[2 * j + 1]
            v_ref[at], w_ref[at] = v1, w2
            at += 1
            yv, yw = rhs(v1), rhs(w2)
            u_map = above[j, 3] if count > 1 else above[0]
            next_v.append(v1 + v2 + dot(ref[2 * j + 1, 0], yv))
            next_w.append(w1 + w2 + dot(ref[2 * j, 1], yw) + dot(u_map, yv))
        vs, ws = next_v, next_w
    lane = lanes((N, 128))
    pay_ref[:N] = root_ref[:N]
    tail = jnp.where(lane == N, vs[0] * cols_ref[0] + flux_ref[...], ws[0])
    pay_ref[N:] = jnp.where(lane < N, root_ref[N:], tail)


def prepare(pair_ref, v_ref, w_ref, n1_ref, n2_ref, n3_ref, n4_ref, t_ref, add_v, add_a, add_x):
    lane = lanes((N, 128))
    part = lane % CELLS
    at, vec = 0, 0
    for level, size, ref in ((1, 8, n2_ref), (2, 16, n3_ref), (3, 32, n4_ref)):
        acc_v = jnp.zeros((N, 128), f32)
        acc_a = jnp.zeros((N, 128), f32)
        for j in range(CELLS // size):
            kw = ref[2 * j + 1, 2]
            wide = kw.astype(f32)
            t_ref[at] = pack(wide + roll(wide, N) + mm(kw, ref[2 * j, 0]))
            at += 1
            here = part // size == j
            acc_v = jnp.where(here, v_ref[vec], acc_v)
            acc_a = jnp.where(here, w_ref[vec] + dot(kw, rhs(v_ref[vec])), acc_a)
            vec += 1
        add_v[level], add_a[level] = acc_v, acc_a

    def repeat(x):
        x = x + roll(x, CELLS)
        return x + roll(x, 2 * CELLS)

    first = jnp.logical_and(lane % 4 == 0, lane < CELLS)
    v0, v1, w0, w1 = [jnp.where(first, pair_ref[i], 0.0) for i in range(4)]
    y = rhs(v0)
    acc_a = jnp.zeros((N, 128), f32)
    for j in range(8):
        kw = n1_ref[2 * j + 1, 2]
        wide = kw.astype(f32)
        t_ref[at] = pack(wide + roll(wide, N) + mm(kw, n1_ref[2 * j, 0]))
        at += 1
        acc_a = jnp.where(lane == 4 * j, dot(kw, y), acc_a)
    acc_a = acc_a + w1
    spread_v = v0 + roll(v0, 1)
    spread_a = acc_a + roll(acc_a, 1)
    add_v[0] = repeat(spread_v + roll(spread_v, 2))
    add_a[0] = repeat(spread_a + roll(spread_a, 2))
    add_x[...] = repeat(w0 + roll(w1, 2) + roll(v0, 1) + roll(v1, 3))


def prepare_last(own_ref, fun_ref, maps_ref, vecs_ref, own_rhs):
    is_low = lax.axis_index("depth") < 2 * ZS
    f, hh, k, g, e = unpack(fun_ref[...])
    maps_ref[0], maps_ref[1] = pack(f), pack(jnp.where(is_low, hh, k))
    vecs_ref[0], vecs_ref[1] = g, e
    v = jnp.broadcast_to(own_ref[:, N : N + 1], (N, 128))
    hi = v.astype(bf16)
    lo = (v - hi.astype(f32)).astype(bf16)
    zero = jnp.zeros((N, 128), bf16)
    own_rhs[0] = jnp.concatenate([hi, zero, hi, zero], axis=0)
    own_rhs[1] = jnp.concatenate([lo, zero, lo, zero], axis=0)


def unpack(b):
    low = lanes((N, 128)) < N
    b1, b2 = b[:N], b[N:]
    r1, r2 = roll(b1, N), roll(b2, N)
    x = jnp.where(low, b1, r1)
    y = jnp.where(low, r1, b1)
    z = jnp.where(low, b2, r2)
    g = jnp.broadcast_to(b2[:, N : N + 1], (N, 128))
    h = jnp.broadcast_to(b2[:, N + 1 : N + 2], (N, 128))
    return x, y, z, g, h


def join(one, two, last=False):
    p1, q1, w1, v1, h1 = one
    p2, q2, w2, v2, h2 = two
    kq1, kp2, kw2 = pack(q1), pack(p2), pack(w2)
    yp1, yv1 = rhs(p1), rhs(v1)
    t = dot(kw2, yp1)
    th = h2 + dot(kw2, yv1)
    v = v2 + dot(kp2, yv1)
    yt, yth = rhs(t), rhs(th)
    w = w1 + dot(kq1, yt)
    h = h1 + dot(kq1, yth)
    yq2 = rhs(q2)
    p, q = (None, None) if last else (dot(kp2, yp1), dot(kq1, yq2))
    return (p, q, w, v, h), (t, th, yp1, yv1, yq2, yt, yth)


def track_first(is_low, one, two, extra):
    eye = eye2()
    t, th = extra[:2]
    return (
        jnp.where(is_low, eye, one[0]),
        jnp.where(is_low, two[1], eye),
        jnp.where(is_low, t, 0.0),
        jnp.where(is_low, 0.0, one[3]),
        jnp.where(is_low, th, 0.0),
    )


def track(is_low, fun, extra):
    f, hh, k, g, e = fun
    t, th, yp1, yv1, yq2, yt, yth = extra
    x1 = pack(jnp.where(is_low, hh, f))
    x2 = pack(jnp.where(is_low, hh, k))
    prod1 = dot(x1, jnp.where(is_low, yq2, yp1))
    prod2 = dot(x2, jnp.where(is_low, yt, yp1))
    vec1 = dot(x1, yv1)
    vec2 = dot(x2, jnp.where(is_low, yth, yv1))
    return (
        jnp.where(is_low, f, prod1),
        jnp.where(is_low, prod1, hh),
        jnp.where(is_low, k + prod2, prod2),
        jnp.where(is_low, g, g + vec1),
        e + vec2,
    )


def put_map(ref, p, q, w, v, h, last=False):
    lane = lanes((N, 128))
    low = lane < N
    tail = jnp.where(low, w, jnp.where(lane == N, v, h))
    if last:
        ref[...] = tail
    else:
        ref[:N] = jnp.where(low, p, q)
        ref[N:] = tail


def combine_four(last, *refs):
    if last:
        own_ref, x1_ref, x2_ref, x3_ref, fun_ref, out_ref, fun_out, slots = refs
    else:
        own_ref, x1_ref, x2_ref, x3_ref, out_ref, fun_out, slots = refs
    depth = lax.axis_index("depth")
    at = ((depth // ZS) % 2) * 2 + (depth % ZS) // 4 if last else depth % 4
    slots[at] = own_ref[...]
    slots[at ^ 1] = x1_ref[...]
    slots[at ^ 2] = x2_ref[...]
    slots[at ^ 3] = x3_ref[...]
    maps = [unpack(slots[i]) for i in range(4)]
    lower, extra_lower = join(maps[0], maps[1])
    upper, extra_upper = join(maps[2], maps[3])
    in_lower = at < 2
    mine = lambda x, y: [jnp.where(in_lower, a, b) for a, b in zip(x, y)]
    if last:
        fun = track(at % 2 == 0, unpack(fun_ref[...]), mine(extra_lower, extra_upper))
    else:
        fun = track_first(
            at % 2 == 0, mine(maps[0], maps[2]), mine(maps[1], maps[3]), mine(extra_lower[:2], extra_upper[:2])
        )
    total, extra = join(lower, upper, last)
    put_map(out_ref, *total, last=last)
    put_map(fun_out, *track(in_lower, fun, extra))


def downsweep(other_ref, maps_ref, vecs_ref, own_rhs, cols_ref, add_v, add_a, add_x, quad_ref, n1_ref, n2_ref, n3_ref,
              n4_ref, t_ref, out_ref):
    is_low = lax.axis_index("depth") < 2 * ZS
    g, e = vecs_ref[0], vecs_ref[1]
    other = other_ref[...]
    hi = other.astype(bf16)
    wide = jnp.concatenate([hi, (other - hi.astype(f32)).astype(bf16)], axis=1)
    v_other = jnp.broadcast_to(other[:, N : N + 1], (N, 128))
    w_other = jnp.broadcast_to(other[:, N + 1 : N + 2], (N, 128))
    t = w_other + jnp.dot(wide, own_rhs[0], preferred_element_type=f32)
    t = t + jnp.dot(wide, own_rhs[1], preferred_element_type=f32)
    up = g + dot(maps_ref[0], rhs(v_other))
    aa = e + dot(maps_ref[1], rhs(jnp.where(is_low, t, v_other)))
    ss = jnp.where(is_low, g, up) * cols_ref[1]
    lane = lanes((N, 128)) % CELLS
    for level, size, ref, base in ((3, 32, n4_ref, 6), (2, 16, n3_ref, 4), (1, 8, n2_ref, 0), (0, 4, n1_ref, 7)):
        ys, ya = rhs(ss), rhs(aa)
        ds = jnp.zeros((N, 128), f32)
        da = jnp.zeros((N, 128), f32)
        for j in range(CELLS // size):
            here = lane // size == j
            ds = jnp.where(here, dot(ref[2 * j, 0], ys), ds)
            da = jnp.where(here, dot(ref[2 * j + 1, 1], ya) + dot(t_ref[base + j], ys), da)
        upper = lane % size >= size // 2
        new_s = ss + add_v[level] + ds
        new_a = aa + add_a[level] + da
        ss = jnp.where(upper, new_s, ss)
        aa = jnp.where(upper, aa, new_a)
    y = pair_rhs(ss, aa)
    x = jnp.zeros((N, 128), f32)
    for j in range(CELLS // 2):
        x = jnp.where(lane == 2 * j, jnp.dot(quad_ref[j, 2], y, preferred_element_type=f32), x)
        x = jnp.where(lane == 2 * j + 1, jnp.dot(quad_ref[j, 3], y, preferred_element_type=f32), x)
    x = x + roll(x, CELLS) + (aa + add_x[...] + jnp.where(lane % 2 == 1, ss, 0.0))
    out_ref[...] = x.T[:CELLS]


def sds(*shape, dtype=f32):
    return jax.ShapeDtypeStruct(shape, dtype)


def call(body, outs, *args, scratch=(), smem=0, hbm=0, flops=0, name=None):
    args = [pltpu.with_memory_space_constraint(x, pltpu.HBM) if smem <= i < smem + hbm else x for i, x in enumerate(args)]
    spaces = [pltpu.SMEM] * smem + [pltpu.HBM] * hbm + [pltpu.VMEM] * (len(args) - smem - hbm)
    return pl.pallas_call(
        body,
        out_shape=outs,
        in_specs=[pl.BlockSpec(memory_space=space) for space in spaces],
        out_specs=jax.tree.map(lambda _: pl.BlockSpec(memory_space=pltpu.VMEM), outs),
        scratch_shapes=scratch,
        cost_estimate=pl.CostEstimate(flops=flops, bytes_accessed=1 << 16, transcendentals=0),
        name=name,
        compiler_params=pltpu.CompilerParams(vmem_limit_bytes=VLIM),
    )(*args)


def node(count):
    return sds(count, 4, N, 128, dtype=bf16)


def on_device(densities, source, jacobian, pattern, transport, lateral, neighbours, factor, coupling):
    line_count, cell_count, species = densities.shape
    u = densities.reshape(CELLS, N)
    src = source.reshape(CELLS, N)
    tran = transport.reshape(CELLS, N)
    lat = lateral.reshape(CELLS, N)
    coup = coupling.reshape(CELLS, N)
    jac = jacobian.reshape(CELLS, N * N)
    fac = factor.reshape(4, 8, 32, 128).transpose(0, 2, 1, 3).reshape(1024, 128)

    def xor_lat(value, bits):
        return lax.ppermute(value, "lat", [(i, i ^ bits) for i in range(8)])

    def xor_depth(value, bits):
        return lax.ppermute(value, "depth", [(i, i ^ bits) for i in range(32)])

    line_a = xor_lat(densities, 1)
    part, flux = call(
        react, (sds(CELLS, N), sds(N, 128)), jac, u, src, tran, pattern, hbm=5, flops=1 << 30, name="react",
        scratch=[pltpu.VMEM((CELLS, N * N), f32)] + [pltpu.VMEM((CELLS, N), f32)] * 3
        + [pltpu.VMEM((8, 8), jnp.int32), pltpu.SemaphoreType.DMA((8,))],
    )
    line_b = xor_lat(jnp.concatenate([densities, line_a], axis=0), 2)
    quad, n1, full, cols = call(
        tree_leaves,
        (sds(16, 4, N, 256, dtype=bf16), sds(16, 3, N, 128, dtype=bf16), sds(16, 3, N, 128), sds(2, N, 128)),
        fac, coup, part, scratch=[pltpu.VMEM((2, N, 128), f32)], flops=2 << 30, name="tree_leaves",
    )
    top_even = xor_depth(lax.optimization_barrier((densities, cols))[0], 1)
    top_odd = lax.ppermute(
        lax.optimization_barrier((densities, line_b))[0], ("depth", "lat"),
        [(8 * i + l, 8 * (i + 1 if i % 2 else i - 1) + l if 0 < i < 31 else 8 * i + (l ^ 1))
         for i in range(32) for l in range(8)],
    )
    line_c = xor_lat(jnp.concatenate([densities, line_a, line_b], axis=0), 6)
    n2, n3, n4, n5, root = call(
        tree_upper,
        (node(8), node(4), node(2), sds(1, N, 128, dtype=bf16), sds(128, 128)),
        n1, full, coup, cols, part, scratch=[pltpu.VMEM((8, 3, N, 128), f32), pltpu.VMEM((4, 3, N, 128), f32)],
        flops=2 << 30, name="tree_upper",
    )
    pay, pair, vs, ws = call(
        upsweep, (sds(128, 128), sds(4, N, 128), sds(7, N, 128), sds(7, N, 128)),
        neighbours, part, line_a, line_b, line_c, top_even, top_odd, flux, u, tran, lat, coup, cols, quad, n1, n2, n3, n4, n5, root,
        smem=1, flops=1 << 25, name="upsweep",
    )
    others = [xor_depth(pay, bits) for bits in (1, 2, 3)]
    tees, add_v, add_a, add_x = call(
        prepare, (sds(15, N, 128, dtype=bf16), sds(4, N, 128), sds(4, N, 128), sds(N, 128)),
        pair, vs, ws, n1, n2, n3, n4, flops=1 << 30, name="prepare",
    )
    slots = [pltpu.VMEM((4, 128, 128), f32)]
    pay, fun = call(
        lambda *refs: combine_four(False, *refs), (sds(128, 128), sds(128, 128)), pay, *others, scratch=slots,
        flops=1 << 24, name="combine_low",
    )
    others = [xor_depth(pay, bits) for bits in (7, 8, 15)]
    pay, fun = call(
        lambda *refs: combine_four(True, *refs), (sds(N, 128), sds(128, 128)), pay, *others, fun, scratch=slots,
        flops=1 << 24, name="combine_high",
    )
    other = xor_depth(pay, 24)
    maps, vecs, own_rhs = call(
        prepare_last,
        (sds(2, N, 128, dtype=bf16), sds(2, N, 128), sds(2, 256, 128, dtype=bf16)),
        pay, fun, flops=1 << 30, name="prepare_last",
    )
    out = call(
        downsweep, sds(CELLS, N), other, maps, vecs, own_rhs, cols, add_v, add_a, add_x, quad, n1, n2, n3, n4, tees,
        flops=1 << 25, name="downsweep",
    )
    return out.reshape(line_count, cell_count, species)


def solution(mesh):
    return jax.shard_map(
        on_device,
        mesh=mesh,
        in_specs=(
            P("lat", "depth", None),
            P("lat", "depth", None),
            P("lat", "depth", None),
            P(),
            P("lat", "depth", None),
            P("lat", "depth", None),
            P("lat", None),
            P("lat", "depth", None),
            P("lat", "depth", None),
        ),
        out_specs=P("lat", "depth", None),
        check_vma=False,
    )
```

```python
import jax
import jax.numpy as jnp
from jax import lax
from jax.experimental import pallas as pl
from jax.experimental.pallas import tpu as pltpu
from jax.sharding import PartitionSpec as P

f32 = jnp.float32
bf16 = jnp.bfloat16

CELLS = 32
N = 64
ZS = 8
VLIM = 16 << 20


def lanes(shape):
    return lax.broadcasted_iota(jnp.int32, shape, len(shape) - 1)


def roll(x, shift):
    shift = shift % x.shape[-1]
    return x if shift == 0 else pltpu.roll(x, shift, x.ndim - 1)


def pack(dup):
    hi = dup.astype(bf16).astype(f32)
    return jnp.where(lanes(dup.shape) < N, hi, dup - hi).astype(bf16)


def mm(a, b):
    r = jnp.dot(a, jnp.concatenate([b, b], axis=0), preferred_element_type=f32)
    return r + roll(r, N)


def rhs(x):
    hi = x.astype(bf16)
    lo = (x - hi.astype(f32)).astype(bf16)
    return jnp.concatenate([hi, hi, lo, lo], axis=0)


def dot(a, y):
    return jnp.dot(jnp.concatenate([a, a], axis=1), y, preferred_element_type=f32)


def column(row):
    return jnp.broadcast_to(row, (128, N)).T


def pair(a, b):
    low = lanes(a.shape) < N
    a_hi, b_hi = a.astype(bf16).astype(f32), b.astype(bf16).astype(f32)
    hi = jnp.where(low, a_hi, b_hi).astype(bf16)
    lo = jnp.where(low, a - a_hi, b - b_hi).astype(bf16)
    return jnp.concatenate([hi, lo], axis=1)


def pair_rhs(x, y):
    def split(z):
        hi = z.astype(bf16).astype(f32)
        return jnp.where(lanes(z.shape) % 64 < CELLS, hi, z - hi).astype(bf16)

    a, b = split(x), split(y)
    return jnp.concatenate([a, b, a, b], axis=0)


def eye2():
    return jnp.where(lanes((N, 128)) % N == lax.broadcasted_iota(jnp.int32, (N, 128), 0), 1.0, 0.0)


def put(node, full, j, p, q, w, u=None):
    node[j, 0], node[j, 1], node[j, 2] = pack(p), pack(q), pack(w)
    full[j, 0], full[j, 1], full[j, 2] = p, q, w
    if u is not None:
        node[j, 3] = pack(u)


def tree_leaves(fac_hbm, coup_hbm, quad_ref, n1_ref, full_ref, cols_ref, fac_ref, coup_ref, rows, sems):
    parts = [pl.ds(i * 256, 256) for i in range(4)]
    pairs = [(coup_hbm, coup_ref)] + [(fac_hbm.at[part], fac_ref.at[part]) for part in parts]
    copies = [pltpu.make_async_copy(a, b, sems.at[i]) for i, (a, b) in enumerate(pairs)]
    for copy in copies:
        copy.start()
    copies[0].wait()
    c = coup_ref[...]
    cols_ref[0] = column(c[CELLS - 1 : CELLS])
    cols_ref[1] = column(1.0 / c[0:1])
    c2 = jnp.concatenate([c, c], axis=1)
    low = lanes((CELLS, 128)) < N
    eye = eye2()

    def leaf(k):
        g, s = divmod(k, 8)
        x = fac_ref[pl.ds(g * 256 + s, 32, stride=8), :]
        y = roll(x, N)
        rows[k % 2, pl.ds(0, 32, stride=2), :] = jnp.where(low, x, y)
        rows[k % 2, pl.ds(1, 32, stride=2), :] = jnp.where(low, y, x)
        a = rows[k % 2]
        before = max(k - 1, 0)
        return a * c2[before : before + 1] - eye, a * c2[k : k + 1] - eye

    for j in range(CELLS // 2):
        if j % 4 == 0:
            copies[1 + j // 4].wait()
        p1, q1 = leaf(2 * j)
        p2, q2 = leaf(2 * j + 1)
        kq1 = pack(q1)
        p = p1 + p2 + dot(pack(p2), rhs(p1))
        q = q1 + q2 + dot(kq1, rhs(q2))
        u = eye + q1 + p2 + dot(kq1, rhs(p2))
        w = (eye + eye) + p1 + q1 + p + dot(kq1, rhs(p))
        put(n1_ref, full_ref, j, p, q, w)
        quad_ref[j, 0] = pair(p, p2)
        quad_ref[j, 1] = pair(w, u)
        quad_ref[j, 2] = pair(w, q)
        quad_ref[j, 3] = pair(p, q2)


def tree_upper(n1_ref, full_ref, coup_ref, cols_ref, after_ref, n2_ref, n3_ref, n4_ref, n5_ref, root_ref, fa, fb):
    del after_ref
    node, full = n1_ref, full_ref
    for count, node_to, full_to in ((8, n2_ref, fa), (4, n3_ref, fb), (2, n4_ref, fa), (1, None, None)):
        for j in range(count):
            one, two = 2 * j, 2 * j + 1
            kq1, yp1 = node[one, 1], rhs(full[one, 0])
            u = full[two, 2] + dot(kq1, rhs(full[two, 2]))
            p = full[one, 0] + full[two, 0] + dot(node[two, 0], yp1)
            q = full[one, 1] + full[two, 1] + dot(kq1, rhs(full[two, 1]))
            ku = pack(u)
            w = full[one, 2] + u + dot(ku, yp1)
            if node_to is None:
                eye = eye2()
                n5_ref[0] = ku
                first = coup_ref[0:1]
                scale = 1.0 / jnp.concatenate([first, first], axis=1)
                root_ref[:N] = jnp.where(lanes((N, 128)) < N, (p + eye) * cols_ref[0] * scale, q + eye)
                root_ref[N:] = w * scale
            else:
                put(node_to, full_to, j, p, q, w, u)
        node, full = node_to, full_to


def react(jac_ref, dens_ref, src_ref, tran_ref, pat_ref, after_ref, out_ref, flux_ref):
    del after_ref
    half = lanes((128, N)) % 2 == lax.broadcasted_iota(jnp.int32, (128, N), 0) // N
    half = jnp.where(half, 1.0, 0.0).astype(bf16)
    u = dens_ref[...]
    u2 = jnp.concatenate([u, u], axis=1)
    lane8 = lanes((8, 128))
    pat = pat_ref[...].astype(f32)
    mask_rows = jnp.zeros((8, 128), f32)
    for t in range(8):
        mask_rows = jnp.where((lane8 % N) // 8 == t, pat[:, t : t + 1], mask_rows)
    lane = lanes((CELLS, N))
    acc = jnp.zeros((CELLS, N), f32)
    for m in range(32):
        y = jac_ref[:, m * 128 : (m + 1) * 128] * (u2 * mask_rows[m // 4 : m // 4 + 1])
        hi = y.astype(bf16)
        lo = (y - hi.astype(f32)).astype(bf16)
        z = jnp.dot(hi, half, preferred_element_type=f32) + jnp.dot(lo, half, preferred_element_type=f32)
        acc = jnp.where(lane // 2 == m, z, acc)
    tran = tran_ref[...]
    flux = tran * u
    flux_ref[...] = column(flux[CELLS - 1 : CELLS])
    row = lax.broadcasted_iota(jnp.int32, (CELLS, N), 0)
    lower = jnp.where(row == 0, 0.0, pltpu.roll(flux, 1, 0))
    upper = jnp.where(row == CELLS - 1, 0.0, pltpu.roll(u, CELLS - 1, 0))
    out_ref[...] = src_ref[...] - acc + lower + tran * upper


def upsweep(neigh_ref, part_ref, a_ref, b_ref, c_ref, even_ref, odd_ref, flux_ref, dens_ref, tran_ref, lat_ref, coup_ref, cols_ref,
            quad_ref, n1_ref, n2_ref, n3_ref, n4_ref, n5_ref, root_ref, pay_ref, pair_ref, v_ref, w_ref):
    me = lax.axis_index("lat")
    u = dens_ref[...]
    total = jnp.zeros((CELLS, N), f32)
    lines = [(0, u), (1, a_ref[0])] + [(2 + i, b_ref[i]) for i in range(2)]
    lines += [((6, 7, 4, 5)[i], c_ref[i]) for i in range(4)]
    for offset, value in lines:
        line = me ^ offset
        count = jnp.int32(0)
        for j in range(4):
            count = count + (neigh_ref[0, j] == line).astype(jnp.int32)
        total = total + count.astype(f32) * value
    row = lax.broadcasted_iota(jnp.int32, (CELLS, N), 0)
    r = part_ref[...] - lat_ref[...] * (4.0 * u - total)
    depth = lax.axis_index("depth")
    above = jnp.where(depth % 2 == 0, even_ref[0, 0:1], odd_ref[0, 0:1])
    above = jnp.where(depth == lax.axis_size("depth") - 1, 0.0, above)
    r = r + jnp.where(row == CELLS - 1, tran_ref[...] * above, 0.0)
    c = coup_ref[...]
    g = r / jnp.where(row == 0, c, pltpu.roll(c, 1, 0))
    x = []
    for i in range(4):
        rolled = g if i == 0 else pltpu.roll(g, CELLS - i, 0)
        x.append(jnp.concatenate([rolled, rolled], axis=0).T)
    lane2 = lanes((N, N)) % CELLS
    lane = lanes((N, CELLS))
    pair_v, pair_w = [], []
    for half in range(2):
        x0, x1 = x[2 * half], x[2 * half + 1]
        y = pair_rhs(x0, x1)
        v = jnp.zeros((N, N), f32)
        w = jnp.zeros((N, N), f32)
        for j in range(8):
            at = 2 * j + half
            here = lane2 == 4 * j
            v = jnp.where(here, jnp.dot(quad_ref[at, 0], y, preferred_element_type=f32), v)
            w = jnp.where(here, jnp.dot(quad_ref[at, 1], y, preferred_element_type=f32), w)
        v = v[:, :CELLS] + v[:, CELLS:] + x0[:, :CELLS] + x1[:, :CELLS]
        w = w[:, :CELLS] + w[:, CELLS:]
        pair_v.append(v)
        pair_w.append(w)
        pair_ref[half, :, 0:CELLS] = pair_v[half]
        pair_ref[2 + half, :, 0:CELLS] = w
    yv, yw = rhs(pair_v[0]), rhs(pair_w[1])
    v, w = pair_v[0] + pair_v[1], pair_w[0] + pair_w[1]
    dv = jnp.zeros((N, CELLS), f32)
    dw = jnp.zeros((N, CELLS), f32)
    for j in range(8):
        here = lane == 4 * j
        dv = jnp.where(here, dot(n1_ref[2 * j + 1, 0], yv), dv)
        dw = jnp.where(here, dot(n1_ref[2 * j, 1], yw) + dot(n2_ref[j, 3], yv), dw)
    v, w = v + dv, w + dw
    vs = [jnp.broadcast_to(v[:, 4 * j : 4 * j + 1], (N, 128)) for j in range(8)]
    ws = [jnp.broadcast_to(w[:, 4 * j : 4 * j + 1], (N, 128)) for j in range(8)]
    at = 0
    for count, ref, above in ((4, n2_ref, n3_ref), (2, n3_ref, n4_ref), (1, n4_ref, n5_ref)):
        next_v, next_w = [], []
        for j in range(count):
            v1, v2, w1, w2 = vs[2 * j], vs[2 * j + 1], ws[2 * j], ws[2 * j + 1]
            v_ref[at], w_ref[at] = v1, w2
            at += 1
            yv, yw = rhs(v1), rhs(w2)
            u_map = above[j, 3] if count > 1 else above[0]
            next_v.append(v1 + v2 + dot(ref[2 * j + 1, 0], yv))
            next_w.append(w1 + w2 + dot(ref[2 * j, 1], yw) + dot(u_map, yv))
        vs, ws = next_v, next_w
    lane = lanes((N, 128))
    pay_ref[:N] = root_ref[:N]
    tail = jnp.where(lane == N, vs[0] * cols_ref[0] + flux_ref[...], ws[0])
    pay_ref[N:] = jnp.where(lane < N, root_ref[N:], tail)


def prepare(pair_ref, v_ref, w_ref, n1_ref, n2_ref, n3_ref, n4_ref, t_ref, add_v, add_a, add_x):
    lane = lanes((N, 128))
    part = lane % CELLS
    at, vec = 0, 0
    for level, size, ref in ((1, 8, n2_ref), (2, 16, n3_ref), (3, 32, n4_ref)):
        acc_v = jnp.zeros((N, 128), f32)
        acc_a = jnp.zeros((N, 128), f32)
        for j in range(CELLS // size):
            kw = ref[2 * j + 1, 2]
            wide = kw.astype(f32)
            t_ref[at] = pack(wide + roll(wide, N) + mm(kw, ref[2 * j, 0]))
            at += 1
            here = part // size == j
            acc_v = jnp.where(here, v_ref[vec], acc_v)
            acc_a = jnp.where(here, w_ref[vec] + dot(kw, rhs(v_ref[vec])), acc_a)
            vec += 1
        add_v[level], add_a[level] = acc_v, acc_a

    def repeat(x):
        x = x + roll(x, CELLS)
        return x + roll(x, 2 * CELLS)

    first = jnp.logical_and(lane % 4 == 0, lane < CELLS)
    v0, v1, w0, w1 = [jnp.where(first, pair_ref[i], 0.0) for i in range(4)]
    y = rhs(v0)
    acc_a = jnp.zeros((N, 128), f32)
    for j in range(8):
        kw = n1_ref[2 * j + 1, 2]
        wide = kw.astype(f32)
        t_ref[at] = pack(wide + roll(wide, N) + mm(kw, n1_ref[2 * j, 0]))
        at += 1
        acc_a = jnp.where(lane == 4 * j, dot(kw, y), acc_a)
    acc_a = acc_a + w1
    spread_v = v0 + roll(v0, 1)
    spread_a = acc_a + roll(acc_a, 1)
    add_v[0] = repeat(spread_v + roll(spread_v, 2))
    add_a[0] = repeat(spread_a + roll(spread_a, 2))
    add_x[...] = repeat(w0 + roll(w1, 2) + roll(v0, 1) + roll(v1, 3))


def unpack(b):
    low = lanes((N, 128)) < N
    b1, b2 = b[:N], b[N:]
    r1, r2 = roll(b1, N), roll(b2, N)
    x = jnp.where(low, b1, r1)
    y = jnp.where(low, r1, b1)
    z = jnp.where(low, b2, r2)
    g = jnp.broadcast_to(b2[:, N : N + 1], (N, 128))
    h = jnp.broadcast_to(b2[:, N + 1 : N + 2], (N, 128))
    return x, y, z, g, h


def join(one, two, last=False):
    p1, q1, w1, v1, h1 = one
    p2, q2, w2, v2, h2 = two
    kq1, kp2, kw2 = pack(q1), pack(p2), pack(w2)
    yp1, yv1 = rhs(p1), rhs(v1)
    t = dot(kw2, yp1)
    th = h2 + dot(kw2, yv1)
    v = v2 + dot(kp2, yv1)
    yt, yth = rhs(t), rhs(th)
    w = w1 + dot(kq1, yt)
    h = h1 + dot(kq1, yth)
    yq2 = rhs(q2)
    p, q = (None, None) if last else (dot(kp2, yp1), dot(kq1, yq2))
    return (p, q, w, v, h), (t, th, yp1, yv1, yq2, yt, yth)


def track_first(is_low, one, two, extra):
    eye = eye2()
    t, th = extra[:2]
    return (
        jnp.where(is_low, eye, one[0]),
        jnp.where(is_low, two[1], eye),
        jnp.where(is_low, t, 0.0),
        jnp.where(is_low, 0.0, one[3]),
        jnp.where(is_low, th, 0.0),
    )


def track(is_low, fun, extra):
    f, hh, k, g, e = fun
    t, th, yp1, yv1, yq2, yt, yth = extra
    x1 = pack(jnp.where(is_low, hh, f))
    x2 = pack(jnp.where(is_low, hh, k))
    prod1 = dot(x1, jnp.where(is_low, yq2, yp1))
    prod2 = dot(x2, jnp.where(is_low, yt, yp1))
    vec1 = dot(x1, yv1)
    vec2 = dot(x2, jnp.where(is_low, yth, yv1))
    return (
        jnp.where(is_low, f, prod1),
        jnp.where(is_low, prod1, hh),
        jnp.where(is_low, k + prod2, prod2),
        jnp.where(is_low, g, g + vec1),
        e + vec2,
    )


def put_map(ref, p, q, w, v, h, last=False):
    lane = lanes((N, 128))
    low = lane < N
    tail = jnp.where(low, w, jnp.where(lane == N, v, h))
    if last:
        ref[...] = tail
    else:
        ref[:N] = jnp.where(low, p, q)
        ref[N:] = tail


def fill(slots, at, refs):
    for bits, ref in enumerate(refs):
        slots[at ^ bits] = ref[...]
    return [unpack(slots[i]) for i in range(4)]


def combine_four(own_ref, x1_ref, x2_ref, x3_ref, out_ref, fun_out, slots):
    at = lax.axis_index("depth") % 4
    maps = fill(slots, at, (own_ref, x1_ref, x2_ref, x3_ref))
    lower, extra_lower = join(maps[0], maps[1])
    upper, extra_upper = join(maps[2], maps[3])
    in_lower = at < 2
    mine = lambda x, y: [jnp.where(in_lower, a, b) for a, b in zip(x, y)]
    fun = track_first(
        at % 2 == 0, mine(maps[0], maps[2]), mine(maps[1], maps[3]), mine(extra_lower[:2], extra_upper[:2])
    )
    total, extra = join(lower, upper)
    put_map(out_ref, *total)
    put_map(fun_out, *track(in_lower, fun, extra))


def combine_two(own_ref, other_ref, fun_ref, out_ref, fun_out):
    is_low = lax.axis_index("depth") % ZS < 4
    own, other = own_ref[...], other_ref[...]
    total, extra = join(unpack(jnp.where(is_low, own, other)), unpack(jnp.where(is_low, other, own)))
    put_map(out_ref, *total)
    for i, value in enumerate(track(is_low, unpack(fun_ref[...]), extra)):
        fun_out[i] = value


def downsweep(own_ref, y1_ref, y2_ref, y3_ref, fun_ref, cols_ref, add_v, add_a, add_x, quad_ref, n1_ref, n2_ref, n3_ref,
              n4_ref, t_ref, out_ref, slots):
    at = lax.axis_index("depth") // ZS
    maps = fill(slots, at, (own_ref, y1_ref, y2_ref, y3_ref))
    lower, extra_lower = join(maps[0], maps[1], last=True)
    upper, extra_upper = join(maps[2], maps[3], last=True)
    is_low = at < 2
    extra = [jnp.where(is_low, a, b) for a, b in zip(extra_lower, extra_upper)]
    f, hh, k, g, e = track(at % 2 == 0, [fun_ref[i] for i in range(5)], extra)
    yv = rhs(lower[3])
    t = upper[4] + dot(pack(upper[2]), yv)
    up = g + dot(pack(f), yv)
    aa = e + dot(pack(jnp.where(is_low, hh, k)), jnp.where(is_low, rhs(t), yv))
    ss = jnp.where(is_low, g, up) * cols_ref[1]
    lane = lanes((N, 128)) % CELLS
    for level, size, ref, base in ((3, 32, n4_ref, 6), (2, 16, n3_ref, 4), (1, 8, n2_ref, 0), (0, 4, n1_ref, 7)):
        ys, ya = rhs(ss), rhs(aa)
        ds = jnp.zeros((N, 128), f32)
        da = jnp.zeros((N, 128), f32)
        for j in range(CELLS // size):
            here = lane // size == j
            ds = jnp.where(here, dot(ref[2 * j, 0], ys), ds)
            da = jnp.where(here, dot(ref[2 * j + 1, 1], ya) + dot(t_ref[base + j], ys), da)
        upper = lane % size >= size // 2
        new_s = ss + add_v[level] + ds
        new_a = aa + add_a[level] + da
        ss = jnp.where(upper, new_s, ss)
        aa = jnp.where(upper, aa, new_a)
    y = pair_rhs(ss, aa)
    x = jnp.zeros((N, 128), f32)
    for j in range(CELLS // 2):
        x = jnp.where(lane == 2 * j, jnp.dot(quad_ref[j, 2], y, preferred_element_type=f32), x)
        x = jnp.where(lane == 2 * j + 1, jnp.dot(quad_ref[j, 3], y, preferred_element_type=f32), x)
    x = x + roll(x, CELLS) + (aa + add_x[...] + jnp.where(lane % 2 == 1, ss, 0.0))
    out_ref[...] = x.T[:CELLS]


def sds(*shape, dtype=f32):
    return jax.ShapeDtypeStruct(shape, dtype)


def call(body, outs, *args, scratch=(), smem=0, hbm=0, flops=0, name=None):
    args = [pltpu.with_memory_space_constraint(x, pltpu.HBM) if smem <= i < smem + hbm else x for i, x in enumerate(args)]
    spaces = [pltpu.SMEM] * smem + [pltpu.HBM] * hbm + [pltpu.VMEM] * (len(args) - smem - hbm)
    return pl.pallas_call(
        body,
        out_shape=outs,
        in_specs=[pl.BlockSpec(memory_space=space) for space in spaces],
        out_specs=jax.tree.map(lambda _: pl.BlockSpec(memory_space=pltpu.VMEM), outs),
        scratch_shapes=scratch,
        cost_estimate=pl.CostEstimate(flops=flops, bytes_accessed=1 << 16, transcendentals=0),
        name=name,
        compiler_params=pltpu.CompilerParams(vmem_limit_bytes=VLIM),
    )(*args)


def node(count):
    return sds(count, 4, N, 128, dtype=bf16)


def on_device(densities, source, jacobian, pattern, transport, lateral, neighbours, factor, coupling):
    line_count, cell_count, species = densities.shape
    u = densities.reshape(CELLS, N)
    src = source.reshape(CELLS, N)
    tran = transport.reshape(CELLS, N)
    lat = lateral.reshape(CELLS, N)
    coup = coupling.reshape(CELLS, N)
    jac = jacobian.reshape(CELLS, N * N)
    fac = factor.reshape(4, 8, 32, 128).transpose(0, 2, 1, 3).reshape(1024, 128)

    def xor_lat(value, bits):
        return lax.ppermute(value, "lat", [(i, i ^ bits) for i in range(8)])

    def xor_depth(value, bits):
        return lax.ppermute(value, "depth", [(i, i ^ bits) for i in range(32)])

    line_a = xor_lat(densities, 1)
    quad, n1, full, cols = call(
        tree_leaves,
        (sds(16, 4, N, 256, dtype=bf16), sds(16, 3, N, 128, dtype=bf16), sds(16, 3, N, 128), sds(2, N, 128)),
        fac, coup, hbm=2, flops=1 << 30, name="tree_leaves",
        scratch=[pltpu.VMEM((1024, 128), f32), pltpu.VMEM((CELLS, N), f32), pltpu.VMEM((2, N, 128), f32),
                 pltpu.SemaphoreType.DMA((5,))],
    )
    line_b = xor_lat(jnp.concatenate([densities, line_a], axis=0), 2)
    part, flux = call(
        react, (sds(CELLS, N), sds(N, 128)), jac, u, src, tran, pattern, cols, flops=1 << 30, name="react",
    )
    top_even = xor_depth(lax.optimization_barrier((densities, part))[0], 1)
    top_odd = lax.ppermute(
        lax.optimization_barrier((densities, line_b))[0], ("depth", "lat"),
        [(8 * i + l, 8 * (i + 1 if i % 2 else i - 1) + l if 0 < i < 31 else 8 * i + (l ^ 1))
         for i in range(32) for l in range(8)],
    )
    line_c = xor_lat(jnp.concatenate([densities, line_a, line_b], axis=0), 6)
    n2, n3, n4, n5, root = call(
        tree_upper,
        (node(8), node(4), node(2), sds(1, N, 128, dtype=bf16), sds(128, 128)),
        n1, full, coup, cols, part, scratch=[pltpu.VMEM((8, 3, N, 128), f32), pltpu.VMEM((4, 3, N, 128), f32)],
        flops=2 << 30, name="tree_upper",
    )
    pay, pair, vs, ws = call(
        upsweep, (sds(128, 128), sds(4, N, 128), sds(7, N, 128), sds(7, N, 128)),
        neighbours, part, line_a, line_b, line_c, top_even, top_odd, flux, u, tran, lat, coup, cols, quad, n1, n2, n3, n4, n5, root,
        smem=1, flops=1 << 25, name="upsweep",
    )
    others = [xor_depth(pay, bits) for bits in (1, 2, 3)]
    slots = [pltpu.VMEM((4, 128, 128), f32)]
    pay, fun = call(
        combine_four, (sds(128, 128), sds(128, 128)), pay, *others, scratch=slots, flops=1 << 24, name="combine_four",
    )
    other = xor_depth(pay, 7)
    pay, fun = call(
        combine_two, (sds(128, 128), sds(5, N, 128)), pay, other, fun, flops=1 << 24, name="combine_two",
    )
    others = [xor_depth(pay, bits) for bits in (8, 16, 24)]
    tees, add_v, add_a, add_x = call(
        prepare, (sds(15, N, 128, dtype=bf16), sds(4, N, 128), sds(4, N, 128), sds(N, 128)),
        pair, vs, ws, n1, n2, n3, n4, flops=1 << 30, name="prepare",
    )
    out = call(
        downsweep, sds(CELLS, N), pay, *others, fun, cols, add_v, add_a, add_x, quad, n1, n2, n3, n4, tees,
        scratch=slots, flops=1 << 25, name="downsweep",
    )
    return out.reshape(line_count, cell_count, species)


def solution(mesh):
    return jax.shard_map(
        on_device,
        mesh=mesh,
        in_specs=(
            P("lat", "depth", None),
            P("lat", "depth", None),
            P("lat", "depth", None),
            P(),
            P("lat", "depth", None),
            P("lat", "depth", None),
            P("lat", None),
            P("lat", "depth", None),
            P("lat", "depth", None),
        ),
        out_specs=P("lat", "depth", None),
        check_vma=False,
    )
```

```python
import jax
import jax.numpy as jnp
from jax import lax
from jax.experimental import pallas as pl
from jax.experimental.pallas import tpu as pltpu
from jax.sharding import PartitionSpec as P

f32 = jnp.float32
bf16 = jnp.bfloat16

CELLS = 32
N = 64
ZS = 8
VLIM = 16 << 20


def lanes(shape):
    return lax.broadcasted_iota(jnp.int32, shape, len(shape) - 1)


def roll(x, shift):
    shift = shift % x.shape[-1]
    return x if shift == 0 else pltpu.roll(x, shift, x.ndim - 1)


def pack(dup):
    hi = dup.astype(bf16).astype(f32)
    return jnp.where(lanes(dup.shape) < N, hi, dup - hi).astype(bf16)


def mm(a, b):
    r = jnp.dot(a, jnp.concatenate([b, b], axis=0), preferred_element_type=f32)
    return r + roll(r, N)


def rhs(x):
    hi = x.astype(bf16)
    lo = (x - hi.astype(f32)).astype(bf16)
    return jnp.concatenate([hi, hi, lo, lo], axis=0)


def dot(a, y):
    return jnp.dot(jnp.concatenate([a, a], axis=1), y, preferred_element_type=f32)


def column(row):
    return jnp.broadcast_to(row, (128, N)).T


def pair(a, b):
    low = lanes(a.shape) < N
    a_hi, b_hi = a.astype(bf16).astype(f32), b.astype(bf16).astype(f32)
    hi = jnp.where(low, a_hi, b_hi).astype(bf16)
    lo = jnp.where(low, a - a_hi, b - b_hi).astype(bf16)
    return jnp.concatenate([hi, lo], axis=1)


def pair_rhs(x, y):
    def split(z):
        hi = z.astype(bf16).astype(f32)
        return jnp.where(lanes(z.shape) % 64 < CELLS, hi, z - hi).astype(bf16)

    a, b = split(x), split(y)
    return jnp.concatenate([a, b, a, b], axis=0)


def eye2():
    return jnp.where(lanes((N, 128)) % N == lax.broadcasted_iota(jnp.int32, (N, 128), 0), 1.0, 0.0)


def put(node, full, j, p, q, w, u=None):
    node[j, 0], node[j, 1], node[j, 2] = pack(p), pack(q), pack(w)
    full[j, 0], full[j, 1], full[j, 2] = p, q, w
    if u is not None:
        node[j, 3] = pack(u)


def tree_leaves(fac_ref, coup_ref, after_ref, quad_ref, n1_ref, full_ref, cols_ref, rows):
    del after_ref
    c = coup_ref[...]
    cols_ref[0] = column(c[CELLS - 1 : CELLS])
    cols_ref[1] = column(1.0 / c[0:1])
    c2 = jnp.concatenate([c, c], axis=1)
    low = lanes((CELLS, 128)) < N
    eye = eye2()

    def leaf(k):
        g, s = divmod(k, 8)
        x = fac_ref[pl.ds(g * 256 + s, 32, stride=8), :]
        y = roll(x, N)
        rows[k % 2, pl.ds(0, 32, stride=2), :] = jnp.where(low, x, y)
        rows[k % 2, pl.ds(1, 32, stride=2), :] = jnp.where(low, y, x)
        a = rows[k % 2]
        before = max(k - 1, 0)
        return a * c2[before : before + 1] - eye, a * c2[k : k + 1] - eye

    for j in range(CELLS // 2):
        p1, q1 = leaf(2 * j)
        p2, q2 = leaf(2 * j + 1)
        kq1 = pack(q1)
        p = p1 + p2 + dot(pack(p2), rhs(p1))
        q = q1 + q2 + dot(kq1, rhs(q2))
        u = eye + q1 + p2 + dot(kq1, rhs(p2))
        w = (eye + eye) + p1 + q1 + p + dot(kq1, rhs(p))
        put(n1_ref, full_ref, j, p, q, w)
        quad_ref[j, 0] = pair(p, p2)
        quad_ref[j, 1] = pair(w, u)
        quad_ref[j, 2] = pair(w, q)
        quad_ref[j, 3] = pair(p, q2)


def tree_upper(n1_ref, full_ref, coup_ref, cols_ref, after_ref, n2_ref, n3_ref, n4_ref, n5_ref, root_ref, fa, fb):
    del after_ref
    node, full = n1_ref, full_ref
    for count, node_to, full_to in ((8, n2_ref, fa), (4, n3_ref, fb), (2, n4_ref, fa), (1, None, None)):
        for j in range(count):
            one, two = 2 * j, 2 * j + 1
            kq1, yp1 = node[one, 1], rhs(full[one, 0])
            u = full[two, 2] + dot(kq1, rhs(full[two, 2]))
            p = full[one, 0] + full[two, 0] + dot(node[two, 0], yp1)
            q = full[one, 1] + full[two, 1] + dot(kq1, rhs(full[two, 1]))
            ku = pack(u)
            w = full[one, 2] + u + dot(ku, yp1)
            if node_to is None:
                eye = eye2()
                n5_ref[0] = ku
                first = coup_ref[0:1]
                scale = 1.0 / jnp.concatenate([first, first], axis=1)
                root_ref[:N] = jnp.where(lanes((N, 128)) < N, (p + eye) * cols_ref[0] * scale, q + eye)
                root_ref[N:] = w * scale
            else:
                put(node_to, full_to, j, p, q, w, u)
        node, full = node_to, full_to


def react(jac_hbm, dens_hbm, src_hbm, tran_hbm, pat_hbm, out_ref, flux_ref, jac_ref, dens_ref, src_ref, tran_ref,
          pat_ref, sems):
    parts = [(slice(None), pl.ds(i * 1024, 1024)) for i in range(4)]
    pairs = [(dens_hbm, dens_ref), (pat_hbm, pat_ref)] + [(jac_hbm.at[part], jac_ref.at[part]) for part in parts]
    pairs += [(src_hbm, src_ref), (tran_hbm, tran_ref)]
    copies = [pltpu.make_async_copy(a, b, sems.at[i]) for i, (a, b) in enumerate(pairs)]
    for copy in copies:
        copy.start()
    half = lanes((128, N)) % 2 == lax.broadcasted_iota(jnp.int32, (128, N), 0) // N
    half = jnp.where(half, 1.0, 0.0).astype(bf16)
    copies[0].wait()
    copies[1].wait()
    u = dens_ref[...]
    u2 = jnp.concatenate([u, u], axis=1)
    lane8 = lanes((8, 128))
    pat = pat_ref[...].astype(f32)
    mask_rows = jnp.zeros((8, 128), f32)
    for t in range(8):
        mask_rows = jnp.where((lane8 % N) // 8 == t, pat[:, t : t + 1], mask_rows)
    lane = lanes((CELLS, N))
    acc = jnp.zeros((CELLS, N), f32)
    for m in range(32):
        if m % 8 == 0:
            copies[2 + m // 8].wait()
        y = jac_ref[:, m * 128 : (m + 1) * 128] * (u2 * mask_rows[m // 4 : m // 4 + 1])
        hi = y.astype(bf16)
        lo = (y - hi.astype(f32)).astype(bf16)
        z = jnp.dot(hi, half, preferred_element_type=f32) + jnp.dot(lo, half, preferred_element_type=f32)
        acc = jnp.where(lane // 2 == m, z, acc)
    copies[6].wait()
    copies[7].wait()
    tran = tran_ref[...]
    flux = tran * u
    flux_ref[...] = column(flux[CELLS - 1 : CELLS])
    row = lax.broadcasted_iota(jnp.int32, (CELLS, N), 0)
    lower = jnp.where(row == 0, 0.0, pltpu.roll(flux, 1, 0))
    upper = jnp.where(row == CELLS - 1, 0.0, pltpu.roll(u, CELLS - 1, 0))
    out_ref[...] = src_ref[...] - acc + lower + tran * upper


def upsweep(neigh_ref, part_ref, a_ref, b_ref, c_ref, even_ref, odd_ref, flux_ref, dens_ref, tran_ref, lat_ref, coup_ref, cols_ref,
            quad_ref, n1_ref, n2_ref, n3_ref, n4_ref, n5_ref, root_ref, pay_ref, pair_ref, v_ref, w_ref):
    me = lax.axis_index("lat")
    u = dens_ref[...]
    total = jnp.zeros((CELLS, N), f32)
    lines = [(0, u), (1, a_ref[0])] + [(2 + i, b_ref[i]) for i in range(2)]
    lines += [((6, 7, 4, 5)[i], c_ref[i]) for i in range(4)]
    for offset, value in lines:
        line = me ^ offset
        count = jnp.int32(0)
        for j in range(4):
            count = count + (neigh_ref[0, j] == line).astype(jnp.int32)
        total = total + count.astype(f32) * value
    row = lax.broadcasted_iota(jnp.int32, (CELLS, N), 0)
    r = part_ref[...] - lat_ref[...] * (4.0 * u - total)
    depth = lax.axis_index("depth")
    above = jnp.where(depth % 2 == 0, even_ref[0, 0:1], odd_ref[0, 0:1])
    above = jnp.where(depth == lax.axis_size("depth") - 1, 0.0, above)
    r = r + jnp.where(row == CELLS - 1, tran_ref[...] * above, 0.0)
    c = coup_ref[...]
    g = r / jnp.where(row == 0, c, pltpu.roll(c, 1, 0))
    x = []
    for i in range(4):
        rolled = g if i == 0 else pltpu.roll(g, CELLS - i, 0)
        x.append(jnp.concatenate([rolled, rolled], axis=0).T)
    lane2 = lanes((N, N)) % CELLS
    lane = lanes((N, CELLS))
    pair_v, pair_w = [], []
    for half in range(2):
        x0, x1 = x[2 * half], x[2 * half + 1]
        y = pair_rhs(x0, x1)
        v = jnp.zeros((N, N), f32)
        w = jnp.zeros((N, N), f32)
        for j in range(8):
            at = 2 * j + half
            here = lane2 == 4 * j
            v = jnp.where(here, jnp.dot(quad_ref[at, 0], y, preferred_element_type=f32), v)
            w = jnp.where(here, jnp.dot(quad_ref[at, 1], y, preferred_element_type=f32), w)
        v = v[:, :CELLS] + v[:, CELLS:] + x0[:, :CELLS] + x1[:, :CELLS]
        w = w[:, :CELLS] + w[:, CELLS:]
        pair_v.append(v)
        pair_w.append(w)
        pair_ref[half, :, 0:CELLS] = pair_v[half]
        pair_ref[2 + half, :, 0:CELLS] = w
    yv, yw = rhs(pair_v[0]), rhs(pair_w[1])
    v, w = pair_v[0] + pair_v[1], pair_w[0] + pair_w[1]
    dv = jnp.zeros((N, CELLS), f32)
    dw = jnp.zeros((N, CELLS), f32)
    for j in range(8):
        here = lane == 4 * j
        dv = jnp.where(here, dot(n1_ref[2 * j + 1, 0], yv), dv)
        dw = jnp.where(here, dot(n1_ref[2 * j, 1], yw) + dot(n2_ref[j, 3], yv), dw)
    v, w = v + dv, w + dw
    vs = [jnp.broadcast_to(v[:, 4 * j : 4 * j + 1], (N, 128)) for j in range(8)]
    ws = [jnp.broadcast_to(w[:, 4 * j : 4 * j + 1], (N, 128)) for j in range(8)]
    at = 0
    for count, ref, above in ((4, n2_ref, n3_ref), (2, n3_ref, n4_ref), (1, n4_ref, n5_ref)):
        next_v, next_w = [], []
        for j in range(count):
            v1, v2, w1, w2 = vs[2 * j], vs[2 * j + 1], ws[2 * j], ws[2 * j + 1]
            v_ref[at], w_ref[at] = v1, w2
            at += 1
            yv, yw = rhs(v1), rhs(w2)
            u_map = above[j, 3] if count > 1 else above[0]
            next_v.append(v1 + v2 + dot(ref[2 * j + 1, 0], yv))
            next_w.append(w1 + w2 + dot(ref[2 * j, 1], yw) + dot(u_map, yv))
        vs, ws = next_v, next_w
    lane = lanes((N, 128))
    pay_ref[:N] = root_ref[:N]
    tail = jnp.where(lane == N, vs[0] * cols_ref[0] + flux_ref[...], ws[0])
    pay_ref[N:] = jnp.where(lane < N, root_ref[N:], tail)


def prepare(pair_ref, v_ref, w_ref, n1_ref, n2_ref, n3_ref, n4_ref, t_ref, add_v, add_a, add_x):
    lane = lanes((N, 128))
    part = lane % CELLS
    at, vec = 0, 0
    for level, size, ref in ((1, 8, n2_ref), (2, 16, n3_ref), (3, 32, n4_ref)):
        acc_v = jnp.zeros((N, 128), f32)
        acc_a = jnp.zeros((N, 128), f32)
        for j in range(CELLS // size):
            kw = ref[2 * j + 1, 2]
            wide = kw.astype(f32)
            t_ref[at] = pack(wide + roll(wide, N) + mm(kw, ref[2 * j, 0]))
            at += 1
            here = part // size == j
            acc_v = jnp.where(here, v_ref[vec], acc_v)
            acc_a = jnp.where(here, w_ref[vec] + dot(kw, rhs(v_ref[vec])), acc_a)
            vec += 1
        add_v[level], add_a[level] = acc_v, acc_a

    def repeat(x):
        x = x + roll(x, CELLS)
        return x + roll(x, 2 * CELLS)

    first = jnp.logical_and(lane % 4 == 0, lane < CELLS)
    v0, v1, w0, w1 = [jnp.where(first, pair_ref[i], 0.0) for i in range(4)]
    y = rhs(v0)
    acc_a = jnp.zeros((N, 128), f32)
    for j in range(8):
        kw = n1_ref[2 * j + 1, 2]
        wide = kw.astype(f32)
        t_ref[at] = pack(wide + roll(wide, N) + mm(kw, n1_ref[2 * j, 0]))
        at += 1
        acc_a = jnp.where(lane == 4 * j, dot(kw, y), acc_a)
    acc_a = acc_a + w1
    spread_v = v0 + roll(v0, 1)
    spread_a = acc_a + roll(acc_a, 1)
    add_v[0] = repeat(spread_v + roll(spread_v, 2))
    add_a[0] = repeat(spread_a + roll(spread_a, 2))
    add_x[...] = repeat(w0 + roll(w1, 2) + roll(v0, 1) + roll(v1, 3))


def unpack(b):
    low = lanes((N, 128)) < N
    b1, b2 = b[:N], b[N:]
    r1, r2 = roll(b1, N), roll(b2, N)
    x = jnp.where(low, b1, r1)
    y = jnp.where(low, r1, b1)
    z = jnp.where(low, b2, r2)
    g = jnp.broadcast_to(b2[:, N : N + 1], (N, 128))
    h = jnp.broadcast_to(b2[:, N + 1 : N + 2], (N, 128))
    return x, y, z, g, h


def join(one, two, last=False):
    p1, q1, w1, v1, h1 = one
    p2, q2, w2, v2, h2 = two
    kq1, kp2, kw2 = pack(q1), pack(p2), pack(w2)
    yp1, yv1 = rhs(p1), rhs(v1)
    t = dot(kw2, yp1)
    th = h2 + dot(kw2, yv1)
    v = v2 + dot(kp2, yv1)
    yt, yth = rhs(t), rhs(th)
    w = w1 + dot(kq1, yt)
    h = h1 + dot(kq1, yth)
    yq2 = rhs(q2)
    p, q = (None, None) if last else (dot(kp2, yp1), dot(kq1, yq2))
    return (p, q, w, v, h), (t, th, yp1, yv1, yq2, yt, yth)


def track_first(is_low, one, two, extra):
    eye = eye2()
    t, th = extra[:2]
    return (
        jnp.where(is_low, eye, one[0]),
        jnp.where(is_low, two[1], eye),
        jnp.where(is_low, t, 0.0),
        jnp.where(is_low, 0.0, one[3]),
        jnp.where(is_low, th, 0.0),
    )


def track(is_low, fun, extra):
    f, hh, k, g, e = fun
    t, th, yp1, yv1, yq2, yt, yth = extra
    x1 = pack(jnp.where(is_low, hh, f))
    x2 = pack(jnp.where(is_low, hh, k))
    prod1 = dot(x1, jnp.where(is_low, yq2, yp1))
    prod2 = dot(x2, jnp.where(is_low, yt, yp1))
    vec1 = dot(x1, yv1)
    vec2 = dot(x2, jnp.where(is_low, yth, yv1))
    return (
        jnp.where(is_low, f, prod1),
        jnp.where(is_low, prod1, hh),
        jnp.where(is_low, k + prod2, prod2),
        jnp.where(is_low, g, g + vec1),
        e + vec2,
    )


def put_map(ref, p, q, w, v, h, last=False):
    lane = lanes((N, 128))
    low = lane < N
    tail = jnp.where(low, w, jnp.where(lane == N, v, h))
    if last:
        ref[...] = tail
    else:
        ref[:N] = jnp.where(low, p, q)
        ref[N:] = tail


def fill(slots, at, refs):
    for bits, ref in enumerate(refs):
        slots[at ^ bits] = ref[...]
    return [unpack(slots[i]) for i in range(4)]


def combine_four(own_ref, x1_ref, x2_ref, x3_ref, out_ref, fun_out, slots):
    at = lax.axis_index("depth") % 4
    maps = fill(slots, at, (own_ref, x1_ref, x2_ref, x3_ref))
    lower, extra_lower = join(maps[0], maps[1])
    upper, extra_upper = join(maps[2], maps[3])
    in_lower = at < 2
    mine = lambda x, y: [jnp.where(in_lower, a, b) for a, b in zip(x, y)]
    fun = track_first(
        at % 2 == 0, mine(maps[0], maps[2]), mine(maps[1], maps[3]), mine(extra_lower[:2], extra_upper[:2])
    )
    total, extra = join(lower, upper)
    put_map(out_ref, *total)
    put_map(fun_out, *track(in_lower, fun, extra))


def combine_two(own_ref, other_ref, fun_ref, out_ref, fun_out):
    is_low = lax.axis_index("depth") % ZS < 4
    own, other = own_ref[...], other_ref[...]
    total, extra = join(unpack(jnp.where(is_low, own, other)), unpack(jnp.where(is_low, other, own)))
    put_map(out_ref, *total)
    for i, value in enumerate(track(is_low, unpack(fun_ref[...]), extra)):
        fun_out[i] = value


def downsweep(own_ref, y1_ref, y2_ref, y3_ref, fun_ref, cols_ref, add_v, add_a, add_x, quad_ref, n1_ref, n2_ref, n3_ref,
              n4_ref, t_ref, out_ref, slots):
    at = lax.axis_index("depth") // ZS
    maps = fill(slots, at, (own_ref, y1_ref, y2_ref, y3_ref))
    lower, extra_lower = join(maps[0], maps[1], last=True)
    upper, extra_upper = join(maps[2], maps[3], last=True)
    is_low = at < 2
    extra = [jnp.where(is_low, a, b) for a, b in zip(extra_lower, extra_upper)]
    f, hh, k, g, e = track(at % 2 == 0, [fun_ref[i] for i in range(5)], extra)
    yv = rhs(lower[3])
    t = upper[4] + dot(pack(upper[2]), yv)
    up = g + dot(pack(f), yv)
    aa = e + dot(pack(jnp.where(is_low, hh, k)), jnp.where(is_low, rhs(t), yv))
    ss = jnp.where(is_low, g, up) * cols_ref[1]
    lane = lanes((N, 128)) % CELLS
    for level, size, ref, base in ((3, 32, n4_ref, 6), (2, 16, n3_ref, 4), (1, 8, n2_ref, 0), (0, 4, n1_ref, 7)):
        ys, ya = rhs(ss), rhs(aa)
        ds = jnp.zeros((N, 128), f32)
        da = jnp.zeros((N, 128), f32)
        for j in range(CELLS // size):
            here = lane // size == j
            ds = jnp.where(here, dot(ref[2 * j, 0], ys), ds)
            da = jnp.where(here, dot(ref[2 * j + 1, 1], ya) + dot(t_ref[base + j], ys), da)
        upper = lane % size >= size // 2
        new_s = ss + add_v[level] + ds
        new_a = aa + add_a[level] + da
        ss = jnp.where(upper, new_s, ss)
        aa = jnp.where(upper, aa, new_a)
    y = pair_rhs(ss, aa)
    x = jnp.zeros((N, 128), f32)
    for j in range(CELLS // 2):
        x = jnp.where(lane == 2 * j, jnp.dot(quad_ref[j, 2], y, preferred_element_type=f32), x)
        x = jnp.where(lane == 2 * j + 1, jnp.dot(quad_ref[j, 3], y, preferred_element_type=f32), x)
    x = x + roll(x, CELLS) + (aa + add_x[...] + jnp.where(lane % 2 == 1, ss, 0.0))
    out_ref[...] = x.T[:CELLS]


def sds(*shape, dtype=f32):
    return jax.ShapeDtypeStruct(shape, dtype)


def call(body, outs, *args, scratch=(), smem=0, hbm=0, flops=0, name=None):
    args = [pltpu.with_memory_space_constraint(x, pltpu.HBM) if smem <= i < smem + hbm else x for i, x in enumerate(args)]
    spaces = [pltpu.SMEM] * smem + [pltpu.HBM] * hbm + [pltpu.VMEM] * (len(args) - smem - hbm)
    return pl.pallas_call(
        body,
        out_shape=outs,
        in_specs=[pl.BlockSpec(memory_space=space) for space in spaces],
        out_specs=jax.tree.map(lambda _: pl.BlockSpec(memory_space=pltpu.VMEM), outs),
        scratch_shapes=scratch,
        cost_estimate=pl.CostEstimate(flops=flops, bytes_accessed=1 << 16, transcendentals=0),
        name=name,
        compiler_params=pltpu.CompilerParams(vmem_limit_bytes=VLIM),
    )(*args)


def node(count):
    return sds(count, 4, N, 128, dtype=bf16)


def on_device(densities, source, jacobian, pattern, transport, lateral, neighbours, factor, coupling):
    line_count, cell_count, species = densities.shape
    u = densities.reshape(CELLS, N)
    src = source.reshape(CELLS, N)
    tran = transport.reshape(CELLS, N)
    lat = lateral.reshape(CELLS, N)
    coup = coupling.reshape(CELLS, N)
    jac = jacobian.reshape(CELLS, N * N)
    fac = factor.reshape(4, 8, 32, 128).transpose(0, 2, 1, 3).reshape(1024, 128)

    def xor_lat(value, bits):
        return lax.ppermute(value, "lat", [(i, i ^ bits) for i in range(8)])

    def xor_depth(value, bits):
        return lax.ppermute(value, "depth", [(i, i ^ bits) for i in range(32)])

    line_a = xor_lat(densities, 1)
    part, flux = call(
        react, (sds(CELLS, N), sds(N, 128)), jac, u, src, tran, pattern, hbm=5, flops=1 << 30, name="react",
        scratch=[pltpu.VMEM((CELLS, N * N), f32)] + [pltpu.VMEM((CELLS, N), f32)] * 3
        + [pltpu.VMEM((8, 8), jnp.int32), pltpu.SemaphoreType.DMA((8,))],
    )
    line_b = xor_lat(jnp.concatenate([densities, line_a], axis=0), 2)
    quad, n1, full, cols = call(
        tree_leaves,
        (sds(16, 4, N, 256, dtype=bf16), sds(16, 3, N, 128, dtype=bf16), sds(16, 3, N, 128), sds(2, N, 128)),
        fac, coup, part, scratch=[pltpu.VMEM((2, N, 128), f32)], flops=2 << 30, name="tree_leaves",
    )
    top_even = xor_depth(lax.optimization_barrier((densities, cols))[0], 1)
    top_odd = lax.ppermute(
        lax.optimization_barrier((densities, line_b))[0], ("depth", "lat"),
        [(8 * i + l, 8 * (i + 1 if i % 2 else i - 1) + l if 0 < i < 31 else 8 * i + (l ^ 1))
         for i in range(32) for l in range(8)],
    )
    line_c = xor_lat(jnp.concatenate([densities, line_a, line_b], axis=0), 6)
    n2, n3, n4, n5, root = call(
        tree_upper,
        (node(8), node(4), node(2), sds(1, N, 128, dtype=bf16), sds(128, 128)),
        n1, full, coup, cols, part, scratch=[pltpu.VMEM((8, 3, N, 128), f32), pltpu.VMEM((4, 3, N, 128), f32)],
        flops=2 << 30, name="tree_upper",
    )
    pay, pair, vs, ws = call(
        upsweep, (sds(128, 128), sds(4, N, 128), sds(7, N, 128), sds(7, N, 128)),
        neighbours, part, line_a, line_b, line_c, top_even, top_odd, flux, u, tran, lat, coup, cols, quad, n1, n2, n3, n4, n5, root,
        smem=1, flops=1 << 25, name="upsweep",
    )
    others = [xor_depth(pay, bits) for bits in (1, 2, 3)]
    slots = [pltpu.VMEM((4, 128, 128), f32)]
    pay, fun = call(
        combine_four, (sds(128, 128), sds(128, 128)), pay, *others, scratch=slots, flops=1 << 24, name="combine_four",
    )
    other = xor_depth(pay, 7)
    pay, fun = call(
        combine_two, (sds(128, 128), sds(5, N, 128)), pay, other, fun, flops=1 << 24, name="combine_two",
    )
    others = [xor_depth(pay, bits) for bits in (8, 16, 24)]
    tees, add_v, add_a, add_x = call(
        prepare, (sds(15, N, 128, dtype=bf16), sds(4, N, 128), sds(4, N, 128), sds(N, 128)),
        pair, vs, ws, n1, n2, n3, n4, flops=1 << 30, name="prepare",
    )
    out = call(
        downsweep, sds(CELLS, N), pay, *others, fun, cols, add_v, add_a, add_x, quad, n1, n2, n3, n4, tees,
        scratch=slots, flops=1 << 25, name="downsweep",
    )
    return out.reshape(line_count, cell_count, species)


def solution(mesh):
    return jax.shard_map(
        on_device,
        mesh=mesh,
        in_specs=(
            P("lat", "depth", None),
            P("lat", "depth", None),
            P("lat", "depth", None),
            P(),
            P("lat", "depth", None),
            P("lat", "depth", None),
            P("lat", None),
            P("lat", "depth", None),
            P("lat", "depth", None),
        ),
        out_specs=P("lat", "depth", None),
        check_vma=False,
    )
```

```python
import jax
import jax.numpy as jnp
from jax import lax
from jax.experimental import pallas as pl
from jax.experimental.pallas import tpu as pltpu
from jax.sharding import PartitionSpec as P


f32 = jnp.float32
bf16 = jnp.bfloat16

CELLS = 32
N = 64
ZS = 8
VLIM = 16 << 20


def lanes(shape):
    return lax.broadcasted_iota(jnp.int32, shape, len(shape) - 1)


def roll(x, shift):
    shift = shift % x.shape[-1]
    return x if shift == 0 else pltpu.roll(x, shift, x.ndim - 1)


def pack(dup):
    hi = dup.astype(bf16).astype(f32)
    return jnp.where(lanes(dup.shape) < N, hi, dup - hi).astype(bf16)


def mm(a, b):
    r = jnp.dot(a, jnp.concatenate([b, b], axis=0), preferred_element_type=f32)
    return r + roll(r, N)


def rhs(x):
    hi = x.astype(bf16)
    lo = (x - hi.astype(f32)).astype(bf16)
    return jnp.concatenate([hi, hi, lo, lo], axis=0)


def dot(a, y):
    return jnp.dot(jnp.concatenate([a, a], axis=1), y, preferred_element_type=f32)


def column(row):
    return jnp.broadcast_to(row, (128, N)).T


def pair(a, b):
    low = lanes(a.shape) < N
    a_hi, b_hi = a.astype(bf16).astype(f32), b.astype(bf16).astype(f32)
    hi = jnp.where(low, a_hi, b_hi).astype(bf16)
    lo = jnp.where(low, a - a_hi, b - b_hi).astype(bf16)
    return jnp.concatenate([hi, lo], axis=1)


def pair_rhs(x, y):
    def split(z):
        hi = z.astype(bf16).astype(f32)
        return jnp.where(lanes(z.shape) % 64 < CELLS, hi, z - hi).astype(bf16)

    a, b = split(x), split(y)
    return jnp.concatenate([a, b, a, b], axis=0)


def eye2():
    return jnp.where(lanes((N, 128)) % N == lax.broadcasted_iota(jnp.int32, (N, 128), 0), 1.0, 0.0)


def put(node, full, j, p, q, w, u=None):
    node[j, 0], node[j, 1], node[j, 2] = pack(p), pack(q), pack(w)
    full[j, 0], full[j, 1], full[j, 2] = p, q, w
    if u is not None:
        node[j, 3] = pack(u)


def tree_leaves(fac_ref, coup_ref, after_ref, quad_ref, n1_ref, full_ref, cols_ref, rows):
    del after_ref
    c = coup_ref[...]
    cols_ref[0] = column(c[CELLS - 1 : CELLS])
    cols_ref[1] = column(1.0 / c[0:1])
    c2 = jnp.concatenate([c, c], axis=1)
    low = lanes((CELLS, 128)) < N
    eye = eye2()

    def leaf(k):
        g, s = divmod(k, 8)
        x = fac_ref[pl.ds(g * 256 + s, 32, stride=8), :]
        y = roll(x, N)
        rows[k % 2, pl.ds(0, 32, stride=2), :] = jnp.where(low, x, y)
        rows[k % 2, pl.ds(1, 32, stride=2), :] = jnp.where(low, y, x)
        a = rows[k % 2]
        before = max(k - 1, 0)
        return a * c2[before : before + 1] - eye, a * c2[k : k + 1] - eye

    for j in range(CELLS // 2):
        p1, q1 = leaf(2 * j)
        p2, q2 = leaf(2 * j + 1)
        kq1 = pack(q1)
        p = p1 + p2 + dot(pack(p2), rhs(p1))
        q = q1 + q2 + dot(kq1, rhs(q2))
        u = eye + q1 + p2 + dot(kq1, rhs(p2))
        w = (eye + eye) + p1 + q1 + p + dot(kq1, rhs(p))
        put(n1_ref, full_ref, j, p, q, w)
        quad_ref[j, 0] = pair(p, p2)
        quad_ref[j, 1] = pair(w, u)
        quad_ref[j, 2] = pair(w, q)
        quad_ref[j, 3] = pair(p, q2)


def tree_upper(n1_ref, full_ref, coup_ref, cols_ref, after_ref, n2_ref, n3_ref, n4_ref, n5_ref, root_ref, fa, fb):
    del after_ref
    node, full = n1_ref, full_ref
    for count, node_to, full_to in ((8, n2_ref, fa), (4, n3_ref, fb), (2, n4_ref, fa), (1, None, None)):
        for j in range(count):
            one, two = 2 * j, 2 * j + 1
            kq1, yp1 = node[one, 1], rhs(full[one, 0])
            u = full[two, 2] + dot(kq1, rhs(full[two, 2]))
            p = full[one, 0] + full[two, 0] + dot(node[two, 0], yp1)
            q = full[one, 1] + full[two, 1] + dot(kq1, rhs(full[two, 1]))
            ku = pack(u)
            w = full[one, 2] + u + dot(ku, yp1)
            if node_to is None:
                eye = eye2()
                n5_ref[0] = ku
                first = coup_ref[0:1]
                scale = 1.0 / jnp.concatenate([first, first], axis=1)
                root_ref[:N] = jnp.where(lanes((N, 128)) < N, (p + eye) * cols_ref[0] * scale, q + eye)
                root_ref[N:] = w * scale
            else:
                put(node_to, full_to, j, p, q, w, u)
        node, full = node_to, full_to


def react(jac_hbm, dens_hbm, src_hbm, tran_hbm, pat_hbm, out_ref, flux_ref, jac_ref, dens_ref, src_ref, tran_ref,
          pat_ref, sems):
    parts = [(slice(None), pl.ds(i * 1024, 1024)) for i in range(4)]
    pairs = [(dens_hbm, dens_ref), (pat_hbm, pat_ref)] + [(jac_hbm.at[part], jac_ref.at[part]) for part in parts]
    pairs += [(src_hbm, src_ref), (tran_hbm, tran_ref)]
    copies = [pltpu.make_async_copy(a, b, sems.at[i]) for i, (a, b) in enumerate(pairs)]
    for copy in copies:
        copy.start()
    half = lanes((128, N)) % 2 == lax.broadcasted_iota(jnp.int32, (128, N), 0) // N
    half = jnp.where(half, 1.0, 0.0).astype(bf16)
    copies[0].wait()
    copies[1].wait()
    u = dens_ref[...]
    u2 = jnp.concatenate([u, u], axis=1)
    lane8 = lanes((8, 128))
    pat = pat_ref[...].astype(f32)
    mask_rows = jnp.zeros((8, 128), f32)
    for t in range(8):
        mask_rows = jnp.where((lane8 % N) // 8 == t, pat[:, t : t + 1], mask_rows)
    lane = lanes((CELLS, N))
    acc = jnp.zeros((CELLS, N), f32)
    for m in range(32):
        if m % 8 == 0:
            copies[2 + m // 8].wait()
        y = jac_ref[:, m * 128 : (m + 1) * 128] * (u2 * mask_rows[m // 4 : m // 4 + 1])
        hi = y.astype(bf16)
        lo = (y - hi.astype(f32)).astype(bf16)
        z = jnp.dot(hi, half, preferred_element_type=f32) + jnp.dot(lo, half, preferred_element_type=f32)
        acc = jnp.where(lane // 2 == m, z, acc)
    copies[6].wait()
    copies[7].wait()
    tran = tran_ref[...]
    flux = tran * u
    flux_ref[...] = column(flux[CELLS - 1 : CELLS])
    row = lax.broadcasted_iota(jnp.int32, (CELLS, N), 0)
    lower = jnp.where(row == 0, 0.0, pltpu.roll(flux, 1, 0))
    upper = jnp.where(row == CELLS - 1, 0.0, pltpu.roll(u, CELLS - 1, 0))
    out_ref[...] = src_ref[...] - acc + lower + tran * upper


def upsweep(neigh_ref, part_ref, a_ref, b_ref, c_ref, even_ref, odd_ref, flux_ref, dens_ref, tran_ref, lat_ref, coup_ref, cols_ref,
            quad_ref, n1_ref, n2_ref, n3_ref, n4_ref, n5_ref, root_ref, pay_ref, pair_ref, v_ref, w_ref):
    me = lax.axis_index("lat")
    u = dens_ref[...]
    total = jnp.zeros((CELLS, N), f32)
    lines = [(0, u), (1, a_ref[0])] + [(2 + i, b_ref[i]) for i in range(2)]
    lines += [((6, 7, 4, 5)[i], c_ref[i]) for i in range(4)]
    for offset, value in lines:
        line = me ^ offset
        count = jnp.int32(0)
        for j in range(4):
            count = count + (neigh_ref[0, j] == line).astype(jnp.int32)
        total = total + count.astype(f32) * value
    row = lax.broadcasted_iota(jnp.int32, (CELLS, N), 0)
    r = part_ref[...] - lat_ref[...] * (4.0 * u - total)
    depth = lax.axis_index("depth")
    above = jnp.where(depth % 2 == 0, even_ref[0, 0:1], odd_ref[0, 0:1])
    above = jnp.where(depth == lax.axis_size("depth") - 1, 0.0, above)
    r = r + jnp.where(row == CELLS - 1, tran_ref[...] * above, 0.0)
    c = coup_ref[...]
    g = r / jnp.where(row == 0, c, pltpu.roll(c, 1, 0))
    x = []
    for i in range(4):
        rolled = g if i == 0 else pltpu.roll(g, CELLS - i, 0)
        x.append(jnp.concatenate([rolled, rolled], axis=0).T)
    lane2 = lanes((N, N)) % CELLS
    lane = lanes((N, CELLS))
    pair_v, pair_w = [], []
    for half in range(2):
        x0, x1 = x[2 * half], x[2 * half + 1]
        y = pair_rhs(x0, x1)
        v = jnp.zeros((N, N), f32)
        w = jnp.zeros((N, N), f32)
        for j in range(8):
            at = 2 * j + half
            here = lane2 == 4 * j
            v = jnp.where(here, jnp.dot(quad_ref[at, 0], y, preferred_element_type=f32), v)
            w = jnp.where(here, jnp.dot(quad_ref[at, 1], y, preferred_element_type=f32), w)
        v = v[:, :CELLS] + v[:, CELLS:] + x0[:, :CELLS] + x1[:, :CELLS]
        w = w[:, :CELLS] + w[:, CELLS:]
        pair_v.append(v)
        pair_w.append(w)
        pair_ref[half, :, 0:CELLS] = pair_v[half]
        pair_ref[2 + half, :, 0:CELLS] = w
    yv, yw = rhs(pair_v[0]), rhs(pair_w[1])
    v, w = pair_v[0] + pair_v[1], pair_w[0] + pair_w[1]
    dv = jnp.zeros((N, CELLS), f32)
    dw = jnp.zeros((N, CELLS), f32)
    for j in range(8):
        here = lane == 4 * j
        dv = jnp.where(here, dot(n1_ref[2 * j + 1, 0], yv), dv)
        dw = jnp.where(here, dot(n1_ref[2 * j, 1], yw) + dot(n2_ref[j, 3], yv), dw)
    v, w = v + dv, w + dw
    vs = [jnp.broadcast_to(v[:, 4 * j : 4 * j + 1], (N, 128)) for j in range(8)]
    ws = [jnp.broadcast_to(w[:, 4 * j : 4 * j + 1], (N, 128)) for j in range(8)]
    at = 0
    for count, ref, above in ((4, n2_ref, n3_ref), (2, n3_ref, n4_ref), (1, n4_ref, n5_ref)):
        next_v, next_w = [], []
        for j in range(count):
            v1, v2, w1, w2 = vs[2 * j], vs[2 * j + 1], ws[2 * j], ws[2 * j + 1]
            v_ref[at], w_ref[at] = v1, w2
            at += 1
            yv, yw = rhs(v1), rhs(w2)
            u_map = above[j, 3] if count > 1 else above[0]
            next_v.append(v1 + v2 + dot(ref[2 * j + 1, 0], yv))
            next_w.append(w1 + w2 + dot(ref[2 * j, 1], yw) + dot(u_map, yv))
        vs, ws = next_v, next_w
    lane = lanes((N, 128))
    pay_ref[:N] = root_ref[:N]
    tail = jnp.where(lane == N, vs[0] * cols_ref[0] + flux_ref[...], ws[0])
    pay_ref[N:] = jnp.where(lane < N, root_ref[N:], tail)


def prepare(pair_ref, v_ref, w_ref, n1_ref, n2_ref, n3_ref, n4_ref, t_ref, add_v, add_a, add_x):
    lane = lanes((N, 128))
    part = lane % CELLS
    at, vec = 0, 0
    for level, size, ref in ((1, 8, n2_ref), (2, 16, n3_ref), (3, 32, n4_ref)):
        acc_v = jnp.zeros((N, 128), f32)
        acc_a = jnp.zeros((N, 128), f32)
        for j in range(CELLS // size):
            kw = ref[2 * j + 1, 2]
            wide = kw.astype(f32)
            t_ref[at] = pack(wide + roll(wide, N) + mm(kw, ref[2 * j, 0]))
            at += 1
            here = part // size == j
            acc_v = jnp.where(here, v_ref[vec], acc_v)
            acc_a = jnp.where(here, w_ref[vec] + dot(kw, rhs(v_ref[vec])), acc_a)
            vec += 1
        add_v[level], add_a[level] = acc_v, acc_a

    def repeat(x):
        x = x + roll(x, CELLS)
        return x + roll(x, 2 * CELLS)

    first = jnp.logical_and(lane % 4 == 0, lane < CELLS)
    v0, v1, w0, w1 = [jnp.where(first, pair_ref[i], 0.0) for i in range(4)]
    y = rhs(v0)
    acc_a = jnp.zeros((N, 128), f32)
    for j in range(8):
        kw = n1_ref[2 * j + 1, 2]
        wide = kw.astype(f32)
        t_ref[at] = pack(wide + roll(wide, N) + mm(kw, n1_ref[2 * j, 0]))
        at += 1
        acc_a = jnp.where(lane == 4 * j, dot(kw, y), acc_a)
    acc_a = acc_a + w1
    spread_v = v0 + roll(v0, 1)
    spread_a = acc_a + roll(acc_a, 1)
    add_v[0] = repeat(spread_v + roll(spread_v, 2))
    add_a[0] = repeat(spread_a + roll(spread_a, 2))
    add_x[...] = repeat(w0 + roll(w1, 2) + roll(v0, 1) + roll(v1, 3))


def unpack(b):
    low = lanes((N, 128)) < N
    b1, b2 = b[:N], b[N:]
    r1, r2 = roll(b1, N), roll(b2, N)
    x = jnp.where(low, b1, r1)
    y = jnp.where(low, r1, b1)
    z = jnp.where(low, b2, r2)
    g = jnp.broadcast_to(b2[:, N : N + 1], (N, 128))
    h = jnp.broadcast_to(b2[:, N + 1 : N + 2], (N, 128))
    return x, y, z, g, h


def join(one, two, last=False):
    p1, q1, w1, v1, h1 = one
    p2, q2, w2, v2, h2 = two
    kq1, kp2, kw2 = pack(q1), pack(p2), pack(w2)
    yp1, yv1 = rhs(p1), rhs(v1)
    t = dot(kw2, yp1)
    th = h2 + dot(kw2, yv1)
    v = v2 + dot(kp2, yv1)
    yt, yth = rhs(t), rhs(th)
    w = w1 + dot(kq1, yt)
    h = h1 + dot(kq1, yth)
    yq2 = rhs(q2)
    p, q = (None, None) if last else (dot(kp2, yp1), dot(kq1, yq2))
    return (p, q, w, v, h), (t, th, yp1, yv1, yq2, yt, yth)


def track_first(is_low, one, two, extra):
    eye = eye2()
    t, th = extra[:2]
    return (
        jnp.where(is_low, eye, one[0]),
        jnp.where(is_low, two[1], eye),
        jnp.where(is_low, t, 0.0),
        jnp.where(is_low, 0.0, one[3]),
        jnp.where(is_low, th, 0.0),
    )


def track(is_low, fun, extra):
    f, hh, k, g, e = fun
    _, _, yp1, yv1, yq2, yt, yth = extra
    x1 = pack(jnp.where(is_low, hh, f))
    x2 = pack(jnp.where(is_low, hh, k))
    prod1 = dot(x1, jnp.where(is_low, yq2, yp1))
    prod2 = dot(x2, jnp.where(is_low, yt, yp1))
    vec1 = dot(x1, yv1)
    vec2 = dot(x2, jnp.where(is_low, yth, yv1))
    return (
        jnp.where(is_low, f, prod1),
        jnp.where(is_low, prod1, hh),
        jnp.where(is_low, k + prod2, prod2),
        jnp.where(is_low, g, g + vec1),
        e + vec2,
    )


def put_map(ref, p, q, w, v, h, last=False):
    lane = lanes((N, 128))
    low = lane < N
    tail = jnp.where(low, w, jnp.where(lane == N, v, h))
    if last:
        ref[...] = tail
    else:
        ref[:N] = jnp.where(low, p, q)
        ref[N:] = tail


def fill(slots, at, refs):
    for bits, ref in enumerate(refs):
        slots[at ^ bits] = ref[...]
    return [unpack(slots[i]) for i in range(4)]


def combine_four(own_ref, x1_ref, x2_ref, x3_ref, out_ref, fun_out, slots):
    at = lax.axis_index("depth") % 4
    maps = fill(slots, at, (own_ref, x1_ref, x2_ref, x3_ref))
    lower, extra_lower = join(maps[0], maps[1])
    upper, extra_upper = join(maps[2], maps[3])
    in_lower = at < 2
    mine = lambda x, y: [jnp.where(in_lower, a, b) for a, b in zip(x, y)]
    fun = track_first(
        at % 2 == 0, mine(maps[0], maps[2]), mine(maps[1], maps[3]), mine(extra_lower[:2], extra_upper[:2])
    )
    total, extra = join(lower, upper)
    put_map(out_ref, *total)
    put_map(fun_out, *track(in_lower, fun, extra))


def combine_two(own_ref, other_ref, fun_ref, after_ref, out_ref, fun_out):
    del after_ref
    is_low = lax.axis_index("depth") % ZS < 4
    own, other = own_ref[...], other_ref[...]
    total, extra = join(unpack(jnp.where(is_low, own, other)), unpack(jnp.where(is_low, other, own)))
    put_map(out_ref, *total)
    for i, value in enumerate(track(is_low, unpack(fun_ref[...]), extra)):
        fun_out[i] = value


def downsweep(own_ref, y1_ref, y2_ref, y3_ref, fun_ref, cols_ref, add_v, add_a, add_x, quad_ref, n1_ref, n2_ref, n3_ref,
              n4_ref, t_ref, out_ref, slots):
    at = lax.axis_index("depth") // ZS
    maps = fill(slots, at, (own_ref, y1_ref, y2_ref, y3_ref))
    lower, extra_lower = join(maps[0], maps[1], last=True)
    upper, extra_upper = join(maps[2], maps[3], last=True)
    is_low = at < 2
    extra = [jnp.where(is_low, a, b) for a, b in zip(extra_lower, extra_upper)]
    f, hh, k, g, e = track(at % 2 == 0, [fun_ref[i] for i in range(5)], extra)
    yv = rhs(lower[3])
    t = upper[4] + dot(pack(upper[2]), yv)
    up = g + dot(pack(f), yv)
    aa = e + dot(pack(jnp.where(is_low, hh, k)), jnp.where(is_low, rhs(t), yv))
    ss = jnp.where(is_low, g, up) * cols_ref[1]
    lane = lanes((N, 128)) % CELLS
    for level, size, ref, base in ((3, 32, n4_ref, 6), (2, 16, n3_ref, 4), (1, 8, n2_ref, 0), (0, 4, n1_ref, 7)):
        ys, ya = rhs(ss), rhs(aa)
        ds = jnp.zeros((N, 128), f32)
        da = jnp.zeros((N, 128), f32)
        for j in range(CELLS // size):
            here = lane // size == j
            ds = jnp.where(here, dot(ref[2 * j, 0], ys), ds)
            da = jnp.where(here, dot(ref[2 * j + 1, 1], ya) + dot(t_ref[base + j], ys), da)
        upper = lane % size >= size // 2
        new_s = ss + add_v[level] + ds
        new_a = aa + add_a[level] + da
        ss = jnp.where(upper, new_s, ss)
        aa = jnp.where(upper, aa, new_a)
    y = pair_rhs(ss, aa)
    x = jnp.zeros((N, 128), f32)
    for j in range(CELLS // 2):
        x = jnp.where(lane == 2 * j, jnp.dot(quad_ref[j, 2], y, preferred_element_type=f32), x)
        x = jnp.where(lane == 2 * j + 1, jnp.dot(quad_ref[j, 3], y, preferred_element_type=f32), x)
    x = x + roll(x, CELLS) + (aa + add_x[...] + jnp.where(lane % 2 == 1, ss, 0.0))
    out_ref[...] = x.T[:CELLS]


def sds(*shape, dtype=f32):
    return jax.ShapeDtypeStruct(shape, dtype)


def call(body, outs, *args, scratch=(), smem=0, hbm=0, flops=0):
    args = [pltpu.with_memory_space_constraint(x, pltpu.HBM) if smem <= i < smem + hbm else x for i, x in enumerate(args)]
    spaces = [pltpu.SMEM] * smem + [pltpu.HBM] * hbm + [pltpu.VMEM] * (len(args) - smem - hbm)
    return pl.pallas_call(
        body,
        out_shape=outs,
        in_specs=[pl.BlockSpec(memory_space=space) for space in spaces],
        out_specs=jax.tree.map(lambda _: pl.BlockSpec(memory_space=pltpu.VMEM), outs),
        scratch_shapes=scratch,
        cost_estimate=pl.CostEstimate(flops=flops, bytes_accessed=1 << 16, transcendentals=0),
        compiler_params=pltpu.CompilerParams(vmem_limit_bytes=VLIM),
    )(*args)


def node(count):
    return sds(count, 4, N, 128, dtype=bf16)


def on_device(densities, source, jacobian, pattern, transport, lateral, neighbours, factor, coupling):
    line_count, cell_count, species = densities.shape
    u = densities.reshape(CELLS, N)
    src = source.reshape(CELLS, N)
    tran = transport.reshape(CELLS, N)
    lat = lateral.reshape(CELLS, N)
    coup = coupling.reshape(CELLS, N)
    jac = jacobian.reshape(CELLS, N * N)
    fac = factor.reshape(4, 8, 32, 128).transpose(0, 2, 1, 3).reshape(1024, 128)

    def xor_lat(value, bits):
        return lax.ppermute(value, "lat", [(i, i ^ bits) for i in range(8)])

    def xor_depth(value, bits):
        return lax.ppermute(value, "depth", [(i, i ^ bits) for i in range(32)])

    line_a = xor_lat(densities, 1)
    part, flux = call(
        react, (sds(CELLS, N), sds(N, 128)), jac, u, src, tran, pattern, hbm=5, flops=1 << 30,
        scratch=[pltpu.VMEM((CELLS, N * N), f32)] + [pltpu.VMEM((CELLS, N), f32)] * 3
        + [pltpu.VMEM((8, 8), jnp.int32), pltpu.SemaphoreType.DMA((8,))],
    )
    line_b = xor_lat(jnp.concatenate([densities, line_a], axis=0), 2)
    quad, n1, full, cols = call(
        tree_leaves,
        (sds(16, 4, N, 256, dtype=bf16), sds(16, 3, N, 128, dtype=bf16), sds(16, 3, N, 128), sds(2, N, 128)),
        fac, coup, part, scratch=[pltpu.VMEM((2, N, 128), f32)], flops=2 << 30,
    )
    top_even = xor_depth(lax.optimization_barrier((densities, cols))[0], 1)
    top_odd = lax.ppermute(
        lax.optimization_barrier((densities, line_b))[0], ("depth", "lat"),
        [(8 * i + l, 8 * (i + 1 if i % 2 else i - 1) + l if 0 < i < 31 else 8 * i + (l ^ 1))
         for i in range(32) for l in range(8)],
    )
    line_c = xor_lat(jnp.concatenate([densities, line_a, line_b], axis=0), 6)
    n2, n3, n4, n5, root = call(
        tree_upper,
        (node(8), node(4), node(2), sds(1, N, 128, dtype=bf16), sds(128, 128)),
        n1, full, coup, cols, part, scratch=[pltpu.VMEM((8, 3, N, 128), f32), pltpu.VMEM((4, 3, N, 128), f32)],
        flops=2 << 30,
    )
    pay, pair, vs, ws = call(
        upsweep, (sds(128, 128), sds(4, N, 128), sds(7, N, 128), sds(7, N, 128)),
        neighbours, part, line_a, line_b, line_c, top_even, top_odd, flux, u, tran, lat, coup, cols, quad, n1, n2, n3, n4, n5, root,
        smem=1, flops=1 << 25,
    )
    others = []
    for bits in (1, 2, 3):
        others.append(xor_depth(pay, bits))
    slots = [pltpu.VMEM((4, 128, 128), f32)]
    pay, fun = call(combine_four, (sds(128, 128), sds(128, 128)), pay, *others, scratch=slots, flops=1 << 24)
    other = xor_depth(pay, 7)
    tees, add_v, add_a, add_x = call(
        prepare, (sds(15, N, 128, dtype=bf16), sds(4, N, 128), sds(4, N, 128), sds(N, 128)),
        pair, vs, ws, n1, n2, n3, n4, flops=1 << 30,
    )
    pay, fun = call(combine_two, (sds(128, 128), sds(5, N, 128)), pay, other, fun, add_x, flops=1 << 24)
    others = [xor_depth(pay, bits) for bits in (8, 16, 24)]
    out = call(
        downsweep, sds(CELLS, N), pay, *others, fun, cols, add_v, add_a, add_x, quad, n1, n2, n3, n4, tees,
        scratch=slots, flops=1 << 25,
    )
    return out.reshape(line_count, cell_count, species)


def solution(mesh):
    return jax.shard_map(
        on_device,
        mesh=mesh,
        in_specs=(
            P("lat", "depth", None),
            P("lat", "depth", None),
            P("lat", "depth", None),
            P(),
            P("lat", "depth", None),
            P("lat", "depth", None),
            P("lat", None),
            P("lat", "depth", None),
            P("lat", "depth", None),
        ),
        out_specs=P("lat", "depth", None),
        check_vma=False,
    )
```

```python
import jax
import jax.numpy as jnp
from jax import lax
from jax.experimental import pallas as pl
from jax.experimental.pallas import tpu as pltpu
from jax.sharding import PartitionSpec as P

f32 = jnp.float32
bf16 = jnp.bfloat16

CELLS = 32
N = 64
ZS = 8
VLIM = 16 << 20


def lanes(shape):
    return lax.broadcasted_iota(jnp.int32, shape, len(shape) - 1)


def roll(x, shift):
    shift = shift % x.shape[-1]
    return x if shift == 0 else pltpu.roll(x, shift, x.ndim - 1)


def pack(dup):
    hi = dup.astype(bf16).astype(f32)
    return jnp.where(lanes(dup.shape) < N, hi, dup - hi).astype(bf16)


def mm(a, b):
    r = jnp.dot(a, jnp.concatenate([b, b], axis=0), preferred_element_type=f32)
    return r + roll(r, N)


def rhs(x):
    hi = x.astype(bf16)
    lo = (x - hi.astype(f32)).astype(bf16)
    return jnp.concatenate([hi, hi, lo, lo], axis=0)


def dot(a, y):
    return jnp.dot(jnp.concatenate([a, a], axis=1), y, preferred_element_type=f32)


def column(row):
    return jnp.broadcast_to(row, (128, N)).T


def pair(a, b):
    low = lanes(a.shape) < N
    a_hi, b_hi = a.astype(bf16).astype(f32), b.astype(bf16).astype(f32)
    hi = jnp.where(low, a_hi, b_hi).astype(bf16)
    lo = jnp.where(low, a - a_hi, b - b_hi).astype(bf16)
    return jnp.concatenate([hi, lo], axis=1)


def pair_rhs(x, y):
    def split(z):
        hi = z.astype(bf16).astype(f32)
        return jnp.where(lanes(z.shape) % 64 < CELLS, hi, z - hi).astype(bf16)

    a, b = split(x), split(y)
    return jnp.concatenate([a, b, a, b], axis=0)


def eye2():
    return jnp.where(lanes((N, 128)) % N == lax.broadcasted_iota(jnp.int32, (N, 128), 0), 1.0, 0.0)


def put(node, full, j, p, q, w, u=None):
    node[j, 0], node[j, 1], node[j, 2] = pack(p), pack(q), pack(w)
    full[j, 0], full[j, 1], full[j, 2] = p, q, w
    if u is not None:
        node[j, 3] = pack(u)


def tree_leaves(fac_ref, coup_ref, after_ref, quad_ref, n1_ref, full_ref, cols_ref, rows):
    del after_ref
    c = coup_ref[...]
    cols_ref[0] = column(c[CELLS - 1 : CELLS])
    cols_ref[1] = column(1.0 / c[0:1])
    c2 = jnp.concatenate([c, c], axis=1)
    low = lanes((CELLS, 128)) < N
    eye = eye2()

    def leaf(k):
        g, s = divmod(k, 8)
        x = fac_ref[pl.ds(g * 256 + s, 32, stride=8), :]
        y = roll(x, N)
        rows[k % 2, pl.ds(0, 32, stride=2), :] = jnp.where(low, x, y)
        rows[k % 2, pl.ds(1, 32, stride=2), :] = jnp.where(low, y, x)
        a = rows[k % 2]
        before = max(k - 1, 0)
        return a * c2[before : before + 1] - eye, a * c2[k : k + 1] - eye

    for j in range(CELLS // 2):
        p1, q1 = leaf(2 * j)
        p2, q2 = leaf(2 * j + 1)
        kq1 = pack(q1)
        p = p1 + p2 + dot(pack(p2), rhs(p1))
        q = q1 + q2 + dot(kq1, rhs(q2))
        u = eye + q1 + p2 + dot(kq1, rhs(p2))
        w = (eye + eye) + p1 + q1 + p + dot(kq1, rhs(p))
        put(n1_ref, full_ref, j, p, q, w)
        quad_ref[j, 0] = pair(p, p2)
        quad_ref[j, 1] = pair(w, u)
        quad_ref[j, 2] = pair(w, q)
        quad_ref[j, 3] = pair(p, q2)


def tree_upper(n1_ref, full_ref, coup_ref, cols_ref, after_ref, n2_ref, n3_ref, n4_ref, n5_ref, root_ref, fa, fb):
    del after_ref
    node, full = n1_ref, full_ref
    for count, node_to, full_to in ((8, n2_ref, fa), (4, n3_ref, fb), (2, n4_ref, fa), (1, None, None)):
        for j in range(count):
            one, two = 2 * j, 2 * j + 1
            kq1, yp1 = node[one, 1], rhs(full[one, 0])
            u = full[two, 2] + dot(kq1, rhs(full[two, 2]))
            p = full[one, 0] + full[two, 0] + dot(node[two, 0], yp1)
            q = full[one, 1] + full[two, 1] + dot(kq1, rhs(full[two, 1]))
            ku = pack(u)
            w = full[one, 2] + u + dot(ku, yp1)
            if node_to is None:
                eye = eye2()
                n5_ref[0] = ku
                first = coup_ref[0:1]
                scale = 1.0 / jnp.concatenate([first, first], axis=1)
                root_ref[:N] = jnp.where(lanes((N, 128)) < N, (p + eye) * cols_ref[0] * scale, q + eye)
                root_ref[N:] = w * scale
            else:
                put(node_to, full_to, j, p, q, w, u)
        node, full = node_to, full_to


def react(jac_hbm, dens_hbm, src_hbm, tran_hbm, pat_hbm, out_ref, flux_ref, jac_ref, dens_ref, src_ref, tran_ref,
          pat_ref, sems):
    parts = [(slice(None), pl.ds(i * 1024, 1024)) for i in range(4)]
    pairs = [(dens_hbm, dens_ref), (pat_hbm, pat_ref)] + [(jac_hbm.at[part], jac_ref.at[part]) for part in parts]
    pairs += [(src_hbm, src_ref), (tran_hbm, tran_ref)]
    copies = [pltpu.make_async_copy(a, b, sems.at[i]) for i, (a, b) in enumerate(pairs)]
    for copy in copies:
        copy.start()
    half = lanes((128, N)) % 2 == lax.broadcasted_iota(jnp.int32, (128, N), 0) // N
    half = jnp.where(half, 1.0, 0.0).astype(bf16)
    copies[0].wait()
    copies[1].wait()
    u = dens_ref[...]
    u2 = jnp.concatenate([u, u], axis=1)
    lane8 = lanes((8, 128))
    pat = pat_ref[...].astype(f32)
    mask_rows = jnp.zeros((8, 128), f32)
    for t in range(8):
        mask_rows = jnp.where((lane8 % N) // 8 == t, pat[:, t : t + 1], mask_rows)
    lane = lanes((CELLS, N))
    acc = jnp.zeros((CELLS, N), f32)
    for m in range(32):
        if m % 8 == 0:
            copies[2 + m // 8].wait()
        y = jac_ref[:, m * 128 : (m + 1) * 128] * (u2 * mask_rows[m // 4 : m // 4 + 1])
        hi = y.astype(bf16)
        lo = (y - hi.astype(f32)).astype(bf16)
        z = jnp.dot(hi, half, preferred_element_type=f32) + jnp.dot(lo, half, preferred_element_type=f32)
        acc = jnp.where(lane // 2 == m, z, acc)
    copies[6].wait()
    copies[7].wait()
    tran = tran_ref[...]
    flux = tran * u
    flux_ref[...] = column(flux[CELLS - 1 : CELLS])
    row = lax.broadcasted_iota(jnp.int32, (CELLS, N), 0)
    lower = jnp.where(row == 0, 0.0, pltpu.roll(flux, 1, 0))
    upper = jnp.where(row == CELLS - 1, 0.0, pltpu.roll(u, CELLS - 1, 0))
    out_ref[...] = src_ref[...] - acc + lower + tran * upper


def upsweep(neigh_ref, part_ref, a_ref, b_ref, c_ref, even_ref, odd_ref, flux_ref, dens_ref, tran_ref, lat_ref, coup_ref, cols_ref,
            quad_ref, n1_ref, n2_ref, n3_ref, n4_ref, n5_ref, root_ref, pay_ref, pair_ref, v_ref, w_ref):
    me = lax.axis_index("lat")
    u = dens_ref[...]
    total = jnp.zeros((CELLS, N), f32)
    lines = [(0, u), (1, a_ref[0])] + [(2 + i, b_ref[i]) for i in range(2)]
    lines += [((6, 7, 4, 5)[i], c_ref[i]) for i in range(4)]
    for offset, value in lines:
        line = me ^ offset
        count = jnp.int32(0)
        for j in range(4):
            count = count + (neigh_ref[0, j] == line).astype(jnp.int32)
        total = total + count.astype(f32) * value
    row = lax.broadcasted_iota(jnp.int32, (CELLS, N), 0)
    r = part_ref[...] - lat_ref[...] * (4.0 * u - total)
    depth = lax.axis_index("depth")
    above = jnp.where(depth % 2 == 0, even_ref[0, 0:1], odd_ref[0, 0:1])
    above = jnp.where(depth == lax.axis_size("depth") - 1, 0.0, above)
    r = r + jnp.where(row == CELLS - 1, tran_ref[...] * above, 0.0)
    c = coup_ref[...]
    g = r / jnp.where(row == 0, c, pltpu.roll(c, 1, 0))
    x = []
    for i in range(4):
        rolled = g if i == 0 else pltpu.roll(g, CELLS - i, 0)
        x.append(jnp.concatenate([rolled, rolled], axis=0).T)
    lane2 = lanes((N, N)) % CELLS
    lane = lanes((N, CELLS))
    pair_v, pair_w = [], []
    for half in range(2):
        x0, x1 = x[2 * half], x[2 * half + 1]
        y = pair_rhs(x0, x1)
        v = jnp.zeros((N, N), f32)
        w = jnp.zeros((N, N), f32)
        for j in range(8):
            at = 2 * j + half
            here = lane2 == 4 * j
            v = jnp.where(here, jnp.dot(quad_ref[at, 0], y, preferred_element_type=f32), v)
            w = jnp.where(here, jnp.dot(quad_ref[at, 1], y, preferred_element_type=f32), w)
        v = v[:, :CELLS] + v[:, CELLS:] + x0[:, :CELLS] + x1[:, :CELLS]
        w = w[:, :CELLS] + w[:, CELLS:]
        pair_v.append(v)
        pair_w.append(w)
        pair_ref[half, :, 0:CELLS] = pair_v[half]
        pair_ref[2 + half, :, 0:CELLS] = w
    yv, yw = rhs(pair_v[0]), rhs(pair_w[1])
    v, w = pair_v[0] + pair_v[1], pair_w[0] + pair_w[1]
    dv = jnp.zeros((N, CELLS), f32)
    dw = jnp.zeros((N, CELLS), f32)
    for j in range(8):
        here = lane == 4 * j
        dv = jnp.where(here, dot(n1_ref[2 * j + 1, 0], yv), dv)
        dw = jnp.where(here, dot(n1_ref[2 * j, 1], yw) + dot(n2_ref[j, 3], yv), dw)
    v, w = v + dv, w + dw
    vs = [jnp.broadcast_to(v[:, 4 * j : 4 * j + 1], (N, 128)) for j in range(8)]
    ws = [jnp.broadcast_to(w[:, 4 * j : 4 * j + 1], (N, 128)) for j in range(8)]
    at = 0
    for count, ref, above in ((4, n2_ref, n3_ref), (2, n3_ref, n4_ref), (1, n4_ref, n5_ref)):
        next_v, next_w = [], []
        for j in range(count):
            v1, v2, w1, w2 = vs[2 * j], vs[2 * j + 1], ws[2 * j], ws[2 * j + 1]
            v_ref[at], w_ref[at] = v1, w2
            at += 1
            yv, yw = rhs(v1), rhs(w2)
            u_map = above[j, 3] if count > 1 else above[0]
            next_v.append(v1 + v2 + dot(ref[2 * j + 1, 0], yv))
            next_w.append(w1 + w2 + dot(ref[2 * j, 1], yw) + dot(u_map, yv))
        vs, ws = next_v, next_w
    lane = lanes((N, 128))
    pay_ref[:N] = root_ref[:N]
    tail = jnp.where(lane == N, vs[0] * cols_ref[0] + flux_ref[...], ws[0])
    pay_ref[N:] = jnp.where(lane < N, root_ref[N:], tail)


def wide(packed):
    x = packed.astype(f32)
    return x + roll(x, N)


def prepare(pair_ref, v_ref, w_ref, n1_ref, n2_ref, n3_ref, n4_ref, t_ref, add_ref, resp_ref):
    lane = lanes((N, 128))
    part = lane % CELLS
    eye = eye2()
    nodes = [(None, None, None)]
    ss = jnp.zeros((N, 128), f32)
    aa = jnp.zeros((N, 128), f32)
    vec = {32: 6, 16: 4, 8: 0}
    for size, ref in ((32, n4_ref), (16, n3_ref), (8, n2_ref)):
        ys, ya = rhs(ss), rhs(aa)
        new_s = jnp.zeros((N, 128), f32)
        new_a = jnp.zeros((N, 128), f32)
        children = []
        for j in range(CELLS // size):
            into_s, cross, into_a = nodes[j]
            ep, eq, kw = ref[2 * j, 0], ref[2 * j + 1, 1], ref[2 * j + 1, 2]
            t = wide(kw) + mm(kw, ep)
            kt = pack(t)
            v1, w2 = v_ref[vec[size] + j], w_ref[vec[size] + j]
            t0 = w2 + dot(kw, rhs(v1))
            here = part // size == j
            if size == 32:
                new_s, new_a = v1, t0
            else:
                new_s = jnp.where(here, v1 + dot(ep, ys), new_s)
                new_a = jnp.where(here, t0 + dot(eq, ya) + dot(kt, ys), new_a)
            through = t if into_s is None else dot(kt, rhs(into_s))
            if cross is not None:
                through = through + cross + dot(eq, rhs(cross))
            first_a = eye + wide(eq) if into_a is None else into_a + dot(eq, rhs(into_a))
            second_s = eye + wide(ep) if into_s is None else into_s + dot(ep, rhs(into_s))
            children += [(into_s, through, first_a), (second_s, cross, into_a)]
        nodes = children
        upper = part % size >= size // 2
        ss, aa = jnp.where(upper, ss + new_s, ss), jnp.where(upper, aa, aa + new_a)
    add_ref[2], add_ref[3] = ss, aa
    for j, maps in enumerate(nodes):
        for i, value in enumerate(maps):
            if value is not None:
                resp_ref[j, i] = pack(value)

    def repeat(x):
        x = x + roll(x, CELLS)
        return x + roll(x, 2 * CELLS)

    first = jnp.logical_and(lane % 4 == 0, lane < CELLS)
    v0, v1, w0, w1 = [jnp.where(first, pair_ref[i], 0.0) for i in range(4)]
    y = rhs(v0)
    acc_a = jnp.zeros((N, 128), f32)
    for j in range(8):
        kw = n1_ref[2 * j + 1, 2]
        t_ref[j] = pack(wide(kw) + mm(kw, n1_ref[2 * j, 0]))
        acc_a = jnp.where(lane == 4 * j, dot(kw, y), acc_a)
    acc_a = acc_a + w1
    spread_v = v0 + roll(v0, 1)
    spread_a = acc_a + roll(acc_a, 1)
    add_ref[0] = repeat(spread_v + roll(spread_v, 2))
    add_ref[1] = repeat(spread_a + roll(spread_a, 2))
    add_ref[4] = repeat(w0 + roll(w1, 2) + roll(v0, 1) + roll(v1, 3))


def unpack(b):
    low = lanes((N, 128)) < N
    b1, b2 = b[:N], b[N:]
    r1, r2 = roll(b1, N), roll(b2, N)
    x = jnp.where(low, b1, r1)
    y = jnp.where(low, r1, b1)
    z = jnp.where(low, b2, r2)
    g = jnp.broadcast_to(b2[:, N : N + 1], (N, 128))
    h = jnp.broadcast_to(b2[:, N + 1 : N + 2], (N, 128))
    return x, y, z, g, h


def join(one, two, last=False):
    p1, q1, w1, v1, h1 = one
    p2, q2, w2, v2, h2 = two
    kq1, kp2, kw2 = pack(q1), pack(p2), pack(w2)
    yp1, yv1 = rhs(p1), rhs(v1)
    t = dot(kw2, yp1)
    th = h2 + dot(kw2, yv1)
    v = v2 + dot(kp2, yv1)
    yt, yth = rhs(t), rhs(th)
    w = w1 + dot(kq1, yt)
    h = h1 + dot(kq1, yth)
    yq2 = rhs(q2)
    p, q = (None, None) if last else (dot(kp2, yp1), dot(kq1, yq2))
    return (p, q, w, v, h), (t, th, yp1, yv1, yq2, yt, yth)


def track_first(is_low, one, two, extra):
    eye = eye2()
    t, th = extra[:2]
    return (
        jnp.where(is_low, eye, one[0]),
        jnp.where(is_low, two[1], eye),
        jnp.where(is_low, t, 0.0),
        jnp.where(is_low, 0.0, one[3]),
        jnp.where(is_low, th, 0.0),
    )


def track(is_low, fun, extra):
    f, hh, k, g, e = fun
    t, th, yp1, yv1, yq2, yt, yth = extra
    x1 = pack(jnp.where(is_low, hh, f))
    x2 = pack(jnp.where(is_low, hh, k))
    prod1 = dot(x1, jnp.where(is_low, yq2, yp1))
    prod2 = dot(x2, jnp.where(is_low, yt, yp1))
    vec1 = dot(x1, yv1)
    vec2 = dot(x2, jnp.where(is_low, yth, yv1))
    return (
        jnp.where(is_low, f, prod1),
        jnp.where(is_low, prod1, hh),
        jnp.where(is_low, k + prod2, prod2),
        jnp.where(is_low, g, g + vec1),
        e + vec2,
    )


def put_map(ref, p, q, w, v, h, last=False):
    lane = lanes((N, 128))
    low = lane < N
    tail = jnp.where(low, w, jnp.where(lane == N, v, h))
    if last:
        ref[...] = tail
    else:
        ref[:N] = jnp.where(low, p, q)
        ref[N:] = tail


def fill(slots, at, refs):
    for bits, ref in enumerate(refs):
        slots[at ^ bits] = ref[...]
    return [unpack(slots[i]) for i in range(4)]


def combine_four(own_ref, x1_ref, x2_ref, x3_ref, after_ref, out_ref, fun_out, slots):
    del after_ref
    at = lax.axis_index("depth") % 4
    maps = fill(slots, at, (own_ref, x1_ref, x2_ref, x3_ref))
    lower, extra_lower = join(maps[0], maps[1])
    upper, extra_upper = join(maps[2], maps[3])
    in_lower = at < 2
    mine = lambda x, y: [jnp.where(in_lower, a, b) for a, b in zip(x, y)]
    fun = track_first(
        at % 2 == 0, mine(maps[0], maps[2]), mine(maps[1], maps[3]), mine(extra_lower[:2], extra_upper[:2])
    )
    total, extra = join(lower, upper)
    put_map(out_ref, *total)
    put_map(fun_out, *track(in_lower, fun, extra))


def combine_two(own_ref, other_ref, fun_ref, out_ref, fun_out):
    is_low = lax.axis_index("depth") % ZS < 4
    own, other = own_ref[...], other_ref[...]
    total, extra = join(unpack(jnp.where(is_low, own, other)), unpack(jnp.where(is_low, other, own)))
    put_map(out_ref, *total)
    for i, value in enumerate(track(is_low, unpack(fun_ref[...]), extra)):
        fun_out[i] = value


def downsweep(own_ref, y1_ref, y2_ref, y3_ref, fun_ref, cols_ref, add_ref, resp_ref, quad_ref, n1_ref, t_ref, out_ref,
              slots):
    at = lax.axis_index("depth") // ZS
    maps = fill(slots, at, (own_ref, y1_ref, y2_ref, y3_ref))
    lower, extra_lower = join(maps[0], maps[1], last=True)
    upper, extra_upper = join(maps[2], maps[3], last=True)
    is_low = at < 2
    extra = [jnp.where(is_low, a, b) for a, b in zip(extra_lower, extra_upper)]
    f, hh, k, g, e = track(at % 2 == 0, [fun_ref[i] for i in range(5)], extra)
    yv = rhs(lower[3])
    t = upper[4] + dot(pack(upper[2]), yv)
    up = g + dot(pack(f), yv)
    aa = e + dot(pack(jnp.where(is_low, hh, k)), jnp.where(is_low, rhs(t), yv))
    ss = jnp.where(is_low, g, up) * cols_ref[1]
    lane = lanes((N, 128)) % CELLS
    ys, ya = rhs(ss), rhs(aa)
    part_s, part_a = ss, aa
    for j in range(8):
        here = lane // 4 == j
        if j > 0:
            part_s = jnp.where(here, dot(resp_ref[j, 0], ys), part_s)
        if j < 7:
            part_a = jnp.where(here, dot(resp_ref[j, 1], ys) + dot(resp_ref[j, 2], ya), part_a)
    ss, aa = part_s + add_ref[2], part_a + add_ref[3]
    ys, ya = rhs(ss), rhs(aa)
    ds = jnp.zeros((N, 128), f32)
    da = jnp.zeros((N, 128), f32)
    for j in range(8):
        here = lane // 4 == j
        ds = jnp.where(here, dot(n1_ref[2 * j, 0], ys), ds)
        da = jnp.where(here, dot(n1_ref[2 * j + 1, 1], ya) + dot(t_ref[j], ys), da)
    upper = lane % 4 >= 2
    ss, aa = (
        jnp.where(upper, ss + add_ref[0] + ds, ss),
        jnp.where(upper, aa, aa + add_ref[1] + da),
    )
    y = pair_rhs(ss, aa)
    x = jnp.zeros((N, 128), f32)
    for j in range(CELLS // 2):
        x = jnp.where(lane == 2 * j, jnp.dot(quad_ref[j, 2], y, preferred_element_type=f32), x)
        x = jnp.where(lane == 2 * j + 1, jnp.dot(quad_ref[j, 3], y, preferred_element_type=f32), x)
    x = x + roll(x, CELLS) + (aa + add_ref[4] + jnp.where(lane % 2 == 1, ss, 0.0))
    out_ref[...] = x.T[:CELLS]


def sds(*shape, dtype=f32):
    return jax.ShapeDtypeStruct(shape, dtype)


def call(body, outs, *args, scratch=(), smem=0, hbm=0, flops=0, name=None):
    args = [pltpu.with_memory_space_constraint(x, pltpu.HBM) if smem <= i < smem + hbm else x for i, x in enumerate(args)]
    spaces = [pltpu.SMEM] * smem + [pltpu.HBM] * hbm + [pltpu.VMEM] * (len(args) - smem - hbm)
    return pl.pallas_call(
        body,
        out_shape=outs,
        in_specs=[pl.BlockSpec(memory_space=space) for space in spaces],
        out_specs=jax.tree.map(lambda _: pl.BlockSpec(memory_space=pltpu.VMEM), outs),
        scratch_shapes=scratch,
        cost_estimate=pl.CostEstimate(flops=flops, bytes_accessed=1 << 16, transcendentals=0),
        name=name,
        compiler_params=pltpu.CompilerParams(vmem_limit_bytes=VLIM),
    )(*args)


def node(count):
    return sds(count, 4, N, 128, dtype=bf16)


def on_device(densities, source, jacobian, pattern, transport, lateral, neighbours, factor, coupling):
    line_count, cell_count, species = densities.shape
    u = densities.reshape(CELLS, N)
    src = source.reshape(CELLS, N)
    tran = transport.reshape(CELLS, N)
    lat = lateral.reshape(CELLS, N)
    coup = coupling.reshape(CELLS, N)
    jac = jacobian.reshape(CELLS, N * N)
    fac = factor.reshape(4, 8, 32, 128).transpose(0, 2, 1, 3).reshape(1024, 128)

    def xor_lat(value, bits):
        return lax.ppermute(value, "lat", [(i, i ^ bits) for i in range(8)])

    def xor_depth(value, bits):
        return lax.ppermute(value, "depth", [(i, i ^ bits) for i in range(32)])

    line_a = xor_lat(densities, 1)
    part, flux = call(
        react, (sds(CELLS, N), sds(N, 128)), jac, u, src, tran, pattern, hbm=5, flops=1 << 30, name="react",
        scratch=[pltpu.VMEM((CELLS, N * N), f32)] + [pltpu.VMEM((CELLS, N), f32)] * 3
        + [pltpu.VMEM((8, 8), jnp.int32), pltpu.SemaphoreType.DMA((8,))],
    )
    line_b = xor_lat(jnp.concatenate([densities, line_a], axis=0), 2)
    quad, n1, full, cols = call(
        tree_leaves,
        (sds(16, 4, N, 256, dtype=bf16), sds(16, 3, N, 128, dtype=bf16), sds(16, 3, N, 128), sds(2, N, 128)),
        fac, coup, part, scratch=[pltpu.VMEM((2, N, 128), f32)], flops=2 << 30, name="tree_leaves",
    )
    top_even = xor_depth(lax.optimization_barrier((densities, cols))[0], 1)
    top_odd = lax.ppermute(
        lax.optimization_barrier((densities, line_b))[0], ("depth", "lat"),
        [(8 * i + l, 8 * (i + 1 if i % 2 else i - 1) + l if 0 < i < 31 else 8 * i + (l ^ 1))
         for i in range(32) for l in range(8)],
    )
    line_c = xor_lat(jnp.concatenate([densities, line_a, line_b], axis=0), 6)
    n2, n3, n4, n5, root = call(
        tree_upper,
        (node(8), node(4), node(2), sds(1, N, 128, dtype=bf16), sds(128, 128)),
        n1, full, coup, cols, part, scratch=[pltpu.VMEM((8, 3, N, 128), f32), pltpu.VMEM((4, 3, N, 128), f32)],
        flops=2 << 30, name="tree_upper",
    )
    pay, pair, vs, ws = call(
        upsweep, (sds(128, 128), sds(4, N, 128), sds(7, N, 128), sds(7, N, 128)),
        neighbours, part, line_a, line_b, line_c, top_even, top_odd, flux, u, tran, lat, coup, cols, quad, n1, n2, n3, n4, n5, root,
        smem=1, flops=1 << 25, name="upsweep",
    )
    others = [xor_depth(pay, bits) for bits in (1, 2, 3)]
    tees, adds, resp = call(
        prepare,
        (sds(8, N, 128, dtype=bf16), sds(5, N, 128), sds(8, 3, N, 128, dtype=bf16)),
        pair, vs, ws, n1, n2, n3, n4, flops=1 << 30, name="prepare",
    )
    slots = [pltpu.VMEM((4, 128, 128), f32)]
    pay, fun = call(
        combine_four, (sds(128, 128), sds(128, 128)), pay, *others, adds, scratch=slots, flops=1 << 24, name="combine_four",
    )
    other = xor_depth(pay, 7)
    pay, fun = call(
        combine_two, (sds(128, 128), sds(5, N, 128)), pay, other, fun, flops=1 << 24, name="combine_two",
    )
    others = [xor_depth(pay, bits) for bits in (8, 16, 24)]
    out = call(
        downsweep, sds(CELLS, N), pay, *others, fun, cols, adds, resp, quad, n1, tees, scratch=slots, flops=1 << 25,
        name="downsweep",
    )
    return out.reshape(line_count, cell_count, species)


def solution(mesh):
    return jax.shard_map(
        on_device,
        mesh=mesh,
        in_specs=(
            P("lat", "depth", None),
            P("lat", "depth", None),
            P("lat", "depth", None),
            P(),
            P("lat", "depth", None),
            P("lat", "depth", None),
            P("lat", None),
            P("lat", "depth", None),
            P("lat", "depth", None),
        ),
        out_specs=P("lat", "depth", None),
        check_vma=False,
    )
```

```python
import jax
import jax.numpy as jnp
from jax import lax
from jax.experimental import pallas as pl
from jax.experimental.pallas import tpu as pltpu
from jax.sharding import PartitionSpec as P

f32 = jnp.float32
bf16 = jnp.bfloat16

CELLS = 32
N = 64
ZS = 8
VLIM = 16 << 20


def lanes(shape):
    return lax.broadcasted_iota(jnp.int32, shape, len(shape) - 1)


def roll(x, shift):
    shift = shift % x.shape[-1]
    return x if shift == 0 else pltpu.roll(x, shift, x.ndim - 1)


def pack(dup):
    hi = dup.astype(bf16).astype(f32)
    return jnp.where(lanes(dup.shape) < N, hi, dup - hi).astype(bf16)


def mm(a, b):
    r = jnp.dot(a, jnp.concatenate([b, b], axis=0), preferred_element_type=f32)
    return r + roll(r, N)


def rhs(x):
    hi = x.astype(bf16)
    lo = (x - hi.astype(f32)).astype(bf16)
    return jnp.concatenate([hi, hi, lo, lo], axis=0)


def dot(a, y):
    return jnp.dot(jnp.concatenate([a, a], axis=1), y, preferred_element_type=f32)


def column(row):
    return jnp.broadcast_to(row, (128, N)).T


def pair(a, b):
    low = lanes(a.shape) < N
    a_hi, b_hi = a.astype(bf16).astype(f32), b.astype(bf16).astype(f32)
    hi = jnp.where(low, a_hi, b_hi).astype(bf16)
    lo = jnp.where(low, a - a_hi, b - b_hi).astype(bf16)
    return jnp.concatenate([hi, lo], axis=1)


def pair_rhs(x, y):
    def split(z):
        hi = z.astype(bf16).astype(f32)
        return jnp.where(lanes(z.shape) % 64 < CELLS, hi, z - hi).astype(bf16)

    a, b = split(x), split(y)
    return jnp.concatenate([a, b, a, b], axis=0)


def eye2():
    return jnp.where(lanes((N, 128)) % N == lax.broadcasted_iota(jnp.int32, (N, 128), 0), 1.0, 0.0)


def put(node, full, j, p, q, w, u=None):
    node[j, 0], node[j, 1], node[j, 2] = pack(p), pack(q), pack(w)
    full[j, 0], full[j, 1], full[j, 2] = p, q, w
    if u is not None:
        node[j, 3] = pack(u)


def tree_leaves(fac_ref, coup_ref, after_ref, quad_ref, n1_ref, full_ref, cols_ref, rows):
    del after_ref
    c = coup_ref[...]
    cols_ref[0] = column(c[CELLS - 1 : CELLS])
    cols_ref[1] = column(1.0 / c[0:1])
    c2 = jnp.concatenate([c, c], axis=1)
    low = lanes((CELLS, 128)) < N
    eye = eye2()

    def leaf(k):
        g, s = divmod(k, 8)
        x = fac_ref[pl.ds(g * 256 + s, 32, stride=8), :]
        y = roll(x, N)
        rows[k % 2, pl.ds(0, 32, stride=2), :] = jnp.where(low, x, y)
        rows[k % 2, pl.ds(1, 32, stride=2), :] = jnp.where(low, y, x)
        a = rows[k % 2]
        before = max(k - 1, 0)
        return a * c2[before : before + 1] - eye, a * c2[k : k + 1] - eye

    for j in range(CELLS // 2):
        p1, q1 = leaf(2 * j)
        p2, q2 = leaf(2 * j + 1)
        kq1 = pack(q1)
        p = p1 + p2 + dot(pack(p2), rhs(p1))
        q = q1 + q2 + dot(kq1, rhs(q2))
        u = eye + q1 + p2 + dot(kq1, rhs(p2))
        w = (eye + eye) + p1 + q1 + p + dot(kq1, rhs(p))
        put(n1_ref, full_ref, j, p, q, w)
        quad_ref[j, 0] = pair(p, p2)
        quad_ref[j, 1] = pair(w, u)
        quad_ref[j, 2] = pair(w, q)
        quad_ref[j, 3] = pair(p, q2)


def tree_upper(n1_ref, full_ref, coup_ref, cols_ref, after_ref, n2_ref, n3_ref, n4_ref, n5_ref, root_ref, fa, fb):
    del after_ref
    node, full = n1_ref, full_ref
    for count, node_to, full_to in ((8, n2_ref, fa), (4, n3_ref, fb), (2, n4_ref, fa), (1, None, None)):
        for j in range(count):
            one, two = 2 * j, 2 * j + 1
            kq1, yp1 = node[one, 1], rhs(full[one, 0])
            u = full[two, 2] + dot(kq1, rhs(full[two, 2]))
            p = full[one, 0] + full[two, 0] + dot(node[two, 0], yp1)
            q = full[one, 1] + full[two, 1] + dot(kq1, rhs(full[two, 1]))
            ku = pack(u)
            w = full[one, 2] + u + dot(ku, yp1)
            if node_to is None:
                eye = eye2()
                n5_ref[0] = ku
                first = coup_ref[0:1]
                scale = 1.0 / jnp.concatenate([first, first], axis=1)
                root_ref[:N] = jnp.where(lanes((N, 128)) < N, (p + eye) * cols_ref[0] * scale, q + eye)
                root_ref[N:] = w * scale
            else:
                put(node_to, full_to, j, p, q, w, u)
        node, full = node_to, full_to


def react(jac_hbm, dens_hbm, src_hbm, tran_hbm, pat_hbm, out_ref, flux_ref, jac_ref, dens_ref, src_ref, tran_ref,
          pat_ref, sems):
    parts = [(slice(None), pl.ds(i * 1024, 1024)) for i in range(4)]
    pairs = [(dens_hbm, dens_ref), (pat_hbm, pat_ref)] + [(jac_hbm.at[part], jac_ref.at[part]) for part in parts]
    pairs += [(src_hbm, src_ref), (tran_hbm, tran_ref)]
    copies = [pltpu.make_async_copy(a, b, sems.at[i]) for i, (a, b) in enumerate(pairs)]
    for copy in copies:
        copy.start()
    half = lanes((128, N)) % 2 == lax.broadcasted_iota(jnp.int32, (128, N), 0) // N
    half = jnp.where(half, 1.0, 0.0).astype(bf16)
    copies[0].wait()
    copies[1].wait()
    u = dens_ref[...]
    u2 = jnp.concatenate([u, u], axis=1)
    lane8 = lanes((8, 128))
    pat = pat_ref[...].astype(f32)
    mask_rows = jnp.zeros((8, 128), f32)
    for t in range(8):
        mask_rows = jnp.where((lane8 % N) // 8 == t, pat[:, t : t + 1], mask_rows)
    lane = lanes((CELLS, N))
    acc = jnp.zeros((CELLS, N), f32)
    for m in range(32):
        if m % 8 == 0:
            copies[2 + m // 8].wait()
        y = jac_ref[:, m * 128 : (m + 1) * 128] * (u2 * mask_rows[m // 4 : m // 4 + 1])
        hi = y.astype(bf16)
        lo = (y - hi.astype(f32)).astype(bf16)
        z = jnp.dot(hi, half, preferred_element_type=f32) + jnp.dot(lo, half, preferred_element_type=f32)
        acc = jnp.where(lane // 2 == m, z, acc)
    copies[6].wait()
    copies[7].wait()
    tran = tran_ref[...]
    flux = tran * u
    flux_ref[...] = column(flux[CELLS - 1 : CELLS])
    row = lax.broadcasted_iota(jnp.int32, (CELLS, N), 0)
    lower = jnp.where(row == 0, 0.0, pltpu.roll(flux, 1, 0))
    upper = jnp.where(row == CELLS - 1, 0.0, pltpu.roll(u, CELLS - 1, 0))
    out_ref[...] = src_ref[...] - acc + lower + tran * upper


def upsweep(neigh_ref, part_ref, a_ref, b_ref, c_ref, top_ref, flux_ref, dens_ref, tran_ref, lat_ref, coup_ref, cols_ref,
            quad_ref, n1_ref, n2_ref, n3_ref, n4_ref, n5_ref, root_ref, pay_ref, pair_ref, v_ref, w_ref):
    me = lax.axis_index("lat")
    u = dens_ref[...]
    total = jnp.zeros((CELLS, N), f32)
    lines = [(0, u), (1, a_ref[0])] + [(2 + i, b_ref[i]) for i in range(2)]
    lines += [((6, 7, 4, 5)[i], c_ref[i]) for i in range(4)]
    for offset, value in lines:
        line = me ^ offset
        count = jnp.int32(0)
        for j in range(4):
            count = count + (neigh_ref[0, j] == line).astype(jnp.int32)
        total = total + count.astype(f32) * value
    row = lax.broadcasted_iota(jnp.int32, (CELLS, N), 0)
    r = part_ref[...] - lat_ref[...] * (4.0 * u - total)
    above = jnp.where(lax.axis_index("depth") == lax.axis_size("depth") - 1, 0.0, top_ref[0, 0:1])
    r = r + jnp.where(row == CELLS - 1, tran_ref[...] * above, 0.0)
    c = coup_ref[...]
    g = r / jnp.where(row == 0, c, pltpu.roll(c, 1, 0))
    x = []
    for i in range(4):
        rolled = g if i == 0 else pltpu.roll(g, CELLS - i, 0)
        x.append(jnp.concatenate([rolled, rolled], axis=0).T)
    lane2 = lanes((N, N)) % CELLS
    lane = lanes((N, CELLS))
    pair_v, pair_w = [], []
    for half in range(2):
        x0, x1 = x[2 * half], x[2 * half + 1]
        y = pair_rhs(x0, x1)
        v = jnp.zeros((N, N), f32)
        w = jnp.zeros((N, N), f32)
        for j in range(8):
            at = 2 * j + half
            here = lane2 == 4 * j
            v = jnp.where(here, jnp.dot(quad_ref[at, 0], y, preferred_element_type=f32), v)
            w = jnp.where(here, jnp.dot(quad_ref[at, 1], y, preferred_element_type=f32), w)
        v = v[:, :CELLS] + v[:, CELLS:] + x0[:, :CELLS] + x1[:, :CELLS]
        w = w[:, :CELLS] + w[:, CELLS:]
        pair_v.append(v)
        pair_w.append(w)
        pair_ref[half, :, 0:CELLS] = pair_v[half]
        pair_ref[2 + half, :, 0:CELLS] = w
    yv, yw = rhs(pair_v[0]), rhs(pair_w[1])
    v, w = pair_v[0] + pair_v[1], pair_w[0] + pair_w[1]
    dv = jnp.zeros((N, CELLS), f32)
    dw = jnp.zeros((N, CELLS), f32)
    for j in range(8):
        here = lane == 4 * j
        dv = jnp.where(here, dot(n1_ref[2 * j + 1, 0], yv), dv)
        dw = jnp.where(here, dot(n1_ref[2 * j, 1], yw) + dot(n2_ref[j, 3], yv), dw)
    v, w = v + dv, w + dw
    vs = [jnp.broadcast_to(v[:, 4 * j : 4 * j + 1], (N, 128)) for j in range(8)]
    ws = [jnp.broadcast_to(w[:, 4 * j : 4 * j + 1], (N, 128)) for j in range(8)]
    at = 0
    for count, ref, above in ((4, n2_ref, n3_ref), (2, n3_ref, n4_ref), (1, n4_ref, n5_ref)):
        next_v, next_w = [], []
        for j in range(count):
            v1, v2, w1, w2 = vs[2 * j], vs[2 * j + 1], ws[2 * j], ws[2 * j + 1]
            v_ref[at], w_ref[at] = v1, w2
            at += 1
            yv, yw = rhs(v1), rhs(w2)
            u_map = above[j, 3] if count > 1 else above[0]
            next_v.append(v1 + v2 + dot(ref[2 * j + 1, 0], yv))
            next_w.append(w1 + w2 + dot(ref[2 * j, 1], yw) + dot(u_map, yv))
        vs, ws = next_v, next_w
    lane = lanes((N, 128))
    pay_ref[:N] = root_ref[:N]
    tail = jnp.where(lane == N, vs[0] * cols_ref[0] + flux_ref[...], ws[0])
    pay_ref[N:] = jnp.where(lane < N, root_ref[N:], tail)


def wide(packed):
    x = packed.astype(f32)
    return x + roll(x, N)


def prepare(pair_ref, v_ref, w_ref, n1_ref, n2_ref, n3_ref, n4_ref, t_ref, add_ref, resp_ref):
    lane = lanes((N, 128))
    part = lane % CELLS
    eye = eye2()
    nodes = [(None, None, None)]
    ss = jnp.zeros((N, 128), f32)
    aa = jnp.zeros((N, 128), f32)
    vec = {32: 6, 16: 4, 8: 0}
    for size, ref in ((32, n4_ref), (16, n3_ref), (8, n2_ref)):
        ys, ya = rhs(ss), rhs(aa)
        new_s = jnp.zeros((N, 128), f32)
        new_a = jnp.zeros((N, 128), f32)
        children = []
        for j in range(CELLS // size):
            into_s, cross, into_a = nodes[j]
            ep, eq, kw = ref[2 * j, 0], ref[2 * j + 1, 1], ref[2 * j + 1, 2]
            t = wide(kw) + mm(kw, ep)
            kt = pack(t)
            v1, w2 = v_ref[vec[size] + j], w_ref[vec[size] + j]
            t0 = w2 + dot(kw, rhs(v1))
            here = part // size == j
            if size == 32:
                new_s, new_a = v1, t0
            else:
                new_s = jnp.where(here, v1 + dot(ep, ys), new_s)
                new_a = jnp.where(here, t0 + dot(eq, ya) + dot(kt, ys), new_a)
            through = t if into_s is None else dot(kt, rhs(into_s))
            if cross is not None:
                through = through + cross + dot(eq, rhs(cross))
            first_a = eye + wide(eq) if into_a is None else into_a + dot(eq, rhs(into_a))
            second_s = eye + wide(ep) if into_s is None else into_s + dot(ep, rhs(into_s))
            children += [(into_s, through, first_a), (second_s, cross, into_a)]
        nodes = children
        upper = part % size >= size // 2
        ss, aa = jnp.where(upper, ss + new_s, ss), jnp.where(upper, aa, aa + new_a)
    add_ref[2], add_ref[3] = ss, aa
    for j, maps in enumerate(nodes):
        for i, value in enumerate(maps):
            if value is not None:
                resp_ref[j, i] = pack(value)

    def repeat(x):
        x = x + roll(x, CELLS)
        return x + roll(x, 2 * CELLS)

    first = jnp.logical_and(lane % 4 == 0, lane < CELLS)
    v0, v1, w0, w1 = [jnp.where(first, pair_ref[i], 0.0) for i in range(4)]
    y = rhs(v0)
    acc_a = jnp.zeros((N, 128), f32)
    for j in range(8):
        kw = n1_ref[2 * j + 1, 2]
        t_ref[j] = pack(wide(kw) + mm(kw, n1_ref[2 * j, 0]))
        acc_a = jnp.where(lane == 4 * j, dot(kw, y), acc_a)
    acc_a = acc_a + w1
    spread_v = v0 + roll(v0, 1)
    spread_a = acc_a + roll(acc_a, 1)
    add_ref[0] = repeat(spread_v + roll(spread_v, 2))
    add_ref[1] = repeat(spread_a + roll(spread_a, 2))
    add_ref[4] = repeat(w0 + roll(w1, 2) + roll(v0, 1) + roll(v1, 3))


def unpack(b):
    low = lanes((N, 128)) < N
    b1, b2 = b[:N], b[N:]
    r1, r2 = roll(b1, N), roll(b2, N)
    x = jnp.where(low, b1, r1)
    y = jnp.where(low, r1, b1)
    z = jnp.where(low, b2, r2)
    g = jnp.broadcast_to(b2[:, N : N + 1], (N, 128))
    h = jnp.broadcast_to(b2[:, N + 1 : N + 2], (N, 128))
    return x, y, z, g, h


def join(one, two, last=False):
    p1, q1, w1, v1, h1 = one
    p2, q2, w2, v2, h2 = two
    kq1, kp2, kw2 = pack(q1), pack(p2), pack(w2)
    yp1, yv1 = rhs(p1), rhs(v1)
    t = dot(kw2, yp1)
    th = h2 + dot(kw2, yv1)
    v = v2 + dot(kp2, yv1)
    yt, yth = rhs(t), rhs(th)
    w = w1 + dot(kq1, yt)
    h = h1 + dot(kq1, yth)
    yq2 = rhs(q2)
    p, q = (None, None) if last else (dot(kp2, yp1), dot(kq1, yq2))
    return (p, q, w, v, h), (t, th, yp1, yv1, yq2, yt, yth)


def track_first(is_low, one, two, extra):
    eye = eye2()
    t, th = extra[:2]
    return (
        jnp.where(is_low, eye, one[0]),
        jnp.where(is_low, two[1], eye),
        jnp.where(is_low, t, 0.0),
        jnp.where(is_low, 0.0, one[3]),
        jnp.where(is_low, th, 0.0),
    )


def track(is_low, fun, extra):
    f, hh, k, g, e = fun
    t, th, yp1, yv1, yq2, yt, yth = extra
    x1 = pack(jnp.where(is_low, hh, f))
    x2 = pack(jnp.where(is_low, hh, k))
    prod1 = dot(x1, jnp.where(is_low, yq2, yp1))
    prod2 = dot(x2, jnp.where(is_low, yt, yp1))
    vec1 = dot(x1, yv1)
    vec2 = dot(x2, jnp.where(is_low, yth, yv1))
    return (
        jnp.where(is_low, f, prod1),
        jnp.where(is_low, prod1, hh),
        jnp.where(is_low, k + prod2, prod2),
        jnp.where(is_low, g, g + vec1),
        e + vec2,
    )


def put_map(ref, p, q, w, v, h, last=False):
    lane = lanes((N, 128))
    low = lane < N
    tail = jnp.where(low, w, jnp.where(lane == N, v, h))
    if last:
        ref[...] = tail
    else:
        ref[:N] = jnp.where(low, p, q)
        ref[N:] = tail


def fill(slots, at, refs):
    for bits, ref in enumerate(refs):
        slots[at ^ bits] = ref[...]
    return [unpack(slots[i]) for i in range(4)]


def combine_four(own_ref, x1_ref, x2_ref, x3_ref, after_ref, out_ref, fun_out, slots):
    del after_ref
    at = lax.axis_index("depth") % 4
    maps = fill(slots, at, (own_ref, x1_ref, x2_ref, x3_ref))
    lower, extra_lower = join(maps[0], maps[1])
    upper, extra_upper = join(maps[2], maps[3])
    in_lower = at < 2
    mine = lambda x, y: [jnp.where(in_lower, a, b) for a, b in zip(x, y)]
    fun = track_first(
        at % 2 == 0, mine(maps[0], maps[2]), mine(maps[1], maps[3]), mine(extra_lower[:2], extra_upper[:2])
    )
    total, extra = join(lower, upper)
    put_map(out_ref, *total)
    put_map(fun_out, *track(in_lower, fun, extra))


def combine_two(own_ref, other_ref, fun_ref, out_ref, fun_out):
    is_low = lax.axis_index("depth") % ZS < 4
    own, other = own_ref[...], other_ref[...]
    total, extra = join(unpack(jnp.where(is_low, own, other)), unpack(jnp.where(is_low, other, own)))
    put_map(out_ref, *total)
    for i, value in enumerate(track(is_low, unpack(fun_ref[...]), extra)):
        fun_out[i] = value


def downsweep(own_ref, y1_ref, y2_ref, y3_ref, fun_ref, cols_ref, add_ref, resp_ref, quad_ref, n1_ref, t_ref, out_ref,
              slots):
    at = lax.axis_index("depth") // ZS
    maps = fill(slots, at, (own_ref, y1_ref, y2_ref, y3_ref))
    lower, extra_lower = join(maps[0], maps[1], last=True)
    upper, extra_upper = join(maps[2], maps[3], last=True)
    is_low = at < 2
    extra = [jnp.where(is_low, a, b) for a, b in zip(extra_lower, extra_upper)]
    f, hh, k, g, e = track(at % 2 == 0, [fun_ref[i] for i in range(5)], extra)
    yv = rhs(lower[3])
    t = upper[4] + dot(pack(upper[2]), yv)
    up = g + dot(pack(f), yv)
    aa = e + dot(pack(jnp.where(is_low, hh, k)), jnp.where(is_low, rhs(t), yv))
    ss = jnp.where(is_low, g, up) * cols_ref[1]
    lane = lanes((N, 128)) % CELLS
    ys, ya = rhs(ss), rhs(aa)
    part_s, part_a = ss, aa
    for j in range(8):
        here = lane // 4 == j
        if j > 0:
            part_s = jnp.where(here, dot(resp_ref[j, 0], ys), part_s)
        if j < 7:
            part_a = jnp.where(here, dot(resp_ref[j, 1], ys) + dot(resp_ref[j, 2], ya), part_a)
    ss, aa = part_s + add_ref[2], part_a + add_ref[3]
    ys, ya = rhs(ss), rhs(aa)
    ds = jnp.zeros((N, 128), f32)
    da = jnp.zeros((N, 128), f32)
    for j in range(8):
        here = lane // 4 == j
        ds = jnp.where(here, dot(n1_ref[2 * j, 0], ys), ds)
        da = jnp.where(here, dot(n1_ref[2 * j + 1, 1], ya) + dot(t_ref[j], ys), da)
    upper = lane % 4 >= 2
    ss, aa = (
        jnp.where(upper, ss + add_ref[0] + ds, ss),
        jnp.where(upper, aa, aa + add_ref[1] + da),
    )
    y = pair_rhs(ss, aa)
    x = jnp.zeros((N, 128), f32)
    for j in range(CELLS // 2):
        x = jnp.where(lane == 2 * j, jnp.dot(quad_ref[j, 2], y, preferred_element_type=f32), x)
        x = jnp.where(lane == 2 * j + 1, jnp.dot(quad_ref[j, 3], y, preferred_element_type=f32), x)
    x = x + roll(x, CELLS) + (aa + add_ref[4] + jnp.where(lane % 2 == 1, ss, 0.0))
    out_ref[...] = x.T[:CELLS]


def sds(*shape, dtype=f32):
    return jax.ShapeDtypeStruct(shape, dtype)


def call(body, outs, *args, scratch=(), smem=0, hbm=0, flops=0, name=None):
    args = [pltpu.with_memory_space_constraint(x, pltpu.HBM) if smem <= i < smem + hbm else x for i, x in enumerate(args)]
    spaces = [pltpu.SMEM] * smem + [pltpu.HBM] * hbm + [pltpu.VMEM] * (len(args) - smem - hbm)
    return pl.pallas_call(
        body,
        out_shape=outs,
        in_specs=[pl.BlockSpec(memory_space=space) for space in spaces],
        out_specs=jax.tree.map(lambda _: pl.BlockSpec(memory_space=pltpu.VMEM), outs),
        scratch_shapes=scratch,
        cost_estimate=pl.CostEstimate(flops=flops, bytes_accessed=1 << 16, transcendentals=0),
        name=name,
        compiler_params=pltpu.CompilerParams(vmem_limit_bytes=VLIM),
    )(*args)


def node(count):
    return sds(count, 4, N, 128, dtype=bf16)


def on_device(densities, source, jacobian, pattern, transport, lateral, neighbours, factor, coupling):
    line_count, cell_count, species = densities.shape
    u = densities.reshape(CELLS, N)
    src = source.reshape(CELLS, N)
    tran = transport.reshape(CELLS, N)
    lat = lateral.reshape(CELLS, N)
    coup = coupling.reshape(CELLS, N)
    jac = jacobian.reshape(CELLS, N * N)
    fac = factor.reshape(4, 8, 32, 128).transpose(0, 2, 1, 3).reshape(1024, 128)

    def xor_lat(value, bits):
        return lax.ppermute(value, "lat", [(i, i ^ bits) for i in range(8)])

    def xor_depth(value, bits):
        return lax.ppermute(value, "depth", [(i, i ^ bits) for i in range(32)])

    line_a = xor_lat(densities, 1)
    part, flux = call(
        react, (sds(CELLS, N), sds(N, 128)), jac, u, src, tran, pattern, hbm=5, flops=1 << 30, name="react",
        scratch=[pltpu.VMEM((CELLS, N * N), f32)] + [pltpu.VMEM((CELLS, N), f32)] * 3
        + [pltpu.VMEM((8, 8), jnp.int32), pltpu.SemaphoreType.DMA((8,))],
    )
    line_b = xor_lat(jnp.concatenate([densities, line_a], axis=0), 2)
    quad, n1, full, cols = call(
        tree_leaves,
        (sds(16, 4, N, 256, dtype=bf16), sds(16, 3, N, 128, dtype=bf16), sds(16, 3, N, 128), sds(2, N, 128)),
        fac, coup, part, scratch=[pltpu.VMEM((2, N, 128), f32)], flops=2 << 30, name="tree_leaves",
    )
    top = lax.ppermute(lax.optimization_barrier((densities, cols))[0], "depth", [((i + 1) % 32, i) for i in range(32)])
    line_c = xor_lat(jnp.concatenate([densities, line_a, line_b], axis=0), 6)
    n2, n3, n4, n5, root = call(
        tree_upper,
        (node(8), node(4), node(2), sds(1, N, 128, dtype=bf16), sds(128, 128)),
        n1, full, coup, cols, part, scratch=[pltpu.VMEM((8, 3, N, 128), f32), pltpu.VMEM((4, 3, N, 128), f32)],
        flops=2 << 30, name="tree_upper",
    )
    pay, pair, vs, ws = call(
        upsweep, (sds(128, 128), sds(4, N, 128), sds(7, N, 128), sds(7, N, 128)),
        neighbours, part, line_a, line_b, line_c, top, flux, u, tran, lat, coup, cols, quad, n1, n2, n3, n4, n5, root,
        smem=1, flops=1 << 25, name="upsweep",
    )
    others = [xor_depth(pay, bits) for bits in (1, 2, 3)]
    tees, adds, resp = call(
        prepare,
        (sds(8, N, 128, dtype=bf16), sds(5, N, 128), sds(8, 3, N, 128, dtype=bf16)),
        pair, vs, ws, n1, n2, n3, n4, flops=1 << 30, name="prepare",
    )
    slots = [pltpu.VMEM((4, 128, 128), f32)]
    pay, fun = call(
        combine_four, (sds(128, 128), sds(128, 128)), pay, *others, adds, scratch=slots, flops=1 << 24, name="combine_four",
    )
    other = xor_depth(pay, 7)
    pay, fun = call(
        combine_two, (sds(128, 128), sds(5, N, 128)), pay, other, fun, flops=1 << 24, name="combine_two",
    )
    others = [xor_depth(pay, bits) for bits in (8, 16, 24)]
    out = call(
        downsweep, sds(CELLS, N), pay, *others, fun, cols, adds, resp, quad, n1, tees, scratch=slots, flops=1 << 25,
        name="downsweep",
    )
    return out.reshape(line_count, cell_count, species)


def solution(mesh):
    return jax.shard_map(
        on_device,
        mesh=mesh,
        in_specs=(
            P("lat", "depth", None),
            P("lat", "depth", None),
            P("lat", "depth", None),
            P(),
            P("lat", "depth", None),
            P("lat", "depth", None),
            P("lat", None),
            P("lat", "depth", None),
            P("lat", "depth", None),
        ),
        out_specs=P("lat", "depth", None),
        check_vma=False,
    )
```

```python
import jax
import jax.numpy as jnp
from jax import lax
from jax.experimental import pallas as pl
from jax.experimental.pallas import tpu as pltpu
from jax.sharding import PartitionSpec as P


f32 = jnp.float32
bf16 = jnp.bfloat16

CELLS = 32
N = 64
ZS = 8
VLIM = 16 << 20


def lanes(shape):
    return lax.broadcasted_iota(jnp.int32, shape, len(shape) - 1)


def roll(x, shift):
    shift = shift % x.shape[-1]
    return x if shift == 0 else pltpu.roll(x, shift, x.ndim - 1)


def pack(dup):
    hi = dup.astype(bf16).astype(f32)
    return jnp.where(lanes(dup.shape) < N, hi, dup - hi).astype(bf16)


def mm(a, b):
    r = jnp.dot(a, jnp.concatenate([b, b], axis=0), preferred_element_type=f32)
    return r + roll(r, N)


def rhs(x):
    hi = x.astype(bf16)
    lo = (x - hi.astype(f32)).astype(bf16)
    return jnp.concatenate([hi, hi, lo, lo], axis=0)


def dot(a, y):
    return jnp.dot(jnp.concatenate([a, a], axis=1), y, preferred_element_type=f32)


def column(row):
    return jnp.broadcast_to(row, (128, N)).T


def pair(a, b):
    low = lanes(a.shape) < N
    a_hi, b_hi = a.astype(bf16).astype(f32), b.astype(bf16).astype(f32)
    hi = jnp.where(low, a_hi, b_hi).astype(bf16)
    lo = jnp.where(low, a - a_hi, b - b_hi).astype(bf16)
    return jnp.concatenate([hi, lo], axis=1)


def pair_rhs(x, y):
    def split(z):
        hi = z.astype(bf16).astype(f32)
        return jnp.where(lanes(z.shape) % 64 < CELLS, hi, z - hi).astype(bf16)

    a, b = split(x), split(y)
    return jnp.concatenate([a, b, a, b], axis=0)


def eye2():
    return jnp.where(lanes((N, 128)) % N == lax.broadcasted_iota(jnp.int32, (N, 128), 0), 1.0, 0.0)


def put(node, full, j, p, q, w, u=None):
    node[j, 0], node[j, 1], node[j, 2] = pack(p), pack(q), pack(w)
    full[j, 0], full[j, 1], full[j, 2] = p, q, w
    if u is not None:
        node[j, 3] = pack(u)


def tree_leaves(fac_ref, coup_ref, after_ref, quad_ref, n1_ref, full_ref, cols_ref, rows):
    del after_ref
    c = coup_ref[...]
    cols_ref[0] = column(c[CELLS - 1 : CELLS])
    cols_ref[1] = column(1.0 / c[0:1])
    c2 = jnp.concatenate([c, c], axis=1)
    low = lanes((CELLS, 128)) < N
    eye = eye2()

    def leaf(k):
        g, s = divmod(k, 8)
        x = fac_ref[pl.ds(g * 256 + s, 32, stride=8), :]
        y = roll(x, N)
        rows[k % 2, pl.ds(0, 32, stride=2), :] = jnp.where(low, x, y)
        rows[k % 2, pl.ds(1, 32, stride=2), :] = jnp.where(low, y, x)
        a = rows[k % 2]
        before = max(k - 1, 0)
        return a * c2[before : before + 1] - eye, a * c2[k : k + 1] - eye

    for j in range(CELLS // 2):
        p1, q1 = leaf(2 * j)
        p2, q2 = leaf(2 * j + 1)
        kq1, kp2 = pack(q1), pack(p2)
        p = p1 + p2 + mm(kp2, pack(p1))
        q = q1 + q2 + mm(kq1, pack(q2))
        u = eye + q1 + p2 + mm(kq1, kp2)
        w = (eye + eye) + p1 + q1 + p + mm(kq1, pack(p))
        put(n1_ref, full_ref, j, p, q, w)
        quad_ref[j, 0] = pair(p, p2)
        quad_ref[j, 1] = pair(w, u)
        quad_ref[j, 2] = pair(w, q)
        quad_ref[j, 3] = pair(p, q2)


def tree_upper(n1_ref, full_ref, coup_ref, cols_ref, after_ref, n2_ref, n3_ref, n4_ref, n5_ref, root_ref, fa, fb):
    del after_ref
    node, full = n1_ref, full_ref
    for count, node_to, full_to in ((8, n2_ref, fa), (4, n3_ref, fb), (2, n4_ref, fa), (1, None, None)):
        for j in range(count):
            one, two = 2 * j, 2 * j + 1
            kq1, yp1 = node[one, 1], rhs(full[one, 0])
            u = full[two, 2] + dot(kq1, rhs(full[two, 2]))
            p = full[one, 0] + full[two, 0] + dot(node[two, 0], yp1)
            q = full[one, 1] + full[two, 1] + dot(kq1, rhs(full[two, 1]))
            ku = pack(u)
            w = full[one, 2] + u + dot(ku, yp1)
            if node_to is None:
                eye = eye2()
                n5_ref[0] = ku
                first = coup_ref[0:1]
                scale = 1.0 / jnp.concatenate([first, first], axis=1)
                root_ref[:N] = jnp.where(lanes((N, 128)) < N, (p + eye) * cols_ref[0] * scale, q + eye)
                root_ref[N:] = w * scale
            else:
                put(node_to, full_to, j, p, q, w, u)
        node, full = node_to, full_to


def react(jac_hbm, dens_hbm, src_hbm, tran_hbm, pat_hbm, out_ref, flux_ref, jac_ref, dens_ref, src_ref, tran_ref,
          pat_ref, sems):
    pairs = [(dens_hbm, dens_ref), (pat_hbm, pat_ref), (jac_hbm, jac_ref), (src_hbm, src_ref), (tran_hbm, tran_ref)]
    copies = [pltpu.make_async_copy(a, b, sems.at[i]) for i, (a, b) in enumerate(pairs)]
    for copy in copies:
        copy.start()
    half = lanes((128, N)) % 2 == lax.broadcasted_iota(jnp.int32, (128, N), 0) // N
    half = jnp.where(half, 1.0, 0.0).astype(bf16)
    copies[0].wait()
    copies[1].wait()
    u = dens_ref[...]
    u2 = jnp.concatenate([u, u], axis=1)
    lane8 = lanes((8, 128))
    pat = pat_ref[...].astype(f32)
    mask_rows = jnp.zeros((8, 128), f32)
    for t in range(8):
        mask_rows = jnp.where((lane8 % N) // 8 == t, pat[:, t : t + 1], mask_rows)
    lane = lanes((CELLS, N))
    acc = jnp.zeros((CELLS, N), f32)
    copies[2].wait()
    for m in range(32):
        y = jac_ref[:, m * 128 : (m + 1) * 128] * (u2 * mask_rows[m // 4 : m // 4 + 1])
        hi = y.astype(bf16)
        lo = (y - hi.astype(f32)).astype(bf16)
        z = jnp.dot(hi, half, preferred_element_type=f32) + jnp.dot(lo, half, preferred_element_type=f32)
        acc = jnp.where(lane // 2 == m, z, acc)
    copies[3].wait()
    copies[4].wait()
    tran = tran_ref[...]
    flux = tran * u
    flux_ref[...] = column(flux[CELLS - 1 : CELLS])
    row = lax.broadcasted_iota(jnp.int32, (CELLS, N), 0)
    lower = jnp.where(row == 0, 0.0, pltpu.roll(flux, 1, 0))
    upper = jnp.where(row == CELLS - 1, 0.0, pltpu.roll(u, CELLS - 1, 0))
    out_ref[...] = src_ref[...] - acc + lower + tran * upper


def upsweep(neigh_ref, part_ref, a_ref, b_ref, c_ref, even_ref, odd_ref, flux_ref, dens_ref, tran_ref, lat_ref, coup_ref, cols_ref,
            quad_ref, n1_ref, n2_ref, n3_ref, n4_ref, n5_ref, root_ref, pay_ref, pair_ref, v_ref, w_ref):
    me = lax.axis_index("lat")
    u = dens_ref[...]
    total = jnp.zeros((CELLS, N), f32)
    lines = [(0, u), (1, a_ref[0])] + [(2 + i, b_ref[i]) for i in range(2)]
    lines += [((6, 7, 4, 5)[i], c_ref[i]) for i in range(4)]
    for offset, value in lines:
        line = me ^ offset
        count = jnp.int32(0)
        for j in range(4):
            count = count + (neigh_ref[0, j] == line).astype(jnp.int32)
        total = total + count.astype(f32) * value
    row = lax.broadcasted_iota(jnp.int32, (CELLS, N), 0)
    r = part_ref[...] - lat_ref[...] * (4.0 * u - total)
    depth = lax.axis_index("depth")
    above = jnp.where(depth % 2 == 0, even_ref[0, 0:1], odd_ref[0, 0:1])
    above = jnp.where(depth == lax.axis_size("depth") - 1, 0.0, above)
    r = r + jnp.where(row == CELLS - 1, tran_ref[...] * above, 0.0)
    c = coup_ref[...]
    g = r / jnp.where(row == 0, c, pltpu.roll(c, 1, 0))
    x = []
    for i in range(4):
        rolled = g if i == 0 else pltpu.roll(g, CELLS - i, 0)
        x.append(jnp.concatenate([rolled, rolled], axis=0).T)
    lane2 = lanes((N, N)) % CELLS
    lane = lanes((N, CELLS))
    pair_v, pair_w = [], []
    for half in range(2):
        x0, x1 = x[2 * half], x[2 * half + 1]
        y = pair_rhs(x0, x1)
        v = jnp.zeros((N, N), f32)
        w = jnp.zeros((N, N), f32)
        for j in range(8):
            at = 2 * j + half
            here = lane2 == 4 * j
            v = jnp.where(here, jnp.dot(quad_ref[at, 0], y, preferred_element_type=f32), v)
            w = jnp.where(here, jnp.dot(quad_ref[at, 1], y, preferred_element_type=f32), w)
        v = v[:, :CELLS] + v[:, CELLS:] + x0[:, :CELLS] + x1[:, :CELLS]
        w = w[:, :CELLS] + w[:, CELLS:]
        pair_v.append(v)
        pair_w.append(w)
        pair_ref[half, :, 0:CELLS] = pair_v[half]
        pair_ref[2 + half, :, 0:CELLS] = w
    yv, yw = rhs(pair_v[0]), rhs(pair_w[1])
    v, w = pair_v[0] + pair_v[1], pair_w[0] + pair_w[1]
    dv = jnp.zeros((N, CELLS), f32)
    dw = jnp.zeros((N, CELLS), f32)
    for j in range(8):
        here = lane == 4 * j
        dv = jnp.where(here, dot(n1_ref[2 * j + 1, 0], yv), dv)
        dw = jnp.where(here, dot(n1_ref[2 * j, 1], yw) + dot(n2_ref[j, 3], yv), dw)
    v, w = v + dv, w + dw
    vs = [jnp.broadcast_to(v[:, 4 * j : 4 * j + 1], (N, 128)) for j in range(8)]
    ws = [jnp.broadcast_to(w[:, 4 * j : 4 * j + 1], (N, 128)) for j in range(8)]
    at = 0
    for count, ref, above in ((4, n2_ref, n3_ref), (2, n3_ref, n4_ref), (1, n4_ref, n5_ref)):
        next_v, next_w = [], []
        for j in range(count):
            v1, v2, w1, w2 = vs[2 * j], vs[2 * j + 1], ws[2 * j], ws[2 * j + 1]
            v_ref[at], w_ref[at] = v1, w2
            at += 1
            yv, yw = rhs(v1), rhs(w2)
            u_map = above[j, 3] if count > 1 else above[0]
            next_v.append(v1 + v2 + dot(ref[2 * j + 1, 0], yv))
            next_w.append(w1 + w2 + dot(ref[2 * j, 1], yw) + dot(u_map, yv))
        vs, ws = next_v, next_w
    lane = lanes((N, 128))
    pay_ref[:N] = root_ref[:N]
    tail = jnp.where(lane == N, vs[0] * cols_ref[0] + flux_ref[...], ws[0])
    pay_ref[N:] = jnp.where(lane < N, root_ref[N:], tail)


def wide(packed):
    x = packed.astype(f32)
    return x + roll(x, N)


def prepare(pair_ref, v_ref, w_ref, n1_ref, n2_ref, n3_ref, n4_ref, t_ref, add_ref, resp_ref):
    lane = lanes((N, 128))
    part = lane % CELLS
    eye = eye2()
    nodes = [(None, None, None)]
    ss = jnp.zeros((N, 128), f32)
    aa = jnp.zeros((N, 128), f32)
    vec = {32: 6, 16: 4, 8: 0}
    for size, ref in ((32, n4_ref), (16, n3_ref), (8, n2_ref)):
        ys, ya = rhs(ss), rhs(aa)
        new_s = jnp.zeros((N, 128), f32)
        new_a = jnp.zeros((N, 128), f32)
        children = []
        for j in range(CELLS // size):
            into_s, cross, into_a = nodes[j]
            ep, eq, kw = ref[2 * j, 0], ref[2 * j + 1, 1], ref[2 * j + 1, 2]
            t = wide(kw) + mm(kw, ep)
            kt = pack(t)
            v1, w2 = v_ref[vec[size] + j], w_ref[vec[size] + j]
            t0 = w2 + dot(kw, rhs(v1))
            here = part // size == j
            if size == 32:
                new_s, new_a = v1, t0
            else:
                new_s = jnp.where(here, v1 + dot(ep, ys), new_s)
                new_a = jnp.where(here, t0 + dot(eq, ya) + dot(kt, ys), new_a)
            through = t if into_s is None else dot(kt, rhs(into_s))
            if cross is not None:
                through = through + cross + dot(eq, rhs(cross))
            first_a = eye + wide(eq) if into_a is None else into_a + dot(eq, rhs(into_a))
            second_s = eye + wide(ep) if into_s is None else into_s + dot(ep, rhs(into_s))
            children += [(into_s, through, first_a), (second_s, cross, into_a)]
        nodes = children
        upper = part % size >= size // 2
        ss, aa = jnp.where(upper, ss + new_s, ss), jnp.where(upper, aa, aa + new_a)
    add_ref[2], add_ref[3] = ss, aa
    for j, maps in enumerate(nodes):
        for i, value in enumerate(maps):
            if value is not None:
                resp_ref[j, i] = pack(value)

    def repeat(x):
        x = x + roll(x, CELLS)
        return x + roll(x, 2 * CELLS)

    first = jnp.logical_and(lane % 4 == 0, lane < CELLS)
    v0, v1, w0, w1 = [jnp.where(first, pair_ref[i], 0.0) for i in range(4)]
    y = rhs(v0)
    acc_a = jnp.zeros((N, 128), f32)
    for j in range(8):
        kw = n1_ref[2 * j + 1, 2]
        t_ref[j] = pack(wide(kw) + mm(kw, n1_ref[2 * j, 0]))
        acc_a = jnp.where(lane == 4 * j, dot(kw, y), acc_a)
    acc_a = acc_a + w1
    spread_v = v0 + roll(v0, 1)
    spread_a = acc_a + roll(acc_a, 1)
    add_ref[0] = repeat(spread_v + roll(spread_v, 2))
    add_ref[1] = repeat(spread_a + roll(spread_a, 2))
    add_ref[4] = repeat(w0 + roll(w1, 2) + roll(v0, 1) + roll(v1, 3))


def unpack(b):
    low = lanes((N, 128)) < N
    b1, b2 = b[:N], b[N:]
    r1, r2 = roll(b1, N), roll(b2, N)
    x = jnp.where(low, b1, r1)
    y = jnp.where(low, r1, b1)
    z = jnp.where(low, b2, r2)
    g = jnp.broadcast_to(b2[:, N : N + 1], (N, 128))
    h = jnp.broadcast_to(b2[:, N + 1 : N + 2], (N, 128))
    return x, y, z, g, h


def join(one, two, last=False):
    p1, q1, w1, v1, h1 = one
    p2, q2, w2, v2, h2 = two
    kq1, kp2, kw2 = pack(q1), pack(p2), pack(w2)
    yp1, yv1 = rhs(p1), rhs(v1)
    t = dot(kw2, yp1)
    th = h2 + dot(kw2, yv1)
    v = v2 + dot(kp2, yv1)
    yt, yth = rhs(t), rhs(th)
    w = w1 + dot(kq1, yt)
    h = h1 + dot(kq1, yth)
    yq2 = rhs(q2)
    p, q = (None, None) if last else (dot(kp2, yp1), dot(kq1, yq2))
    return (p, q, w, v, h), (t, th, yp1, yv1, yq2, yt, yth)


def track_first(is_low, one, two, extra):
    eye = eye2()
    t, th = extra[:2]
    return (
        jnp.where(is_low, eye, one[0]),
        jnp.where(is_low, two[1], eye),
        jnp.where(is_low, t, 0.0),
        jnp.where(is_low, 0.0, one[3]),
        jnp.where(is_low, th, 0.0),
    )


def track(is_low, fun, extra):
    f, hh, k, g, e = fun
    _, _, yp1, yv1, yq2, yt, yth = extra
    x1 = pack(jnp.where(is_low, hh, f))
    x2 = pack(jnp.where(is_low, hh, k))
    prod1 = dot(x1, jnp.where(is_low, yq2, yp1))
    prod2 = dot(x2, jnp.where(is_low, yt, yp1))
    vec1 = dot(x1, yv1)
    vec2 = dot(x2, jnp.where(is_low, yth, yv1))
    return (
        jnp.where(is_low, f, prod1),
        jnp.where(is_low, prod1, hh),
        jnp.where(is_low, k + prod2, prod2),
        jnp.where(is_low, g, g + vec1),
        e + vec2,
    )


def put_map(ref, p, q, w, v, h, last=False):
    lane = lanes((N, 128))
    low = lane < N
    tail = jnp.where(low, w, jnp.where(lane == N, v, h))
    if last:
        ref[...] = tail
    else:
        ref[:N] = jnp.where(low, p, q)
        ref[N:] = tail


def fill(slots, at, refs):
    for bits, ref in enumerate(refs):
        slots[at ^ bits] = ref[...]
    return [unpack(slots[i]) for i in range(4)]


def combine_four(own_ref, x1_ref, x2_ref, x3_ref, after_ref, out_ref, fun_out, slots):
    del after_ref
    at = lax.axis_index("depth") % 4
    maps = fill(slots, at, (own_ref, x1_ref, x2_ref, x3_ref))
    lower, extra_lower = join(maps[0], maps[1])
    upper, extra_upper = join(maps[2], maps[3])
    in_lower = at < 2
    mine = lambda x, y: [jnp.where(in_lower, a, b) for a, b in zip(x, y)]
    fun = track_first(
        at % 2 == 0, mine(maps[0], maps[2]), mine(maps[1], maps[3]), mine(extra_lower[:2], extra_upper[:2])
    )
    total, extra = join(lower, upper)
    put_map(out_ref, *total)
    put_map(fun_out, *track(in_lower, fun, extra))


def combine_two(own_ref, other_ref, fun_ref, out_ref, fun_out):
    is_low = lax.axis_index("depth") % ZS < 4
    own, other = own_ref[...], other_ref[...]
    total, extra = join(unpack(jnp.where(is_low, own, other)), unpack(jnp.where(is_low, other, own)))
    put_map(out_ref, *total)
    for i, value in enumerate(track(is_low, unpack(fun_ref[...]), extra)):
        fun_out[i] = value


def downsweep(own_ref, y1_ref, y2_ref, y3_ref, fun_ref, cols_ref, add_ref, resp_ref, quad_ref, n1_ref, t_ref, out_ref,
              slots):
    at = lax.axis_index("depth") // ZS
    maps = fill(slots, at, (own_ref, y1_ref, y2_ref, y3_ref))
    lower, extra_lower = join(maps[0], maps[1], last=True)
    upper, extra_upper = join(maps[2], maps[3], last=True)
    is_low = at < 2
    extra = [jnp.where(is_low, a, b) for a, b in zip(extra_lower, extra_upper)]
    f, hh, k, g, e = track(at % 2 == 0, [fun_ref[i] for i in range(5)], extra)
    yv = rhs(lower[3])
    t = upper[4] + dot(pack(upper[2]), yv)
    up = g + dot(pack(f), yv)
    aa = e + dot(pack(jnp.where(is_low, hh, k)), jnp.where(is_low, rhs(t), yv))
    ss = jnp.where(is_low, g, up) * cols_ref[1]
    lane = lanes((N, 128)) % CELLS
    ys, ya = rhs(ss), rhs(aa)
    part_s, part_a = ss, aa
    for j in range(8):
        here = lane // 4 == j
        if j > 0:
            part_s = jnp.where(here, dot(resp_ref[j, 0], ys), part_s)
        if j < 7:
            part_a = jnp.where(here, dot(resp_ref[j, 1], ys) + dot(resp_ref[j, 2], ya), part_a)
    ss, aa = part_s + add_ref[2], part_a + add_ref[3]
    ys, ya = rhs(ss), rhs(aa)
    ds = jnp.zeros((N, 128), f32)
    da = jnp.zeros((N, 128), f32)
    for j in range(8):
        here = lane // 4 == j
        ds = jnp.where(here, dot(n1_ref[2 * j, 0], ys), ds)
        da = jnp.where(here, dot(n1_ref[2 * j + 1, 1], ya) + dot(t_ref[j], ys), da)
    upper = lane % 4 >= 2
    ss, aa = (
        jnp.where(upper, ss + add_ref[0] + ds, ss),
        jnp.where(upper, aa, aa + add_ref[1] + da),
    )
    y = pair_rhs(ss, aa)
    x = jnp.zeros((N, 128), f32)
    for j in range(CELLS // 2):
        x = jnp.where(lane == 2 * j, jnp.dot(quad_ref[j, 2], y, preferred_element_type=f32), x)
        x = jnp.where(lane == 2 * j + 1, jnp.dot(quad_ref[j, 3], y, preferred_element_type=f32), x)
    x = x + roll(x, CELLS) + (aa + add_ref[4] + jnp.where(lane % 2 == 1, ss, 0.0))
    out_ref[...] = x.T[:CELLS]


def sds(*shape, dtype=f32):
    return jax.ShapeDtypeStruct(shape, dtype)


def call(body, outs, *args, scratch=(), smem=0, hbm=0, flops=0):
    args = [pltpu.with_memory_space_constraint(x, pltpu.HBM) if smem <= i < smem + hbm else x for i, x in enumerate(args)]
    spaces = [pltpu.SMEM] * smem + [pltpu.HBM] * hbm + [pltpu.VMEM] * (len(args) - smem - hbm)
    return pl.pallas_call(
        body,
        out_shape=outs,
        in_specs=[pl.BlockSpec(memory_space=space) for space in spaces],
        out_specs=jax.tree.map(lambda _: pl.BlockSpec(memory_space=pltpu.VMEM), outs),
        scratch_shapes=scratch,
        cost_estimate=pl.CostEstimate(flops=flops, bytes_accessed=1 << 16, transcendentals=0),
        compiler_params=pltpu.CompilerParams(vmem_limit_bytes=VLIM),
    )(*args)


def node(count):
    return sds(count, 4, N, 128, dtype=bf16)


def on_device(densities, source, jacobian, pattern, transport, lateral, neighbours, factor, coupling):
    line_count, cell_count, species = densities.shape
    u = densities.reshape(CELLS, N)
    src = source.reshape(CELLS, N)
    tran = transport.reshape(CELLS, N)
    lat = lateral.reshape(CELLS, N)
    coup = coupling.reshape(CELLS, N)
    jac = jacobian.reshape(CELLS, N * N)
    fac = factor.reshape(4, 8, 32, 128).transpose(0, 2, 1, 3).reshape(1024, 128)

    def xor_lat(value, bits):
        return lax.ppermute(value, "lat", [(i, i ^ bits) for i in range(8)])

    def xor_depth(value, bits):
        return lax.ppermute(value, "depth", [(i, i ^ bits) for i in range(32)])

    def named_round(value, all_bits):
        received = []
        for bits in all_bits:
            received.append(xor_depth(value, bits))
        return received

    line_a = xor_lat(densities, 1)
    part, flux = call(
        react, (sds(CELLS, N), sds(N, 128)), jac, u, src, tran, pattern, hbm=5, flops=1 << 30,
        scratch=[pltpu.VMEM((CELLS, N * N), f32)] + [pltpu.VMEM((CELLS, N), f32)] * 3
        + [pltpu.VMEM((8, 8), jnp.int32), pltpu.SemaphoreType.DMA((5,))],
    )
    line_b = xor_lat(jnp.concatenate([densities, line_a], axis=0), 2)
    quad, n1, full, cols = call(
        tree_leaves,
        (sds(16, 4, N, 256, dtype=bf16), sds(16, 3, N, 128, dtype=bf16), sds(16, 3, N, 128), sds(2, N, 128)),
        fac, coup, part, scratch=[pltpu.VMEM((2, N, 128), f32)], flops=2 << 30,
    )
    top_even = xor_depth(lax.optimization_barrier((densities, cols))[0], 1)
    top_odd = lax.ppermute(
        lax.optimization_barrier((densities, line_b))[0], ("depth", "lat"),
        [(8 * i + l, 8 * (i + 1 if i % 2 else i - 1) + l if 0 < i < 31 else 8 * i + (l ^ 1))
         for i in range(32) for l in range(8)],
    )
    line_c = xor_lat(jnp.concatenate([densities, line_a, line_b], axis=0), 6)
    n2, n3, n4, n5, root = call(
        tree_upper,
        (node(8), node(4), node(2), sds(1, N, 128, dtype=bf16), sds(128, 128)),
        n1, full, coup, cols, part, scratch=[pltpu.VMEM((8, 3, N, 128), f32), pltpu.VMEM((4, 3, N, 128), f32)],
        flops=2 << 30,
    )
    pay, pair, vs, ws = call(
        upsweep, (sds(128, 128), sds(4, N, 128), sds(7, N, 128), sds(7, N, 128)),
        neighbours, part, line_a, line_b, line_c, top_even, top_odd, flux, u, tran, lat, coup, cols, quad, n1, n2, n3, n4, n5, root,
        smem=1, flops=1 << 25,
    )
    others = named_round(pay, (1, 2, 3))
    tees, adds, resp = call(
        prepare,
        (sds(8, N, 128, dtype=bf16), sds(5, N, 128), sds(8, 3, N, 128, dtype=bf16)),
        pair, vs, ws, n1, n2, n3, n4, flops=1 << 30,
    )
    slots = [pltpu.VMEM((4, 128, 128), f32)]
    pay, fun = call(combine_four, (sds(128, 128), sds(128, 128)), pay, *others, adds, scratch=slots, flops=1 << 24)
    other = xor_depth(pay, 6)
    pay, fun = call(combine_two, (sds(128, 128), sds(5, N, 128)), pay, other, fun, flops=1 << 24)
    others = named_round(pay, (8, 16, 24))
    out = call(
        downsweep, sds(CELLS, N), pay, *others, fun, cols, adds, resp, quad, n1, tees, scratch=slots, flops=1 << 25,
    )
    return out.reshape(line_count, cell_count, species)


def solution(mesh):
    return jax.shard_map(
        on_device,
        mesh=mesh,
        in_specs=(
            P("lat", "depth", None),
            P("lat", "depth", None),
            P("lat", "depth", None),
            P(),
            P("lat", "depth", None),
            P("lat", "depth", None),
            P("lat", None),
            P("lat", "depth", None),
            P("lat", "depth", None),
        ),
        out_specs=P("lat", "depth", None),
        check_vma=False,
    )
```
